32 devices in a mesh: head: 4 (over x, core), blk: 8 (over z, y).
Axes of the slice: x: 2, y: 2, z: 4, core: 2. Of those that a mesh axis runs over, the one named last changes fastest.
Arguments:
- layer_input: bfloat16 [4096, 1024], P(('head', 'blk')), may hold values from -6 to 6
- out_grad: bfloat16 [4096, 1024], P(('head', 'blk')), may hold values from -6 to 6
- lengths: int32 [4], replicated, may hold values from 1 to 2048, 3072 in all
- ln_attn: bfloat16 [1024], P(('head', 'blk')), may hold values from 0.5 to 1.5
- w_qkv: bfloat16 [1024, 3072], P(('head', 'blk')), may hold values from -0.1875 to 0.1875
- w_attn_out: bfloat16 [1024, 1024], P(('head', 'blk')), may hold values from -6 to 6
- ln_mlp: bfloat16 [1024], P(('head', 'blk')), may hold values from 0.5 to 1.5
- w_in: bfloat16 [1024, 5248], P(('head', 'blk')), may hold values from -0.1875 to 0.1875
- w_mlp_out: bfloat16 [2624, 1024], P(None, ('head', 'blk')), may hold values from -0.125 to 0.125
Outputs:
- layer_output: float32 [4096, 1024], P(('head', 'blk'))
- input_grad: float32 [4096, 1024], P(('head', 'blk'))
- d_ln_attn: float32 [1024], P(('head', 'blk'))
- d_w_qkv: float32 [1024, 3072], P(('head', 'blk'))
- d_w_attn_out: float32 [1024, 1024], P(('head', 'blk'))
- d_ln_mlp: float32 [1024], P(('head', 'blk'))
- d_w_in: float32 [1024, 5248], P(('head', 'blk'))
- d_w_mlp_out: float32 [2624, 1024], P(None, ('head', 'blk'))
The draws below stay inside these ranges and needn't reach their ends.
Inputs may be any that keep to these rules, and one draw needn't show every extreme that they name: lengths of the 4 sequences packed from slot 0; they sum to 3072 and the longest is exactly 2048; the remaining slots are padding.
All inputs are finite; a program needn't handle non-finite values.
Results may differ from the reference program's by a relative error of at most 0.023.
Values may be sent and summed in bfloat16 or wider, within the bound.
A program may use at most 192 MiB of HBM per device.

```python
import math
import jax
import jax.numpy as jnp
import numpy as np
from jax import lax

D = 1024
H = 16
DH = 64
FF = 2624
NSEQ = 4
TOKENS = 4096
VALID = 3072
LONGEST = 2048


def spiked(entries, own_key, source, target, parts, factor):
    def block_of(dim):
        return (jnp.arange(entries.shape[dim]) // (entries.shape[dim] // parts)).reshape((-1,) + (1,) * (entries.ndim - 1 - dim))

    one_side = jax.random.permutation(own_key, parts)[block_of(target)]
    other_side = (block_of(target) + parts // 2) % parts
    return jnp.where((block_of(source) == one_side) | (block_of(source) == other_side), factor * entries, entries)


def levels(key, dims, cuts, smallest, top_value):
    def one(dim, shards_of):
        steps = jax.random.uniform(jax.random.fold_in(jax.random.fold_in(key, 6), dim), (shards_of,), jnp.float32, smallest / len(cuts), top_value / len(cuts))
        return jnp.repeat(jnp.exp(steps), dims[dim] // shards_of).reshape((-1,) + (1,) * (len(dims) - dim - 1))

    loudness = one(*cuts[0])
    for cut in cuts[1:]:
        loudness = loudness * one(*cut)
    return loudness


def length_profile(number_of, total, bound, skew):
    loads = [(1 << 20) // math.isqrt(standing ** skew) + 1 for standing in range(2, number_of + 1)]
    rest, counts = total - bound - (number_of - 1), [1] * (number_of - 1)
    while rest > 0:
        free = [i for i in range(number_of - 1) if counts[i] < bound]
        whole, remaining = sum([loads[i] for i in free]), rest
        for i in free:
            extra = min(bound - counts[i], max(1, remaining * loads[i] // whole), rest)
            counts[i] = counts[i] + extra
            rest = rest - extra
    return np.array([bound] + counts)


def ragged(stream_key, number_of, total, reach, lean):
    if number_of == 2:
        one = jax.random.randint(stream_key, (), max(1, total - reach), min(reach, total - 1) + 1)
        return jnp.stack([one, total - one])
    tallies = jnp.asarray(length_profile(number_of, total, reach, lean), jnp.int32)
    twos = (number_of - 1) // 2
    donor, taker = tallies[1:1 + 2 * twos:2], tallies[2:2 + 2 * twos:2]
    room = jnp.minimum(donor - 1, reach - taker)
    shifted = jax.random.randint(jax.random.fold_in(stream_key, 1), (twos,), 0, 1 << 20) % (room + 1)
    tallies = tallies.at[1:1 + 2 * twos:2].set(donor - shifted).at[2:2 + 2 * twos:2].set(taker + shifted)
    return tallies[jax.random.permutation(jax.random.fold_in(stream_key, 2), number_of)]


def bell_draw(rng, shape, deviation, most, split=(), held_as=jnp.bfloat16):
    factor_of = levels(rng, shape, split, -0.22, 0.18) if split else 1.0
    values = jax.random.normal(rng, shape, jnp.float32) * deviation * factor_of
    return jnp.minimum(jnp.maximum(values, -most), most).astype(held_as)


def bell_draw_with(rng, shape, width, most, cuts, heavy, held_as=jnp.bfloat16):
    result = width * jax.random.normal(rng, shape, jnp.float32)
    if cuts:
        result = result * levels(rng, shape, cuts, -0.22, 0.18)
    return jnp.clip(spiked(result, jax.random.fold_in(rng, 3), *heavy), -most, most).astype(held_as)


def setup_inputs(seed: int = 0) -> dict:
    streams_of = jax.random.split(jax.random.key(seed), 10)
    layer_input = bell_draw_with(streams_of[0], (TOKENS, D), 1.0, 6.0, ((0, 32),), (0, 1, 32, 2.75))
    out_grad = bell_draw_with(streams_of[1], (TOKENS, D), 1.0, 6.0, ((0, 32),), (0, 1, 32, 2.75))
    lengths = ragged(streams_of[2], NSEQ, VALID, LONGEST, 2).astype(jnp.int32)
    ln_attn = jnp.clip(1.0 + 0.1 * jax.random.normal(streams_of[3], (D,), jnp.float32), 0.5, 1.5).astype(jnp.bfloat16)
    w_qkv = bell_draw(streams_of[4], (D, 3 * D), D ** -0.5, 0.1875, ((0, 32),))
    w_attn_out = bell_draw(streams_of[5], (D, D), 1 ** -0.5, 6.0, ((0, 32),))
    ln_mlp = jnp.clip(1.0 + 0.1 * jax.random.normal(streams_of[6], (D,), jnp.float32), 0.5, 1.5).astype(jnp.bfloat16)
    w_in = bell_draw(streams_of[7], (D, 2 * FF), D ** -0.5, 0.1875, ((0, 32),))
    w_mlp_out = bell_draw(streams_of[8], (FF, D), FF ** -0.5, 0.125, ((1, 32),))
    return dict(layer_input=layer_input, out_grad=out_grad, lengths=lengths, ln_attn=ln_attn, w_qkv=w_qkv, w_attn_out=w_attn_out, ln_mlp=ln_mlp, w_in=w_in, w_mlp_out=w_mlp_out)


@jax.custom_vjp
def low(v):
    return lax.optimization_barrier(v.astype(jnp.bfloat16)).astype(jnp.float32)

@jax.custom_vjp
def low_back(v):
    return v

def low_keep(v):
    return (low(v), None)

def low_pass(kept, grad):
    return (grad,)

def back_keep(v):
    return (v, None)

def back_low(kept, grad):
    return (low(grad),)
low.defvjp(low_keep, low_pass)
low_back.defvjp(back_keep, back_low)
ROPE_BASE = 160000.0
NORM_EPS = 1e-05
MASK_FLOOR = -1e+30
HIGHEST_PREC = lax.Precision.HIGHEST

def layer_norm(values, gain):
    centre = values - lax.optimization_barrier(jnp.mean(values, axis=-1, keepdims=True))
    variance = lax.optimization_barrier(jnp.mean(centre * centre, axis=-1, keepdims=True))
    return centre * lax.rsqrt(variance + NORM_EPS) * gain

def locate(rows_at, lengths):
    seq_ends = jnp.cumsum(lengths).astype(jnp.int32)
    segment = lax.optimization_barrier(jnp.sum((rows_at[:, None] >= seq_ends[None, :]).astype(jnp.int32), axis=1))
    seq_starts = jnp.concatenate([seq_ends - lengths, seq_ends[-1:]]).astype(jnp.int32)
    picked = segment[:, None] == lax.iota(jnp.int32, seq_starts.shape[0])[None, :]
    begins = lax.optimization_barrier(jnp.sum(jnp.where(picked, seq_starts[None, :], 0), axis=1)).astype(jnp.int32)
    return (segment, rows_at - begins)

def rotate(values, position, sign_value):
    half_dim = values.shape[-1] // 2
    inv_freq = jnp.power(ROPE_BASE, -2.0 * lax.iota(jnp.float32, half_dim) / values.shape[-1])
    angles = position.astype(jnp.float32)[:, None] * inv_freq[None, :]
    cosine = jnp.cos(angles)[:, None, :]
    sine_part = sign_value * jnp.sin(angles)[:, None, :]
    front_part = values[..., :half_dim]
    back_part = values[..., half_dim:]
    return jnp.concatenate([front_part * cosine - back_part * sine_part, back_part * cosine + front_part * sine_part], axis=-1)

def attention(queries, keys_all, values_all, segment):
    q_span = min(512, TOKENS)
    k_window = min(TOKENS, 2 * LONGEST + q_span)

    def one_block(block_at):
        q_first = (block_at * q_span).astype(jnp.int32)
        k_first = jnp.clip(q_first - LONGEST, 0, TOKENS - k_window).astype(jnp.int32)
        query_rows = lax.dynamic_slice_in_dim(queries, q_first, q_span, 0)
        key_rows = lax.dynamic_slice_in_dim(keys_all, k_first, k_window, 0)
        value_rows = lax.dynamic_slice_in_dim(values_all, k_first, k_window, 0)
        seg_query = lax.dynamic_slice_in_dim(segment, q_first, q_span, 0)
        seg_key = lax.dynamic_slice_in_dim(segment, k_first, k_window, 0)
        scores = low_back(jnp.einsum('qhd,khd->hqk', query_rows, key_rows, precision=HIGHEST_PREC) * 0.125)
        same_seq = (seg_query[:, None] == seg_key[None, :])[None]
        masked = jnp.where(same_seq, scores, MASK_FLOOR)
        log_total = jax.nn.logsumexp(masked, axis=-1, keepdims=True)
        probs = low(jnp.where(same_seq, jnp.exp(masked - log_total), 0.0))
        return jnp.einsum('hqk,khd->qhd', probs, value_rows, precision=HIGHEST_PREC)
    blocks = lax.map(jax.checkpoint(one_block), lax.iota(jnp.int32, TOKENS // q_span))
    return blocks.reshape(TOKENS, H, DH)

def forward(x_in, ln_attn, w_qkv, w_attn_out, ln_mlp, w_in, w_mlp_out, segment, position, valid):
    normed_in = low(layer_norm(x_in, ln_attn))
    qkv_all = low_back(jnp.dot(normed_in, w_qkv, precision=HIGHEST_PREC)).reshape(TOKENS, 3, H, DH)
    queries = low_back(low(rotate(qkv_all[:, 0], position, 1.0)))
    keys_all = low_back(low(rotate(qkv_all[:, 1], position, 1.0)))
    values_all = low_back(low(qkv_all[:, 2]))
    mixed = attention(queries, keys_all, values_all, segment)
    mixed = low_back(low(mixed)).reshape(TOKENS, D)
    attn_out = low_back(jnp.dot(mixed, w_attn_out, precision=HIGHEST_PREC))
    hidden = x_in + attn_out
    normed_mid = low(layer_norm(hidden, ln_mlp))
    gate_up = low_back(jnp.dot(normed_mid, w_in, precision=HIGHEST_PREC))
    product = low(jax.nn.gelu(gate_up[:, :FF], approximate=False) * gate_up[:, FF:])
    mlp_out = low_back(jnp.dot(product, w_mlp_out, precision=HIGHEST_PREC))
    return valid[:, None] * (hidden + mlp_out)

def reference(layer_input, out_grad, lengths, ln_attn, w_qkv, w_attn_out, ln_mlp, w_in, w_mlp_out):
    segment, position = locate(lax.iota(jnp.int32, TOKENS), lengths)
    valid = (segment < NSEQ).astype(jnp.float32)
    weights = tuple((tensor.astype(jnp.float32) for tensor in (ln_attn, w_qkv, w_attn_out, ln_mlp, w_in, w_mlp_out)))

    def apply_layer(x_in, ln_one, w_one, w_two, ln_two, w_three, w_four):
        return forward(x_in, ln_one, w_one, w_two, ln_two, w_three, w_four, segment, position, valid)
    output, pull_back = jax.vjp(apply_layer, layer_input.astype(jnp.float32), *weights)
    gradients = pull_back(out_grad.astype(jnp.float32))
    return (output, gradients[0], gradients[1], gradients[2], gradients[3], gradients[4], gradients[5], gradients[6])
```

```python
import functools
import math

import jax
import jax.numpy as jnp
from jax import lax
from jax.experimental import pallas as pl
from jax.experimental.pallas import tpu as pltpu
from jax.sharding import PartitionSpec as P

DH = 64
ROPE_BASE = 160000.0
NORM_EPS = 1e-05
MASK_FLOOR = -1e30
KEY_BLOCK = 512
EXP_SCALE = 0.125 * math.log2(math.e)
BF16 = jnp.bfloat16
F32 = jnp.float32
MESH_ID = pl.DeviceIdType.MESH
ANY = pl.BlockSpec(memory_space=pl.ANY)
VM = pl.BlockSpec(memory_space=pltpu.VMEM)


def dims():
    nh = lax.axis_size("head")
    nb = lax.axis_size("blk")
    return nh, nb


def me():
    return lax.axis_index("head"), lax.axis_index("blk")


def comm_call(body, name, cid, out_shape, in_specs, out_specs, scratch, args, vmem=None):
    return pl.pallas_call(
        body,
        out_shape=out_shape,
        in_specs=in_specs,
        out_specs=out_specs,
        scratch_shapes=scratch,
        name=name,
        compiler_params=pltpu.CompilerParams(
            collective_id=cid, has_side_effects=True, vmem_limit_bytes=vmem
        ),
    )(*args)


def remote(src, dst, send, recv, h, b):
    return pltpu.make_async_remote_copy(
        src_ref=src,
        dst_ref=dst,
        send_sem=send,
        recv_sem=recv,
        device_id=(h, b),
        device_id_type=MESH_ID,
    )


def barrier_with(peers):
    sem = pltpu.get_barrier_semaphore()
    for h, b in peers:
        pl.semaphore_signal(sem, inc=1, device_id=(h, b), device_id_type=MESH_ID)
    pl.semaphore_wait(sem, len(peers))


def barrier_all(nh, nb, h, b):
    sem = pltpu.get_barrier_semaphore()

    @pl.loop(1, nh * nb)
    def _(i):
        pl.semaphore_signal(
            sem,
            inc=1,
            device_id=((h + i // nb) % nh, (b + i % nb) % nb),
            device_id_type=MESH_ID,
        )

    pl.semaphore_wait(sem, nh * nb - 1)


def head_peers(nh, h, b):
    return [((h + i) % nh, b) for i in range(1, nh)]


class HeadGather:
    def __init__(self, nh, h, b, src, dst, sems):
        self.nh, self.h, self.b, self.dst, self.sems = nh, h, b, dst, sems
        nx = nh // 2
        self.nx = nx
        x, c = h // 2, h % 2
        sib = x * 2 + 1 - c
        self.sib = sib
        self.across = []
        for k in range(1, nx):
            self.across.append(
                remote(src, dst.at[h], sems.at[0, k], sems.at[1, k], ((x + k) % nx) * 2 + c, b)
            )
        self.near = remote(src, dst.at[h], sems.at[0, 0], sems.at[1, 0], sib, b)
        self.local = pltpu.make_async_copy(src, dst.at[h], sems.at[2, 0])
        self.forward = []
        for k in range(1, nx):
            got = ((x + nx - k) % nx) * 2 + c
            self.forward.append(
                remote(dst.at[got], dst.at[got], sems.at[2, k], sems.at[3, k], sib, b)
            )

    @staticmethod
    def sem_shape(nh):
        return pltpu.SemaphoreType.DMA((4, nh // 2))

    def start(self):
        for cp in self.across:
            cp.start()
        self.near.start()
        self.local.start()

    def pass_on(self):
        for cp, fw in zip(self.across, self.forward):
            cp.wait_recv()
            fw.start()

    def finish(self):
        for cp in self.across:
            cp.wait_send()
        self.near.wait()
        self.local.wait()
        for fw in self.forward:
            fw.wait()


def first_body(nh, nb, x_ref, g_ref, wq_ref, wo_ref, wm_ref, xg, gg, wq_all, wo_all, wm_h, xs, gs, qsem, osem, msem, lsem):
    h, b = me()
    barrier_all(nh, nb, h, b)
    own = h * nb + b
    gx = HeadGather(nh, h, b, x_ref, xg, xs)
    gg_ = HeadGather(nh, h, b, g_ref, gg, gs)
    gx.start()

    def wq_copy(i):
        th, tb = (h + i // nb) % nh, (b + i % nb) % nb
        return remote(wq_ref.at[th], wq_all.at[own], qsem.at[0, i], qsem.at[1, i], th, tb)

    def wo_copy(i):
        return remote(wo_ref, wo_all.at[b], osem.at[0, i], osem.at[1, i], h, (b + i) % nb)

    @pl.loop(1, nh * nb)
    def _(i):
        wq_copy(i).start()

    lq = pltpu.make_async_copy(wq_ref.at[h], wq_all.at[own], lsem.at[0])
    lo = pltpu.make_async_copy(wo_ref, wo_all.at[b], lsem.at[1])
    lm = pltpu.make_async_copy(wm_ref.at[h], wm_h.at[h], lsem.at[2])
    for cp in (lq, lo, lm):
        cp.start()
    mcs = [
        remote(wm_ref.at[(h + i) % nh], wm_h.at[h], msem.at[0, i], msem.at[1, i], (h + i) % nh, b)
        for i in range(1, nh)
    ]
    for cp in mcs:
        cp.start()
    gx.pass_on()
    gg_.start()

    @pl.loop(1, nb)
    def _(i):
        wo_copy(i).start()

    gg_.pass_on()
    gx.finish()
    gg_.finish()
    for cp in (lq, lo, lm):
        cp.wait()
    for cp in mcs:
        cp.wait()

    @pl.loop(1, nh * nb)
    def _(i):
        wq_copy(i).wait()

    @pl.loop(1, nb)
    def _(i):
        wo_copy(i).wait()


def first_exchange(x, g, wq, wo, wm):
    nh, nb = dims()
    rows, width = x.shape
    own_rows = wq.shape[1]
    shapes = (
        jax.ShapeDtypeStruct((nh, rows, width), BF16),
        jax.ShapeDtypeStruct((nh, rows, width), BF16),
        jax.ShapeDtypeStruct((nh * nb, own_rows, wq.shape[2]), BF16),
        jax.ShapeDtypeStruct((nb,) + wo.shape, BF16),
        jax.ShapeDtypeStruct(wm.shape, BF16),
    )
    dma = pltpu.SemaphoreType.DMA
    return comm_call(
        functools.partial(first_body, nh, nb),
        "first_exchange",
        0,
        shapes,
        [ANY] * 5,
        [ANY] * 5,
        [
            HeadGather.sem_shape(nh),
            HeadGather.sem_shape(nh),
            dma((2, nh * nb)),
            dma((2, nb)),
            dma((2, nh)),
            dma((3,)),
        ],
        (x, g, wq, wo, wm),
    )


class Place:
    def __init__(self, nh, nb, hl):
        h, b = me()
        self.h, self.b, self.hl = h, b, hl
        self.x, self.c = h // 2, h % 2
        self.cb = nb // (2 * hl)
        self.qs = 2 * self.cb
        self.nz = nb // self.qs
        self.sib = self.x * 2 + 1 - self.c
        self.split = b % self.qs
        self.zi = b // self.qs
        self.t = b // self.cb
        self.u = b % self.cb
        self.my_l = self.t // 2
        self.my_src_h = self.x * 2 + self.t % 2

    def query_dest(self, l):
        return self.x * 2 + self.split % 2, (2 * l + self.c) * self.cb + self.split // 2

    def query_source(self, zi):
        return self.my_src_h, zi * self.qs + self.u * 2 + self.c


def barrier_plane(pc, nb):
    sem = pltpu.get_barrier_semaphore()

    @pl.loop(0, nb)
    def _(i):
        pl.semaphore_signal(
            sem, inc=1, device_id=(pc.sib, (pc.b + i) % nb), device_id_type=MESH_ID
        )

    @pl.loop(1, nb)
    def _(i):
        pl.semaphore_signal(sem, inc=1, device_id=(pc.h, (pc.b + i) % nb), device_id_type=MESH_ID)

    pl.semaphore_wait(sem, 2 * nb - 1)


def routed(pc, src, dst, send, recv, th, tb, act):
    mine = jnp.logical_and(th == pc.h, tb == pc.b)

    @pl.when(mine)
    def _():
        if act == "start":
            pltpu.make_async_copy(src, dst, recv).start()

    @pl.when(jnp.logical_not(mine))
    def _():
        cp = remote(src, dst, send, recv, th, tb)
        if act == "start":
            cp.start()
        else:
            cp.wait_send()


def wait_on(ref, sem):
    pltpu.make_async_copy(ref, ref, sem).wait()


def queries_out(pc, q_ref, qin, qsem, act):
    for l in range(pc.hl):
        th, tb = pc.query_dest(l)
        routed(pc, q_ref.at[l], qin.at[pc.zi], qsem.at[0, l], qsem.at[1, pc.zi], th, tb, act)


def queries_back(pc, o_ref, og, osem, act):
    for zi in range(pc.nz):
        th, tb = pc.query_source(zi)
        routed(pc, o_ref.at[zi], og.at[pc.my_l], osem.at[0, zi], osem.at[1, pc.my_l], th, tb, act)


def to_heads_body(nh, nb, hl, q_ref, kv_ref, qin, kvin, qsem, ksem, fsem):
    pc = Place(nh, nb, hl)
    barrier_plane(pc, nb)
    core = pc.b % 2

    def keys_out(act):
        for l in range(hl):
            for u in range(pc.cb):
                routed(
                    pc,
                    kv_ref.at[l],
                    kvin.at[:, pc.b],
                    ksem.at[0, l * pc.cb + u],
                    ksem.at[1, pc.b // 2],
                    pc.x * 2 + core,
                    (2 * l + pc.c) * pc.cb + u,
                    act,
                )

    keys_out("start")
    queries_out(pc, q_ref, qin, qsem, "start")

    def forward(k):
        at = kvin.at[:, 2 * k + pc.c]
        return remote(at, at, fsem.at[0, k], fsem.at[1, k], pc.sib, pc.b)

    @pl.loop(0, nb // 2)
    def _(k):
        wait_on(kvin.at[:, 2 * k + pc.c], ksem.at[1, k])
        forward(k).start()

    keys_out("wait_send")
    queries_out(pc, q_ref, qin, qsem, "wait_send")
    for zi in range(pc.nz):
        wait_on(qin.at[zi], qsem.at[1, zi])

    @pl.loop(0, nb // 2)
    def _(k):
        forward(k).wait()


def to_heads(q, kv):
    nh, nb = dims()
    hl, _, group = q.shape
    cb = nb // (2 * hl)
    nz = nb // (2 * cb)
    rows = group // nh
    dma = pltpu.SemaphoreType.DMA
    return comm_call(
        functools.partial(to_heads_body, nh, nb, hl),
        "to_heads",
        1,
        (
            jax.ShapeDtypeStruct((nz, DH, group), BF16),
            jax.ShapeDtypeStruct((nh, nb, rows, 2 * DH), BF16),
        ),
        [ANY] * 2,
        [ANY] * 2,
        [dma((2, max(hl, nz))), dma((2, max(hl * cb, nb // 2))), dma((2, nb // 2))],
        (q, kv),
    )


def move_body(nh, nb, hl, outward, q_ref, qin, qsem):
    pc = Place(nh, nb, hl)
    barrier_plane(pc, nb)
    fn = queries_out if outward else queries_back
    fn(pc, q_ref, qin, qsem, "start")
    fn(pc, q_ref, qin, qsem, "wait_send")
    for i in range(pc.nz if outward else hl):
        wait_on(qin.at[i], qsem.at[1, i])


def move_queries(q, hl, outward, cid):
    nh, nb = dims()
    nz = nb // (2 * (nb // (2 * hl)))
    count = nz if outward else hl
    return comm_call(
        functools.partial(move_body, nh, nb, hl, outward),
        "queries_out" if outward else "queries_back",
        cid,
        jax.ShapeDtypeStruct((count,) + q.shape[1:], BF16),
        [ANY],
        ANY,
        [pltpu.SemaphoreType.DMA((2, max(hl, nz)))],
        (q,),
    )


def grads_back_body(nh, nb, hl, dq_ref, dkv_ref, dq_out, dkv_out, got, sums, qsem, psem, ksem):
    pc = Place(nh, nb, hl)
    barrier_plane(pc, nb)

    def pair(k):
        return remote(
            dkv_ref.at[:, 2 * k + 1 - pc.c], got.at[k], psem.at[0, k], psem.at[1, k], pc.sib, pc.b
        )

    def back(k, act):
        routed(
            pc,
            sums.at[k],
            dkv_out.at[pc.my_l, pc.u],
            ksem.at[0, k],
            ksem.at[1, pc.my_l * pc.cb + pc.u],
            pc.my_src_h,
            2 * k + pc.c,
            act,
        )

    half = nb // 2

    @pl.loop(0, half)
    def _(k):
        pair(k).start()

    queries_back(pc, dq_ref, dq_out, qsem, "start")

    @pl.loop(0, half)
    def _(k):
        pair(k).wait_recv()
        sums[k] = (dkv_ref[:, 2 * k + pc.c].astype(F32) + got[k].astype(F32)).astype(BF16)
        back(k, "start")

    @pl.loop(0, half)
    def _(k):
        pair(k).wait_send()
        back(k, "wait_send")

    queries_back(pc, dq_ref, dq_out, qsem, "wait_send")
    for l in range(hl):
        wait_on(dq_out.at[l], qsem.at[1, l])
        for u in range(pc.cb):
            wait_on(dkv_out.at[l, u], ksem.at[1, l * pc.cb + u])


def grads_back(dq, dkv, hl):
    nh, nb = dims()
    cb = nb // (2 * hl)
    nz = nb // (2 * cb)
    rows = dkv.shape[2]
    dma = pltpu.SemaphoreType.DMA
    return comm_call(
        functools.partial(grads_back_body, nh, nb, hl),
        "grads_back",
        2,
        (
            jax.ShapeDtypeStruct((hl,) + dq.shape[1:], BF16),
            jax.ShapeDtypeStruct((hl, cb, nh, rows, 2 * DH), BF16),
        ),
        [ANY, VM],
        [ANY, ANY],
        [
            pltpu.VMEM((nb // 2, nh, rows, 2 * DH), BF16),
            pltpu.VMEM((nb // 2, nh, rows, 2 * DH), BF16),
            dma((2, max(hl, nz))),
            dma((2, nb // 2)),
            dma((2, max(hl * cb, nb // 2))),
        ],
        (dq, dkv),
        vmem=40 << 20,
    )


def query_tile(ref):
    return jnp.concatenate([ref[0], ref[1]], axis=1)


def allowed(block_at, first_ref, last_ref, lanes):
    at = block_at * KEY_BLOCK + lax.broadcasted_iota(jnp.int32, (KEY_BLOCK, lanes), 0)
    return jnp.logical_and(at >= first_ref[0], at < last_ref[0])


def attend_body(lo_ref, hi_ref, q_ref, kv_ref, first_ref, last_ref, o_ref, of_ref, lse_ref):
    tile = pl.program_id(0)
    q = query_tile(q_ref)
    lanes = q.shape[1]
    q_pad = jnp.concatenate([q, jnp.zeros_like(q)], axis=0)

    def step(j, carry):
        top, total, acc = carry
        kv = kv_ref[pl.ds(pl.multiple_of(j * KEY_BLOCK, KEY_BLOCK), KEY_BLOCK), :]
        s = jnp.dot(kv, q_pad, preferred_element_type=F32)
        s = jnp.where(allowed(j, first_ref, last_ref, lanes), s, MASK_FLOOR)
        new_top = jnp.maximum(top, jnp.max(s, axis=0, keepdims=True))
        p = jnp.exp2((s - new_top) * EXP_SCALE)
        alpha = jnp.exp2((top - new_top) * EXP_SCALE)
        total = total * alpha + jnp.sum(p, axis=0, keepdims=True)
        acc = acc * alpha + lax.dot_general(
            kv, p.astype(BF16), (((0,), (0,)), ((), ())), preferred_element_type=F32
        )
        return new_top, total, acc

    top, total, acc = lax.fori_loop(
        lo_ref[tile],
        hi_ref[tile],
        step,
        (
            jnp.full((1, lanes), MASK_FLOOR, F32),
            jnp.zeros((1, lanes), F32),
            jnp.zeros((2 * DH, lanes), F32),
        ),
    )
    o = acc[DH:] / total
    half = lanes // 2
    for i in range(2):
        part = o[:, i * half : (i + 1) * half]
        of_ref[i] = part
        o_ref[i] = part.astype(BF16)
    lse_ref[0] = top * EXP_SCALE + jnp.log2(total)


def attend_specs(kv_rows, rows, pairs):
    tile_spec = pl.BlockSpec((2, DH, rows), lambda i, *_: (i % pairs, 0, i // pairs))
    row_spec = pl.BlockSpec((1, 1, 2 * rows), lambda i, *_: (i, 0, 0))
    kv_spec = pl.BlockSpec((kv_rows, 2 * DH), lambda i, *_: (0, 0))
    return tile_spec, row_spec, kv_spec


def attend(q, kv, first, last, lo, hi, rows):
    nz, _, group = q.shape
    tiles = lo.shape[0]
    tile_spec, row_spec, kv_spec = attend_specs(kv.shape[0], rows, nz // 2)
    return pl.pallas_call(
        attend_body,
        grid_spec=pltpu.PrefetchScalarGridSpec(
            num_scalar_prefetch=2,
            grid=(tiles,),
            in_specs=[tile_spec, kv_spec, row_spec, row_spec],
            out_specs=[tile_spec, tile_spec, row_spec],
        ),
        out_shape=(
            jax.ShapeDtypeStruct(q.shape, BF16),
            jax.ShapeDtypeStruct(q.shape, F32),
            jax.ShapeDtypeStruct((tiles, 1, 2 * rows), F32),
        ),
        name="attend",
        compiler_params=pltpu.CompilerParams(vmem_limit_bytes=48 << 20),
    )(lo, hi, q, kv, first, last)


def attend_grad_body(lo_ref, hi_ref, q_ref, do_ref, of_ref, kv_ref, first_ref, last_ref, lse_ref, dq_ref, dkv_ref, acc_ref):
    tile = pl.program_id(0)

    @pl.when(tile == 0)
    def _():
        acc_ref[...] = jnp.zeros_like(acc_ref)

    q = query_tile(q_ref)
    do = query_tile(do_ref)
    lanes = q.shape[1]
    zero = jnp.zeros_like(q)
    both = jnp.concatenate(
        [jnp.concatenate([q, zero], axis=0), jnp.concatenate([zero, do], axis=0)], axis=1
    )
    delta = jnp.sum(do.astype(F32) * query_tile(of_ref), axis=0, keepdims=True)
    lse = lse_ref[0]

    def step(j, dq):
        at = pl.ds(pl.multiple_of(j * KEY_BLOCK, KEY_BLOCK), KEY_BLOCK)
        kv = kv_ref[at, :]
        sd = jnp.dot(kv, both, preferred_element_type=F32)
        s, dp = sd[:, :lanes], sd[:, lanes:]
        p = jnp.exp2(
            jnp.where(
                allowed(j, first_ref, last_ref, lanes), s * EXP_SCALE - lse, MASK_FLOOR
            )
        )
        ds = (p * (dp - delta)).astype(BF16)
        acc_ref[at, :] += lax.dot_general(
            jnp.concatenate([ds, p.astype(BF16)], axis=1),
            both,
            (((1,), (1,)), ((), ())),
            preferred_element_type=F32,
        )
        return dq + lax.dot_general(
            kv, ds, (((0,), (0,)), ((), ())), preferred_element_type=F32
        )

    dq = lax.fori_loop(lo_ref[tile], hi_ref[tile], step, jnp.zeros((2 * DH, lanes), F32))
    half = lanes // 2
    for i in range(2):
        dq_ref[i] = (dq[:DH, i * half : (i + 1) * half] * 0.125).astype(BF16)

    @pl.when(tile == pl.num_programs(0) - 1)
    def _():
        lane = lax.broadcasted_iota(jnp.int32, (1, 2 * DH), 1)
        dkv_ref[...] = (acc_ref[...] * jnp.where(lane < DH, 0.125, 1.0)).astype(BF16)


def attend_grad(q, do, of, kv, first, last, lse, lo, hi, rows):
    nz, _, group = q.shape
    tiles = lo.shape[0]
    tile_spec, row_spec, kv_spec = attend_specs(kv.shape[0], rows, nz // 2)
    return pl.pallas_call(
        attend_grad_body,
        grid_spec=pltpu.PrefetchScalarGridSpec(
            num_scalar_prefetch=2,
            grid=(tiles,),
            in_specs=[tile_spec, tile_spec, tile_spec, kv_spec, row_spec, row_spec, row_spec],
            out_specs=[tile_spec, kv_spec],
            scratch_shapes=[pltpu.VMEM(kv.shape, F32)],
        ),
        out_shape=(jax.ShapeDtypeStruct(q.shape, BF16), jax.ShapeDtypeStruct(kv.shape, BF16)),
        name="attend_grad",
        compiler_params=pltpu.CompilerParams(vmem_limit_bytes=56 << 20),
    )(lo, hi, q, do, of, kv, first, last, lse)


class HeadSum:
    def __init__(self, nh, h, b, part, near, far, out, sems):
        self.nx = nh // 2
        self.x, self.c = h // 2, h % 2
        self.h, self.part, self.near, self.far, self.out = h, part, near, far, out
        sib = self.x * 2 + 1 - self.c
        self.pairs = [
            remote(
                part.at[((self.x + k) % self.nx) * 2 + 1 - self.c],
                near.at[k],
                sems.at[0, k],
                sems.at[1, k],
                sib,
                b,
            )
            for k in range(self.nx)
        ]
        self.across = [
            remote(
                out.at[k],
                far.at[k],
                sems.at[2, k],
                sems.at[3, k],
                ((self.x + k) % self.nx) * 2 + self.c,
                b,
            )
            for k in range(1, self.nx)
        ]

    @staticmethod
    def sem_shape(nh):
        return pltpu.SemaphoreType.DMA((4, nh // 2))

    @staticmethod
    def buffers(nh, rows, width):
        return [pltpu.VMEM((nh // 2, rows, width), BF16)] * 3

    def start(self):
        for k in list(range(1, self.nx)) + [0]:
            self.pairs[k].start()

    def send(self):
        for k in range(1, self.nx):
            self.pairs[k].wait_recv()
            at = ((self.x + k) % self.nx) * 2 + self.c
            self.out[k] = (self.part[at].astype(F32) + self.near[k].astype(F32)).astype(BF16)
            self.across[k - 1].start()

    def total(self):
        self.pairs[0].wait_recv()
        total = self.part[self.h].astype(F32) + self.near[0].astype(F32)
        for k in range(1, self.nx):
            self.across[k - 1].wait_recv()
            total = total + self.far[k].astype(F32)
        return total

    def finish(self):
        for cp in self.pairs:
            cp.wait_send()
        for cp in self.across:
            cp.wait_send()


def norm_of(values):
    centre = values - jnp.mean(values, axis=-1, keepdims=True)
    scale = lax.rsqrt(jnp.mean(centre * centre, axis=-1, keepdims=True) + NORM_EPS)
    return centre * scale, scale


def norm_pull(grad, normed, scale):
    one = jnp.mean(grad, axis=-1, keepdims=True)
    two = jnp.mean(grad * normed, axis=-1, keepdims=True)
    return scale * (grad - one - normed * two)


def mid_body(nh, part, x_ref, hid_ref, ng_ref, near, far, out, nbuf, ssem, gsem):
    h, b = me()
    barrier_with(head_peers(nh, h, b))
    hs = HeadSum(nh, h, b, part, near, far, out, ssem)
    hs.start()
    hs.send()
    hid = x_ref[...].astype(F32) + hs.total()
    hid_ref[...] = hid
    nbuf[...] = norm_of(hid)[0].astype(BF16)
    hg = HeadGather(nh, h, b, nbuf, ng_ref, gsem)
    hg.start()
    hg.pass_on()
    hs.finish()
    hg.finish()


def mid_exchange(part, x):
    nh, _ = dims()
    rows, width = x.shape
    return comm_call(
        functools.partial(mid_body, nh),
        "mid_exchange",
        3,
        (jax.ShapeDtypeStruct(x.shape, F32), jax.ShapeDtypeStruct((nh, rows, width), BF16)),
        [VM, VM],
        [VM, VM],
        HeadSum.buffers(nh, rows, width)
        + [pltpu.VMEM((rows, width), BF16), HeadSum.sem_shape(nh), HeadGather.sem_shape(nh)],
        (part, x),
    )


def back_body(nh, dpart, ypart, hid_ref, g_ref, valid_ref, y_ref, dh_ref, dg_ref, n1, f1, o1, n2, f2, o2, dbuf, s1, s2, gsem):
    h, b = me()
    barrier_with(head_peers(nh, h, b))
    hd = HeadSum(nh, h, b, dpart, n1, f1, o1, s1)
    hy = HeadSum(nh, h, b, ypart, n2, f2, o2, s2)
    hd.start()
    hd.send()
    hy.start()
    hid = hid_ref[...]
    normed, scale = norm_of(hid)
    valid = valid_ref[...]
    gy = g_ref[...].astype(F32) * valid
    dh = gy + norm_pull(hd.total(), normed, scale)
    dh_ref[...] = dh
    dbuf[...] = dh.astype(BF16)
    hg = HeadGather(nh, h, b, dbuf, dg_ref, gsem)
    hg.start()
    hy.send()
    hg.pass_on()
    y_ref[...] = valid * (hid + hy.total())
    hd.finish()
    hy.finish()
    hg.finish()


def back_exchange(dpart, ypart, hid, g, valid):
    nh, _ = dims()
    rows, width = hid.shape
    return comm_call(
        functools.partial(back_body, nh),
        "back_exchange",
        4,
        (
            jax.ShapeDtypeStruct(hid.shape, F32),
            jax.ShapeDtypeStruct(hid.shape, F32),
            jax.ShapeDtypeStruct((nh, rows, width), BF16),
        ),
        [VM] * 5,
        [VM] * 3,
        HeadSum.buffers(nh, rows, width)
        + HeadSum.buffers(nh, rows, width)
        + [
            pltpu.VMEM((rows, width), BF16),
            HeadSum.sem_shape(nh),
            HeadSum.sem_shape(nh),
            HeadGather.sem_shape(nh),
        ],
        (dpart, ypart, hid, g, valid),
    )


def last_body(nh, nb, dpart, x_ref, dh_ref, gq_ref, go_ref, gm_ref, dx_ref, gq_all, go_all, gm_all, near, far, out, ssem, qsem, osem, msem, lsem):
    h, b = me()
    barrier_all(nh, nb, h, b)
    own = h * nb + b
    hs = HeadSum(nh, h, b, dpart, near, far, out, ssem)
    hs.start()

    def gq_copy(i):
        th, tb = (h + i // nb) % nh, (b + i % nb) % nb
        return remote(
            gq_ref.at[th * nb + tb], gq_all.at[own], qsem.at[0, i], qsem.at[1, i], th, tb
        )

    def go_copy(i):
        tb = (b + i) % nb
        return remote(go_ref.at[tb], go_all.at[b], osem.at[0, i], osem.at[1, i], h, tb)

    @pl.loop(1, nh * nb)
    def _(i):
        gq_copy(i).start()

    @pl.loop(1, nb)
    def _(i):
        go_copy(i).start()

    lq = pltpu.make_async_copy(gq_ref.at[own], gq_all.at[own], lsem.at[0])
    lo = pltpu.make_async_copy(go_ref.at[b], go_all.at[b], lsem.at[1])
    lm = pltpu.make_async_copy(gm_ref.at[h], gm_all.at[h], lsem.at[2])
    for cp in (lq, lo, lm):
        cp.start()
    mcs = [
        remote(gm_ref.at[(h + i) % nh], gm_all.at[h], msem.at[0, i], msem.at[1, i], (h + i) % nh, b)
        for i in range(1, nh)
    ]
    for cp in mcs:
        cp.start()
    hs.send()
    normed, scale = norm_of(x_ref[...].astype(F32))
    dx_ref[...] = dh_ref[...] + norm_pull(hs.total(), normed, scale)
    hs.finish()
    for cp in (lq, lo, lm):
        cp.wait()
    for cp in mcs:
        cp.wait()

    @pl.loop(1, nh * nb)
    def _(i):
        gq_copy(i).wait()

    @pl.loop(1, nb)
    def _(i):
        go_copy(i).wait()


def last_exchange(dpart, x, dh, gq, go, gm):
    nh, nb = dims()
    rows, width = x.shape
    dma = pltpu.SemaphoreType.DMA
    return comm_call(
        functools.partial(last_body, nh, nb),
        "last_exchange",
        5,
        (
            jax.ShapeDtypeStruct(x.shape, F32),
            jax.ShapeDtypeStruct(gq.shape, BF16),
            jax.ShapeDtypeStruct(go.shape, BF16),
            jax.ShapeDtypeStruct(gm.shape, BF16),
        ),
        [VM, VM, VM, ANY, ANY, ANY],
        [VM, ANY, ANY, ANY],
        HeadSum.buffers(nh, rows, width)
        + [HeadSum.sem_shape(nh), dma((2, nh * nb)), dma((2, nb)), dma((2, nh)), dma((3,))],
        (dpart, x, dh, gq, go, gm),
    )


def dot(a, b, ca=1, cb=0):
    return lax.dot_general(a, b, (((ca,), (cb,)), ((), ())), preferred_element_type=F32)


def spans(rows_at, lengths):
    ends = jnp.cumsum(lengths)
    total = ends[-1]
    starts = ends - lengths
    inside = jnp.logical_and(rows_at[..., None] >= starts, rows_at[..., None] < ends)
    first = jnp.sum(jnp.where(inside, starts, 0), axis=-1)
    last = jnp.sum(jnp.where(inside, ends, 0), axis=-1)
    pad = rows_at >= total
    return jnp.where(pad, total, first), last, pad


def turn(values, cos, sin):
    half = DH // 2
    a, b = values[:, :half], values[:, half:]
    return jnp.concatenate([a * cos - b * sin, b * cos + a * sin], axis=1)


def shards(layer_input, out_grad, lengths, ln_attn, w_qkv, w_attn_out, ln_mlp, w_in, w_mlp_out):
    nh, nb = dims()
    h, b = me()
    rows, width = layer_input.shape
    heads = width // DH
    hl = heads // nh
    lw = hl * DH
    group = nh * rows
    slots = nh * nb * rows
    own_rows = w_qkv.shape[0]
    ff = w_mlp_out.shape[0]
    fl = ff // nh
    cb = nb // (2 * hl)
    qs = 2 * cb
    nz = nb // qs

    gain_attn = ln_attn.astype(F32)[:, None]
    gain_mlp = ln_mlp.astype(F32)[:, None]
    wq_own = w_qkv.astype(F32).reshape(own_rows, 3, nh, lw).transpose(2, 0, 1, 3)
    wq_own = wq_own.reshape(nh, own_rows, 3 * lw)
    win_own = w_in.astype(F32).reshape(own_rows, 2, nh, fl).transpose(2, 0, 1, 3)
    win_own = win_own.reshape(nh, own_rows, 2 * fl)
    wd_own = w_mlp_out.T.reshape(own_rows, nh, fl).transpose(1, 0, 2)
    wq_send = (wq_own * gain_attn).astype(BF16)
    wm_send = jnp.concatenate([(win_own * gain_mlp).astype(BF16), wd_own], axis=2)

    xg, gg, wq, wo, wm_h = first_exchange(layer_input, out_grad, wq_send, w_attn_out, wm_send)
    wm = lax.all_gather(wm_h, "blk", axis=1, tiled=True).reshape(width, 3 * fl)
    wq = wq.reshape(width, 3 * lw)
    wo = wo.reshape(lw, width)

    row = lax.iota(jnp.int32, rows)
    group_at = ((lax.iota(jnp.int32, nh) * nb + b)[:, None] * rows + row).reshape(group)
    first, _, pad = spans(group_at, lengths)
    position = (group_at - first).astype(F32)
    half = DH // 2
    inv_freq = jnp.power(ROPE_BASE, -2.0 * lax.iota(F32, half) / DH)
    angles = inv_freq[:, None] * position[None, :]
    cos, sin = jnp.cos(angles), jnp.sin(angles)
    valid_group = jnp.where(pad, 0.0, 1.0)
    own_at = (h * nb + b) * rows + row
    valid = jnp.where(spans(own_at, lengths)[2], 0.0, 1.0)[:, None]

    split = (b % cb) * 2 + h % 2
    tile_block = (
        lax.iota(jnp.int32, nh)[:, None, None] * nb
        + (lax.iota(jnp.int32, nz // 2)[None, :, None] * 2 + lax.iota(jnp.int32, 2)) * qs
        + split
    )
    tiles = nh * nz // 2
    query_at = (tile_block[..., None] * rows + row).reshape(tiles, 1, 2 * rows)
    q_first, q_last, q_pad = spans(query_at, lengths)
    q_last = jnp.where(q_pad, slots, q_last)
    lo = q_first[:, 0, 0] // KEY_BLOCK
    hi = (q_last[:, 0, -1] + KEY_BLOCK - 1) // KEY_BLOCK

    n1 = norm_of(xg.reshape(group, width).astype(F32))[0].astype(BF16)
    qt = dot(wq[:, :lw], n1, 0, 1).reshape(hl, DH, group)
    kt = dot(wq[:, lw : 2 * lw], n1, 0, 1).reshape(hl, DH, group)
    vt = dot(wq[:, 2 * lw :], n1, 0, 1).reshape(hl, DH, group)
    qt = turn(qt, cos, sin).astype(BF16)
    kt = turn(kt, cos, sin).astype(BF16)
    kv = jnp.concatenate([kt, vt.astype(BF16)], axis=1).transpose(0, 2, 1)
    qin, kvin = to_heads(qt, kv.reshape(hl, nh, rows, 2 * DH))
    kv_all = kvin.reshape(slots, 2 * DH)
    ot, of, lse = attend(qin, kv_all, q_first, q_last, lo, hi, rows)
    og = move_queries(ot, hl, False, 6).reshape(lw, group)
    part = dot(og, wo, 0, 0).astype(BF16).reshape(nh, rows, width)
    hid, n2 = mid_exchange(part, layer_input)

    n2 = n2.reshape(group, width)
    gy = (gg.reshape(group, width).astype(F32) * valid_group[:, None]).astype(BF16)
    win, wd = wm[:, : 2 * fl], wm[:, 2 * fl :]
    z = dot(n2, win)
    dm = dot(gy, wd)
    gate, up = z[:, :fl], z[:, fl:]
    cdf = 0.5 * (1.0 + lax.erf(gate * math.sqrt(0.5)))
    act = gate * cdf
    slope = cdf + gate * jnp.exp(-0.5 * gate * gate) * (1.0 / math.sqrt(2.0 * math.pi))
    m = (act * up).astype(BF16)
    dz = jnp.concatenate([dm * up * slope, dm * act], axis=1).astype(BF16)
    ypart = dot(m, wd, 1, 1).astype(BF16).reshape(nh, rows, width)
    dpart = dot(dz, win, 1, 1).astype(BF16).reshape(nh, rows, width)
    y_out, dh, dg = back_exchange(dpart, ypart, hid, out_grad, valid)
    g_in = dot(n2, dz, 0, 0).astype(BF16)
    g_down = dot(gy, m, 0, 0).astype(BF16)
    gm = jnp.concatenate([g_in, g_down], axis=1).reshape(nh, nb * own_rows, 3 * fl)
    gm = lax.psum_scatter(gm, "blk", scatter_dimension=1, tiled=True)

    dg = dg.reshape(group, width)
    dot_t = dot(wo, dg, 1, 1).astype(BF16).reshape(hl, DH, group)
    g_out = dot(og, dg).astype(BF16).reshape(nb, own_rows, width)
    do_in = move_queries(dot_t, hl, True, 7)
    dq, dkv = attend_grad(qin, do_in, of, kv_all, q_first, q_last, lse, lo, hi, rows)
    dqg, dkvg = grads_back(dq, dkv.reshape(nh, nb, rows, 2 * DH), hl)
    dkv_t = jnp.sum(dkvg.astype(F32), axis=1).reshape(hl, group, 2 * DH).transpose(0, 2, 1)
    dq_t = turn(dqg.astype(F32), cos, -sin).astype(BF16).reshape(lw, group)
    dk_t = turn(dkv_t[:, :DH].astype(BF16).astype(F32), cos, -sin).astype(BF16).reshape(lw, group)
    dv_t = dkv_t[:, DH:].astype(BF16).reshape(lw, group)
    dqkv_t = jnp.concatenate([dq_t, dk_t, dv_t], axis=0)
    g_qkv = dot(n1, dqkv_t, 0, 1).astype(BF16).reshape(nh * nb, own_rows, 3 * lw)
    dpart1 = dot(dqkv_t, wq, 0, 1).astype(BF16).reshape(nh, rows, width)
    dx, gq_all, go_all, gm_all = last_exchange(
        dpart1, layer_input, dh, g_qkv, g_out, gm.reshape(nh, own_rows, 3 * fl)
    )

    gq_sum = jnp.sum(gq_all.astype(F32).reshape(nh, nb, own_rows, 3 * lw), axis=1)
    d_ln_attn = jnp.sum(gq_sum * wq_own, axis=(0, 2))
    d_wqkv = (gq_sum * gain_attn).reshape(nh, own_rows, 3, lw).transpose(1, 2, 0, 3)
    d_wqkv = d_wqkv.reshape(own_rows, 3 * width)
    d_wout = jnp.sum(go_all.astype(F32), axis=0)
    gm_all = gm_all.astype(F32)
    gin = gm_all[:, :, : 2 * fl]
    d_ln_mlp = jnp.sum(gin * win_own, axis=(0, 2))
    d_win = (gin * gain_mlp).reshape(nh, own_rows, 2, fl).transpose(1, 2, 0, 3)
    d_win = d_win.reshape(own_rows, 2 * ff)
    d_wdown = gm_all[:, :, 2 * fl :].transpose(0, 2, 1).reshape(ff, own_rows)
    return (y_out, dx, d_ln_attn, d_wqkv, d_wout, d_ln_mlp, d_win, d_wdown)


def solution(mesh):
    both = ("head", "blk")
    row_split = P(both, None)
    return jax.shard_map(
        shards,
        mesh=mesh,
        in_specs=(
            row_split,
            row_split,
            P(),
            P(both),
            row_split,
            row_split,
            P(both),
            row_split,
            P(None, both),
        ),
        out_specs=(
            row_split,
            row_split,
            P(both),
            row_split,
            row_split,
            P(both),
            row_split,
            P(None, both),
        ),
        check_vma=False,
    )
```

```python
import functools
import math

import jax
import jax.numpy as jnp
from jax import lax
from jax.experimental import pallas as pl
from jax.experimental.pallas import tpu as pltpu
from jax.sharding import PartitionSpec as P

DH = 64
ROPE_BASE = 160000.0
NORM_EPS = 1e-05
MASK_FLOOR = -1e30
KEY_BLOCK = 512
EXP_SCALE = 0.125 * math.log2(math.e)
BF16 = jnp.bfloat16
F32 = jnp.float32
MESH_ID = pl.DeviceIdType.MESH
ANY = pl.BlockSpec(memory_space=pl.ANY)
VM = pl.BlockSpec(memory_space=pltpu.VMEM)


def dims():
    nh = lax.axis_size("head")
    nb = lax.axis_size("blk")
    return nh, nb


def me():
    return lax.axis_index("head"), lax.axis_index("blk")


def comm_call(body, name, cid, out_shape, in_specs, out_specs, scratch, args, vmem=None):
    return pl.pallas_call(
        body,
        out_shape=out_shape,
        in_specs=in_specs,
        out_specs=out_specs,
        scratch_shapes=scratch,
        name=name,
        compiler_params=pltpu.CompilerParams(
            collective_id=cid, has_side_effects=True, vmem_limit_bytes=vmem
        ),
    )(*args)


def remote(src, dst, send, recv, h, b):
    return pltpu.make_async_remote_copy(
        src_ref=src,
        dst_ref=dst,
        send_sem=send,
        recv_sem=recv,
        device_id=(h, b),
        device_id_type=MESH_ID,
    )


def signal(h, b):
    pl.semaphore_signal(
        pltpu.get_barrier_semaphore(), inc=1, device_id=(h, b), device_id_type=MESH_ID
    )


def signal_head(nh, h, b):
    for i in range(1, nh):
        signal((h + i) % nh, b)


def wait_head(nh):
    pl.semaphore_wait(pltpu.get_barrier_semaphore(), nh - 1)


def signal_all(nh, nb, h, b):
    @pl.loop(1, nh * nb)
    def _(i):
        signal((h + i // nb) % nh, (b + i % nb) % nb)


def wait_all(nh, nb):
    pl.semaphore_wait(pltpu.get_barrier_semaphore(), nh * nb - 1)


class HeadGather:
    def __init__(self, nh, h, b, src, dst, sems):
        self.nh, self.h, self.b, self.dst, self.sems = nh, h, b, dst, sems
        nx = nh // 2
        self.nx = nx
        x, c = h // 2, h % 2
        sib = x * 2 + 1 - c
        self.sib = sib
        self.across = []
        for k in range(1, nx):
            self.across.append(
                remote(src, dst.at[h], sems.at[0, k], sems.at[1, k], ((x + k) % nx) * 2 + c, b)
            )
        self.near = remote(src, dst.at[h], sems.at[0, 0], sems.at[1, 0], sib, b)
        self.local = pltpu.make_async_copy(src, dst.at[h], sems.at[2, 0])
        self.forward = []
        for k in range(1, nx):
            got = ((x + nx - k) % nx) * 2 + c
            self.forward.append(
                remote(dst.at[got], dst.at[got], sems.at[2, k], sems.at[3, k], sib, b)
            )

    @staticmethod
    def sem_shape(nh):
        return pltpu.SemaphoreType.DMA((4, nh // 2))

    def start(self):
        for cp in self.across:
            cp.start()
        self.near.start()
        self.local.start()

    def pass_on(self):
        for cp, fw in zip(self.across, self.forward):
            cp.wait_recv()
            fw.start()

    def finish(self):
        for cp in self.across:
            cp.wait_send()
        self.near.wait()
        self.local.wait()
        for fw in self.forward:
            fw.wait()


def lane_roll(values, shift):
    return pltpu.roll(values, shift % values.shape[1], 1)


def lanes_of(values):
    return lax.broadcasted_iota(jnp.int32, (1, values.shape[1]), 1)


def widen(values, width):
    extra = width - values.shape[1]
    if extra <= 0:
        return values[:, :width]
    return jnp.concatenate([values, jnp.zeros((values.shape[0], extra), values.dtype)], axis=1)


def ff_widths(fl):
    up = lambda v: (v + 127) // 128 * 128
    return up(3 * fl), up(2 * fl), 2 * fl // 128 * 128


class PairedSpread:
    def __init__(self, nh, nb, h, b, block, out, sems, over_head):
        self.nh = nh if over_head else 1
        self.nb, self.h, self.b, self.block, self.out, self.sems = nb, h, b, block, out, sems
        self.over_head = over_head
        self.nk = nb // 2
        self.y, self.k = b % 2, b // 2
        self.count = self.nh * self.nk

    @staticmethod
    def sem_shape(n):
        return pltpu.SemaphoreType.DMA((4, n))

    def place(self, h, b):
        return self.out.at[h * self.nb + b] if self.over_head else self.out.at[b]

    def target(self, i, sign):
        dh, dk = i // self.nk, i % self.nk
        if sign < 0:
            dh, dk = self.nh - dh, self.nk - dk
        th = (self.h + dh) % self.nh if self.over_head else self.h
        return th, ((self.k + dk) % self.nk) * 2 + self.y

    def send(self, i):
        th, tb = self.target(i, 1)
        return remote(
            self.block(th), self.place(self.h, self.b), self.sems.at[0, i], self.sems.at[1, i], th, tb
        )

    def forward(self, i):
        ref = self.place(*self.target(i, -1))
        return remote(
            ref, ref, self.sems.at[2, i], self.sems.at[3, i], self.h, self.b + 1 - 2 * self.y
        )

    def local(self):
        return pltpu.make_async_copy(
            self.block(self.h), self.place(self.h, self.b), self.sems.at[0, 0]
        )

    def start(self):
        @pl.loop(1, self.count)
        def _(i):
            self.send(i).start()

        self.local().start()

    def pass_on(self):
        self.local().wait()
        self.forward(0).start()

        @pl.loop(1, self.count)
        def _(i):
            self.send(i).wait_recv()
            self.forward(i).start()

    def finish(self):
        @pl.loop(1, self.count)
        def _(i):
            self.send(i).wait_send()

        @pl.loop(0, self.count)
        def _(i):
            self.forward(i).wait()


def first_body(nh, nb, lw, fl, x_ref, wq_ref, ga_ref, win_hbm, gf_ref, wd_hbm, xg, wm_h, wq_all, pack, wmp, win_ref, wd_ref, xs, sems, msem, stage):
    h, b = me()
    loads = [
        pltpu.make_async_copy(win_hbm, win_ref, stage.at[0]),
        pltpu.make_async_copy(wd_hbm, wd_ref, stage.at[1]),
    ]
    for cp in loads:
        cp.start()
    signal_all(nh, nb, h, b)
    gain = ga_ref[...]
    width = nh * lw
    for i in range(nh):
        for c in range(3):
            at = c * width + i * lw
            pack[i, :, c * lw : (c + 1) * lw] = (
                wq_ref[:, at : at + lw].astype(F32) * gain
            ).astype(BF16)
    wait_all(nh, nb)
    spread = PairedSpread(nh, nb, h, b, lambda th: pack.at[th], wq_all, sems, True)
    gx = HeadGather(nh, h, b, x_ref, xg, xs)
    gx.start()
    spread.start()
    for cp in loads:
        cp.wait()
    total, _, _ = ff_widths(fl)
    ff = nh * fl
    win = win_ref[...].astype(F32) * gf_ref[...]
    wd = widen(wd_ref[...].astype(F32), total if total > ff else (ff + 127) // 128 * 128)
    lane = lax.broadcasted_iota(jnp.int32, (1, total), 1)
    for i in range(nh):
        gate = widen(lane_roll(win, -i * fl), total)
        up = widen(lane_roll(win, fl - ff - i * fl), total)
        down = widen(lane_roll(wd, 2 * fl - i * fl), total)
        piece = jnp.where(
            lane < fl,
            gate,
            jnp.where(lane < 2 * fl, up, jnp.where(lane < 3 * fl, down, 0.0)),
        )
        wmp[i] = piece.astype(BF16)
    own = pltpu.make_async_copy(wmp.at[h], wm_h.at[h], msem.at[0, 0])
    own.start()
    copies = [
        remote(wmp.at[(h + i) % nh], wm_h.at[h], msem.at[0, i], msem.at[1, i], (h + i) % nh, b)
        for i in range(1, nh)
    ]
    for cp in copies:
        cp.start()
    gx.pass_on()
    spread.pass_on()
    spread.finish()
    gx.finish()
    own.wait()
    for cp in copies:
        cp.wait()


def first_exchange(x, w_qkv, gain_attn, w_in, gain_mlp, wd_t, fl):
    nh, nb = dims()
    rows, width = x.shape
    lw = width // nh
    own_rows = w_in.shape[0]
    total = ff_widths(fl)[0]
    dma = pltpu.SemaphoreType.DMA
    return comm_call(
        functools.partial(first_body, nh, nb, lw, fl),
        "first_exchange",
        0,
        (
            jax.ShapeDtypeStruct((nh, rows, width), BF16),
            jax.ShapeDtypeStruct((nh, own_rows, total), BF16),
            jax.ShapeDtypeStruct((nh * nb, own_rows, 3 * lw), BF16),
        ),
        [ANY, VM, VM, ANY, VM, ANY],
        [ANY, ANY, ANY],
        [
            pltpu.VMEM((nh, own_rows, 3 * lw), BF16),
            pltpu.VMEM((nh, own_rows, total), BF16),
            pltpu.VMEM(w_in.shape, BF16),
            pltpu.VMEM(wd_t.shape, BF16),
            HeadGather.sem_shape(nh),
            PairedSpread.sem_shape(nh * nb // 2),
            dma((2, nh)),
            dma((2,)),
        ],
        (x, w_qkv, gain_attn, w_in, gain_mlp, wd_t),
        vmem=60 << 20,
    )


class Place:
    def __init__(self, nh, nb, hl):
        h, b = me()
        self.h, self.b, self.hl = h, b, hl
        self.x, self.c = h // 2, h % 2
        self.cb = nb // (2 * hl)
        self.qs = 2 * self.cb
        self.nz = nb // self.qs
        self.sib = self.x * 2 + 1 - self.c
        self.split = b % self.qs
        self.zi = b // self.qs
        self.t = b // self.cb
        self.u = b % self.cb
        self.my_l = self.t // 2
        self.my_src_h = self.x * 2 + self.t % 2

    def query_dest(self, l):
        return self.x * 2 + self.split % 2, (2 * l + self.c) * self.cb + self.split // 2

    def query_source(self, zi):
        return self.my_src_h, zi * self.qs + self.u * 2 + self.c


def signal_plane(pc, nb):
    @pl.loop(0, nb)
    def _(i):
        signal(pc.sib, (pc.b + i) % nb)

    @pl.loop(1, nb)
    def _(i):
        signal(pc.h, (pc.b + i) % nb)


def signal_plane_and_head(pc, nh, nb):
    signal_plane(pc, nb)
    for k in range(1, nh // 2):
        for core in range(2):
            signal(((pc.x + k) % (nh // 2)) * 2 + core, pc.b)


def wait_plane(nb):
    pl.semaphore_wait(pltpu.get_barrier_semaphore(), 2 * nb - 1)


def wait_plane_and_head(nh, nb):
    pl.semaphore_wait(pltpu.get_barrier_semaphore(), 2 * nb - 1 + nh - 2)


def routed(pc, src, dst, send, recv, th, tb, act):
    mine = jnp.logical_and(th == pc.h, tb == pc.b)

    @pl.when(mine)
    def _():
        if act == "start":
            pltpu.make_async_copy(src, dst, recv).start()

    @pl.when(jnp.logical_not(mine))
    def _():
        cp = remote(src, dst, send, recv, th, tb)
        if act == "start":
            cp.start()
        else:
            cp.wait_send()


def wait_on(ref, sem):
    pltpu.make_async_copy(ref, ref, sem).wait()


def queries_out(pc, q_ref, qin, qsem, act):
    for l in range(pc.hl):
        th, tb = pc.query_dest(l)
        routed(pc, q_ref.at[l], qin.at[pc.zi], qsem.at[0, l], qsem.at[1, pc.zi], th, tb, act)


def queries_back(pc, o_ref, og, osem, act):
    for zi in range(pc.nz):
        th, tb = pc.query_source(zi)
        routed(pc, o_ref.at[zi], og.at[pc.my_l], osem.at[0, zi], osem.at[1, pc.my_l], th, tb, act)


def halves_swapped(tile):
    lane = lanes_of(tile)
    return jnp.where(lane % DH < DH // 2, lane_roll(tile, -(DH // 2)), lane_roll(tile, DH // 2))


def turned(tile, cos, sin):
    return tile * cos + halves_swapped(tile) * sin


def to_heads_body(nh, nb, hl, xg_hbm, w_hbm, cos_ref, sin_ref, g_ref, wo_ref, qin, kvin, n1_ref, gg, wo_all, qbuf, kvbuf, xg_ref, w_ref, qsem, ksem, fsem, gsem, osem, stage):
    pc = Place(nh, nb, hl)
    loads = [
        pltpu.make_async_copy(xg_hbm, xg_ref, stage.at[0]),
        pltpu.make_async_copy(w_hbm, w_ref, stage.at[1]),
    ]
    for cp in loads:
        cp.start()
    signal_plane_and_head(pc, nh, nb)
    rows = xg_ref.shape[1]
    lw = hl * DH
    loads[0].wait()
    for i in range(nh):
        n1_ref[i * rows : (i + 1) * rows, :] = norm_of(xg_ref[i].astype(F32))[0].astype(BF16)
    n1 = n1_ref[...]
    cos, sin = cos_ref[...], sin_ref[...]
    loads[1].wait()
    kk = jnp.dot(n1, w_ref[:, lw : 2 * lw], preferred_element_type=F32)
    vv = jnp.dot(n1, w_ref[:, 2 * lw :], preferred_element_type=F32)
    for p in range(hl // 2):
        k = turned(kk[:, p * 128 : (p + 1) * 128], cos, sin)
        v = vv[:, p * 128 : (p + 1) * 128]
        low = lanes_of(k) < DH
        even = jnp.where(low, k, lane_roll(v, DH)).astype(BF16)
        odd = jnp.where(low, lane_roll(k, DH), v).astype(BF16)
        for i in range(nh):
            kvbuf[2 * p, i] = even[i * rows : (i + 1) * rows]
            kvbuf[2 * p + 1, i] = odd[i * rows : (i + 1) * rows]
    wait_plane_and_head(nh, nb)
    core = pc.b % 2

    def keys_out(act):
        for l in range(hl):
            for u in range(pc.cb):
                routed(
                    pc,
                    kvbuf.at[l],
                    kvin.at[:, pc.b],
                    ksem.at[0, l * pc.cb + u],
                    ksem.at[1, pc.b // 2],
                    pc.x * 2 + core,
                    (2 * l + pc.c) * pc.cb + u,
                    act,
                )

    keys_out("start")
    qq = jnp.dot(n1, w_ref[:, :lw], preferred_element_type=F32)
    for p in range(hl // 2):
        q = turned(qq[:, p * 128 : (p + 1) * 128], cos, sin).T.astype(BF16)
        qbuf[2 * p] = q[:DH]
        qbuf[2 * p + 1] = q[DH:]
    queries_out(pc, qbuf, qin, qsem, "start")
    hg = HeadGather(nh, pc.h, pc.b, g_ref, gg, gsem)
    hg.start()
    spread = PairedSpread(nh, nb, pc.h, pc.b, lambda th: wo_ref, wo_all, osem, False)
    spread.start()

    def forward(k):
        at = kvin.at[:, 2 * k + pc.c]
        return remote(at, at, fsem.at[0, k], fsem.at[1, k], pc.sib, pc.b)

    @pl.loop(0, nb // 2)
    def _(k):
        wait_on(kvin.at[:, 2 * k + pc.c], ksem.at[1, k])
        forward(k).start()

    hg.pass_on()
    spread.pass_on()
    keys_out("wait_send")
    queries_out(pc, qbuf, qin, qsem, "wait_send")
    for zi in range(pc.nz):
        wait_on(qin.at[zi], qsem.at[1, zi])

    @pl.loop(0, nb // 2)
    def _(k):
        forward(k).wait()

    spread.finish()
    hg.finish()


def to_heads(xg, wq, cos, sin, g, wo, hl):
    nh, nb = dims()
    _, rows, width = xg.shape
    group = nh * rows
    cb = nb // (2 * hl)
    nz = nb // (2 * cb)
    dma = pltpu.SemaphoreType.DMA
    return comm_call(
        functools.partial(to_heads_body, nh, nb, hl),
        "to_heads",
        2,
        (
            jax.ShapeDtypeStruct((nz, DH, group), BF16),
            jax.ShapeDtypeStruct((nh, nb, rows, 2 * DH), BF16),
            jax.ShapeDtypeStruct((group, width), BF16),
            jax.ShapeDtypeStruct((nh, rows, width), BF16),
            jax.ShapeDtypeStruct((nb,) + wo.shape, BF16),
        ),
        [ANY, ANY, VM, VM, ANY, ANY],
        [ANY, ANY, VM, ANY, ANY],
        [
            pltpu.VMEM((hl, DH, group), BF16),
            pltpu.VMEM((hl, nh, rows, 2 * DH), BF16),
            pltpu.VMEM(xg.shape, BF16),
            pltpu.VMEM(wq.shape, BF16),
            dma((2, max(hl, nz))),
            dma((2, max(hl * cb, nb // 2))),
            dma((2, nb // 2)),
            HeadGather.sem_shape(nh),
            PairedSpread.sem_shape(nb // 2),
            dma((2,)),
        ],
        (xg, wq, cos, sin, g, wo),
        vmem=60 << 20,
    )


def query_tile(ref):
    return jnp.concatenate([ref[0], ref[1]], axis=1)


def allowed(block_at, first_ref, last_ref, lanes):
    at = block_at * KEY_BLOCK + lax.broadcasted_iota(jnp.int32, (KEY_BLOCK, lanes), 0)
    return jnp.logical_and(at >= first_ref[0], at < last_ref[0])


def attend_body(lo_ref, hi_ref, q_ref, kv_ref, first_ref, last_ref, o_ref, of_ref, lse_ref):
    tile = pl.program_id(0)
    q = query_tile(q_ref)
    lanes = q.shape[1]
    q_pad = jnp.concatenate([q, jnp.zeros_like(q)], axis=0)

    def step(j, carry):
        top, total, acc = carry
        kv = kv_ref[pl.ds(pl.multiple_of(j * KEY_BLOCK, KEY_BLOCK), KEY_BLOCK), :]
        s = jnp.dot(kv, q_pad, preferred_element_type=F32)
        s = jnp.where(allowed(j, first_ref, last_ref, lanes), s, MASK_FLOOR)
        new_top = jnp.maximum(top, jnp.max(s, axis=0, keepdims=True))
        p = jnp.exp2((s - new_top) * EXP_SCALE)
        alpha = jnp.exp2((top - new_top) * EXP_SCALE)
        total = total * alpha + jnp.sum(p, axis=0, keepdims=True)
        acc = acc * alpha + lax.dot_general(
            kv, p.astype(BF16), (((0,), (0,)), ((), ())), preferred_element_type=F32
        )
        return new_top, total, acc

    top, total, acc = lax.fori_loop(
        lo_ref[tile],
        hi_ref[tile],
        step,
        (
            jnp.full((1, lanes), MASK_FLOOR, F32),
            jnp.zeros((1, lanes), F32),
            jnp.zeros((2 * DH, lanes), F32),
        ),
    )
    o = acc[DH:] / total
    half = lanes // 2
    for i in range(2):
        part = o[:, i * half : (i + 1) * half]
        of_ref[i] = part
        o_ref[i] = part.astype(BF16)
    lse_ref[0] = top * EXP_SCALE + jnp.log2(total)


def attend_specs(kv_rows, rows, pairs):
    tile_spec = pl.BlockSpec((2, DH, rows), lambda i, *_: (i % pairs, 0, i // pairs))
    row_spec = pl.BlockSpec((1, 1, 2 * rows), lambda i, *_: (i, 0, 0))
    kv_spec = pl.BlockSpec((kv_rows, 2 * DH), lambda i, *_: (0, 0))
    return tile_spec, row_spec, kv_spec


def attend(q, kv, first, last, lo, hi, rows):
    nz, _, group = q.shape
    tiles = lo.shape[0]
    tile_spec, row_spec, kv_spec = attend_specs(kv.shape[0], rows, nz // 2)
    return pl.pallas_call(
        attend_body,
        grid_spec=pltpu.PrefetchScalarGridSpec(
            num_scalar_prefetch=2,
            grid=(tiles,),
            in_specs=[tile_spec, kv_spec, row_spec, row_spec],
            out_specs=[tile_spec, tile_spec, row_spec],
        ),
        out_shape=(
            jax.ShapeDtypeStruct(q.shape, BF16),
            jax.ShapeDtypeStruct(q.shape, F32),
            jax.ShapeDtypeStruct((tiles, 1, 2 * rows), F32),
        ),
        name="attend",
        compiler_params=pltpu.CompilerParams(vmem_limit_bytes=60 << 20),
    )(lo, hi, q, kv, first, last)


def attend_grad_body(lo_ref, hi_ref, q_ref, do_ref, of_ref, kv_ref, first_ref, last_ref, lse_ref, dq_ref, dkv_ref, acc_ref):
    tile = pl.program_id(0)

    @pl.when(tile == 0)
    def _():
        acc_ref[...] = jnp.zeros_like(acc_ref)

    q = query_tile(q_ref)
    do = query_tile(do_ref)
    lanes = q.shape[1]
    zero = jnp.zeros_like(q)
    both = jnp.concatenate(
        [jnp.concatenate([q, zero], axis=0), jnp.concatenate([zero, do], axis=0)], axis=1
    )
    delta = jnp.sum(do.astype(F32) * query_tile(of_ref), axis=0, keepdims=True)
    lse = lse_ref[0]

    def step(j, dq):
        at = pl.ds(pl.multiple_of(j * KEY_BLOCK, KEY_BLOCK), KEY_BLOCK)
        kv = kv_ref[at, :]
        sd = jnp.dot(kv, both, preferred_element_type=F32)
        s, dp = sd[:, :lanes], sd[:, lanes:]
        p = jnp.exp2(
            jnp.where(
                allowed(j, first_ref, last_ref, lanes), s * EXP_SCALE - lse, MASK_FLOOR
            )
        )
        ds = (p * (dp - delta)).astype(BF16)
        acc_ref[at, :] += lax.dot_general(
            jnp.concatenate([ds, p.astype(BF16)], axis=1),
            both,
            (((1,), (1,)), ((), ())),
            preferred_element_type=F32,
        )
        return dq + lax.dot_general(
            kv, ds, (((0,), (0,)), ((), ())), preferred_element_type=F32
        )

    dq = lax.fori_loop(lo_ref[tile], hi_ref[tile], step, jnp.zeros((2 * DH, lanes), F32))
    half = lanes // 2
    for i in range(2):
        dq_ref[i] = (dq[:DH, i * half : (i + 1) * half] * 0.125).astype(BF16)

    @pl.when(tile == pl.num_programs(0) - 1)
    def _():
        lane = lax.broadcasted_iota(jnp.int32, (1, 2 * DH), 1)
        dkv_ref[...] = (acc_ref[...] * jnp.where(lane < DH, 0.125, 1.0)).astype(BF16)


def attend_grad(q, do, of, kv, first, last, lse, lo, hi, rows):
    nz, _, group = q.shape
    tiles = lo.shape[0]
    tile_spec, row_spec, kv_spec = attend_specs(kv.shape[0], rows, nz // 2)
    return pl.pallas_call(
        attend_grad_body,
        grid_spec=pltpu.PrefetchScalarGridSpec(
            num_scalar_prefetch=2,
            grid=(tiles,),
            in_specs=[tile_spec, tile_spec, tile_spec, kv_spec, row_spec, row_spec, row_spec],
            out_specs=[tile_spec, kv_spec],
            scratch_shapes=[pltpu.VMEM(kv.shape, F32)],
        ),
        out_shape=(jax.ShapeDtypeStruct(q.shape, BF16), jax.ShapeDtypeStruct(kv.shape, BF16)),
        name="attend_grad",
        compiler_params=pltpu.CompilerParams(vmem_limit_bytes=60 << 20),
    )(lo, hi, q, do, of, kv, first, last, lse)


class HeadSum:
    def __init__(self, nh, h, b, part, near, far, out, sems):
        self.nx = nh // 2
        self.x, self.c = h // 2, h % 2
        self.h, self.part, self.near, self.far, self.out = h, part, near, far, out
        sib = self.x * 2 + 1 - self.c
        self.pairs = [
            remote(
                part.at[((self.x + k) % self.nx) * 2 + 1 - self.c],
                near.at[k],
                sems.at[0, k],
                sems.at[1, k],
                sib,
                b,
            )
            for k in range(self.nx)
        ]
        self.across = [
            remote(
                out.at[k],
                far.at[k],
                sems.at[2, k],
                sems.at[3, k],
                ((self.x + k) % self.nx) * 2 + self.c,
                b,
            )
            for k in range(1, self.nx)
        ]

    @staticmethod
    def sem_shape(nh):
        return pltpu.SemaphoreType.DMA((4, nh // 2))

    @staticmethod
    def buffers(nh, rows, width):
        return [pltpu.VMEM((nh // 2, rows, width), BF16)] * 3

    def start(self):
        for k in list(range(1, self.nx)) + [0]:
            self.pairs[k].start()

    def send(self):
        for k in range(1, self.nx):
            self.pairs[k].wait_recv()
            at = ((self.x + k) % self.nx) * 2 + self.c
            self.out[k] = (self.part[at].astype(F32) + self.near[k].astype(F32)).astype(BF16)
            self.across[k - 1].start()

    def total(self):
        self.pairs[0].wait_recv()
        total = self.part[self.h].astype(F32) + self.near[0].astype(F32)
        for k in range(1, self.nx):
            self.across[k - 1].wait_recv()
            total = total + self.far[k].astype(F32)
        return total

    def finish(self):
        for cp in self.pairs:
            cp.wait_send()
        for cp in self.across:
            cp.wait_send()


def norm_of(values):
    centre = values - jnp.mean(values, axis=-1, keepdims=True)
    scale = lax.rsqrt(jnp.mean(centre * centre, axis=-1, keepdims=True) + NORM_EPS)
    return centre * scale, scale


def norm_pull(grad, normed, scale):
    one = jnp.mean(grad, axis=-1, keepdims=True)
    two = jnp.mean(grad * normed, axis=-1, keepdims=True)
    return scale * (grad - one - normed * two)


CHUNKS = 2


def chunk_of(ref, j, axis):
    size = ref.shape[axis] // CHUNKS
    at = pl.ds(j * size, size)
    return ref.at[at] if axis == 0 else ref.at[:, at]


def head_sums(nh, h, b, part, bufs, sems):
    near, far, out = bufs
    return [
        HeadSum(
            nh,
            h,
            b,
            chunk_of(part, j, 1),
            chunk_of(near, j, 1),
            chunk_of(far, j, 1),
            chunk_of(out, j, 1),
            sems.at[j],
        )
        for j in range(CHUNKS)
    ]


def head_gathers(nh, h, b, src, dst, sems):
    return [
        HeadGather(nh, h, b, chunk_of(src, j, 0), chunk_of(dst, j, 1), sems.at[j])
        for j in range(CHUNKS)
    ]


def chunk_sems(nh):
    return pltpu.SemaphoreType.DMA((CHUNKS, 4, nh // 2))


def mid_body(nh, nb, hl, o_ref, wo_ref, x_ref, og, hid_ref, ng_ref, part, near, far, out, nbuf, osem, ssem, gsem):
    pc = Place(nh, nb, hl)
    h, b = pc.h, pc.b
    signal_plane_and_head(pc, nh, nb)
    wait_plane_and_head(nh, nb)
    rows, width = x_ref.shape
    queries_back(pc, o_ref, og, osem, "start")
    queries_back(pc, o_ref, og, osem, "wait_send")
    for l in range(hl):
        wait_on(og.at[l], osem.at[1, l])
    o = og[...].reshape(hl * DH, nh * rows)
    wo = wo_ref[...]
    for i in range(nh):
        part[i] = lax.dot_general(
            o[:, i * rows : (i + 1) * rows], wo, (((0,), (0,)), ((), ())), preferred_element_type=F32
        ).astype(BF16)
    hss = head_sums(nh, h, b, part, (near, far, out), ssem)
    hgs = head_gathers(nh, h, b, nbuf, ng_ref, gsem)
    for hs in hss:
        hs.start()
    for hs in hss:
        hs.send()
    size = rows // CHUNKS
    for j, (hs, hg) in enumerate(zip(hss, hgs)):
        at = pl.ds(j * size, size)
        hid = x_ref[at, :].astype(F32) + hs.total()
        hid_ref[at, :] = hid
        nbuf[at, :] = norm_of(hid)[0].astype(BF16)
        hg.start()
    for hg in hgs:
        hg.pass_on()
    for hs, hg in zip(hss, hgs):
        hs.finish()
        hg.finish()


def mid_exchange(ot, wo, x, hl):
    nh, nb = dims()
    rows, width = x.shape
    nz = ot.shape[0]
    return comm_call(
        functools.partial(mid_body, nh, nb, hl),
        "mid_exchange",
        3,
        (
            jax.ShapeDtypeStruct((hl,) + ot.shape[1:], BF16),
            jax.ShapeDtypeStruct(x.shape, F32),
            jax.ShapeDtypeStruct((nh, rows, width), BF16),
        ),
        [ANY, VM, VM],
        [VM, VM, VM],
        [pltpu.VMEM((nh, rows, width), BF16)]
        + HeadSum.buffers(nh, rows, width)
        + [
            pltpu.VMEM((rows, width), BF16),
            pltpu.SemaphoreType.DMA((2, max(hl, nz))),
            chunk_sems(nh),
            chunk_sems(nh),
        ],
        (ot, wo, x),
        vmem=60 << 20,
    )


def ffn_body(nh, nb, fl, split_rows, n_ref, g_ref, valid_ref, w_ref, y_ref, d_ref, ga_ref, gb_ref, gy, mm, dz):
    rows, width = n_ref.shape[1], n_ref.shape[2]
    group = nh * rows
    total, zc, off = ff_widths(fl)
    wide = total - off
    shift = 2 * fl - off
    step = 2 * rows
    lane = lax.broadcasted_iota(jnp.int32, (1, wide), 1)
    real = lane < fl

    @pl.loop(0, group // step)
    def _(r):
        at = pl.ds(pl.multiple_of(r * step, step), step)
        n = n_ref[pl.ds(r * 2, 2)].reshape(step, width)
        g = (g_ref[pl.ds(r * 2, 2)].reshape(step, width).astype(F32) * valid_ref[at, :]).astype(
            BF16
        )
        gy[at, :] = g
        z = jnp.dot(n, w_ref[:, :zc], preferred_element_type=F32)
        dm = lane_roll(jnp.dot(g, w_ref[:, off:], preferred_element_type=F32), -shift)
        gate, up = z[:, :wide], lane_roll(z, -fl)[:, :wide]
        cdf = 0.5 * (1.0 + lax.erf(gate * math.sqrt(0.5)))
        act = gate * cdf
        slope = cdf + gate * jnp.exp(-0.5 * gate * gate) * (1.0 / math.sqrt(2.0 * math.pi))
        m = lane_roll(jnp.where(real, act * up, 0.0), shift).astype(BF16)
        mm[at, :] = m
        d_gate = widen(jnp.where(real, dm * up * slope, 0.0), zc)
        d_up = lane_roll(widen(jnp.where(real, dm * act, 0.0), zc), fl)
        d = (d_gate + d_up).astype(BF16)
        dz[at, :] = d
        nt = (((1,), (1,)), ((), ()))
        dpart = lax.dot_general(d, w_ref[:, :zc], nt, preferred_element_type=F32)
        d_ref[pl.ds(r * 2, 2)] = dpart.astype(BF16).reshape(2, rows, width)
        ypart = lax.dot_general(m, w_ref[:, off:], nt, preferred_element_type=F32)
        y_ref[pl.ds(r * 2, 2)] = ypart.astype(BF16).reshape(2, rows, width)

    block = width // nh

    @pl.loop(0, nh)
    def _(i):
        cols = pl.ds(pl.multiple_of(i * block, block), block)
        tn = (((0,), (0,)), ((), ()))
        n = n_ref[:, :, cols].reshape(group, block)
        g_in = lax.dot_general(n, dz[...], tn, preferred_element_type=F32)
        g_down = lax.dot_general(gy[:, cols], mm[...], tn, preferred_element_type=F32)
        first = g_in[:, :off].astype(BF16)
        rest = jnp.concatenate(
            [g_in[:, off:] + g_down[:, : zc - off], g_down[:, zc - off :]], axis=1
        ).astype(BF16)
        if split_rows:
            ga_ref[:, i] = first.reshape(nb, block // nb, off)
            gb_ref[:, i] = rest.reshape(nb, block // nb, wide)
        else:
            ga_ref[pl.ds(i * block, block), :] = first
            gb_ref[pl.ds(i * block, block), :] = rest


def ffn(n2, g, valid, wm, fl, own_rows):
    nh, nb = dims()
    _, rows, width = n2.shape
    group = nh * rows
    total, zc, off = ff_widths(fl)
    split_rows = own_rows % 16 == 0
    lead = (nb, nh, own_rows) if split_rows else (width,)
    return pl.pallas_call(
        functools.partial(ffn_body, nh, nb, fl, split_rows),
        out_shape=(
            jax.ShapeDtypeStruct(n2.shape, BF16),
            jax.ShapeDtypeStruct(n2.shape, BF16),
            jax.ShapeDtypeStruct(lead + (off,), BF16),
            jax.ShapeDtypeStruct(lead + (total - off,), BF16),
        ),
        in_specs=[VM] * 4,
        out_specs=[VM] * 4,
        scratch_shapes=[
            pltpu.VMEM((group, width), BF16),
            pltpu.VMEM((group, total - off), BF16),
            pltpu.VMEM((group, zc), BF16),
        ],
        name="ffn",
        compiler_params=pltpu.CompilerParams(vmem_limit_bytes=60 << 20),
    )(n2, g, valid, wm)


def back_body(nh, nb, hl, dpart, ypart, hid_ref, g_ref, valid_ref, wo_ref, og_ref, gb_ref, y_ref, dh_ref, do_in, go_ref, gb_sum, n1, f1, o1, n2, f2, o2, dbuf, dg, dots, nearb, sumb, farb, s1, s2, gsem, qsem, pb, fb):
    pc = Place(nh, nb, hl)
    h, b = pc.h, pc.b
    signal_plane_and_head(pc, nh, nb)
    wait_plane_and_head(nh, nb)
    rows, width = hid_ref.shape
    hds = head_sums(nh, h, b, dpart, (n1, f1, o1), s1)
    hy = HeadSum(nh, h, b, ypart, n2, f2, o2, s2)
    hgs = head_gathers(nh, h, b, dbuf, dg, gsem)
    nk = nb // 2
    par, kb = b % 2, b // 2

    def pair_b(i):
        k = (kb + i) % nk
        return remote(
            gb_ref.at[k, 1 - par], nearb.at[k], pb.at[0, i], pb.at[1, i], h, b + 1 - 2 * par
        )

    def far_b(i):
        k = (kb + i) % nk
        return remote(sumb.at[k], farb.at[kb], fb.at[0, i], fb.at[1, i], h, 2 * k + par)

    def add_b(i):
        k = (kb + i) % nk
        pair_b(i).wait_recv()
        return (gb_ref[k, par].astype(F32) + nearb[k].astype(F32)).astype(BF16)

    def send_b(i):
        sumb[(kb + i) % nk] = add_b(i)
        far_b(i).start()

    for hd in hds:
        hd.start()

    @pl.loop(1, nk + 1)
    def _(i):
        pair_b(i % nk).start()

    for hd in hds:
        hd.send()
    size = rows // CHUNKS
    for j, (hd, hg) in enumerate(zip(hds, hgs)):
        at = pl.ds(j * size, size)
        normed, scale = norm_of(hid_ref[at, :])
        gy = g_ref[at, :].astype(F32) * valid_ref[at, :]
        dh = gy + norm_pull(hd.total(), normed, scale)
        dh_ref[at, :] = dh
        dbuf[at, :] = dh.astype(BF16)
        hg.start()
    hy.start()
    early = (nk - 1) // 2

    @pl.loop(1, 1 + early)
    def _(i):
        send_b(i)

    for hg in hgs:
        hg.pass_on()
    hy.send()
    for hd, hg in zip(hds, hgs):
        hd.finish()
        hg.finish()
    wo = wo_ref[...]
    lw = hl * DH
    nt = (((1,), (1,)), ((), ()))
    for i in range(nh):
        part = lax.dot_general(wo, dg[i], nt, preferred_element_type=F32).astype(BF16)
        dots[:, :, i * rows : (i + 1) * rows] = part.reshape(hl, DH, rows)
    queries_out(pc, dots, do_in, qsem, "start")
    og = og_ref[...].reshape(lw, nh * rows)
    go_ref[...] = jnp.dot(
        og, dg[...].reshape(nh * rows, width), preferred_element_type=F32
    ).astype(BF16)
    @pl.loop(1 + early, nk)
    def _(i):
        send_b(i)

    farb[kb] = add_b(0)
    y_ref[...] = valid_ref[...] * (hid_ref[...] + hy.total())
    hy.finish()

    @pl.loop(1, nk)
    def _(i):
        far_b(i).wait()

    @pl.loop(0, nk)
    def _(i):
        pair_b(i).wait_send()

    gb_sum[...] = jnp.sum(farb[...].astype(F32), axis=0).astype(BF16)
    queries_out(pc, dots, do_in, qsem, "wait_send")
    for zi in range(pc.nz):
        wait_on(do_in.at[zi], qsem.at[1, zi])


def back_exchange(dpart, ypart, hid, g, valid, wo, og, gb):
    nh, nb = dims()
    rows, width = hid.shape
    hl, _, group = og.shape
    nz = nb // (2 * (nb // (2 * hl)))
    return comm_call(
        functools.partial(back_body, nh, nb, hl),
        "back_exchange",
        4,
        (
            jax.ShapeDtypeStruct(hid.shape, F32),
            jax.ShapeDtypeStruct(hid.shape, F32),
            jax.ShapeDtypeStruct((nz, DH, group), BF16),
            jax.ShapeDtypeStruct((hl * DH, width), BF16),
            jax.ShapeDtypeStruct(gb.shape[2:], BF16),
        ),
        [VM] * 8,
        [VM, VM, ANY, VM, VM],
        HeadSum.buffers(nh, rows, width)
        + HeadSum.buffers(nh, rows, width)
        + [
            pltpu.VMEM((rows, width), BF16),
            pltpu.VMEM((nh, rows, width), BF16),
            pltpu.VMEM((hl, DH, group), BF16),
            pltpu.VMEM((nb // 2,) + gb.shape[2:], BF16),
            pltpu.VMEM((nb // 2,) + gb.shape[2:], BF16),
            pltpu.VMEM((nb // 2,) + gb.shape[2:], BF16),
            chunk_sems(nh),
            HeadSum.sem_shape(nh),
            chunk_sems(nh),
            pltpu.SemaphoreType.DMA((2, max(hl, nz))),
            pltpu.SemaphoreType.DMA((2, nb // 2)),
            pltpu.SemaphoreType.DMA((2, nb // 2)),
        ],
        (dpart, ypart, hid, g, valid, wo, og, gb),
        vmem=60 << 20,
    )


def grads_back_body(nh, nb, hl, dq_ref, dkv_ref, cos_ref, sin_ref, n1_ref, w_ref, gq_ref, dpart, got, sums, dq_out, dkv_out, dqkv, qsem, psem, ksem):
    pc = Place(nh, nb, hl)
    signal_plane(pc, nb)
    wait_plane(nb)
    rows = dkv_ref.shape[2]
    group = nh * rows
    width = n1_ref.shape[1]
    lw = hl * DH

    def pair(k):
        return remote(
            dkv_ref.at[:, 2 * k + 1 - pc.c], got.at[k], psem.at[0, k], psem.at[1, k], pc.sib, pc.b
        )

    def back(k, act):
        routed(
            pc,
            sums.at[k],
            dkv_out.at[pc.my_l, pc.u],
            ksem.at[0, k],
            ksem.at[1, pc.my_l * pc.cb + pc.u],
            pc.my_src_h,
            2 * k + pc.c,
            act,
        )

    half = nb // 2

    @pl.loop(0, half)
    def _(k):
        pair(k).start()

    queries_back(pc, dq_ref, dq_out, qsem, "start")

    @pl.loop(0, half)
    def _(k):
        pair(k).wait_recv()
        sums[k] = (dkv_ref[:, 2 * k + pc.c].astype(F32) + got[k].astype(F32)).astype(BF16)
        back(k, "start")

    @pl.loop(0, half)
    def _(k):
        pair(k).wait_send()
        back(k, "wait_send")

    queries_back(pc, dq_ref, dq_out, qsem, "wait_send")
    for l in range(hl):
        wait_on(dq_out.at[l], qsem.at[1, l])
    cos, sin = cos_ref[...], -sin_ref[...]
    for p in range(hl // 2):
        q = dq_out[2 * p : 2 * p + 2].reshape(2 * DH, group).astype(F32).T
        dqkv[:, p * 128 : (p + 1) * 128] = turned(q, cos, sin).astype(BF16)
    for l in range(hl):
        for u in range(pc.cb):
            wait_on(dkv_out.at[l, u], ksem.at[1, l * pc.cb + u])
    for p in range(hl // 2):
        even, odd = [
            jnp.sum(dkv_out[2 * p + i].astype(F32), axis=0).reshape(group, 2 * DH)
            for i in range(2)
        ]
        low = lanes_of(even) < DH
        k = jnp.where(low, even, lane_roll(odd, DH)).astype(BF16).astype(F32)
        v = jnp.where(low, lane_roll(even, DH), odd)
        dqkv[:, lw + p * 128 : lw + (p + 1) * 128] = turned(k, cos, sin).astype(BF16)
        dqkv[:, 2 * lw + p * 128 : 2 * lw + (p + 1) * 128] = v.astype(BF16)
    nt = (((1,), (1,)), ((), ()))
    tn = (((0,), (0,)), ((), ()))

    @pl.loop(0, nh)
    def _(i):
        cols = pl.ds(pl.multiple_of(i * (width // nh), width // nh), width // nh)
        gq_ref[cols, :] = lax.dot_general(
            n1_ref[:, cols], dqkv[...], tn, preferred_element_type=F32
        ).astype(BF16)
        at = pl.ds(pl.multiple_of(i * rows, rows), rows)
        dpart[i] = lax.dot_general(
            dqkv[at, :], w_ref[...], nt, preferred_element_type=F32
        ).astype(BF16)


def grads_back(dq, dkv, cos, sin, n1, wq, hl):
    nh, nb = dims()
    cb = nb // (2 * hl)
    nz = nb // (2 * cb)
    rows = dkv.shape[2]
    width = n1.shape[1]
    lw = hl * DH
    dma = pltpu.SemaphoreType.DMA
    return comm_call(
        functools.partial(grads_back_body, nh, nb, hl),
        "grads_back",
        5,
        (
            jax.ShapeDtypeStruct((width, 3 * lw), BF16),
            jax.ShapeDtypeStruct((nh, rows, width), BF16),
        ),
        [ANY] + [VM] * 5,
        [VM, VM],
        [
            pltpu.VMEM((nb // 2, nh, rows, 2 * DH), BF16),
            pltpu.VMEM((nb // 2, nh, rows, 2 * DH), BF16),
            pltpu.VMEM((hl,) + dq.shape[1:], BF16),
            pltpu.VMEM((hl, cb, nh, rows, 2 * DH), BF16),
            pltpu.VMEM((nh * rows, 3 * lw), BF16),
            dma((2, max(hl, nz))),
            dma((2, nb // 2)),
            dma((2, max(hl * cb, nb // 2))),
        ],
        (dq, dkv, cos, sin, n1, wq),
        vmem=60 << 20,
    )


def last_body(nh, nb, dpart, gq_ref, go_ref, gma_ref, gmb_ref, dn_ref, farq, faro, gma_all, gmb_all, near, far, out, nearq, sumq, nearo, sumo, ssem, pq, fq, po, fo, msem):
    h, b = me()
    signal_all(nh, nb, h, b)
    wait_all(nh, nb)
    nk = nb // 2
    y, kb = b % 2, b // 2
    other = b + 1 - 2 * y

    def pair_q(i):
        k = (kb + i) % nk
        return remote(gq_ref.at[:, k, 1 - y], nearq.at[k], pq.at[0, i], pq.at[1, i], h, other)

    pair_o = remote(go_ref.at[:, 1 - y], nearo, po.at[0], po.at[1], h, other)

    def far_q(i, j):
        k, th = (kb + i) % nk, (h + j) % nh
        slot = i * nh + j
        return remote(
            sumq.at[k, th], farq.at[h, kb], fq.at[0, slot], fq.at[1, slot], th, 2 * k + y
        )

    def far_o(i):
        k = (kb + i) % nk
        return remote(sumo.at[k], faro.at[kb], fo.at[0, i], fo.at[1, i], h, 2 * k + y)

    @pl.loop(1, nk + 1)
    def _(i):
        pair_q(i % nk).start()

    hs = HeadSum(nh, h, b, dpart, near, far, out, ssem)
    hs.start()
    pair_o.start()
    moves = []
    for n, (ref, dst) in enumerate(((gma_ref, gma_all), (gmb_ref, gmb_all))):
        for i in range(1, nh):
            th = (h + i) % nh
            moves.append(remote(ref.at[th], dst.at[h], msem.at[0, n, i], msem.at[1, n, i], th, b))
        moves.append(pltpu.make_async_copy(ref.at[h], dst.at[h], msem.at[0, n, 0]))
    for cp in moves:
        cp.start()
    hs.send()

    @pl.loop(1, nk)
    def _(i):
        k = (kb + i) % nk
        pair_q(i).wait_recv()
        sumq[k] = (gq_ref[:, k, y].astype(F32) + nearq[k].astype(F32)).astype(BF16)
        for j in range(nh):
            far_q(i, j).start()

    pair_q(0).wait_recv()
    sumq[kb] = (gq_ref[:, kb, y].astype(F32) + nearq[kb].astype(F32)).astype(BF16)
    for j in range(1, nh):
        far_q(0, j).start()
    farq[h, kb] = sumq[kb, h]
    pair_o.wait_recv()
    sumo[...] = (go_ref[:, y].astype(F32) + nearo[...].astype(F32)).astype(BF16)

    @pl.loop(1, nk)
    def _(i):
        far_o(i).start()

    faro[kb] = sumo[kb]
    dn_ref[...] = hs.total()
    hs.finish()
    for cp in moves:
        cp.wait()

    @pl.loop(1, nk)
    def _(i):
        for j in range(nh):
            far_q(i, j).wait()

    for j in range(1, nh):
        far_q(0, j).wait()

    @pl.loop(0, nk)
    def _(i):
        pair_q(i).wait_send()

    @pl.loop(1, nk)
    def _(i):
        far_o(i).wait()

    pair_o.wait_send()


def last_exchange(dpart, gq, go, gma, gmb):
    nh, nb = dims()
    _, rows, width = dpart.shape
    own_rows, cols = gq.shape[3:]
    nk = nb // 2
    dma = pltpu.SemaphoreType.DMA
    return comm_call(
        functools.partial(last_body, nh, nb),
        "last_exchange",
        6,
        (
            jax.ShapeDtypeStruct((rows, width), F32),
            jax.ShapeDtypeStruct((nh, nk, own_rows, cols), BF16),
            jax.ShapeDtypeStruct((nk, own_rows, width), BF16),
            jax.ShapeDtypeStruct(gma.shape, BF16),
            jax.ShapeDtypeStruct(gmb.shape, BF16),
        ),
        [VM] * 3 + [ANY] * 2,
        [VM] * 3 + [ANY] * 2,
        HeadSum.buffers(nh, rows, width)
        + [pltpu.VMEM((nk, nh, own_rows, cols), BF16)] * 2
        + [pltpu.VMEM((nk, own_rows, width), BF16)] * 2
        + [
            HeadSum.sem_shape(nh),
            dma((2, nk)),
            dma((2, nh * nk)),
            dma((2,)),
            dma((2, nk)),
            dma((2, 2, nh)),
        ],
        (dpart, gq, go, gma, gmb),
        vmem=60 << 20,
    )


def finish_body(nh, lw, fl, dn_ref, x_ref, dh_ref, y_in, farq, faro, gma, gmb, wq_ref, win_ref, ga_ref, gf_ref,
                y_ref, dx_ref, lna_ref, dq_ref, do_ref, lnm_ref, din_ref, dwd_ref):
    y_ref[...] = y_in[...]
    normed, scale = norm_of(x_ref[...].astype(F32))
    dx_ref[...] = dh_ref[...] + norm_pull(dn_ref[...], normed, scale)
    do_ref[...] = jnp.sum(faro[...].astype(F32), axis=0)
    width = nh * lw
    gain = ga_ref[...]
    rowsum = 0.0
    for i in range(nh):
        g = jnp.sum(farq[i].astype(F32), axis=0)
        for c in range(3):
            at = c * width + i * lw
            piece = g[:, c * lw : (c + 1) * lw]
            dq_ref[:, at : at + lw] = piece * gain
            rowsum = rowsum + jnp.sum(
                piece * wq_ref[:, at : at + lw].astype(F32), axis=1, keepdims=True
            )
    lna_ref[...] = rowsum
    ff = nh * fl
    total, _, _ = ff_widths(fl)
    tiles = lambda v: (v + 127) // 128 * 128
    gate_up, down = 0.0, 0.0
    for i in range(nh):
        piece = jnp.concatenate([gma[i].astype(F32), gmb[i].astype(F32)], axis=1)
        lane = lanes_of(piece)
        gate = widen(jnp.where(lane < fl, piece, 0.0), tiles(2 * ff))
        up = jnp.where(jnp.logical_and(lane >= fl, lane < 2 * fl), piece, 0.0)
        up = widen(up, tiles(2 * ff))
        gate_up = gate_up + lane_roll(gate, i * fl) + lane_roll(up, ff - fl + i * fl)
        dn = jnp.where(jnp.logical_and(lane >= 2 * fl, lane < 3 * fl), piece, 0.0)
        down = down + lane_roll(widen(dn, max(total, tiles(ff))), i * fl - 2 * fl)
    gate_up = gate_up[:, : 2 * ff]
    dwd_ref[...] = down[:, :ff]
    din_ref[...] = gate_up * gf_ref[...]
    lnm_ref[...] = jnp.sum(gate_up * win_ref[...].astype(F32), axis=1, keepdims=True)


def finish(dn, x, dh, y, farq, faro, gma, gmb, w_qkv, w_in, gain_attn, gain_mlp, fl):
    nh, _ = dims()
    rows, width = x.shape
    own_rows = w_qkv.shape[0]
    ff = nh * fl
    f32 = lambda *shape: jax.ShapeDtypeStruct(shape, F32)
    return pl.pallas_call(
        functools.partial(finish_body, nh, width // nh, fl),
        out_shape=(
            f32(rows, width),
            f32(rows, width),
            f32(own_rows, 1),
            f32(own_rows, 3 * width),
            f32(own_rows, width),
            f32(own_rows, 1),
            f32(own_rows, 2 * ff),
            f32(own_rows, ff),
        ),
        in_specs=[VM] * 12,
        out_specs=[VM] * 8,
        name="finish",
        compiler_params=pltpu.CompilerParams(vmem_limit_bytes=60 << 20),
    )(dn, x, dh, y, farq, faro, gma, gmb, w_qkv, w_in, gain_attn, gain_mlp)


def spans(rows_at, lengths):
    ends = jnp.cumsum(lengths)
    total = ends[-1]
    starts = ends - lengths
    inside = jnp.logical_and(rows_at[..., None] >= starts, rows_at[..., None] < ends)
    first = jnp.sum(jnp.where(inside, starts, 0), axis=-1)
    last = jnp.sum(jnp.where(inside, ends, 0), axis=-1)
    pad = rows_at >= total
    return jnp.where(pad, total, first), last, pad


def shards(layer_input, out_grad, lengths, ln_attn, w_qkv, w_attn_out, ln_mlp, w_in, w_mlp_out):
    nh, nb = dims()
    h, b = me()
    rows, width = layer_input.shape
    heads = width // DH
    hl = heads // nh
    lw = hl * DH
    group = nh * rows
    slots = nh * nb * rows
    own_rows = w_qkv.shape[0]
    ff = w_mlp_out.shape[0]
    fl = ff // nh
    total = ff_widths(fl)[0]
    cb = nb // (2 * hl)
    qs = 2 * cb
    nz = nb // qs

    gain_attn = ln_attn.astype(F32)[:, None]
    gain_mlp = ln_mlp.astype(F32)[:, None]
    xg, wm_h, wq = first_exchange(
        layer_input, w_qkv, gain_attn, w_in, gain_mlp, w_mlp_out.T, fl
    )
    wm = lax.all_gather(wm_h, "blk", axis=1, tiled=True).reshape(width, total)
    wq = wq.reshape(width, 3 * lw)

    row = lax.iota(jnp.int32, rows)
    group_at = ((lax.iota(jnp.int32, nh) * nb + b)[:, None] * rows + row).reshape(group)
    first, _, pad = spans(group_at, lengths)
    position = (group_at - first).astype(F32)
    half = DH // 2
    lane = lax.iota(jnp.int32, 2 * DH)
    inv_freq = jnp.power(ROPE_BASE, -2.0 * (lane % half).astype(F32) / DH)
    angles = position[:, None] * inv_freq[None, :]
    sign = jnp.where(lane % DH < half, -1.0, 1.0)
    cos, sin = jnp.cos(angles), jnp.sin(angles) * sign
    valid_group = jnp.where(pad, 0.0, 1.0)[:, None]
    own_at = (h * nb + b) * rows + row
    valid = jnp.where(spans(own_at, lengths)[2], 0.0, 1.0)[:, None]

    split = (b % cb) * 2 + h % 2
    tile_block = (
        lax.iota(jnp.int32, nh)[:, None, None] * nb
        + (lax.iota(jnp.int32, nz // 2)[None, :, None] * 2 + lax.iota(jnp.int32, 2)) * qs
        + split
    )
    tiles = nh * nz // 2
    query_at = (tile_block[..., None] * rows + row).reshape(tiles, 1, 2 * rows)
    q_first, q_last, q_pad = spans(query_at, lengths)
    q_last = jnp.where(q_pad, slots, q_last)
    lo = q_first[:, 0, 0] // KEY_BLOCK
    hi = (q_last[:, 0, -1] + KEY_BLOCK - 1) // KEY_BLOCK

    qin, kvin, n1, gg, wo = to_heads(xg, wq, cos, sin, out_grad, w_attn_out, hl)
    wo = wo.reshape(lw, width)
    kv_all = kvin.reshape(slots, 2 * DH)
    ot, of, lse = attend(qin, kv_all, q_first, q_last, lo, hi, rows)
    og, hid, n2 = mid_exchange(ot, wo, layer_input, hl)
    ypart, dpart, gma, gmb = ffn(n2, gg, valid_group, wm, fl, own_rows)
    if gma.ndim == 4:
        gma = lax.psum_scatter(gma, "blk", scatter_dimension=0, tiled=True)
        gmb = gmb.reshape((nb // 2, 2) + gmb.shape[1:])
    else:
        gma = gma.reshape(nh, nb * own_rows, gma.shape[1])
        gma = lax.psum_scatter(gma, "blk", scatter_dimension=1, tiled=True)
        gmb = gmb.reshape(nh, nb // 2, 2, own_rows, gmb.shape[1]).transpose(1, 2, 0, 3, 4)
    gma = gma.reshape(nh, own_rows, gma.shape[-1])
    y_out, dh, do_in, go, gmb = back_exchange(
        dpart, ypart, hid, out_grad, valid, wo, og, gmb
    )
    dq, dkv = attend_grad(qin, do_in, of, kv_all, q_first, q_last, lse, lo, hi, rows)
    gq, dpart1 = grads_back(dq, dkv.reshape(nh, nb, rows, 2 * DH), cos, sin, n1, wq, hl)
    dn, farq, faro, gma, gmb = last_exchange(
        dpart1,
        gq.reshape(nh, nb // 2, 2, own_rows, 3 * lw),
        go.reshape(nb // 2, 2, own_rows, width),
        gma,
        gmb,
    )
    y_out, dx, d_ln_attn, d_wqkv, d_wout, d_ln_mlp, d_win, d_wd = finish(
        dn, layer_input, dh, y_out, farq, faro, gma, gmb, w_qkv, w_in, gain_attn, gain_mlp, fl
    )
    return (
        y_out,
        dx,
        d_ln_attn.reshape(own_rows),
        d_wqkv,
        d_wout,
        d_ln_mlp.reshape(own_rows),
        d_win,
        d_wd.T,
    )


def solution(mesh):
    both = ("head", "blk")
    row_split = P(both, None)
    return jax.shard_map(
        shards,
        mesh=mesh,
        in_specs=(
            row_split,
            row_split,
            P(),
            P(both),
            row_split,
            row_split,
            P(both),
            row_split,
            P(None, both),
        ),
        out_specs=(
            row_split,
            row_split,
            P(both),
            row_split,
            row_split,
            P(both),
            row_split,
            P(None, both),
        ),
        check_vma=False,
    )
```

```python
import functools
import math

import jax
import jax.numpy as jnp
from jax import lax
from jax.experimental import pallas as pl
from jax.experimental.pallas import tpu as pltpu
from jax.sharding import PartitionSpec as P

DH = 64
ROPE_BASE = 160000.0
NORM_EPS = 1e-05
MASK_FLOOR = -1e30
KEY_BLOCK = 512
GRAD_CUT = 1280
EXP_SCALE = 0.125 * math.log2(math.e)
BF16 = jnp.bfloat16
F32 = jnp.float32
MESH_ID = pl.DeviceIdType.MESH
ANY = pl.BlockSpec(memory_space=pl.ANY)
VM = pl.BlockSpec(memory_space=pltpu.VMEM)
SM = pl.BlockSpec(memory_space=pltpu.SMEM)


def dims():
    nh = lax.axis_size("head")
    nb = lax.axis_size("blk")
    return nh, nb


def me():
    return lax.axis_index("head"), lax.axis_index("blk")


def comm_call(body, name, cid, out_shape, in_specs, out_specs, scratch, args, vmem=None):
    return pl.pallas_call(
        body,
        out_shape=out_shape,
        in_specs=in_specs,
        out_specs=out_specs,
        scratch_shapes=scratch,
        name=name,
        compiler_params=pltpu.CompilerParams(
            collective_id=cid, has_side_effects=True, vmem_limit_bytes=vmem
        ),
    )(*args)


def remote(src, dst, send, recv, h, b):
    return pltpu.make_async_remote_copy(
        src_ref=src,
        dst_ref=dst,
        send_sem=send,
        recv_sem=recv,
        device_id=(h, b),
        device_id_type=MESH_ID,
    )


def signal(h, b):
    pl.semaphore_signal(
        pltpu.get_barrier_semaphore(), inc=1, device_id=(h, b), device_id_type=MESH_ID
    )


def signal_head(nh, h, b):
    for i in range(1, nh):
        signal((h + i) % nh, b)


def wait_head(nh):
    pl.semaphore_wait(pltpu.get_barrier_semaphore(), nh - 1)


def signal_all(nh, nb, h, b):
    @pl.loop(1, nh * nb)
    def _(i):
        signal((h + i // nb) % nh, (b + i % nb) % nb)


def wait_all(nh, nb):
    pl.semaphore_wait(pltpu.get_barrier_semaphore(), nh * nb - 1)


class HeadGather:
    def __init__(self, nh, h, b, src, dst, sems):
        self.nh, self.h, self.b, self.dst, self.sems = nh, h, b, dst, sems
        nx = nh // 2
        self.nx = nx
        x, c = h // 2, h % 2
        sib = x * 2 + 1 - c
        self.sib = sib
        self.across = []
        for k in range(1, nx):
            self.across.append(
                remote(src, dst.at[h], sems.at[0, k], sems.at[1, k], ((x + k) % nx) * 2 + c, b)
            )
        self.near = remote(src, dst.at[h], sems.at[0, 0], sems.at[1, 0], sib, b)
        self.local = pltpu.make_async_copy(src, dst.at[h], sems.at[2, 0])
        self.forward = []
        for k in range(1, nx):
            got = ((x + nx - k) % nx) * 2 + c
            self.forward.append(
                remote(dst.at[got], dst.at[got], sems.at[2, k], sems.at[3, k], sib, b)
            )

    @staticmethod
    def sem_shape(nh):
        return pltpu.SemaphoreType.DMA((4, nh // 2))

    def start(self):
        for cp in self.across:
            cp.start()
        self.near.start()
        self.local.start()

    def pass_on(self):
        for cp, fw in zip(self.across, self.forward):
            cp.wait_recv()
            fw.start()

    def finish(self):
        for cp in self.across:
            cp.wait_send()
        self.near.wait()
        self.local.wait()
        for fw in self.forward:
            fw.wait()


def lane_roll(values, shift):
    return pltpu.roll(values, shift % values.shape[1], 1)


def lanes_of(values):
    return lax.broadcasted_iota(jnp.int32, (1, values.shape[1]), 1)


def widen(values, width):
    extra = width - values.shape[1]
    if extra <= 0:
        return values[:, :width]
    return jnp.concatenate([values, jnp.zeros((values.shape[0], extra), values.dtype)], axis=1)


def column(row):
    n = row.shape[1]
    same = lax.broadcasted_iota(jnp.int32, (n, n), 0) == lax.broadcasted_iota(jnp.int32, (n, n), 1)
    return jnp.sum(jnp.where(same, row, 0.0), axis=1, keepdims=True)


def as_row(col):
    n = col.shape[0]
    same = lax.broadcasted_iota(jnp.int32, (n, n), 0) == lax.broadcasted_iota(jnp.int32, (n, n), 1)
    return jnp.sum(jnp.where(same, col, 0.0), axis=0, keepdims=True)


def sequence_ends(len_ref):
    ends, total = [], 0
    for i in range(len_ref.shape[0]):
        total = total + len_ref[i]
        ends.append(total)
    return ends


def segment_first(slot, ends):
    first = jnp.zeros_like(slot)
    for end in ends:
        first = jnp.where(slot >= end, end, first)
    return first


def segment_end(slot, ends, slots):
    last = jnp.zeros_like(slot) + slots
    for end in reversed(ends):
        last = jnp.where(slot < end, end, last)
    return last


def half_pick(low_src, high_src, low_at, high_at):
    low = low_src if low_at == 0 else lane_roll(low_src, DH)
    high = high_src if high_at == 1 else lane_roll(high_src, DH)
    return jnp.where(lanes_of(low) < DH, low, high)


def ff_widths(fl):
    up = lambda v: (v + 127) // 128 * 128
    return up(3 * fl), up(2 * fl), 2 * fl // 128 * 128


class LineGather:
    def __init__(self, pc, src, place, sems):
        self.pc, self.src, self.place, self.sems = pc, src, place, sems

    @staticmethod
    def sem_shape(nz):
        return pltpu.SemaphoreType.DMA((5, nz))

    def origin(self, t, up):
        return self.pc.zi - t if up else self.pc.zi + t

    def move(self, t, up):
        pc = self.pc
        at = self.place(self.origin(t, up))
        n = 0 if up else 2
        return remote(
            self.src if t == 0 else at,
            at,
            self.sems.at[n, t],
            self.sems.at[n + 1, t],
            pc.h,
            pc.b + pc.qs if up else pc.b - pc.qs,
        )

    def sends(self, t, up):
        zi, nz = self.pc.zi, self.pc.nz
        if up:
            return jnp.logical_and(zi - t >= 0, zi + 1 < nz)
        return jnp.logical_and(zi + t < nz, zi - 1 >= 0)

    def local(self):
        return pltpu.make_async_copy(self.src, self.place(self.pc.zi), self.sems.at[4, 0])

    def start(self):
        for up in (True, False):

            @pl.when(self.sends(0, up))
            def _():
                self.move(0, up).start()

        self.local().start()

    def step(self, t, arrived=None):
        low = self.pc.zi < self.pc.nz // 2
        self.take(t, False, jnp.logical_not(low), arrived)
        self.take(t, True, True, arrived)
        self.take(t, False, low, arrived)

    def take(self, t, up, now, arrived):
        zi, nz = self.pc.zi, self.pc.nz
        origin = self.origin(t, up)
        here = jnp.logical_and(now, origin >= 0 if up else origin < nz)

        @pl.when(here)
        def _():
            wait_on(self.place(origin), self.sems.at[1 if up else 3, t - 1])

        if t < nz - 1:

            @pl.when(jnp.logical_and(now, self.sends(t, up)))
            def _():
                self.move(t, up).start()

        if arrived is not None:

            @pl.when(here)
            def _():
                arrived(origin)

    def finish(self):
        self.local().wait()
        for t in range(self.pc.nz - 1):
            for up in (True, False):

                @pl.when(self.sends(t, up))
                def _():
                    self.move(t, up).wait_send()


class BlkGather:
    def __init__(self, pc, src, out, sems, ssem):
        self.pc, self.out, self.ssem, self.src = pc, out, ssem, src
        self.line = LineGather(pc, src, lambda zi: out.at[:, zi, pc.s], sems)

    @staticmethod
    def sem_shapes(nz, qs):
        return [LineGather.sem_shape(nz), pltpu.SemaphoreType.DMA((2, nz, qs))]

    def side(self, zi, ds, own=False):
        pc = self.pc
        ref = self.out.at[:, zi, pc.s]
        return remote(
            self.src if own else ref,
            ref,
            self.ssem.at[0, zi, ds],
            self.ssem.at[1, zi, ds],
            pc.h,
            pc.zi * pc.qs + (pc.s + ds) % pc.qs,
        )

    def spread(self, zi, own=False):
        for ds in range(1, self.pc.qs):
            self.side(zi, ds, own).start()

    def start(self):
        self.line.start()
        self.spread(self.pc.zi, True)

    def step(self, t):
        self.line.step(t, self.spread)

    def finish(self):
        self.line.finish()

        @pl.loop(0, self.pc.nz)
        def _(zi):
            for ds in range(1, self.pc.qs):
                self.side(zi, ds).wait()


class LineSum:
    def __init__(self, pc, term, sent, got, sems):
        self.pc, self.term, self.sent, self.got, self.sems = pc, term, sent, got, sems

    @staticmethod
    def scratch(nz, shape):
        return [
            pltpu.VMEM((2, nz) + shape, BF16),
            pltpu.VMEM((2, nz) + shape, BF16),
            pltpu.SemaphoreType.DMA((4, nz)),
        ]

    def move(self, d, up):
        pc = self.pc
        n = 0 if up else 1
        return remote(
            self.sent.at[n, d],
            self.got.at[n, d],
            self.sems.at[2 * n, d],
            self.sems.at[2 * n + 1, d],
            pc.h,
            pc.b + pc.qs if up else pc.b - pc.qs,
        )

    def takes(self, up):
        return self.pc.zi > 0 if up else self.pc.zi < self.pc.nz - 1

    def lead(self, j):
        self.step(j, False)

    def follow(self, j):
        self.step(j, True)

    def step(self, j, taking):
        low = self.pc.zi < self.pc.nz // 2
        if taking:
            self.one(j, False, jnp.logical_not(low), True)
            self.one(j, True, True, True)
            self.one(j, False, low, True)
        else:
            self.one(j, True, True, False)
            self.one(j, False, True, False)

    def one(self, j, up, now, taking):
        zi, nz = self.pc.zi, self.pc.nz
        d = nz - 1 - j if up else j
        n = 0 if up else 1
        takes = self.takes(up)
        far = jnp.logical_and(now, zi < d if up else zi > d)

        @pl.when(jnp.logical_and(far, takes if taking else jnp.logical_not(takes)))
        def _():
            if taking:
                wait_on(self.got.at[n, d], self.sems.at[2 * n + 1, d])
                self.sent[n, d] = (self.term(d) + self.got[n, d].astype(F32)).astype(BF16)
            else:
                self.sent[n, d] = self.term(d).astype(BF16)
            self.move(d, up).start()

    def total(self, total_ref):
        zi = self.pc.zi
        total_ref[...] = self.term(zi)
        for up in (True, False):
            n = 0 if up else 1

            @pl.when(self.takes(up))
            def _():
                wait_on(self.got.at[n, zi], self.sems.at[2 * n + 1, zi])
                total_ref[...] += self.got[n, zi].astype(F32)

    def finish(self):
        zi, nz = self.pc.zi, self.pc.nz
        for j in range(nz - 1):
            for up in (True, False):
                d = nz - 1 - j if up else j

                @pl.when(zi < d if up else zi > d)
                def _():
                    self.move(d, up).wait_send()


class StretchSum:
    def __init__(self, pc, part, got, sems):
        self.pc, self.part, self.got, self.sems = pc, part, got, sems

    @staticmethod
    def scratch(nz, shape):
        return [pltpu.VMEM((nz,) + shape, BF16), pltpu.SemaphoreType.DMA((2, nz))]

    def move(self, i):
        pc = self.pc
        to = (pc.zi + i) % pc.nz
        return remote(
            self.part.at[to],
            self.got.at[pc.zi],
            self.sems.at[0, i],
            self.sems.at[1, i],
            pc.h,
            to * pc.qs + pc.s,
        )

    def start(self):
        for i in range(1, self.pc.nz):
            self.move(i).start()

    def total(self):
        pc = self.pc
        total = self.part[pc.zi].astype(F32)
        for i in range(1, pc.nz):
            self.move(i).wait_recv()
            total = total + self.got[(pc.zi + pc.nz - i) % pc.nz].astype(F32)
        return total

    def finish(self):
        for i in range(1, self.pc.nz):
            self.move(i).wait_send()


class PlaneWeights:
    def __init__(self, pc, pack, out, sems, ksem):
        self.pc, self.pack, self.out, self.sems, self.ksem = pc, pack, out, sems, ksem

    @staticmethod
    def sem_shapes(nh, nz, qs):
        dma = pltpu.SemaphoreType.DMA
        return [dma((2, nz)), dma((4, nh // 2 * qs))]

    def along(self, i):
        pc = self.pc
        to = (pc.zi + i) % pc.nz
        return remote(
            self.pack.at[to],
            self.out.at[pc.h, pc.zi, pc.s],
            self.sems.at[0, i],
            self.sems.at[1, i],
            pc.h,
            to * pc.qs + pc.s,
        )

    def local(self):
        pc = self.pc
        return pltpu.make_async_copy(
            self.pack.at[pc.zi], self.out.at[pc.h, pc.zi, pc.s], self.sems.at[0, 0]
        )

    def place(self, i, sign):
        pc = self.pc
        nx = pc.nh // 2
        dx, ds = i // pc.qs, i % pc.qs
        if sign < 0:
            dx, ds = nx - dx, pc.qs - ds
        return ((pc.x + dx) % nx) * 2 + pc.c, (pc.s + ds) % pc.qs

    def across(self, i):
        pc = self.pc
        th, ts = self.place(i, 1)
        ref = self.out.at[pc.h, :, pc.s]
        return remote(
            ref, ref, self.ksem.at[0, i], self.ksem.at[1, i], th, pc.zi * pc.qs + ts
        )

    def near(self, i):
        pc = self.pc
        gh, gs = self.place(i, -1)
        ref = self.out.at[gh, :, gs]
        return remote(ref, ref, self.ksem.at[2, i], self.ksem.at[3, i], pc.sib, pc.b)

    def start(self):
        for i in range(1, self.pc.nz):
            self.along(i).start()
        self.local().start()

    def spread(self):
        pc = self.pc
        self.local().wait()
        for i in range(1, pc.nz):
            self.along(i).wait_recv()

        @pl.loop(1, pc.nh // 2 * pc.qs)
        def _(i):
            self.across(i).start()

        self.near(0).start()

    def pass_on(self):
        @pl.loop(1, self.pc.nh // 2 * self.pc.qs)
        def _(i):
            self.across(i).wait_recv()
            self.near(i).start()

    def finish(self):
        for i in range(1, self.pc.nz):
            self.along(i).wait_send()

        @pl.loop(1, self.pc.nh // 2 * self.pc.qs)
        def _(i):
            self.across(i).wait_send()

        @pl.loop(0, self.pc.nh // 2 * self.pc.qs)
        def _(i):
            self.near(i).wait()


def first_body(nh, nb, hl, fl, len_ref, x_ref, wq_ref, ga_ref, win_hbm, gf_ref, wd_hbm, g_ref, n1_all, wma, wmb, wq_all, gg, cos_ref, sin_ref, own_n, pack, wmp, win_ref, wd_ref, lsem, wsem, ksem, gsem, msem, stage):
    pc = Place(nh, nb, hl)
    h, b = pc.h, pc.b
    loads = [
        pltpu.make_async_copy(win_hbm, win_ref, stage.at[0]),
        pltpu.make_async_copy(wd_hbm, wd_ref, stage.at[1]),
    ]
    for cp in loads:
        cp.start()
    signal_all(nh, nb, h, b)
    width = x_ref.shape[1]
    lw = width // pc.nz
    gain = column(ga_ref[...].astype(F32))
    for c in range(3):
        w = wq_ref[:, c * width : (c + 1) * width].astype(F32) * gain
        tile = lambda l, i: w[:, l * pc.nz * DH + i // 2 * 128 : l * pc.nz * DH + i // 2 * 128 + 128]
        for i in range(pc.nz):
            for p in range(nh // 2):
                both = half_pick(tile(2 * p, i), tile(2 * p + 1, i), i % 2, i % 2)
                at = c * lw + p * 128
                pack[i, :, at : at + 128] = both.astype(BF16)
    own_n[...] = norm_of(x_ref[...].astype(F32))[0].astype(BF16)
    wait_all(nh, nb)
    weights = PlaneWeights(pc, pack, wq_all, wsem, ksem)
    line = LineGather(pc, own_n, lambda zi: n1_all.at[zi], lsem)
    gather = HeadGather(nh, h, b, g_ref, gg, gsem)
    weights.start()
    line.start()
    gather.start()
    for cp in loads:
        cp.wait()
    total, _, off = ff_widths(fl)
    ff = nh * fl
    win = win_ref[...].astype(F32) * column(gf_ref[...].astype(F32))
    wd = widen(wd_ref[...].astype(F32), total if total > ff else (ff + 127) // 128 * 128)
    lane = lax.broadcasted_iota(jnp.int32, (1, total), 1)
    for i in range(nh):
        gate = widen(lane_roll(win, -i * fl), total)
        up = widen(lane_roll(win, fl - ff - i * fl), total)
        down = widen(lane_roll(wd, 2 * fl - i * fl), total)
        piece = jnp.where(
            lane < fl,
            gate,
            jnp.where(lane < 2 * fl, up, jnp.where(lane < 3 * fl, down, 0.0)),
        )
        wmp[i] = piece.astype(BF16)
    copies = []
    for n, (dst, cols) in enumerate(((wma, pl.ds(0, off)), (wmb, pl.ds(off, total - off)))):
        for i in range(1, nh):
            th = (h + i) % nh
            src = wmp.at[th, :, cols]
            copies.append(remote(src, dst.at[h], msem.at[0, n, i], msem.at[1, n, i], th, b))
        copies.append(pltpu.make_async_copy(wmp.at[h, :, cols], dst.at[h], msem.at[0, n, 0]))
    weights.spread()
    for cp in copies:
        cp.start()
    ends = sequence_ends(len_ref)
    rows = x_ref.shape[0]
    lane = lax.broadcasted_iota(jnp.int32, (1, 2 * DH), 1)
    power = (lane % (DH // 2)).astype(F32) * (-2.0 / DH)
    inv_freq = jnp.exp2(power * math.log2(ROPE_BASE))
    sign = jnp.where(lane % DH < DH // 2, -1.0, 1.0)
    line.step(1)
    for i in range(pc.nz):
        slot = (h * nb + i * pc.qs + pc.s) * rows + lax.broadcasted_iota(jnp.int32, (rows, 1), 0)
        angle = (slot - segment_first(slot, ends)).astype(F32) * inv_freq
        cos_ref[i * rows : (i + 1) * rows, :] = jnp.cos(angle)
        sin_ref[i * rows : (i + 1) * rows, :] = jnp.sin(angle) * sign
    gather.pass_on()
    for t in range(2, pc.nz):
        line.step(t)
    weights.pass_on()
    for cp in copies:
        cp.wait()
    weights.finish()
    line.finish()
    gather.finish()


def first_exchange(lengths, x, w_qkv, gain_attn, w_in, gain_mlp, wd_t, g, hl, fl):
    nh, nb = dims()
    rows, width = x.shape
    nz, qs = hl, nb // hl
    lw = width // nz
    own_rows = w_in.shape[0]
    total, _, off = ff_widths(fl)
    dma = pltpu.SemaphoreType.DMA
    return comm_call(
        functools.partial(first_body, nh, nb, hl, fl),
        "first_exchange",
        0,
        (
            jax.ShapeDtypeStruct((nz, rows, width), BF16),
            jax.ShapeDtypeStruct((nh, own_rows, off), BF16),
            jax.ShapeDtypeStruct((nh, own_rows, total - off), BF16),
            jax.ShapeDtypeStruct((nh, nz, qs, own_rows, 3 * lw), BF16),
            jax.ShapeDtypeStruct((nh, rows, width), BF16),
            jax.ShapeDtypeStruct((nz * rows, 2 * DH), F32),
            jax.ShapeDtypeStruct((nz * rows, 2 * DH), F32),
        ),
        [SM, VM, VM, VM, ANY, VM, ANY, ANY],
        [ANY] * 5 + [VM] * 2,
        [
            pltpu.VMEM((rows, width), BF16),
            pltpu.VMEM((nz, own_rows, 3 * lw), BF16),
            pltpu.VMEM((nh, own_rows, total), BF16),
            pltpu.VMEM(w_in.shape, BF16),
            pltpu.VMEM(wd_t.shape, BF16),
            LineGather.sem_shape(nz),
        ]
        + PlaneWeights.sem_shapes(nh, nz, qs)
        + [
            HeadGather.sem_shape(nh),
            dma((2, 2, nh)),
            dma((2,)),
        ],
        (lengths, x, w_qkv, gain_attn, w_in, gain_mlp, wd_t, g),
        vmem=60 << 20,
    )


class Place:
    def __init__(self, nh, nb, hl):
        h, b = me()
        self.nh, self.nb, self.h, self.b = nh, nb, h, b
        self.x, self.c = h // 2, h % 2
        self.nz = hl
        self.qs = nb // hl
        self.cb = self.qs // 2
        self.sib = self.x * 2 + 1 - self.c
        self.zi, self.s = b // self.qs, b % self.qs
        self.head = self.x * 2 + self.s // self.cb
        self.u = self.s % self.cb
        self.from_s = self.u * 2 + self.c

    def attends(self, zi, l, core, u):
        return (l // 2) * 2 + core, zi * self.qs + (l % 2) * self.cb + u


def routed(pc, src, dst, send, recv, th, tb, act):
    mine = jnp.logical_and(th == pc.h, tb == pc.b)

    @pl.when(mine)
    def _():
        if act == "start":
            pltpu.make_async_copy(src, dst, recv).start()

    @pl.when(jnp.logical_not(mine))
    def _():
        cp = remote(src, dst, send, recv, th, tb)
        if act == "start":
            cp.start()
        else:
            cp.wait_send()


def wait_on(ref, sem):
    pltpu.make_async_copy(ref, ref, sem).wait()


def stretch_lanes(ref, zi, rows):
    return ref.at[:, :, pl.ds(pl.multiple_of(zi * rows, rows), rows)]


def outputs_back(pc, o_ref, og, osem, act):
    rows = og.shape[3]
    for zi in range(pc.nz):
        routed(
            pc,
            stretch_lanes(o_ref, zi, rows),
            og.at[pc.zi],
            osem.at[0, zi],
            osem.at[1, pc.zi],
            pc.head,
            zi * pc.qs + pc.from_s,
            act,
        )


def grads_out(pc, dots, do_in, qsem, act):
    rows = dots.shape[3]
    for zi in range(pc.nz):
        th, tb = pc.attends(zi, pc.h, pc.s % 2, pc.s // 2)
        routed(
            pc,
            dots.at[zi],
            stretch_lanes(do_in, pc.zi, rows),
            qsem.at[0, zi],
            qsem.at[1, pc.zi],
            th,
            tb,
            act,
        )


def halves_swapped(tile):
    lane = lanes_of(tile)
    return jnp.where(lane % DH < DH // 2, lane_roll(tile, -(DH // 2)), lane_roll(tile, DH // 2))


def turned(tile, cos, sin):
    return tile * cos + halves_swapped(tile) * sin


def to_heads_body(nh, nb, hl, n1_hbm, w_hbm, cos_ref, sin_ref, wo_ref, qin, kvin, wo_all, qbuf, kvbuf, n1_ref, w_ref, qsem, ksem, fsem, osem, osem2, stage):
    pc = Place(nh, nb, hl)
    loads = [
        pltpu.make_async_copy(n1_hbm, n1_ref, stage.at[0]),
        pltpu.make_async_copy(w_hbm, w_ref, stage.at[1]),
    ]
    for cp in loads:
        cp.start()
    signal_all(nh, nb, pc.h, pc.b)
    rows = kvbuf.shape[2]
    lw = nh * DH
    for cp in loads:
        cp.wait()
    n1 = n1_ref[...]
    cos, sin = cos_ref[...], sin_ref[...]
    kk = jnp.dot(n1, w_ref[:, lw : 2 * lw], preferred_element_type=F32)
    vv = jnp.dot(n1, w_ref[:, 2 * lw :], preferred_element_type=F32)
    for p in range(nh // 2):
        k = turned(kk[:, p * 128 : (p + 1) * 128], cos, sin)
        v = vv[:, p * 128 : (p + 1) * 128]
        low = lanes_of(k) < DH
        even = jnp.where(low, k, lane_roll(v, DH)).astype(BF16)
        odd = jnp.where(low, lane_roll(k, DH), v).astype(BF16)
        for i in range(pc.nz):
            kvbuf[2 * p, i] = even[i * rows : (i + 1) * rows]
            kvbuf[2 * p + 1, i] = odd[i * rows : (i + 1) * rows]
    wait_all(nh, nb)

    def keys_out(act):
        for l in range(nh):
            for u in range(pc.cb):
                th, tb = pc.attends(pc.zi, l, pc.s % 2, u)
                routed(
                    pc,
                    kvbuf.at[l],
                    kvin.at[pc.h, :, pc.s],
                    ksem.at[0, l * pc.cb + u],
                    ksem.at[1, pc.h * pc.cb + pc.s // 2],
                    th,
                    tb,
                    act,
                )

    def queries_out(act):
        for l in range(nh):
            th, tb = pc.attends(pc.zi, l, pc.s % 2, pc.s // 2)
            routed(
                pc, qbuf.at[l], qin.at[pc.h], qsem.at[0, l], qsem.at[1, pc.h], th, tb, act
            )

    spread = BlkGather(pc, wo_ref, wo_all, osem, osem2)
    keys_out("start")
    spread.start()
    qq = jnp.dot(n1, w_ref[:, :lw], preferred_element_type=F32)
    for p in range(nh // 2):
        q = turned(qq[:, p * 128 : (p + 1) * 128], cos, sin).T.astype(BF16)
        qbuf[2 * p] = q[:DH]
        qbuf[2 * p + 1] = q[DH:]
    queries_out("start")
    count = nh * pc.cb

    def forward(i):
        at = kvin.at[i // pc.cb, :, 2 * (i % pc.cb) + pc.c]
        return remote(at, at, fsem.at[0, i], fsem.at[1, i], pc.sib, pc.b)

    @pl.loop(0, count)
    def _(i):
        wait_on(kvin.at[i // pc.cb, :, 2 * (i % pc.cb) + pc.c], ksem.at[1, i])
        forward(i).start()

    for t in range(1, pc.nz):
        spread.step(t)
    keys_out("wait_send")
    queries_out("wait_send")
    for i in range(nh):
        wait_on(qin.at[i], qsem.at[1, i])

    @pl.loop(0, count)
    def _(i):
        forward(i).wait()

    spread.finish()


def to_heads(n1, wq, cos, sin, wo, hl):
    nh, nb = dims()
    group, width = n1.shape
    nz, qs = hl, nb // hl
    cb = qs // 2
    rows = group // nz
    dma = pltpu.SemaphoreType.DMA
    return comm_call(
        functools.partial(to_heads_body, nh, nb, hl),
        "to_heads",
        1,
        (
            jax.ShapeDtypeStruct((nh, DH, group), BF16),
            jax.ShapeDtypeStruct((nh, nz, qs, rows, 2 * DH), BF16),
            jax.ShapeDtypeStruct((1, nz, qs) + wo.shape[1:], BF16),
        ),
        [ANY, ANY, VM, VM, ANY],
        [ANY, ANY, ANY],
        [
            pltpu.VMEM((nh, DH, group), BF16),
            pltpu.VMEM((nh, nz, rows, 2 * DH), BF16),
            pltpu.VMEM(n1.shape, BF16),
            pltpu.VMEM(wq.shape, BF16),
            dma((2, nh)),
            dma((2, nh * cb)),
            dma((2, nh * cb)),
        ]
        + BlkGather.sem_shapes(nz, qs)
        + [dma((2,))],
        (n1, wq, cos, sin, wo),
        vmem=60 << 20,
    )


class Queries:
    def __init__(self, nh, nb, hl, len_ref, lanes, slots):
        pc = Place(nh, nb, hl)
        tile = pl.program_id(0)
        rows = lanes // 2
        each = pc.nz // 2
        ends = sequence_ends(len_ref)
        base = (tile // each) * nb + (tile % each) * 2 * pc.qs + pc.from_s
        lane = lax.broadcasted_iota(jnp.int32, (1, lanes), 1)
        slot = (base + jnp.where(lane < rows, 0, pc.qs)) * rows + lane % rows
        self.first = segment_first(slot, ends)
        self.last = segment_end(slot, ends, slots)
        self.lo = segment_first(base * rows, ends) // KEY_BLOCK
        far = (base + pc.qs) * rows + rows - 1
        self.hi = (segment_end(far, ends, slots) + KEY_BLOCK - 1) // KEY_BLOCK
        self.lanes = lanes

    def allowed(self, block_at):
        at = block_at * KEY_BLOCK + lax.broadcasted_iota(jnp.int32, (KEY_BLOCK, self.lanes), 0)
        return jnp.logical_and(at >= self.first, at < self.last)


def attend_body(nh, nb, hl, len_ref, q_ref, kv_ref, o_ref, of_ref, lse_ref):
    q = q_ref[0]
    lanes = q.shape[1]
    at = Queries(nh, nb, hl, len_ref, lanes, kv_ref.shape[0])
    q_pad = jnp.concatenate([q, jnp.zeros_like(q)], axis=0)

    def step(j, carry):
        top, total, acc = carry
        kv = kv_ref[pl.ds(pl.multiple_of(j * KEY_BLOCK, KEY_BLOCK), KEY_BLOCK), :]
        s = jnp.dot(kv, q_pad, preferred_element_type=F32)
        s = jnp.where(at.allowed(j), s, MASK_FLOOR)
        new_top = jnp.maximum(top, jnp.max(s, axis=0, keepdims=True))
        p = jnp.exp2((s - new_top) * EXP_SCALE)
        alpha = jnp.exp2((top - new_top) * EXP_SCALE)
        total = total * alpha + jnp.sum(p, axis=0, keepdims=True)
        acc = acc * alpha + lax.dot_general(
            kv, p.astype(BF16), (((0,), (0,)), ((), ())), preferred_element_type=F32
        )
        return new_top, total, acc

    top, total, acc = lax.fori_loop(
        at.lo,
        at.hi,
        step,
        (
            jnp.full((1, lanes), MASK_FLOOR, F32),
            jnp.zeros((1, lanes), F32),
            jnp.zeros((2 * DH, lanes), F32),
        ),
    )
    o = acc[DH:] / total
    of_ref[0] = o
    o_ref[0] = o.astype(BF16)
    lse_ref[0] = top * EXP_SCALE + jnp.log2(total)


def attend_specs(kv_rows, lanes, tiles_each):
    tile_spec = pl.BlockSpec((1, DH, lanes), lambda i, *_: (i // tiles_each, 0, i % tiles_each))
    row_spec = pl.BlockSpec((1, 1, lanes), lambda i, *_: (i, 0, 0))
    kv_spec = pl.BlockSpec((kv_rows, 2 * DH), lambda i, *_: (0, 0))
    return tile_spec, row_spec, kv_spec


def attend(lengths, q, kv, lanes, hl):
    nh, nb = dims()
    each = q.shape[2] // lanes
    tiles = q.shape[0] * each
    tile_spec, row_spec, kv_spec = attend_specs(kv.shape[0], lanes, each)
    return pl.pallas_call(
        functools.partial(attend_body, nh, nb, hl),
        grid_spec=pltpu.PrefetchScalarGridSpec(
            num_scalar_prefetch=1,
            grid=(tiles,),
            in_specs=[tile_spec, kv_spec],
            out_specs=[tile_spec, tile_spec, row_spec],
        ),
        out_shape=(
            jax.ShapeDtypeStruct(q.shape, BF16),
            jax.ShapeDtypeStruct(q.shape, F32),
            jax.ShapeDtypeStruct((tiles, 1, lanes), F32),
        ),
        name="attend",
        compiler_params=pltpu.CompilerParams(vmem_limit_bytes=60 << 20),
    )(lengths, q, kv)


def attend_grad_body(nh, nb, hl, len_ref, q_ref, do_ref, of_ref, kv_ref, lse_ref, dq_ref, dkv_ref, acc_ref):
    tile = pl.program_id(0)

    @pl.when(tile == 0)
    def _():
        acc_ref[...] = jnp.zeros_like(acc_ref)

    q = q_ref[0]
    do = do_ref[0]
    lanes = q.shape[1]
    place = Queries(nh, nb, hl, len_ref, lanes, kv_ref.shape[0])
    zero = jnp.zeros_like(q)
    both = jnp.concatenate(
        [jnp.concatenate([q, zero], axis=0), jnp.concatenate([zero, do], axis=0)], axis=1
    )
    delta = jnp.sum(do.astype(F32) * of_ref[0], axis=0, keepdims=True)
    lse = lse_ref[0]

    def step(j, dq):
        at = pl.ds(pl.multiple_of(j * KEY_BLOCK, KEY_BLOCK), KEY_BLOCK)
        kv = kv_ref[at, :]
        sd = jnp.dot(kv, both, preferred_element_type=F32)
        s, dp = sd[:, :lanes], sd[:, lanes:]
        p = jnp.exp2(
            jnp.where(place.allowed(j), s * EXP_SCALE - lse, MASK_FLOOR)
        )
        ds = (p * (dp - delta)).astype(BF16)
        acc_ref[at, :] += lax.dot_general(
            jnp.concatenate([ds, p.astype(BF16)], axis=1),
            both,
            (((1,), (1,)), ((), ())),
            preferred_element_type=F32,
        )
        return dq + lax.dot_general(
            kv, ds, (((0,), (0,)), ((), ())), preferred_element_type=F32
        )

    dq = lax.fori_loop(place.lo, place.hi, step, jnp.zeros((2 * DH, lanes), F32))
    dq_ref[0] = (dq[:DH] * 0.125).astype(BF16)

    @pl.when(tile == pl.num_programs(0) - 1)
    def _():
        lane = lax.broadcasted_iota(jnp.int32, (1, 2 * DH), 1)
        dkv_ref[...] = (acc_ref[...] * jnp.where(lane < DH, 0.125, 1.0)).astype(BF16)


def attend_grad(lengths, q, do, of, kv, lse, hl):
    nh, nb = dims()
    tiles, _, lanes = lse.shape
    tile_spec, row_spec, kv_spec = attend_specs(kv.shape[0], lanes, tiles // q.shape[0])
    return pl.pallas_call(
        functools.partial(attend_grad_body, nh, nb, hl),
        grid_spec=pltpu.PrefetchScalarGridSpec(
            num_scalar_prefetch=1,
            grid=(tiles,),
            in_specs=[tile_spec, tile_spec, tile_spec, kv_spec, row_spec],
            out_specs=[tile_spec, kv_spec],
            scratch_shapes=[pltpu.VMEM(kv.shape, F32)],
        ),
        out_shape=(jax.ShapeDtypeStruct(q.shape, BF16), jax.ShapeDtypeStruct(kv.shape, BF16)),
        name="attend_grad",
        compiler_params=pltpu.CompilerParams(vmem_limit_bytes=60 << 20),
    )(lengths, q, do, of, kv, lse)


class HeadSum:
    def __init__(self, nh, h, b, part, near, far, out, sems):
        self.nx = nh // 2
        self.x, self.c = h // 2, h % 2
        self.h, self.part, self.near, self.far, self.out = h, part, near, far, out
        sib = self.x * 2 + 1 - self.c
        self.pairs = [
            remote(
                part.at[((self.x + k) % self.nx) * 2 + 1 - self.c],
                near.at[k],
                sems.at[0, k],
                sems.at[1, k],
                sib,
                b,
            )
            for k in range(self.nx)
        ]
        self.across = [
            remote(
                out.at[k],
                far.at[k],
                sems.at[2, k],
                sems.at[3, k],
                ((self.x + k) % self.nx) * 2 + self.c,
                b,
            )
            for k in range(1, self.nx)
        ]

    @staticmethod
    def sem_shape(nh):
        return pltpu.SemaphoreType.DMA((4, nh // 2))

    @staticmethod
    def buffers(nh, rows, width):
        return [pltpu.VMEM((nh // 2, rows, width), BF16)] * 3

    def start(self):
        for k in list(range(1, self.nx)) + [0]:
            self.pairs[k].start()

    def send(self):
        for k in range(1, self.nx):
            self.pairs[k].wait_recv()
            at = ((self.x + k) % self.nx) * 2 + self.c
            self.out[k] = (self.part[at].astype(F32) + self.near[k].astype(F32)).astype(BF16)
            self.across[k - 1].start()

    def total(self):
        self.pairs[0].wait_recv()
        total = self.part[self.h].astype(F32) + self.near[0].astype(F32)
        for k in range(1, self.nx):
            self.across[k - 1].wait_recv()
            total = total + self.far[k].astype(F32)
        return total

    def finish(self):
        for cp in self.pairs:
            cp.wait_send()
        for cp in self.across:
            cp.wait_send()


def norm_of(values):
    centre = values - jnp.mean(values, axis=-1, keepdims=True)
    scale = lax.rsqrt(jnp.mean(centre * centre, axis=-1, keepdims=True) + NORM_EPS)
    return centre * scale, scale


def norm_pull(grad, normed, scale):
    one = jnp.mean(grad, axis=-1, keepdims=True)
    two = jnp.mean(grad * normed, axis=-1, keepdims=True)
    return scale * (grad - one - normed * two)


CHUNKS = 2


def chunk_of(ref, j, axis):
    size = ref.shape[axis] // CHUNKS
    at = pl.ds(j * size, size)
    return ref.at[at] if axis == 0 else ref.at[:, at]


def head_sums(nh, h, b, part, bufs, sems):
    near, far, out = bufs
    return [
        HeadSum(
            nh,
            h,
            b,
            chunk_of(part, j, 1),
            chunk_of(near, j, 1),
            chunk_of(far, j, 1),
            chunk_of(out, j, 1),
            sems.at[j],
        )
        for j in range(CHUNKS)
    ]


def head_gathers(nh, h, b, src, dst, sems):
    return [
        HeadGather(nh, h, b, chunk_of(src, j, 0), chunk_of(dst, j, 1), sems.at[j])
        for j in range(CHUNKS)
    ]


def chunk_sems(nh):
    return pltpu.SemaphoreType.DMA((CHUNKS, 4, nh // 2))


def mid_body(nh, nb, hl, o_ref, wo_ref, x_ref, wmb_ref, og, hid_ref, ng_ref, wmb_all, part, near, far, out, nbuf, osem, ssem, gsem, wsem, wsem2):
    pc = Place(nh, nb, hl)
    h, b = pc.h, pc.b
    signal_all(nh, nb, h, b)
    wait_all(nh, nb)
    rows, width = x_ref.shape
    outputs_back(pc, o_ref, og, osem, "start")
    spread = BlkGather(pc, wmb_ref, wmb_all, wsem, wsem2)
    spread.start()
    outputs_back(pc, o_ref, og, osem, "wait_send")
    for zi in range(pc.nz):
        wait_on(og.at[zi], osem.at[1, zi])
    wo = wo_ref[...]
    for i in range(nh):
        part[i] = lax.dot_general(
            og[:, i].reshape(pc.nz * DH, rows),
            wo,
            (((0,), (0,)), ((), ())),
            preferred_element_type=F32,
        ).astype(BF16)
    hss = head_sums(nh, h, b, part, (near, far, out), ssem)
    hgs = head_gathers(nh, h, b, nbuf, ng_ref, gsem)
    for hs in hss:
        hs.start()
    spread.step(1)
    for hs in hss:
        hs.send()
    size = rows // CHUNKS
    for j, (hs, hg) in enumerate(zip(hss, hgs)):
        at = pl.ds(j * size, size)
        hid = x_ref[at, :].astype(F32) + hs.total()
        hid_ref[at, :] = hid
        nbuf[at, :] = norm_of(hid)[0].astype(BF16)
        hg.start()
    spread.step(2)
    for hg in hgs:
        hg.pass_on()
    for t in range(3, pc.nz):
        spread.step(t)
    for hs, hg in zip(hss, hgs):
        hs.finish()
        hg.finish()
    spread.finish()


def mid_exchange(ot, wo, x, wmb, hl):
    nh, nb = dims()
    rows, width = x.shape
    nz = hl
    return comm_call(
        functools.partial(mid_body, nh, nb, hl),
        "mid_exchange",
        2,
        (
            jax.ShapeDtypeStruct((nz, nh, DH, rows), BF16),
            jax.ShapeDtypeStruct(x.shape, F32),
            jax.ShapeDtypeStruct((nh, rows, width), BF16),
            jax.ShapeDtypeStruct((nh, nz, nb // nz) + wmb.shape[1:], BF16),
        ),
        [ANY, VM, VM, ANY],
        [VM, VM, VM, ANY],
        [pltpu.VMEM((nh, rows, width), BF16)]
        + HeadSum.buffers(nh, rows, width)
        + [
            pltpu.VMEM((rows, width), BF16),
            pltpu.SemaphoreType.DMA((2, nz)),
            chunk_sems(nh),
            chunk_sems(nh),
        ]
        + BlkGather.sem_shapes(nz, nb // nz),
        (ot, wo, x, wmb),
        vmem=60 << 20,
    )


def ffn_body(nh, nb, fl, split_rows, cut, len_ref, n_hbm, g_hbm, wa_hbm, wb_hbm, y_hbm, d_hbm, ga_hbm, gb_hbm, n_ref, g_ref, w_ref, y_ref, d_ref, ga_ref, gb_ref, gy, mm, dz, stage, drain):
    rows, width = n_ref.shape[1], n_ref.shape[2]
    group = nh * rows
    total, zc, off = ff_widths(fl)
    wide = total - off
    shift = 2 * fl - off
    step = 2 * rows
    lane = lax.broadcasted_iota(jnp.int32, (1, wide), 1)
    real = lane < fl
    valid = sequence_ends(len_ref)[-1]
    blk = lax.axis_index("blk")
    loads = [
        pltpu.make_async_copy(n_hbm, n_ref, stage.at[0]),
        pltpu.make_async_copy(wa_hbm, w_ref.at[:, pl.ds(0, off)], stage.at[1]),
        pltpu.make_async_copy(wb_hbm, w_ref.at[:, pl.ds(off, wide)], stage.at[2]),
        pltpu.make_async_copy(g_hbm, g_ref, stage.at[3]),
    ]
    for cp in loads:
        cp.start()
    for cp in loads:
        cp.wait()

    def out_rows(r):
        at = pl.ds(r * 2, 2)
        return [
            pltpu.make_async_copy(d_ref.at[at], d_hbm.at[at], drain.at[0, r]),
            pltpu.make_async_copy(y_ref.at[at], y_hbm.at[at], drain.at[1, r]),
        ]

    @pl.loop(0, group // step)
    def _(r):
        at = pl.ds(pl.multiple_of(r * step, step), step)
        n = n_ref[pl.ds(r * 2, 2)].reshape(step, width)
        row = lax.broadcasted_iota(jnp.int32, (step, 1), 0)
        slot = ((r * 2 + row // rows) * nb + blk) * rows + row % rows
        g = g_ref[pl.ds(r * 2, 2)].reshape(step, width)
        g = jnp.where(slot < valid, g.astype(F32), 0.0).astype(BF16)
        gy[at, :] = g
        z = jnp.dot(n, w_ref[:, :zc], preferred_element_type=F32)
        dm = lane_roll(jnp.dot(g, w_ref[:, off:], preferred_element_type=F32), -shift)
        gate, up = z[:, :wide], lane_roll(z, -fl)[:, :wide]
        cdf = 0.5 * (1.0 + lax.erf(gate * math.sqrt(0.5)))
        act = gate * cdf
        slope = cdf + gate * jnp.exp(-0.5 * gate * gate) * (1.0 / math.sqrt(2.0 * math.pi))
        m = lane_roll(jnp.where(real, act * up, 0.0), shift).astype(BF16)
        mm[at, :] = m
        d_gate = widen(jnp.where(real, dm * up * slope, 0.0), zc)
        d_up = lane_roll(widen(jnp.where(real, dm * act, 0.0), zc), fl)
        d = (d_gate + d_up).astype(BF16)
        dz[at, :] = d
        nt = (((1,), (1,)), ((), ()))
        dpart = lax.dot_general(d, w_ref[:, :zc], nt, preferred_element_type=F32)
        d_ref[pl.ds(r * 2, 2)] = dpart.astype(BF16).reshape(2, rows, width)
        ypart = lax.dot_general(m, w_ref[:, off:], nt, preferred_element_type=F32)
        y_ref[pl.ds(r * 2, 2)] = ypart.astype(BF16).reshape(2, rows, width)
        for cp in out_rows(r):
            cp.start()

    block = width // nh

    def out_block(i):
        at = (slice(None), i) if split_rows else (pl.ds(i * block, block),)
        return [
            pltpu.make_async_copy(ga_ref.at[i], ga_hbm.at[at], drain.at[2, i]),
            pltpu.make_async_copy(gb_ref.at[i], gb_hbm.at[at], drain.at[3, i]),
        ]

    @pl.loop(0, nh)
    def _(i):
        cols = pl.ds(pl.multiple_of(i * block, block), block)
        tn = (((0,), (0,)), ((), ()))
        n = n_ref[:, :, cols].reshape(group, block)
        g_in = lax.dot_general(n, dz[...], tn, preferred_element_type=F32)
        g_down = lax.dot_general(gy[:, cols], mm[...], tn, preferred_element_type=F32)
        both = jnp.concatenate(
            [g_in[:, :off], g_in[:, off:] + g_down[:, : zc - off], g_down[:, zc - off :]], axis=1
        ).astype(BF16)
        for ref, part in ((ga_ref, both[:, :cut]), (gb_ref, both[:, cut:])):
            if split_rows:
                part = part.reshape(nb, block // nb, part.shape[1])
            ref[i] = part
        for cp in out_block(i):
            cp.start()

    @pl.loop(0, nh)
    def _(i):
        for cp in out_block(i):
            cp.wait()

    @pl.loop(0, group // step)
    def _(r):
        for cp in out_rows(r):
            cp.wait()


def ffn(lengths, n2, g, wma, wmb, fl, own_rows, cut):
    nh, nb = dims()
    _, rows, width = n2.shape
    group = nh * rows
    total, zc, off = ff_widths(fl)
    split_rows = own_rows % 16 == 0
    lead = (nb, nh, own_rows) if split_rows else (width,)
    held = (nh, nb, own_rows) if split_rows else (nh, width // nh)
    return pl.pallas_call(
        functools.partial(ffn_body, nh, nb, fl, split_rows, cut),
        out_shape=(
            jax.ShapeDtypeStruct(n2.shape, BF16),
            jax.ShapeDtypeStruct(n2.shape, BF16),
            jax.ShapeDtypeStruct(lead + (cut,), BF16),
            jax.ShapeDtypeStruct(lead + (total - cut,), BF16),
        ),
        in_specs=[SM, ANY, ANY, ANY, ANY],
        out_specs=[ANY] * 4,
        scratch_shapes=[
            pltpu.VMEM(n2.shape, BF16),
            pltpu.VMEM(n2.shape, BF16),
            pltpu.VMEM((width, total), BF16),
            pltpu.VMEM(n2.shape, BF16),
            pltpu.VMEM(n2.shape, BF16),
            pltpu.VMEM(held + (cut,), BF16),
            pltpu.VMEM(held + (total - cut,), BF16),
            pltpu.VMEM((group, width), BF16),
            pltpu.VMEM((group, total - off), BF16),
            pltpu.VMEM((group, zc), BF16),
            pltpu.SemaphoreType.DMA((4,)),
            pltpu.SemaphoreType.DMA((4, nh)),
        ],
        name="ffn",
        compiler_params=pltpu.CompilerParams(vmem_limit_bytes=60 << 20),
    )(lengths, n2, g, wma, wmb)


def back_body(nh, nb, hl, len_ref, dpart, ypart, hid_ref, g_ref, wo_ref, og_ref, gb_hbm, y_ref, dh_ref, do_in, go_ref, gb_out, n1, f1, o1, n2, f2, o2, dbuf, dg, dots, gb_ref, nearb, s1, s2, gsem, qsem, pb, stage):
    pc = Place(nh, nb, hl)
    h, b = pc.h, pc.b
    mine = pltpu.make_async_copy(gb_hbm.at[:, pc.s], gb_ref, stage)
    mine.start()
    signal_all(nh, nb, h, b)
    wait_all(nh, nb)
    pairs = [
        remote(
            gb_hbm.at[:, (pc.s + ds) % pc.qs],
            nearb.at[ds - 1],
            pb.at[0, ds],
            pb.at[1, ds],
            h,
            pc.zi * pc.qs + (pc.s + ds) % pc.qs,
        )
        for ds in range(1, pc.qs)
    ]
    rows, width = hid_ref.shape
    slot = (h * nb + b) * rows + lax.broadcasted_iota(jnp.int32, (rows, 1), 0)
    valid = slot < sequence_ends(len_ref)[-1]
    hds = head_sums(nh, h, b, dpart, (n1, f1, o1), s1)
    hy = HeadSum(nh, h, b, ypart, n2, f2, o2, s2)
    hgs = head_gathers(nh, h, b, dbuf, dg, gsem)
    for hd in hds:
        hd.start()
    for cp in pairs:
        cp.start()
    for hd in hds:
        hd.send()
    size = rows // CHUNKS
    for j, (hd, hg) in enumerate(zip(hds, hgs)):
        at = pl.ds(j * size, size)
        normed, scale = norm_of(hid_ref[at, :])
        gy = jnp.where(valid[j * size : (j + 1) * size], g_ref[at, :].astype(F32), 0.0)
        dh = gy + norm_pull(hd.total(), normed, scale)
        dh_ref[at, :] = dh
        dbuf[at, :] = dh.astype(BF16)
        hg.start()
    hy.start()
    for hg in hgs:
        hg.pass_on()
    hy.send()
    for hd, hg in zip(hds, hgs):
        hd.finish()
        hg.finish()
    wo = wo_ref[...]
    nt = (((1,), (1,)), ((), ()))
    for i in range(nh):
        part = lax.dot_general(wo, dg[i], nt, preferred_element_type=F32).astype(BF16)
        dots[:, i] = part.reshape(pc.nz, DH, rows)
    grads_out(pc, dots, do_in, qsem, "start")
    total = 0.0
    for i in range(nh):
        total = total + jnp.dot(
            og_ref[:, i].reshape(pc.nz * DH, rows), dg[i], preferred_element_type=F32
        )
    go_ref[...] = total.astype(BF16)
    y_ref[...] = jnp.where(valid, hid_ref[...] + hy.total(), 0.0)
    hy.finish()
    mine.wait()
    for cp in pairs:
        cp.wait()

    @pl.loop(0, pc.nz)
    def _(d):
        others = jnp.sum(nearb[:, d].astype(F32), axis=0)
        gb_out[d] = (gb_ref[d].astype(F32) + others).astype(BF16)

    grads_out(pc, dots, do_in, qsem, "wait_send")
    for zi in range(pc.nz):
        wait_on(stretch_lanes(do_in, zi, rows), qsem.at[1, zi])


def back_exchange(lengths, dpart, ypart, hid, g, wo, og, gb):
    nh, nb = dims()
    rows, width = hid.shape
    nz = hl = og.shape[0]
    return comm_call(
        functools.partial(back_body, nh, nb, hl),
        "back_exchange",
        3,
        (
            jax.ShapeDtypeStruct(hid.shape, F32),
            jax.ShapeDtypeStruct(hid.shape, F32),
            jax.ShapeDtypeStruct((nh, DH, nz * rows), BF16),
            jax.ShapeDtypeStruct((nz * DH, width), BF16),
            jax.ShapeDtypeStruct(gb.shape[:1] + gb.shape[2:], BF16),
        ),
        [SM] + [VM] * 6 + [ANY],
        [VM, VM, ANY, VM, VM],
        HeadSum.buffers(nh, rows, width)
        + HeadSum.buffers(nh, rows, width)
        + [
            pltpu.VMEM((rows, width), BF16),
            pltpu.VMEM((nh, rows, width), BF16),
            pltpu.VMEM(og.shape, BF16),
            pltpu.VMEM(gb.shape[:1] + gb.shape[2:], BF16),
            pltpu.VMEM((gb.shape[1] - 1, nz) + gb.shape[2:], BF16),
            chunk_sems(nh),
            HeadSum.sem_shape(nh),
            chunk_sems(nh),
            pltpu.SemaphoreType.DMA((2, nz)),
            pltpu.SemaphoreType.DMA((2, gb.shape[1])),
            pltpu.SemaphoreType.DMA,
        ],
        (lengths, dpart, ypart, hid, g, wo, og, gb),
        vmem=60 << 20,
    )


def grads_back_body(nh, nb, hl, dq_ref, dkv_ref, cos_ref, sin_ref, n1_hbm, w_hbm, go_ref, gb_ref, gq_ref, dpart, do_ref, gb_sum, got, sums, dq_out, dkv_out, dqkv, n1_ref, w_ref, nearo, sumo, goto, lsem, gotb, bsem, qsem, psem, ksem, stage, po):
    pc = Place(nh, nb, hl)
    loads = [
        pltpu.make_async_copy(n1_hbm, n1_ref, stage.at[0]),
        pltpu.make_async_copy(w_hbm, w_ref, stage.at[1]),
    ]
    for cp in loads:
        cp.start()
    signal_all(nh, nb, pc.h, pc.b)
    wait_all(nh, nb)
    rows = dkv_ref.shape[3]
    group = pc.nz * rows
    width = n1_ref.shape[1]
    lw = nh * DH
    count = nh * pc.cb

    def pair(k):
        src = dkv_ref.at[k // pc.cb, :, 2 * (k % pc.cb) + 1 - pc.c]
        return remote(src, got.at[k], psem.at[0, k], psem.at[1, k], pc.sib, pc.b)

    def back(k, act):
        routed(
            pc,
            sums.at[k],
            dkv_out.at[pc.head, pc.u],
            ksem.at[0, k],
            ksem.at[1, pc.head * pc.cb + pc.u],
            k // pc.cb,
            pc.zi * pc.qs + 2 * (k % pc.cb) + pc.c,
            act,
        )

    def queries_back(act):
        for i in range(nh):
            routed(
                pc,
                dq_ref.at[i],
                dq_out.at[pc.head],
                qsem.at[0, i],
                qsem.at[1, pc.head],
                i,
                pc.zi * pc.qs + pc.from_s,
                act,
            )

    pairs_o = [
        remote(
            go_ref.at[:, (pc.s + ds) % pc.qs],
            nearo.at[ds - 1],
            po.at[0, ds],
            po.at[1, ds],
            pc.h,
            pc.zi * pc.qs + (pc.s + ds) % pc.qs,
        )
        for ds in range(1, pc.qs)
    ]
    along_o = StretchSum(pc, sumo, goto, lsem)
    along_b = StretchSum(pc, gb_ref, gotb, bsem)

    @pl.loop(0, count)
    def _(k):
        pair(k).start()

    queries_back("start")
    for cp in pairs_o:
        cp.start()
    along_b.start()

    @pl.loop(0, count)
    def _(k):
        pair(k).wait_recv()
        mine = dkv_ref[k // pc.cb, :, 2 * (k % pc.cb) + pc.c]
        sums[k] = (mine.astype(F32) + got[k].astype(F32)).astype(BF16)
        back(k, "start")

    for cp in pairs_o:
        cp.wait_recv()
    sumo[...] = (go_ref[:, pc.s].astype(F32) + jnp.sum(nearo[...].astype(F32), axis=0)).astype(BF16)
    along_o.start()
    cos, sin = cos_ref[...], -sin_ref[...]
    for l in range(nh):
        wait_on(dq_out.at[l], qsem.at[1, l])
    for p in range(nh // 2):
        q = dq_out[2 * p : 2 * p + 2].reshape(2 * DH, group).astype(F32).T
        dqkv[:, p * 128 : (p + 1) * 128] = turned(q, cos, sin).astype(BF16)
    for l in range(nh):
        for u in range(pc.cb):
            wait_on(dkv_out.at[l, u], ksem.at[1, l * pc.cb + u])
    for p in range(nh // 2):
        even, odd = [
            jnp.sum(dkv_out[2 * p + i].astype(F32), axis=0).reshape(group, 2 * DH)
            for i in range(2)
        ]
        low = lanes_of(even) < DH
        k = jnp.where(low, even, lane_roll(odd, DH)).astype(BF16).astype(F32)
        v = jnp.where(low, lane_roll(even, DH), odd)
        dqkv[:, lw + p * 128 : lw + (p + 1) * 128] = turned(k, cos, sin).astype(BF16)
        dqkv[:, 2 * lw + p * 128 : 2 * lw + (p + 1) * 128] = v.astype(BF16)
    nt = (((1,), (1,)), ((), ()))
    tn = (((0,), (0,)), ((), ()))
    for cp in loads:
        cp.wait()

    @pl.loop(0, nh)
    def _(i):
        cols = pl.ds(pl.multiple_of(i * (width // nh), width // nh), width // nh)
        gq_ref[cols, :] = lax.dot_general(
            n1_ref[:, cols], dqkv[...], tn, preferred_element_type=F32
        ).astype(BF16)

    @pl.loop(0, pc.nz)
    def _(i):
        at = pl.ds(pl.multiple_of(i * rows, rows), rows)
        dpart[i] = lax.dot_general(
            dqkv[at, :], w_ref[...], nt, preferred_element_type=F32
        ).astype(BF16)

    @pl.loop(0, count)
    def _(k):
        pair(k).wait_send()
        back(k, "wait_send")

    queries_back("wait_send")
    do_ref[...] = along_o.total()
    gb_sum[...] = along_b.total().astype(BF16)
    along_o.finish()
    along_b.finish()
    for cp in pairs_o:
        cp.wait_send()


def grads_back(dq, dkv, cos, sin, n1, wq, go, gb, hl):
    nh, nb = dims()
    nz, qs = hl, nb // hl
    cb = qs // 2
    rows = dkv.shape[3]
    width = n1.shape[1]
    lw = nh * DH
    dma = pltpu.SemaphoreType.DMA
    return comm_call(
        functools.partial(grads_back_body, nh, nb, hl),
        "grads_back",
        4,
        (
            jax.ShapeDtypeStruct((width, 3 * lw), BF16),
            jax.ShapeDtypeStruct((nz, rows, width), BF16),
            jax.ShapeDtypeStruct(go.shape[2:], F32),
            jax.ShapeDtypeStruct(gb.shape[1:], BF16),
        ),
        [ANY, VM, VM, VM, ANY, ANY, VM, VM],
        [VM] * 4,
        [
            pltpu.VMEM((nh * cb, nz, rows, 2 * DH), BF16),
            pltpu.VMEM((nh * cb, nz, rows, 2 * DH), BF16),
            pltpu.VMEM(dq.shape, BF16),
            pltpu.VMEM((nh, cb, nz, rows, 2 * DH), BF16),
            pltpu.VMEM((nz * rows, 3 * lw), BF16),
            pltpu.VMEM(n1.shape, BF16),
            pltpu.VMEM(wq.shape, BF16),
            pltpu.VMEM((qs - 1, nz) + go.shape[2:], BF16),
            pltpu.VMEM((nz,) + go.shape[2:], BF16),
        ]
        + StretchSum.scratch(nz, go.shape[2:])
        + StretchSum.scratch(nz, gb.shape[1:])
        + [
            dma((2, nh)),
            dma((2, nh * cb)),
            dma((2, nh * cb)),
            dma((2,)),
            dma((2, qs)),
        ],
        (dq, dkv, cos, sin, n1, wq, go, gb),
        vmem=60 << 20,
    )


def last_body(nh, nb, hl, dpart, gq_ref, gma_ref, gmb_ref, dn_ref, quarters, gma_all, gmb_all, nearq, sumq, farq, totq, sentz, gotz, zsem, pq, fq, cq, msem):
    pc = Place(nh, nb, hl)
    h, b = pc.h, pc.b
    signal_all(nh, nb, h, b)
    wait_all(nh, nb)
    nx, nz, qs = nh // 2, pc.nz, pc.qs
    def pair_q(k):
        return remote(
            gq_ref.at[2 * k + 1 - pc.c], nearq.at[k], pq.at[0, k], pq.at[1, k], pc.sib, b
        )

    line = LineSum(pc, lambda d: dpart[d].astype(F32), sentz, gotz, zsem)

    def plane_q(i):
        tx, ts = (pc.x + i // qs) % nx, (pc.s + i % qs) % qs
        return remote(
            sumq.at[tx, :, ts],
            farq.at[pc.x, pc.s],
            fq.at[0, i],
            fq.at[1, i],
            tx * 2 + pc.c,
            pc.zi * qs + ts,
        )

    def quarter(i):
        to = (pc.zi + i) % nz
        return remote(
            totq.at[to], quarters.at[pc.zi], cq.at[0, i], cq.at[1, i], h, to * qs + pc.s
        )

    for k in range(nx):
        pair_q(k).start()
    line.lead(0)
    moves = []
    for n, (ref, dst) in enumerate(((gma_ref, gma_all), (gmb_ref, gmb_all))):
        for i in range(1, nh):
            th = (h + i) % nh
            moves.append(remote(ref.at[th], dst.at[h], msem.at[0, n, i], msem.at[1, n, i], th, b))
        moves.append(pltpu.make_async_copy(ref.at[h], dst.at[h], msem.at[0, n, 0]))
    for k in range(nx):
        pair_q(k).wait_recv()
        sumq[k] = (gq_ref[2 * k + pc.c].astype(F32) + nearq[k].astype(F32)).astype(BF16)

    @pl.loop(1, nx * qs)
    def _(i):
        plane_q(i).start()

    farq[pc.x, pc.s] = sumq[pc.x, :, pc.s]
    for cp in moves:
        cp.start()
    line.follow(0)
    line.lead(1)

    @pl.loop(1, nx * qs)
    def _(i):
        plane_q(i).wait_recv()

    totq[...] = jnp.sum(
        farq[...].astype(F32).reshape((nx * qs,) + totq.shape), axis=0
    ).astype(BF16)
    for i in range(1, nz):
        quarter(i).start()
    quarters[pc.zi] = totq[pc.zi]
    for j in range(1, nz - 1):
        line.follow(j)
        if j + 1 < nz - 1:
            line.lead(j + 1)
    line.total(dn_ref)
    line.finish()
    for i in range(1, nz):
        quarter(i).wait()
    for cp in moves:
        cp.wait()
    for k in range(nx):
        pair_q(k).wait_send()

    @pl.loop(1, nx * qs)
    def _(i):
        plane_q(i).wait_send()


def last_exchange(dpart, gq, gma, gmb):
    nh, nb = dims()
    nz, rows, width = dpart.shape
    qs = nb // nz
    own_rows, cols = gq.shape[3:]
    nx = nh // 2
    dma = pltpu.SemaphoreType.DMA
    return comm_call(
        functools.partial(last_body, nh, nb, nz),
        "last_exchange",
        5,
        (
            jax.ShapeDtypeStruct((rows, width), F32),
            jax.ShapeDtypeStruct((nz, own_rows, cols), BF16),
            jax.ShapeDtypeStruct(gma.shape, BF16),
            jax.ShapeDtypeStruct(gmb.shape, BF16),
        ),
        [VM] * 2 + [ANY] * 2,
        [VM] * 2 + [ANY] * 2,
        [
            pltpu.VMEM((nx, nz, qs, own_rows, cols), BF16),
            pltpu.VMEM((nx, nz, qs, own_rows, cols), BF16),
            pltpu.VMEM((nx, qs, nz, own_rows, cols), BF16),
            pltpu.VMEM((nz, own_rows, cols), BF16),
        ]
        + LineSum.scratch(nz, (rows, width))
        + [
            dma((2, nx)),
            dma((2, nx * qs)),
            dma((2, nz)),
            dma((2, 2, nh)),
        ],
        (dpart, gq, gma, gmb),
        vmem=60 << 20,
    )


def finish_body(nh, fl, dn_ref, x_ref, dh_ref, y_in, quarters, do_in, gma, gmb, wq_ref, win_ref, ga_ref, gf_ref,
                y_ref, dx_ref, lna_ref, dq_ref, do_ref, lnm_ref, din_ref, dwd_ref):
    y_ref[...] = y_in[...]
    do_ref[...] = do_in[...]
    normed, scale = norm_of(x_ref[...].astype(F32))
    dx_ref[...] = dh_ref[...] + norm_pull(dn_ref[...], normed, scale)
    width = x_ref.shape[1]
    gain = column(ga_ref[...].astype(F32))
    nz = quarters.shape[0]
    rowsum = 0.0
    for c in range(3):
        for l in range(nh):
            src = (c * nh * DH + l // 2 * 128) // 128 * 128
            for p in range(nz // 2):
                tiles = [quarters[2 * p + i, :, src : src + 128].astype(F32) for i in range(2)]
                piece = half_pick(tiles[0], tiles[1], l % 2, l % 2)
                at = c * width + l * nz * DH + p * 128
                dq_ref[:, at : at + 128] = piece * gain
                rowsum = rowsum + jnp.sum(
                    piece * wq_ref[:, at : at + 128].astype(F32), axis=1, keepdims=True
                )
    lna_ref[...] = as_row(rowsum)
    ff = nh * fl
    total, _, _ = ff_widths(fl)
    tiles = lambda v: (v + 127) // 128 * 128
    gate_up, down = 0.0, 0.0
    for i in range(nh):
        piece = jnp.concatenate([gma[i].astype(F32), gmb[i].astype(F32)], axis=1)
        lane = lanes_of(piece)
        gate = widen(jnp.where(lane < fl, piece, 0.0), tiles(2 * ff))
        up = jnp.where(jnp.logical_and(lane >= fl, lane < 2 * fl), piece, 0.0)
        up = widen(up, tiles(2 * ff))
        gate_up = gate_up + lane_roll(gate, i * fl) + lane_roll(up, ff - fl + i * fl)
        dn = jnp.where(jnp.logical_and(lane >= 2 * fl, lane < 3 * fl), piece, 0.0)
        down = down + lane_roll(widen(dn, max(total, tiles(ff))), i * fl - 2 * fl)
    gate_up = gate_up[:, : 2 * ff]
    dwd_ref[...] = down[:, :ff]
    din_ref[...] = gate_up * column(gf_ref[...].astype(F32))
    lnm_ref[...] = as_row(jnp.sum(gate_up * win_ref[...].astype(F32), axis=1, keepdims=True))


def finish(dn, x, dh, y, quarters, d_wout, gma, gmb, w_qkv, w_in, gain_attn, gain_mlp, fl):
    nh, _ = dims()
    rows, width = x.shape
    own_rows = w_qkv.shape[0]
    ff = nh * fl
    f32 = lambda *shape: jax.ShapeDtypeStruct(shape, F32)
    return pl.pallas_call(
        functools.partial(finish_body, nh, fl),
        out_shape=(
            f32(rows, width),
            f32(rows, width),
            f32(1, own_rows),
            f32(own_rows, 3 * width),
            f32(own_rows, width),
            f32(1, own_rows),
            f32(own_rows, 2 * ff),
            f32(own_rows, ff),
        ),
        in_specs=[VM] * 12,
        out_specs=[VM] * 8,
        name="finish",
        compiler_params=pltpu.CompilerParams(vmem_limit_bytes=60 << 20),
    )(dn, x, dh, y, quarters, d_wout, gma, gmb, w_qkv, w_in, gain_attn, gain_mlp)


def shards(layer_input, out_grad, lengths, ln_attn, w_qkv, w_attn_out, ln_mlp, w_in, w_mlp_out):
    nh, nb = dims()
    h, b = me()
    rows, width = layer_input.shape
    heads = width // DH
    hl = heads // nh
    group = nh * rows
    slots = nh * nb * rows
    own_rows = w_qkv.shape[0]
    ff = w_mlp_out.shape[0]
    fl = ff // nh
    nz, qs = hl, nb // hl
    lw = nh * DH

    gain_attn = ln_attn.reshape(1, own_rows)
    gain_mlp = ln_mlp.reshape(1, own_rows)
    n1, wma, wmb, wq, gg, cos, sin = first_exchange(
        lengths, layer_input, w_qkv, gain_attn, w_in, gain_mlp, w_mlp_out.T, out_grad, hl, fl
    )
    wma = lax.all_gather(wma, "blk", axis=1, tiled=True).reshape(width, -1)
    wq = wq.reshape(width, 3 * lw)
    n1 = n1.reshape(group, width)
    qin, kvin, wo = to_heads(n1, wq, cos, sin, w_attn_out[None], hl)
    wo = wo.reshape(nz * DH, width)
    kv_all = kvin.reshape(slots, 2 * DH)
    ot, of, lse = attend(lengths, qin, kv_all, 2 * rows, hl)
    og, hid, n2, wmb = mid_exchange(ot, wo, layer_input, wmb, hl)
    wmb = wmb.reshape(width, -1)
    ypart, dpart, gma, gmb = ffn(lengths, n2, gg, wma, wmb, fl, own_rows, GRAD_CUT)
    if gma.ndim == 4:
        gma = lax.psum_scatter(gma, "blk", scatter_dimension=0, tiled=True)
        gmb = gmb.reshape((nz, qs) + gmb.shape[1:])
    else:
        gma = gma.reshape(nh, nb * own_rows, gma.shape[1])
        gma = lax.psum_scatter(gma, "blk", scatter_dimension=1, tiled=True)
        gmb = gmb.reshape(nh, nz, qs, own_rows, gmb.shape[1]).transpose(1, 2, 0, 3, 4)
    gma = gma.reshape(nh, own_rows, gma.shape[-1])
    y_out, dh, do_in, go, gmb = back_exchange(
        lengths, dpart, ypart, hid, out_grad, wo, og, gmb
    )
    dq, dkv = attend_grad(lengths, qin, do_in, of, kv_all, lse, hl)
    go = go.reshape(nz, qs, own_rows, width)
    gq, dpart1, d_wout, gmb = grads_back(
        dq, dkv.reshape(kvin.shape), cos, sin, n1, wq, go, gmb, hl
    )
    dn, quarters, gma, gmb = last_exchange(
        dpart1, gq.reshape(nh, nz, qs, own_rows, 3 * lw), gma, gmb
    )
    y_out, dx, d_ln_attn, d_wqkv, d_wout, d_ln_mlp, d_win, d_wd = finish(
        dn,
        layer_input,
        dh,
        y_out,
        quarters,
        d_wout,
        gma,
        gmb,
        w_qkv,
        w_in,
        gain_attn,
        gain_mlp,
        fl,
    )
    return (
        y_out,
        dx,
        d_ln_attn.reshape(own_rows),
        d_wqkv,
        d_wout,
        d_ln_mlp.reshape(own_rows),
        d_win,
        d_wd.T,
    )


def solution(mesh):
    both = ("head", "blk")
    row_split = P(both, None)
    return jax.shard_map(
        shards,
        mesh=mesh,
        in_specs=(
            row_split,
            row_split,
            P(),
            P(both),
            row_split,
            row_split,
            P(both),
            row_split,
            P(None, both),
        ),
        out_specs=(
            row_split,
            row_split,
            P(both),
            row_split,
            row_split,
            P(both),
            row_split,
            P(None, both),
        ),
        check_vma=False,
    )
```

```python
import functools
import math

import jax
import jax.numpy as jnp
from jax import lax
from jax.experimental import pallas as pl
from jax.experimental.pallas import tpu as pltpu
from jax.sharding import PartitionSpec as P

DH = 64
ROPE_BASE = 160000.0
NORM_EPS = 1e-05
MASK_FLOOR = -1e30
GRAD_CUT = 1536
FF_BLOCKS = 2
WEIGHT_CUTS = (768, 1024)
EXP_SCALE = 0.125 * math.log2(math.e)
BF16 = jnp.bfloat16
F32 = jnp.float32
MESH_ID = pl.DeviceIdType.MESH
ANY = pl.BlockSpec(memory_space=pl.ANY)
VM = pl.BlockSpec(memory_space=pltpu.VMEM)
SM = pl.BlockSpec(memory_space=pltpu.SMEM)


def dims():
    nh = lax.axis_size("head")
    nb = lax.axis_size("blk")
    return nh, nb


def me():
    return lax.axis_index("head"), lax.axis_index("blk")


class Staged:
    def __init__(self, loads, drains):
        self.loads, self.drains = loads, drains

    def need(self, *which):
        for i in which:
            self.loads[i].wait()

    def put(self, *which):
        for i in which:
            self.drains[i].start()


def comm_call(body, name, cid, out_shape, in_specs, out_specs, scratch, args, vmem=None, late=(), early=()):
    n_in, n_out, n_late, n_early = len(args), len(out_shape), len(late), len(early)
    in_specs = [ANY if i in late else spec for i, spec in enumerate(in_specs)]
    out_specs = [ANY if i in early else spec for i, spec in enumerate(out_specs)]
    held = [pltpu.VMEM(args[i].shape, args[i].dtype) for i in late]
    held += [pltpu.VMEM(out_shape[i].shape, out_shape[i].dtype) for i in early]
    held.append(pltpu.SemaphoreType.DMA((max(n_late + n_early, 1),)))

    def staged_body(*refs):
        ins, outs = list(refs[:n_in]), list(refs[n_in : n_in + n_out])
        bufs = refs[n_in + n_out : n_in + n_out + n_late + n_early]
        sems = refs[n_in + n_out + n_late + n_early]
        rest = refs[n_in + n_out + n_late + n_early + 1 :]
        loads, drains = {}, {}
        for k, i in enumerate(late):
            loads[i] = pltpu.make_async_copy(ins[i], bufs[k], sems.at[k])
            loads[i].start()
            ins[i] = bufs[k]
        for k, i in enumerate(early):
            k += n_late
            drains[i] = pltpu.make_async_copy(bufs[k], outs[i], sems.at[k])
            outs[i] = bufs[k]
        body(Staged(loads, drains), *ins, *outs, *rest)
        for cp in drains.values():
            cp.wait()

    return pl.pallas_call(
        staged_body,
        out_shape=out_shape,
        in_specs=in_specs,
        out_specs=out_specs,
        scratch_shapes=held + list(scratch),
        name=name,
        compiler_params=pltpu.CompilerParams(
            collective_id=cid, has_side_effects=True, vmem_limit_bytes=vmem
        ),
    )(*args)


def remote(src, dst, send, recv, h, b):
    return pltpu.make_async_remote_copy(
        src_ref=src,
        dst_ref=dst,
        send_sem=send,
        recv_sem=recv,
        device_id=(h, b),
        device_id_type=MESH_ID,
    )


def signal(h, b):
    pl.semaphore_signal(
        pltpu.get_barrier_semaphore(), inc=1, device_id=(h, b), device_id_type=MESH_ID
    )


class HeadGather:
    def __init__(self, nh, h, b, src, dst, sems):
        self.nh, self.h, self.b, self.dst, self.sems = nh, h, b, dst, sems
        nx = nh // 2
        self.nx = nx
        x, c = h // 2, h % 2
        sib = x * 2 + 1 - c
        self.sib = sib
        self.across = []
        for k in range(1, nx):
            self.across.append(
                remote(src, dst.at[h], sems.at[0, k], sems.at[1, k], ((x + k) % nx) * 2 + c, b)
            )
        self.near = remote(src, dst.at[h], sems.at[0, 0], sems.at[1, 0], sib, b)
        self.local = pltpu.make_async_copy(src, dst.at[h], sems.at[2, 0])
        self.forward = []
        for k in range(1, nx):
            got = ((x + nx - k) % nx) * 2 + c
            self.forward.append(
                remote(dst.at[got], dst.at[got], sems.at[2, k], sems.at[3, k], sib, b)
            )

    @staticmethod
    def sem_shape(nh):
        return pltpu.SemaphoreType.DMA((4, nh // 2))

    def start(self):
        for cp in self.across:
            cp.start()
        self.near.start()
        self.local.start()

    def pass_on(self):
        for cp, fw in zip(self.across, self.forward):
            cp.wait_recv()
            fw.start()

    def finish(self):
        for cp in self.across:
            cp.wait_send()
        self.near.wait()
        self.local.wait()
        for fw in self.forward:
            fw.wait()


def lane_roll(values, shift):
    return pltpu.roll(values, shift % values.shape[1], 1)


def lanes_of(values):
    return lax.broadcasted_iota(jnp.int32, (1, values.shape[1]), 1)


def widen(values, width):
    extra = width - values.shape[1]
    if extra <= 0:
        return values[:, :width]
    return jnp.concatenate([values, jnp.zeros((values.shape[0], extra), values.dtype)], axis=1)


def weight_parts(total):
    marks = (0,) + WEIGHT_CUTS + (total,)
    return list(zip(marks[:-1], marks[1:]))


def column(row):
    n = row.shape[1]
    same = lax.broadcasted_iota(jnp.int32, (n, n), 0) == lax.broadcasted_iota(jnp.int32, (n, n), 1)
    return jnp.sum(jnp.where(same, row, 0.0), axis=1, keepdims=True)


def as_row(col):
    n = col.shape[0]
    same = lax.broadcasted_iota(jnp.int32, (n, n), 0) == lax.broadcasted_iota(jnp.int32, (n, n), 1)
    return jnp.sum(jnp.where(same, col, 0.0), axis=0, keepdims=True)


def sequence_ends(len_ref):
    ends, total = [], 0
    for i in range(len_ref.shape[0]):
        total = total + len_ref[i]
        ends.append(total)
    return ends


def segment_first(slot, ends):
    first = jnp.zeros_like(slot)
    for end in ends:
        first = jnp.where(slot >= end, end, first)
    return first


def segment_end(slot, ends, slots):
    last = jnp.zeros_like(slot) + slots
    for end in reversed(ends):
        last = jnp.where(slot < end, end, last)
    return last


def half_pick(low_src, high_src, low_at, high_at):
    low = low_src if low_at == 0 else lane_roll(low_src, DH)
    high = high_src if high_at == 1 else lane_roll(high_src, DH)
    return jnp.where(lanes_of(low) < DH, low, high)


def ff_widths(fl):
    up = lambda v: (v + 127) // 128 * 128
    return up(3 * fl), up(2 * fl), 2 * fl // 128 * 128


class LineGather:
    def __init__(self, pc, src, place, sems):
        self.pc, self.src, self.place, self.sems = pc, src, place, sems

    @staticmethod
    def sem_shape(nz):
        return pltpu.SemaphoreType.DMA((5, nz))

    def origin(self, t, up):
        return self.pc.zi - t if up else self.pc.zi + t

    def move(self, t, up):
        pc = self.pc
        at = self.place(self.origin(t, up))
        n = 0 if up else 2
        return remote(
            self.src if t == 0 else at,
            at,
            self.sems.at[n, t],
            self.sems.at[n + 1, t],
            pc.h,
            pc.b + pc.qs if up else pc.b - pc.qs,
        )

    def sends(self, t, up):
        zi, nz = self.pc.zi, self.pc.nz
        if up:
            return jnp.logical_and(zi - t >= 0, zi + 1 < nz)
        return jnp.logical_and(zi + t < nz, zi - 1 >= 0)

    def local(self):
        return pltpu.make_async_copy(self.src, self.place(self.pc.zi), self.sems.at[4, 0])

    def start(self):
        for up in (True, False):

            @pl.when(self.sends(0, up))
            def _():
                self.move(0, up).start()

        self.local().start()

    def step(self, t, arrived=None):
        low = self.pc.zi < self.pc.nz // 2
        self.take(t, False, jnp.logical_not(low), arrived)
        self.take(t, True, True, arrived)
        self.take(t, False, low, arrived)

    def take(self, t, up, now, arrived):
        zi, nz = self.pc.zi, self.pc.nz
        origin = self.origin(t, up)
        here = jnp.logical_and(now, origin >= 0 if up else origin < nz)

        @pl.when(here)
        def _():
            wait_on(self.place(origin), self.sems.at[1 if up else 3, t - 1])

        if t < nz - 1:

            @pl.when(jnp.logical_and(now, self.sends(t, up)))
            def _():
                self.move(t, up).start()

        if arrived is not None:

            @pl.when(here)
            def _():
                arrived(origin)

    def finish(self):
        self.local().wait()
        for t in range(self.pc.nz - 1):
            for up in (True, False):

                @pl.when(self.sends(t, up))
                def _():
                    self.move(t, up).wait_send()


class BlkGather:
    def __init__(self, pc, src, out, sems, ssem):
        self.pc, self.out, self.ssem, self.src = pc, out, ssem, src
        self.line = LineGather(pc, src, lambda zi: out.at[:, zi, pc.s], sems)

    @staticmethod
    def sem_shapes(nz, qs):
        return [LineGather.sem_shape(nz), pltpu.SemaphoreType.DMA((2, nz, qs))]

    def side(self, zi, ds, own=False):
        pc = self.pc
        ref = self.out.at[:, zi, pc.s]
        return remote(
            self.src if own else ref,
            ref,
            self.ssem.at[0, zi, ds],
            self.ssem.at[1, zi, ds],
            pc.h,
            pc.zi * pc.qs + (pc.s + ds) % pc.qs,
        )

    def spread(self, zi, own=False):
        for ds in range(1, self.pc.qs):
            self.side(zi, ds, own).start()

    def start(self):
        self.line.start()
        self.spread(self.pc.zi, True)

    def step(self, t):
        self.line.step(t, self.spread)

    def finish(self):
        self.line.finish()

        @pl.loop(0, self.pc.nz)
        def _(zi):
            for ds in range(1, self.pc.qs):
                self.side(zi, ds).wait()


class LineSum:
    def __init__(self, pc, term, sent, got, sems):
        self.pc, self.term, self.sent, self.got, self.sems = pc, term, sent, got, sems

    @staticmethod
    def scratch(nz, shape):
        return [
            pltpu.VMEM((2, nz) + shape, BF16),
            pltpu.VMEM((2, nz) + shape, BF16),
            pltpu.SemaphoreType.DMA((4, nz)),
        ]

    def move(self, d, up):
        pc = self.pc
        n = 0 if up else 1
        return remote(
            self.sent.at[n, d],
            self.got.at[n, d],
            self.sems.at[2 * n, d],
            self.sems.at[2 * n + 1, d],
            pc.h,
            pc.b + pc.qs if up else pc.b - pc.qs,
        )

    def takes(self, up):
        return self.pc.zi > 0 if up else self.pc.zi < self.pc.nz - 1

    def lead(self, j):
        self.step(j, False)

    def follow(self, j):
        self.step(j, True)

    def step(self, j, taking):
        low = self.pc.zi < self.pc.nz // 2
        if taking:
            self.one(j, False, jnp.logical_not(low), True)
            self.one(j, True, True, True)
            self.one(j, False, low, True)
        else:
            self.one(j, True, True, False)
            self.one(j, False, True, False)

    def one(self, j, up, now, taking):
        zi, nz = self.pc.zi, self.pc.nz
        d = nz - 1 - j if up else j
        n = 0 if up else 1
        takes = self.takes(up)
        far = jnp.logical_and(now, zi < d if up else zi > d)

        @pl.when(jnp.logical_and(far, takes if taking else jnp.logical_not(takes)))
        def _():
            if taking:
                wait_on(self.got.at[n, d], self.sems.at[2 * n + 1, d])
                self.sent[n, d] = (self.term(d) + self.got[n, d].astype(F32)).astype(BF16)
            else:
                self.sent[n, d] = self.term(d).astype(BF16)
            self.move(d, up).start()

    def total(self, total_ref):
        zi = self.pc.zi
        total_ref[...] = self.term(zi)
        for up in (True, False):
            n = 0 if up else 1

            @pl.when(self.takes(up))
            def _():
                wait_on(self.got.at[n, zi], self.sems.at[2 * n + 1, zi])
                total_ref[...] += self.got[n, zi].astype(F32)

    def finish(self):
        zi, nz = self.pc.zi, self.pc.nz
        for j in range(nz - 1):
            for up in (True, False):
                d = nz - 1 - j if up else j

                @pl.when(zi < d if up else zi > d)
                def _():
                    self.move(d, up).wait_send()


class StretchSum:
    def __init__(self, pc, part, got, sems):
        self.pc, self.part, self.got, self.sems = pc, part, got, sems

    @staticmethod
    def scratch(nz, shape):
        return [pltpu.VMEM((nz,) + shape, BF16), pltpu.SemaphoreType.DMA((2, nz))]

    def move(self, i):
        pc = self.pc
        to = (pc.zi + i) % pc.nz
        return remote(
            self.part.at[to],
            self.got.at[pc.zi],
            self.sems.at[0, i],
            self.sems.at[1, i],
            pc.h,
            to * pc.qs + pc.s,
        )

    def start(self):
        for i in range(1, self.pc.nz):
            self.move(i).start()

    def total(self):
        pc = self.pc
        total = self.part[pc.zi].astype(F32)
        for i in range(1, pc.nz):
            self.move(i).wait_recv()
            total = total + self.got[(pc.zi + pc.nz - i) % pc.nz].astype(F32)
        return total

    def finish(self):
        for i in range(1, self.pc.nz):
            self.move(i).wait_send()


class PlaneWeights:
    def __init__(self, pc, pack, out, sems, ksem):
        self.pc, self.pack, self.out, self.sems, self.ksem = pc, pack, out, sems, ksem

    @staticmethod
    def sem_shapes(nh, nz, qs):
        dma = pltpu.SemaphoreType.DMA
        return [dma((2, nz)), dma((4, nh // 2 * qs))]

    def along(self, i):
        pc = self.pc
        to = (pc.zi + i) % pc.nz
        return remote(
            self.pack.at[to],
            self.out.at[pc.h, pc.zi, pc.s],
            self.sems.at[0, i],
            self.sems.at[1, i],
            pc.h,
            to * pc.qs + pc.s,
        )

    def local(self):
        pc = self.pc
        return pltpu.make_async_copy(
            self.pack.at[pc.zi], self.out.at[pc.h, pc.zi, pc.s], self.sems.at[0, 0]
        )

    def place(self, i, sign):
        pc = self.pc
        nx = pc.nh // 2
        dx, ds = i // pc.qs, i % pc.qs
        if sign < 0:
            dx, ds = nx - dx, pc.qs - ds
        return ((pc.x + dx) % nx) * 2 + pc.c, (pc.s + ds) % pc.qs

    def across(self, i):
        pc = self.pc
        th, ts = self.place(i, 1)
        ref = self.out.at[pc.h, :, pc.s]
        return remote(
            ref, ref, self.ksem.at[0, i], self.ksem.at[1, i], th, pc.zi * pc.qs + ts
        )

    def near(self, i):
        pc = self.pc
        gh, gs = self.place(i, -1)
        ref = self.out.at[gh, :, gs]
        return remote(ref, ref, self.ksem.at[2, i], self.ksem.at[3, i], pc.sib, pc.b)

    def start(self):
        for i in range(1, self.pc.nz):
            self.along(i).start()
        self.local().start()

    def spread(self):
        pc = self.pc
        self.local().wait()
        for i in range(1, pc.nz):
            self.along(i).wait_recv()

        @pl.loop(1, pc.nh // 2 * pc.qs)
        def _(i):
            self.across(i).start()

        self.near(0).start()

    def pass_on(self):
        @pl.loop(1, self.pc.nh // 2 * self.pc.qs)
        def _(i):
            self.across(i).wait_recv()
            self.near(i).start()

    def finish(self):
        for i in range(1, self.pc.nz):
            self.along(i).wait_send()

        @pl.loop(1, self.pc.nh // 2 * self.pc.qs)
        def _(i):
            self.across(i).wait_send()

        @pl.loop(0, self.pc.nh // 2 * self.pc.qs)
        def _(i):
            self.near(i).wait()


def first_body(nh, nb, hl, fl, io, len_ref, x_ref, wq_ref, ga_ref, win_hbm, gf_ref, wd_hbm, g_ref, n1_all, wma, wmb, wmc, wq_all, gg, cos_ref, sin_ref, own_n, pack, wmp, win_ref, wd_ref, lsem, wsem, ksem, gsem, msem, stage):
    pc = Place(nh, nb, hl)
    h, b = pc.h, pc.b
    loads = [
        pltpu.make_async_copy(win_hbm, win_ref, stage.at[0]),
        pltpu.make_async_copy(wd_hbm, wd_ref, stage.at[1]),
    ]
    for cp in loads:
        cp.start()
    signal_near(pc)
    width = x_ref.shape[1]
    lw = width // pc.nz
    gain = column(ga_ref[...].astype(F32))
    io.need(2)
    for c in range(3):
        w = wq_ref[:, c * width : (c + 1) * width].astype(F32) * gain
        tile = lambda l, i: w[:, l * pc.nz * DH + i // 2 * 128 : l * pc.nz * DH + i // 2 * 128 + 128]
        for i in range(pc.nz):
            for p in range(nh // 2):
                both = half_pick(tile(2 * p, i), tile(2 * p + 1, i), i % 2, i % 2)
                at = c * lw + p * 128
                pack[i, :, at : at + 128] = both.astype(BF16)
    io.need(1)
    own_n[...] = norm_of(x_ref[...].astype(F32))[0].astype(BF16)
    wait_near(pc)
    weights = PlaneWeights(pc, pack, wq_all, wsem, ksem)
    line = LineGather(pc, own_n, lambda zi: n1_all.at[zi], lsem)
    gather = HeadGather(nh, h, b, g_ref, gg, gsem)
    weights.start()
    line.start()
    gather.start()
    for cp in loads:
        cp.wait()
    total = ff_widths(fl)[0]
    ff = nh * fl
    win = win_ref[...].astype(F32) * column(gf_ref[...].astype(F32))
    wd = widen(wd_ref[...].astype(F32), total if total > ff else (ff + 127) // 128 * 128)
    lane = lax.broadcasted_iota(jnp.int32, (1, total), 1)
    for i in range(nh):
        gate = widen(lane_roll(win, -i * fl), total)
        up = widen(lane_roll(win, fl - ff - i * fl), total)
        down = widen(lane_roll(wd, 2 * fl - i * fl), total)
        piece = jnp.where(
            lane < fl,
            gate,
            jnp.where(lane < 2 * fl, up, jnp.where(lane < 3 * fl, down, 0.0)),
        )
        wmp[i] = piece.astype(BF16)
    copies = []
    for n, (dst, (begin, end)) in enumerate(zip((wma, wmb, wmc), weight_parts(total))):
        cols = pl.ds(begin, end - begin)
        for i in range(1, nh):
            th = (h + i) % nh
            src = wmp.at[th, :, cols]
            copies.append(remote(src, dst.at[h], msem.at[0, n, i], msem.at[1, n, i], th, b))
        copies.append(pltpu.make_async_copy(wmp.at[h, :, cols], dst.at[h], msem.at[0, n, 0]))
    weights.spread()
    for cp in copies:
        cp.start()
    ends = sequence_ends(len_ref)
    rows = x_ref.shape[0]
    lane = lax.broadcasted_iota(jnp.int32, (1, 2 * DH), 1)
    power = (lane % (DH // 2)).astype(F32) * (-2.0 / DH)
    inv_freq = jnp.exp2(power * math.log2(ROPE_BASE))
    sign = jnp.where(lane % DH < DH // 2, -1.0, 1.0)
    line.step(1)
    for i in range(pc.nz):
        slot = (h * nb + i * pc.qs + pc.s) * rows + lax.broadcasted_iota(jnp.int32, (rows, 1), 0)
        angle = (slot - segment_first(slot, ends)).astype(F32) * inv_freq
        cos_ref[i * rows : (i + 1) * rows, :] = jnp.cos(angle)
        sin_ref[i * rows : (i + 1) * rows, :] = jnp.sin(angle) * sign
    io.put(6, 7)
    gather.pass_on()
    for t in range(2, pc.nz):
        line.step(t)
    weights.pass_on()
    for cp in copies:
        cp.wait()
    weights.finish()
    line.finish()
    gather.finish()


def first_exchange(lengths, x, w_qkv, gain_attn, w_in, gain_mlp, wd_t, g, hl, fl):
    nh, nb = dims()
    rows, width = x.shape
    nz, qs = hl, nb // hl
    lw = width // nz
    own_rows = w_in.shape[0]
    total = ff_widths(fl)[0]
    dma = pltpu.SemaphoreType.DMA
    return comm_call(
        functools.partial(first_body, nh, nb, hl, fl),
        "first_exchange",
        0,
        (
            jax.ShapeDtypeStruct((nz, rows, width), BF16),
            *[
                jax.ShapeDtypeStruct((nh, own_rows, end - begin), BF16)
                for begin, end in weight_parts(total)
            ],
            jax.ShapeDtypeStruct((nh, nz, qs, own_rows, 3 * lw), BF16),
            jax.ShapeDtypeStruct((nh, rows, width), BF16),
            jax.ShapeDtypeStruct((nz * rows, 2 * DH), F32),
            jax.ShapeDtypeStruct((nz * rows, 2 * DH), F32),
        ),
        [SM, VM, VM, VM, ANY, VM, ANY, ANY],
        [ANY] * 6 + [VM] * 2,
        [
            pltpu.VMEM((rows, width), BF16),
            pltpu.VMEM((nz, own_rows, 3 * lw), BF16),
            pltpu.VMEM((nh, own_rows, total), BF16),
            pltpu.VMEM(w_in.shape, BF16),
            pltpu.VMEM(wd_t.shape, BF16),
            LineGather.sem_shape(nz),
        ]
        + PlaneWeights.sem_shapes(nh, nz, qs)
        + [
            HeadGather.sem_shape(nh),
            dma((2, 3, nh)),
            dma((2,)),
        ],
        (lengths, x, w_qkv, gain_attn, w_in, gain_mlp, wd_t, g),
        vmem=60 << 20,
        late=(2, 1),
        early=(6, 7),
    )


class Place:
    def __init__(self, nh, nb, hl):
        h, b = me()
        self.nh, self.nb, self.h, self.b = nh, nb, h, b
        self.x, self.c = h // 2, h % 2
        self.nz = hl
        self.qs = nb // hl
        self.cb = self.qs // 2
        self.sib = self.x * 2 + 1 - self.c
        self.zi, self.s = b // self.qs, b % self.qs
        self.head = self.x * 2 + self.s // self.cb
        self.u = self.s % self.cb
        self.from_s = self.u * 2 + self.c

    def attends(self, zi, l, core, u):
        return (l // 2) * 2 + core, zi * self.qs + (l % 2) * self.cb + u


def signal_near(pc):
    here = pc.nh * pc.qs

    @pl.loop(1, here)
    def _(i):
        signal((pc.h + i // pc.qs) % pc.nh, pc.zi * pc.qs + (pc.s + i % pc.qs) % pc.qs)

    @pl.loop(1, pc.nz)
    def _(i):
        signal(pc.h, (pc.zi + i) % pc.nz * pc.qs + pc.s)


def wait_near(pc, more=0):
    pl.semaphore_wait(pltpu.get_barrier_semaphore(), pc.nh * pc.qs + pc.nz - 2 + more)


def enter_with(pc, source):
    signal_near(pc)
    for i in range(1, pc.nz):
        signal(*source((pc.zi + i) % pc.nz))
    wait_near(pc, pc.nz - 1)


def routed(pc, src, dst, send, recv, th, tb, act):
    mine = jnp.logical_and(th == pc.h, tb == pc.b)

    @pl.when(mine)
    def _():
        if act == "start":
            pltpu.make_async_copy(src, dst, recv).start()

    @pl.when(jnp.logical_not(mine))
    def _():
        cp = remote(src, dst, send, recv, th, tb)
        if act == "start":
            cp.start()
        else:
            cp.wait_send()


def wait_on(ref, sem):
    pltpu.make_async_copy(ref, ref, sem).wait()


def stretch_lanes(ref, zi, rows):
    return ref.at[:, :, pl.ds(pl.multiple_of(zi * rows, rows), rows)]


def outputs_back(pc, o_ref, og, osem, act):
    rows = og.shape[3]
    for zi in range(pc.nz):
        routed(
            pc,
            stretch_lanes(o_ref, zi, rows),
            og.at[pc.zi],
            osem.at[0, zi],
            osem.at[1, pc.zi],
            pc.head,
            zi * pc.qs + pc.from_s,
            act,
        )


def grads_out(pc, dots, do_in, qsem, act):
    rows = dots.shape[3]
    for zi in range(pc.nz):
        th, tb = pc.attends(zi, pc.h, pc.s % 2, pc.s // 2)
        routed(
            pc,
            dots.at[zi],
            stretch_lanes(do_in, pc.zi, rows),
            qsem.at[0, zi],
            qsem.at[1, pc.zi],
            th,
            tb,
            act,
        )


def halves_swapped(tile):
    lane = lanes_of(tile)
    return jnp.where(lane % DH < DH // 2, lane_roll(tile, -(DH // 2)), lane_roll(tile, DH // 2))


def turned(tile, cos, sin):
    return tile * cos + halves_swapped(tile) * sin


def to_heads_body(nh, nb, hl, io, n1_hbm, w_hbm, cos_ref, sin_ref, wo_ref, wmb_ref, qin, kvin, wo_all, wmb_all, qbuf, kvbuf, n1_ref, w_ref, qsem, ksem, fsem, osem, osem2, bsem, bsem2, stage):
    pc = Place(nh, nb, hl)
    loads = [
        pltpu.make_async_copy(n1_hbm, n1_ref, stage.at[0]),
        pltpu.make_async_copy(w_hbm, w_ref, stage.at[1]),
    ]
    for cp in loads:
        cp.start()
    signal_near(pc)
    rows = kvbuf.shape[2]
    lw = nh * DH
    for cp in loads:
        cp.wait()
    n1 = n1_ref[...]
    io.need(2, 3)
    cos, sin = cos_ref[...], sin_ref[...]
    kk = jnp.dot(n1, w_ref[:, lw : 2 * lw], preferred_element_type=F32)
    vv = jnp.dot(n1, w_ref[:, 2 * lw :], preferred_element_type=F32)
    for p in range(nh // 2):
        k = turned(kk[:, p * 128 : (p + 1) * 128], cos, sin)
        v = vv[:, p * 128 : (p + 1) * 128]
        low = lanes_of(k) < DH
        even = jnp.where(low, k, lane_roll(v, DH)).astype(BF16)
        odd = jnp.where(low, lane_roll(k, DH), v).astype(BF16)
        for i in range(pc.nz):
            kvbuf[2 * p, i] = even[i * rows : (i + 1) * rows]
            kvbuf[2 * p + 1, i] = odd[i * rows : (i + 1) * rows]
    wait_near(pc)

    def keys_out(act):
        for l in range(nh):
            for u in range(pc.cb):
                th, tb = pc.attends(pc.zi, l, pc.s % 2, u)
                routed(
                    pc,
                    kvbuf.at[l],
                    kvin.at[pc.h, :, pc.s],
                    ksem.at[0, l * pc.cb + u],
                    ksem.at[1, pc.h * pc.cb + pc.s // 2],
                    th,
                    tb,
                    act,
                )

    def queries_out(act):
        for l in range(nh):
            th, tb = pc.attends(pc.zi, l, pc.s % 2, pc.s // 2)
            routed(
                pc, qbuf.at[l], qin.at[pc.h], qsem.at[0, l], qsem.at[1, pc.h], th, tb, act
            )

    spread = BlkGather(pc, wo_ref, wo_all, osem, osem2)
    spread_b = BlkGather(pc, wmb_ref, wmb_all, bsem, bsem2)
    keys_out("start")
    spread.start()
    spread_b.start()
    qq = jnp.dot(n1, w_ref[:, :lw], preferred_element_type=F32)
    for p in range(nh // 2):
        q = turned(qq[:, p * 128 : (p + 1) * 128], cos, sin).T.astype(BF16)
        qbuf[2 * p] = q[:DH]
        qbuf[2 * p + 1] = q[DH:]
    queries_out("start")
    count = nh * pc.cb

    def forward(i):
        at = kvin.at[i // pc.cb, :, 2 * (i % pc.cb) + pc.c]
        return remote(at, at, fsem.at[0, i], fsem.at[1, i], pc.sib, pc.b)

    @pl.loop(0, count)
    def _(i):
        wait_on(kvin.at[i // pc.cb, :, 2 * (i % pc.cb) + pc.c], ksem.at[1, i])
        forward(i).start()

    for t in range(1, pc.nz):
        spread.step(t)
        spread_b.step(t)
    keys_out("wait_send")
    queries_out("wait_send")
    for i in range(nh):
        wait_on(qin.at[i], qsem.at[1, i])

    @pl.loop(0, count)
    def _(i):
        forward(i).wait()

    spread.finish()
    spread_b.finish()


def to_heads(n1, wq, cos, sin, wo, wmb, hl):
    nh, nb = dims()
    group, width = n1.shape
    nz, qs = hl, nb // hl
    cb = qs // 2
    rows = group // nz
    dma = pltpu.SemaphoreType.DMA
    return comm_call(
        functools.partial(to_heads_body, nh, nb, hl),
        "to_heads",
        1,
        (
            jax.ShapeDtypeStruct((nh, DH, group), BF16),
            jax.ShapeDtypeStruct((nh, nz, qs, rows, 2 * DH), BF16),
            jax.ShapeDtypeStruct((1, nz, qs) + wo.shape[1:], BF16),
            jax.ShapeDtypeStruct((nh, nz, qs) + wmb.shape[1:], BF16),
        ),
        [ANY, ANY, VM, VM, ANY, ANY],
        [ANY] * 4,
        [
            pltpu.VMEM((nh, DH, group), BF16),
            pltpu.VMEM((nh, nz, rows, 2 * DH), BF16),
            pltpu.VMEM(n1.shape, BF16),
            pltpu.VMEM(wq.shape, BF16),
            dma((2, nh)),
            dma((2, nh * cb)),
            dma((2, nh * cb)),
        ]
        + BlkGather.sem_shapes(nz, qs) * 2
        + [dma((2,))],
        (n1, wq, cos, sin, wo, wmb),
        vmem=60 << 20,
        late=(2, 3),
    )


class Queries:
    def __init__(self, nh, nb, hl, len_ref, lanes, slots, size):
        pc = Place(nh, nb, hl)
        tile = pl.program_id(0)
        rows = slots // (nh * nb)
        count = lanes // rows
        each = pc.nz // count
        ends = sequence_ends(len_ref)
        base = (tile // each) * nb + (tile % each) * count * pc.qs + pc.from_s
        lane = lax.broadcasted_iota(jnp.int32, (1, lanes), 1)
        slot = (base + lane // rows * pc.qs) * rows + lane % rows
        self.first = segment_first(slot, ends)
        self.last = segment_end(slot, ends, slots)
        near = base * rows
        far = (base + (count - 1) * pc.qs) * rows + rows - 1
        self.size = size
        self.lo = segment_first(near, ends) // size
        self.hi = (segment_end(far, ends, slots) + size - 1) // size
        self.open = jnp.minimum((segment_first(far, ends) + size - 1) // size, self.hi)
        self.close = jnp.maximum(segment_end(near, ends, slots) // size, self.open)
        self.lanes = lanes

    def allowed(self, block_at):
        at = block_at * self.size + lax.broadcasted_iota(jnp.int32, (self.size, self.lanes), 0)
        return jnp.logical_and(at >= self.first, at < self.last)

    def walk(self, step, carry):
        masked = lambda j, kept: step(j, kept, True)
        carry = lax.fori_loop(self.lo, self.open, masked, carry)
        carry = lax.fori_loop(self.open, self.close, lambda j, kept: step(j, kept, False), carry)
        return lax.fori_loop(self.close, self.hi, masked, carry)


def attend_body(nh, nb, hl, size, len_ref, q_ref, kv_ref, o_ref, of_ref, lse_ref):
    q = q_ref[0]
    lanes = q.shape[1]
    at = Queries(nh, nb, hl, len_ref, lanes, kv_ref.shape[0], size)
    q_pad = jnp.concatenate([q, jnp.zeros_like(q)], axis=0)
    is_key = lax.broadcasted_iota(jnp.int32, (1, 2 * DH), 1) < DH

    def step(j, carry, masked):
        top, acc = carry
        kv = kv_ref[pl.ds(pl.multiple_of(j * size, size), size), :]
        s = jnp.dot(kv, q_pad, preferred_element_type=F32)
        if masked:
            s = jnp.where(at.allowed(j), s, MASK_FLOOR)
        new_top = jnp.maximum(top, jnp.max(s, axis=0, keepdims=True))
        p = jnp.exp2((s - new_top) * EXP_SCALE).astype(BF16)
        alpha = jnp.exp2((top - new_top) * EXP_SCALE)
        ones_values = jnp.where(is_key, jnp.ones_like(kv), kv)
        acc = acc * alpha + lax.dot_general(
            ones_values, p, (((0,), (0,)), ((), ())), preferred_element_type=F32
        )
        return new_top, acc

    top, acc = at.walk(
        step, (jnp.full((1, lanes), MASK_FLOOR, F32), jnp.zeros((2 * DH, lanes), F32))
    )
    total = acc[:1]
    o = acc[DH:] / total
    of_ref[0] = o
    o_ref[0] = o.astype(BF16)
    lse_ref[0] = top * EXP_SCALE + jnp.log2(total)


def attend_specs(kv_rows, lanes, tiles_each):
    tile_spec = pl.BlockSpec((1, DH, lanes), lambda i, *_: (i // tiles_each, 0, i % tiles_each))
    row_spec = pl.BlockSpec((1, 1, lanes), lambda i, *_: (i, 0, 0))
    kv_spec = pl.BlockSpec((kv_rows, 2 * DH), lambda i, *_: (0, 0))
    return tile_spec, row_spec, kv_spec


def attend(lengths, q, kv, lanes, size, hl):
    nh, nb = dims()
    each = q.shape[2] // lanes
    tiles = q.shape[0] * each
    tile_spec, row_spec, kv_spec = attend_specs(kv.shape[0], lanes, each)
    return pl.pallas_call(
        functools.partial(attend_body, nh, nb, hl, size),
        grid_spec=pltpu.PrefetchScalarGridSpec(
            num_scalar_prefetch=1,
            grid=(tiles,),
            in_specs=[tile_spec, kv_spec],
            out_specs=[tile_spec, tile_spec, row_spec],
        ),
        out_shape=(
            jax.ShapeDtypeStruct(q.shape, BF16),
            jax.ShapeDtypeStruct(q.shape, F32),
            jax.ShapeDtypeStruct((tiles, 1, lanes), F32),
        ),
        name="attend",
        compiler_params=pltpu.CompilerParams(vmem_limit_bytes=60 << 20),
    )(lengths, q, kv)


def attend_grad_body(nh, nb, hl, size, len_ref, q_ref, do_ref, of_ref, kv_ref, lse_ref, dq_ref, dkv_ref, acc_ref):
    tile = pl.program_id(0)

    @pl.when(tile == 0)
    def _():
        acc_ref[...] = jnp.zeros_like(acc_ref)

    q = q_ref[0]
    do = do_ref[0]
    lanes = q.shape[1]
    place = Queries(nh, nb, hl, len_ref, lanes, kv_ref.shape[0], size)
    zero = jnp.zeros_like(q)
    both = jnp.concatenate(
        [jnp.concatenate([q, zero], axis=0), jnp.concatenate([zero, do], axis=0)], axis=1
    )
    delta = jnp.sum(do.astype(F32) * of_ref[0], axis=0, keepdims=True)
    lse = lse_ref[0]

    def step(j, dq, masked):
        at = pl.ds(pl.multiple_of(j * size, size), size)
        kv = kv_ref[at, :]
        sd = jnp.dot(kv, both, preferred_element_type=F32)
        s, dp = sd[:, :lanes], sd[:, lanes:]
        power = s * EXP_SCALE - lse
        if masked:
            power = jnp.where(place.allowed(j), power, MASK_FLOOR)
        p = jnp.exp2(power)
        ds = (p * (dp - delta)).astype(BF16)
        acc_ref[at, :] += lax.dot_general(
            jnp.concatenate([ds, p.astype(BF16)], axis=1),
            both,
            (((1,), (1,)), ((), ())),
            preferred_element_type=F32,
        )
        return dq + lax.dot_general(
            kv, ds, (((0,), (0,)), ((), ())), preferred_element_type=F32
        )

    dq = place.walk(step, jnp.zeros((2 * DH, lanes), F32))
    dq_ref[0] = (dq[:DH] * 0.125).astype(BF16)

    @pl.when(tile == pl.num_programs(0) - 1)
    def _():
        lane = lax.broadcasted_iota(jnp.int32, (1, 2 * DH), 1)
        dkv_ref[...] = (acc_ref[...] * jnp.where(lane < DH, 0.125, 1.0)).astype(BF16)


def attend_grad(lengths, q, do, of, kv, lse, lanes, size, hl):
    nh, nb = dims()
    tiles = lse.size // lanes
    lse = lse.reshape(tiles, 1, lanes)
    tile_spec, row_spec, kv_spec = attend_specs(kv.shape[0], lanes, tiles // q.shape[0])
    return pl.pallas_call(
        functools.partial(attend_grad_body, nh, nb, hl, size),
        grid_spec=pltpu.PrefetchScalarGridSpec(
            num_scalar_prefetch=1,
            grid=(tiles,),
            in_specs=[tile_spec, tile_spec, tile_spec, kv_spec, row_spec],
            out_specs=[tile_spec, kv_spec],
            scratch_shapes=[pltpu.VMEM(kv.shape, F32)],
        ),
        out_shape=(jax.ShapeDtypeStruct(q.shape, BF16), jax.ShapeDtypeStruct(kv.shape, BF16)),
        name="attend_grad",
        compiler_params=pltpu.CompilerParams(vmem_limit_bytes=60 << 20),
    )(lengths, q, do, of, kv, lse)


class HeadSum:
    def __init__(self, nh, h, b, part, near, far, out, sems):
        self.nx = nh // 2
        self.x, self.c = h // 2, h % 2
        self.h, self.part, self.near, self.far, self.out = h, part, near, far, out
        sib = self.x * 2 + 1 - self.c
        self.pairs = [
            remote(
                part.at[((self.x + k) % self.nx) * 2 + 1 - self.c],
                near.at[k],
                sems.at[0, k],
                sems.at[1, k],
                sib,
                b,
            )
            for k in range(self.nx)
        ]
        self.across = [
            remote(
                out.at[k],
                far.at[k],
                sems.at[2, k],
                sems.at[3, k],
                ((self.x + k) % self.nx) * 2 + self.c,
                b,
            )
            for k in range(1, self.nx)
        ]

    @staticmethod
    def sem_shape(nh):
        return pltpu.SemaphoreType.DMA((4, nh // 2))

    @staticmethod
    def buffers(nh, rows, width):
        return [pltpu.VMEM((nh // 2, rows, width), BF16)] * 3

    def start(self):
        for k in list(range(1, self.nx)) + [0]:
            self.pairs[k].start()

    def send(self):
        for k in range(1, self.nx):
            self.pairs[k].wait_recv()
            at = ((self.x + k) % self.nx) * 2 + self.c
            self.out[k] = (self.part[at].astype(F32) + self.near[k].astype(F32)).astype(BF16)
            self.across[k - 1].start()

    def total(self):
        self.pairs[0].wait_recv()
        total = self.part[self.h].astype(F32) + self.near[0].astype(F32)
        for k in range(1, self.nx):
            self.across[k - 1].wait_recv()
            total = total + self.far[k].astype(F32)
        return total

    def finish(self):
        for cp in self.pairs:
            cp.wait_send()
        for cp in self.across:
            cp.wait_send()


def norm_of(values):
    centre = values - jnp.mean(values, axis=-1, keepdims=True)
    scale = lax.rsqrt(jnp.mean(centre * centre, axis=-1, keepdims=True) + NORM_EPS)
    return centre * scale, scale


def norm_pull(grad, normed, scale):
    one = jnp.mean(grad, axis=-1, keepdims=True)
    two = jnp.mean(grad * normed, axis=-1, keepdims=True)
    return scale * (grad - one - normed * two)


CHUNKS = 2


def chunk_of(ref, j, axis):
    size = ref.shape[axis] // CHUNKS
    at = pl.ds(j * size, size)
    return ref.at[at] if axis == 0 else ref.at[:, at]


def head_sums(nh, h, b, part, bufs, sems):
    near, far, out = bufs
    return [
        HeadSum(
            nh,
            h,
            b,
            chunk_of(part, j, 1),
            chunk_of(near, j, 1),
            chunk_of(far, j, 1),
            chunk_of(out, j, 1),
            sems.at[j],
        )
        for j in range(CHUNKS)
    ]


def head_gathers(nh, h, b, src, dst, sems):
    return [
        HeadGather(nh, h, b, chunk_of(src, j, 0), chunk_of(dst, j, 1), sems.at[j])
        for j in range(CHUNKS)
    ]


def chunk_sems(nh):
    return pltpu.SemaphoreType.DMA((CHUNKS, 4, nh // 2))


def mid_body(nh, nb, hl, io, o_ref, wo_ref, x_ref, wmb_ref, og, hid_ref, ng_ref, wmb_all, part, near, far, out, nbuf, osem, ssem, gsem, wsem, wsem2):
    pc = Place(nh, nb, hl)
    h, b = pc.h, pc.b
    enter_with(pc, lambda zi: pc.attends(zi, h, pc.s % 2, pc.s // 2))
    rows, width = x_ref.shape
    outputs_back(pc, o_ref, og, osem, "start")
    spread = BlkGather(pc, wmb_ref, wmb_all, wsem, wsem2)
    spread.start()
    outputs_back(pc, o_ref, og, osem, "wait_send")
    for zi in range(pc.nz):
        wait_on(og.at[zi], osem.at[1, zi])
    io.put(0)
    io.need(1)
    wo = wo_ref[...]
    for i in range(nh):
        part[i] = lax.dot_general(
            og[:, i].reshape(pc.nz * DH, rows),
            wo,
            (((0,), (0,)), ((), ())),
            preferred_element_type=F32,
        ).astype(BF16)
    hss = head_sums(nh, h, b, part, (near, far, out), ssem)
    hgs = head_gathers(nh, h, b, nbuf, ng_ref, gsem)
    for hs in hss:
        hs.start()
    spread.step(1)
    for hs in hss:
        hs.send()
    size = rows // CHUNKS
    io.need(2)
    for j, (hs, hg) in enumerate(zip(hss, hgs)):
        at = pl.ds(j * size, size)
        hid = x_ref[at, :].astype(F32) + hs.total()
        hid_ref[at, :] = hid
        nbuf[at, :] = norm_of(hid)[0].astype(BF16)
        hg.start()
    io.put(1)
    spread.step(2)
    for hg in hgs:
        hg.pass_on()
    for t in range(3, pc.nz):
        spread.step(t)
    for hs, hg in zip(hss, hgs):
        hs.finish()
        hg.finish()
    spread.finish()


def mid_exchange(ot, wo, x, wmb, hl):
    nh, nb = dims()
    rows, width = x.shape
    nz = hl
    return comm_call(
        functools.partial(mid_body, nh, nb, hl),
        "mid_exchange",
        2,
        (
            jax.ShapeDtypeStruct((nz, nh, DH, rows), BF16),
            jax.ShapeDtypeStruct(x.shape, F32),
            jax.ShapeDtypeStruct((nh, rows, width), BF16),
            jax.ShapeDtypeStruct((nh, nz, nb // nz) + wmb.shape[1:], BF16),
        ),
        [ANY] * 4,
        [ANY] * 4,
        [pltpu.VMEM((nh, rows, width), BF16)]
        + HeadSum.buffers(nh, rows, width)
        + [
            pltpu.VMEM((rows, width), BF16),
            pltpu.SemaphoreType.DMA((2, nz)),
            chunk_sems(nh),
            chunk_sems(nh),
        ]
        + BlkGather.sem_shapes(nz, nb // nz),
        (ot, wo, x, wmb),
        vmem=60 << 20,
        late=(1, 2),
        early=(0, 1),
    )


def ffn_body(nh, nb, fl, split_rows, cut, len_ref, n_hbm, g_hbm, wa_hbm, wb_hbm, wc_hbm, y_hbm, d_hbm, ga_hbm, gb_hbm, n_ref, g_ref, w_ref, y_ref, d_ref, ga_ref, gb_ref, gy, mm, dz, stage, drain):
    rows, width = n_ref.shape[1], n_ref.shape[2]
    group = nh * rows
    total, zc, off = ff_widths(fl)
    wide = total - off
    shift = 2 * fl - off
    step = FF_BLOCKS * rows
    lane = lax.broadcasted_iota(jnp.int32, (1, wide), 1)
    real = lane < fl
    valid = sequence_ends(len_ref)[-1]
    blk = lax.axis_index("blk")
    loads = [
        pltpu.make_async_copy(n_hbm, n_ref, stage.at[0]),
        pltpu.make_async_copy(g_hbm, g_ref, stage.at[1]),
    ]
    for n, (w, (begin, end)) in enumerate(zip((wa_hbm, wb_hbm, wc_hbm), weight_parts(total))):
        dst = w_ref.at[:, pl.ds(begin, end - begin)]
        loads.append(pltpu.make_async_copy(w, dst, stage.at[2 + n]))
    for cp in loads:
        cp.start()
    for cp in loads:
        cp.wait()

    def out_rows(r):
        at = pl.ds(r * FF_BLOCKS, FF_BLOCKS)
        return [
            pltpu.make_async_copy(d_ref.at[at], d_hbm.at[at], drain.at[0, r]),
            pltpu.make_async_copy(y_ref.at[at], y_hbm.at[at], drain.at[1, r]),
        ]

    @pl.loop(0, group // step)
    def _(r):
        at = pl.ds(pl.multiple_of(r * step, step), step)
        n = n_ref[pl.ds(r * FF_BLOCKS, FF_BLOCKS)].reshape(step, width)
        row = lax.broadcasted_iota(jnp.int32, (step, 1), 0)
        slot = ((r * FF_BLOCKS + row // rows) * nb + blk) * rows + row % rows
        g = g_ref[pl.ds(r * FF_BLOCKS, FF_BLOCKS)].reshape(step, width)
        g = jnp.where(slot < valid, g.astype(F32), 0.0).astype(BF16)
        gy[at, :] = g
        z = jnp.dot(n, w_ref[:, :zc], preferred_element_type=F32)
        dm = lane_roll(jnp.dot(g, w_ref[:, off:], preferred_element_type=F32), -shift)
        gate, up = z[:, :wide], lane_roll(z, -fl)[:, :wide]
        cdf = 0.5 * (1.0 + lax.erf(gate * math.sqrt(0.5)))
        act = gate * cdf
        slope = cdf + gate * jnp.exp(-0.5 * gate * gate) * (1.0 / math.sqrt(2.0 * math.pi))
        m = lane_roll(jnp.where(real, act * up, 0.0), shift).astype(BF16)
        mm[at, :] = m
        d_gate = widen(jnp.where(real, dm * up * slope, 0.0), zc)
        d_up = lane_roll(widen(jnp.where(real, dm * act, 0.0), zc), fl)
        d = (d_gate + d_up).astype(BF16)
        dz[at, :] = d
        nt = (((1,), (1,)), ((), ()))
        dpart = lax.dot_general(d, w_ref[:, :zc], nt, preferred_element_type=F32)
        d_ref[pl.ds(r * FF_BLOCKS, FF_BLOCKS)] = dpart.astype(BF16).reshape(FF_BLOCKS, rows, width)
        ypart = lax.dot_general(m, w_ref[:, off:], nt, preferred_element_type=F32)
        y_ref[pl.ds(r * FF_BLOCKS, FF_BLOCKS)] = ypart.astype(BF16).reshape(FF_BLOCKS, rows, width)
        for cp in out_rows(r):
            cp.start()

    block = width // nh

    def out_block(i):
        at = (slice(None), i) if split_rows else (pl.ds(i * block, block),)
        return [
            pltpu.make_async_copy(ga_ref.at[i], ga_hbm.at[at], drain.at[2, i]),
            pltpu.make_async_copy(gb_ref.at[i], gb_hbm.at[at], drain.at[3, i]),
        ]

    @pl.loop(0, nh)
    def _(i):
        cols = pl.ds(pl.multiple_of(i * block, block), block)
        tn = (((0,), (0,)), ((), ()))
        n = n_ref[:, :, cols].reshape(group, block)
        g_in = lax.dot_general(n, dz[...], tn, preferred_element_type=F32)
        g_down = lax.dot_general(gy[:, cols], mm[...], tn, preferred_element_type=F32)
        both = jnp.concatenate(
            [g_in[:, :off], g_in[:, off:] + g_down[:, : zc - off], g_down[:, zc - off :]], axis=1
        ).astype(BF16)
        for ref, part in ((ga_ref, both[:, :cut]), (gb_ref, both[:, cut:])):
            if split_rows:
                part = part.reshape(nb, block // nb, part.shape[1])
            ref[i] = part
        for cp in out_block(i):
            cp.start()

    @pl.loop(0, nh)
    def _(i):
        for cp in out_block(i):
            cp.wait()

    @pl.loop(0, group // step)
    def _(r):
        for cp in out_rows(r):
            cp.wait()


def ffn(lengths, n2, g, weights, fl, own_rows, cut):
    nh, nb = dims()
    _, rows, width = n2.shape
    group = nh * rows
    total, zc, off = ff_widths(fl)
    split_rows = own_rows % 16 == 0
    lead = (nb, nh, own_rows) if split_rows else (width,)
    held = (nh, nb, own_rows) if split_rows else (nh, width // nh)
    return pl.pallas_call(
        functools.partial(ffn_body, nh, nb, fl, split_rows, cut),
        out_shape=(
            jax.ShapeDtypeStruct(n2.shape, BF16),
            jax.ShapeDtypeStruct(n2.shape, BF16),
            jax.ShapeDtypeStruct(lead + (cut,), BF16),
            jax.ShapeDtypeStruct(lead + (total - cut,), BF16),
        ),
        in_specs=[SM] + [ANY] * 5,
        out_specs=[ANY] * 4,
        scratch_shapes=[
            pltpu.VMEM(n2.shape, BF16),
            pltpu.VMEM(n2.shape, BF16),
            pltpu.VMEM((width, total), BF16),
            pltpu.VMEM(n2.shape, BF16),
            pltpu.VMEM(n2.shape, BF16),
            pltpu.VMEM(held + (cut,), BF16),
            pltpu.VMEM(held + (total - cut,), BF16),
            pltpu.VMEM((group, width), BF16),
            pltpu.VMEM((group, total - off), BF16),
            pltpu.VMEM((group, zc), BF16),
            pltpu.SemaphoreType.DMA((5,)),
            pltpu.SemaphoreType.DMA((4, nh)),
        ],
        name="ffn",
        compiler_params=pltpu.CompilerParams(vmem_limit_bytes=60 << 20),
    )(lengths, n2, g, *weights)


def back_body(nh, nb, hl, io, len_ref, dpart, ypart, hid_ref, g_ref, wo_ref, og_ref, gb_hbm, y_ref, dh_ref, do_in, go_ref, gb_out, n1, f1, o1, n2, f2, o2, dbuf, dg, dots, gb_ref, nearb, s1, s2, gsem, qsem, pb, stage):
    pc = Place(nh, nb, hl)
    h, b = pc.h, pc.b
    mine = pltpu.make_async_copy(gb_hbm.at[:, pc.s], gb_ref, stage)
    mine.start()
    enter_with(pc, lambda zi: (pc.head, zi * pc.qs + pc.from_s))
    pairs = [
        remote(
            gb_hbm.at[:, (pc.s + ds) % pc.qs],
            nearb.at[ds - 1],
            pb.at[0, ds],
            pb.at[1, ds],
            h,
            pc.zi * pc.qs + (pc.s + ds) % pc.qs,
        )
        for ds in range(1, pc.qs)
    ]
    rows, width = hid_ref.shape
    slot = (h * nb + b) * rows + lax.broadcasted_iota(jnp.int32, (rows, 1), 0)
    valid = slot < sequence_ends(len_ref)[-1]
    hds = head_sums(nh, h, b, dpart, (n1, f1, o1), s1)
    hy = HeadSum(nh, h, b, ypart, n2, f2, o2, s2)
    hgs = head_gathers(nh, h, b, dbuf, dg, gsem)
    io.need(1)
    for hd in hds:
        hd.start()
    for cp in pairs:
        cp.start()
    for hd in hds:
        hd.send()
    size = rows // CHUNKS
    io.need(3, 4)
    for j, (hd, hg) in enumerate(zip(hds, hgs)):
        at = pl.ds(j * size, size)
        normed, scale = norm_of(hid_ref[at, :])
        gy = jnp.where(valid[j * size : (j + 1) * size], g_ref[at, :].astype(F32), 0.0)
        dh = gy + norm_pull(hd.total(), normed, scale)
        dh_ref[at, :] = dh
        dbuf[at, :] = dh.astype(BF16)
        hg.start()
    io.put(1)
    io.need(2)
    hy.start()
    for hg in hgs:
        hg.pass_on()
    hy.send()
    for hd, hg in zip(hds, hgs):
        hd.finish()
        hg.finish()
    io.need(5)
    wo = wo_ref[...]
    nt = (((1,), (1,)), ((), ()))
    for i in range(nh):
        part = lax.dot_general(wo, dg[i], nt, preferred_element_type=F32).astype(BF16)
        dots[:, i] = part.reshape(pc.nz, DH, rows)
    grads_out(pc, dots, do_in, qsem, "start")
    total = 0.0
    io.need(6)
    for i in range(nh):
        total = total + jnp.dot(
            og_ref[:, i].reshape(pc.nz * DH, rows), dg[i], preferred_element_type=F32
        )
    go_ref[...] = total.astype(BF16)
    io.put(3)
    y_ref[...] = jnp.where(valid, hid_ref[...] + hy.total(), 0.0)
    io.put(0)
    hy.finish()
    mine.wait()
    for cp in pairs:
        cp.wait()

    @pl.loop(0, pc.nz)
    def _(d):
        others = jnp.sum(nearb[:, d].astype(F32), axis=0)
        gb_out[d] = (gb_ref[d].astype(F32) + others).astype(BF16)

    io.put(4)
    grads_out(pc, dots, do_in, qsem, "wait_send")
    for zi in range(pc.nz):
        wait_on(stretch_lanes(do_in, zi, rows), qsem.at[1, zi])


def back_exchange(lengths, dpart, ypart, hid, g, wo, og, gb):
    nh, nb = dims()
    rows, width = hid.shape
    nz = hl = og.shape[0]
    return comm_call(
        functools.partial(back_body, nh, nb, hl),
        "back_exchange",
        3,
        (
            jax.ShapeDtypeStruct(hid.shape, F32),
            jax.ShapeDtypeStruct(hid.shape, F32),
            jax.ShapeDtypeStruct((nh, DH, nz * rows), BF16),
            jax.ShapeDtypeStruct((nz * DH, width), BF16),
            jax.ShapeDtypeStruct(gb.shape[:1] + gb.shape[2:], BF16),
        ),
        [SM] + [VM] * 6 + [ANY],
        [VM, VM, ANY, VM, VM],
        HeadSum.buffers(nh, rows, width)
        + HeadSum.buffers(nh, rows, width)
        + [
            pltpu.VMEM((rows, width), BF16),
            pltpu.VMEM((nh, rows, width), BF16),
            pltpu.VMEM(og.shape, BF16),
            pltpu.VMEM(gb.shape[:1] + gb.shape[2:], BF16),
            pltpu.VMEM((gb.shape[1] - 1, nz) + gb.shape[2:], BF16),
            chunk_sems(nh),
            HeadSum.sem_shape(nh),
            chunk_sems(nh),
            pltpu.SemaphoreType.DMA((2, nz)),
            pltpu.SemaphoreType.DMA((2, gb.shape[1])),
            pltpu.SemaphoreType.DMA,
        ],
        (lengths, dpart, ypart, hid, g, wo, og, gb),
        vmem=60 << 20,
        late=(1, 3, 4, 2, 5, 6),
        early=(0, 1, 3, 4),
    )


def grads_back_body(nh, nb, hl, io, dq_ref, dkv_ref, cos_ref, sin_ref, n1_hbm, w_hbm, go_ref, gb_ref, gq_ref, dpart, do_ref, gb_sum, got, sums, dq_out, dkv_out, dqkv, n1_ref, w_ref, nearo, sumo, goto, lsem, gotb, bsem, qsem, psem, ksem, stage, po):
    pc = Place(nh, nb, hl)
    loads = [
        pltpu.make_async_copy(n1_hbm, n1_ref, stage.at[0]),
        pltpu.make_async_copy(w_hbm, w_ref, stage.at[1]),
    ]
    for cp in loads:
        cp.start()
    signal_near(pc)
    wait_near(pc)
    rows = dkv_ref.shape[3]
    group = pc.nz * rows
    width = n1_ref.shape[1]
    lw = nh * DH
    count = nh * pc.cb

    def pair(k):
        src = dkv_ref.at[k // pc.cb, :, 2 * (k % pc.cb) + 1 - pc.c]
        return remote(src, got.at[k], psem.at[0, k], psem.at[1, k], pc.sib, pc.b)

    def back(k, act):
        routed(
            pc,
            sums.at[k],
            dkv_out.at[pc.head, pc.u],
            ksem.at[0, k],
            ksem.at[1, pc.head * pc.cb + pc.u],
            k // pc.cb,
            pc.zi * pc.qs + 2 * (k % pc.cb) + pc.c,
            act,
        )

    def queries_back(act):
        for i in range(nh):
            routed(
                pc,
                dq_ref.at[i],
                dq_out.at[pc.head],
                qsem.at[0, i],
                qsem.at[1, pc.head],
                i,
                pc.zi * pc.qs + pc.from_s,
                act,
            )

    pairs_o = [
        remote(
            go_ref.at[:, (pc.s + ds) % pc.qs],
            nearo.at[ds - 1],
            po.at[0, ds],
            po.at[1, ds],
            pc.h,
            pc.zi * pc.qs + (pc.s + ds) % pc.qs,
        )
        for ds in range(1, pc.qs)
    ]
    along_o = StretchSum(pc, sumo, goto, lsem)
    along_b = StretchSum(pc, gb_ref, gotb, bsem)

    io.need(1)

    @pl.loop(0, count)
    def _(k):
        pair(k).start()

    queries_back("start")
    io.need(6, 7)
    for cp in pairs_o:
        cp.start()
    along_b.start()

    @pl.loop(0, count)
    def _(k):
        pair(k).wait_recv()
        mine = dkv_ref[k // pc.cb, :, 2 * (k % pc.cb) + pc.c]
        sums[k] = (mine.astype(F32) + got[k].astype(F32)).astype(BF16)
        back(k, "start")

    for cp in pairs_o:
        cp.wait_recv()
    sumo[...] = (go_ref[:, pc.s].astype(F32) + jnp.sum(nearo[...].astype(F32), axis=0)).astype(BF16)
    along_o.start()
    io.need(2, 3)
    cos, sin = cos_ref[...], -sin_ref[...]
    for l in range(nh):
        wait_on(dq_out.at[l], qsem.at[1, l])
    for p in range(nh // 2):
        q = dq_out[2 * p : 2 * p + 2].reshape(2 * DH, group).astype(F32).T
        dqkv[:, p * 128 : (p + 1) * 128] = turned(q, cos, sin).astype(BF16)
    for l in range(nh):
        for u in range(pc.cb):
            wait_on(dkv_out.at[l, u], ksem.at[1, l * pc.cb + u])
    for p in range(nh // 2):
        even, odd = [
            jnp.sum(dkv_out[2 * p + i].astype(F32), axis=0).reshape(group, 2 * DH)
            for i in range(2)
        ]
        low = lanes_of(even) < DH
        k = jnp.where(low, even, lane_roll(odd, DH)).astype(BF16).astype(F32)
        v = jnp.where(low, lane_roll(even, DH), odd)
        dqkv[:, lw + p * 128 : lw + (p + 1) * 128] = turned(k, cos, sin).astype(BF16)
        dqkv[:, 2 * lw + p * 128 : 2 * lw + (p + 1) * 128] = v.astype(BF16)
    nt = (((1,), (1,)), ((), ()))
    tn = (((0,), (0,)), ((), ()))
    for cp in loads:
        cp.wait()

    @pl.loop(0, nh)
    def _(i):
        cols = pl.ds(pl.multiple_of(i * (width // nh), width // nh), width // nh)
        gq_ref[cols, :] = lax.dot_general(
            n1_ref[:, cols], dqkv[...], tn, preferred_element_type=F32
        ).astype(BF16)

    io.put(0)

    @pl.loop(0, pc.nz)
    def _(i):
        at = pl.ds(pl.multiple_of(i * rows, rows), rows)
        dpart[i] = lax.dot_general(
            dqkv[at, :], w_ref[...], nt, preferred_element_type=F32
        ).astype(BF16)

    io.put(1)

    @pl.loop(0, count)
    def _(k):
        pair(k).wait_send()
        back(k, "wait_send")

    queries_back("wait_send")
    do_ref[...] = along_o.total()
    io.put(2)
    gb_sum[...] = along_b.total().astype(BF16)
    io.put(3)
    along_o.finish()
    along_b.finish()
    for cp in pairs_o:
        cp.wait_send()


def grads_back(dq, dkv, cos, sin, n1, wq, go, gb, hl):
    nh, nb = dims()
    nz, qs = hl, nb // hl
    cb = qs // 2
    rows = dkv.shape[3]
    width = n1.shape[1]
    lw = nh * DH
    dma = pltpu.SemaphoreType.DMA
    return comm_call(
        functools.partial(grads_back_body, nh, nb, hl),
        "grads_back",
        4,
        (
            jax.ShapeDtypeStruct((width, 3 * lw), BF16),
            jax.ShapeDtypeStruct((nz, rows, width), BF16),
            jax.ShapeDtypeStruct(go.shape[2:], F32),
            jax.ShapeDtypeStruct(gb.shape[1:], BF16),
        ),
        [ANY, VM, VM, VM, ANY, ANY, VM, VM],
        [VM] * 4,
        [
            pltpu.VMEM((nh * cb, nz, rows, 2 * DH), BF16),
            pltpu.VMEM((nh * cb, nz, rows, 2 * DH), BF16),
            pltpu.VMEM(dq.shape, BF16),
            pltpu.VMEM((nh, cb, nz, rows, 2 * DH), BF16),
            pltpu.VMEM((nz * rows, 3 * lw), BF16),
            pltpu.VMEM(n1.shape, BF16),
            pltpu.VMEM(wq.shape, BF16),
            pltpu.VMEM((qs - 1, nz) + go.shape[2:], BF16),
            pltpu.VMEM((nz,) + go.shape[2:], BF16),
        ]
        + StretchSum.scratch(nz, go.shape[2:])
        + StretchSum.scratch(nz, gb.shape[1:])
        + [
            dma((2, nh)),
            dma((2, nh * cb)),
            dma((2, nh * cb)),
            dma((2,)),
            dma((2, qs)),
        ],
        (dq, dkv, cos, sin, n1, wq, go, gb),
        vmem=60 << 20,
        late=(1, 6, 7, 2, 3),
        early=(0, 1, 2, 3),
    )


def last_body(nh, nb, hl, io, dpart, gq_ref, gma_ref, gmb_ref, dn_ref, quarters, gma_all, gmb_all, nearq, sumq, farq, totq, sentz, gotz, zsem, pq, fq, cq, msem):
    pc = Place(nh, nb, hl)
    h, b = pc.h, pc.b
    signal_near(pc)
    wait_near(pc)
    nx, nz, qs = nh // 2, pc.nz, pc.qs
    def pair_q(k):
        return remote(
            gq_ref.at[2 * k + 1 - pc.c], nearq.at[k], pq.at[0, k], pq.at[1, k], pc.sib, b
        )

    line = LineSum(pc, lambda d: dpart[d].astype(F32), sentz, gotz, zsem)

    def plane_q(i):
        tx, ts = (pc.x + i // qs) % nx, (pc.s + i % qs) % qs
        return remote(
            sumq.at[tx, :, ts],
            farq.at[pc.x, pc.s],
            fq.at[0, i],
            fq.at[1, i],
            tx * 2 + pc.c,
            pc.zi * qs + ts,
        )

    def quarter(i):
        to = (pc.zi + i) % nz
        return remote(
            totq.at[to], quarters.at[pc.zi], cq.at[0, i], cq.at[1, i], h, to * qs + pc.s
        )

    io.need(1)
    for k in range(nx):
        pair_q(k).start()
    io.need(0)
    line.lead(0)
    moves = []
    for n, (ref, dst) in enumerate(((gma_ref, gma_all), (gmb_ref, gmb_all))):
        for i in range(1, nh):
            th = (h + i) % nh
            moves.append(remote(ref.at[th], dst.at[h], msem.at[0, n, i], msem.at[1, n, i], th, b))
        moves.append(pltpu.make_async_copy(ref.at[h], dst.at[h], msem.at[0, n, 0]))
    for k in range(nx):
        pair_q(k).wait_recv()
        sumq[k] = (gq_ref[2 * k + pc.c].astype(F32) + nearq[k].astype(F32)).astype(BF16)

    @pl.loop(1, nx * qs)
    def _(i):
        plane_q(i).start()

    farq[pc.x, pc.s] = sumq[pc.x, :, pc.s]
    for cp in moves:
        cp.start()
    line.follow(0)
    line.lead(1)

    @pl.loop(1, nx * qs)
    def _(i):
        plane_q(i).wait_recv()

    totq[...] = jnp.sum(
        farq[...].astype(F32).reshape((nx * qs,) + totq.shape), axis=0
    ).astype(BF16)
    for i in range(1, nz):
        quarter(i).start()
    quarters[pc.zi] = totq[pc.zi]
    for j in range(1, nz - 1):
        line.follow(j)
        if j + 1 < nz - 1:
            line.lead(j + 1)
    line.total(dn_ref)
    io.put(0)
    line.finish()
    for i in range(1, nz):
        quarter(i).wait()
    io.put(1)
    for cp in moves:
        cp.wait()
    for k in range(nx):
        pair_q(k).wait_send()

    @pl.loop(1, nx * qs)
    def _(i):
        plane_q(i).wait_send()


def last_exchange(dpart, gq, gma, gmb):
    nh, nb = dims()
    nz, rows, width = dpart.shape
    qs = nb // nz
    own_rows, cols = gq.shape[3:]
    nx = nh // 2
    dma = pltpu.SemaphoreType.DMA
    return comm_call(
        functools.partial(last_body, nh, nb, nz),
        "last_exchange",
        5,
        (
            jax.ShapeDtypeStruct((rows, width), F32),
            jax.ShapeDtypeStruct((nz, own_rows, cols), BF16),
            jax.ShapeDtypeStruct(gma.shape, BF16),
            jax.ShapeDtypeStruct(gmb.shape, BF16),
        ),
        [VM] * 2 + [ANY] * 2,
        [VM] * 2 + [ANY] * 2,
        [
            pltpu.VMEM((nx, nz, qs, own_rows, cols), BF16),
            pltpu.VMEM((nx, nz, qs, own_rows, cols), BF16),
            pltpu.VMEM((nx, qs, nz, own_rows, cols), BF16),
            pltpu.VMEM((nz, own_rows, cols), BF16),
        ]
        + LineSum.scratch(nz, (rows, width))
        + [
            dma((2, nx)),
            dma((2, nx * qs)),
            dma((2, nz)),
            dma((2, 2, nh)),
        ],
        (dpart, gq, gma, gmb),
        vmem=60 << 20,
        late=(1, 0),
        early=(0, 1),
    )


def finish_body(nh, fl, dn_ref, x_ref, dh_ref, y_in, quarters, do_in, gma, gmb, wq_ref, win_ref, ga_ref, gf_ref,
                y_ref, dx_ref, lna_ref, dq_ref, do_ref, lnm_ref, din_ref, dwd_ref):
    y_ref[...] = y_in[...]
    do_ref[...] = do_in[...]
    normed, scale = norm_of(x_ref[...].astype(F32))
    dx_ref[...] = dh_ref[...] + norm_pull(dn_ref[...], normed, scale)
    width = x_ref.shape[1]
    gain = column(ga_ref[...].astype(F32))
    nz = quarters.shape[0]
    rowsum = 0.0
    for c in range(3):
        for l in range(nh):
            src = (c * nh * DH + l // 2 * 128) // 128 * 128
            for p in range(nz // 2):
                tiles = [quarters[2 * p + i, :, src : src + 128].astype(F32) for i in range(2)]
                piece = half_pick(tiles[0], tiles[1], l % 2, l % 2)
                at = c * width + l * nz * DH + p * 128
                dq_ref[:, at : at + 128] = piece * gain
                rowsum = rowsum + jnp.sum(
                    piece * wq_ref[:, at : at + 128].astype(F32), axis=1, keepdims=True
                )
    lna_ref[...] = as_row(rowsum)
    ff = nh * fl
    total, _, _ = ff_widths(fl)
    tiles = lambda v: (v + 127) // 128 * 128
    gate_up, down = 0.0, 0.0
    for i in range(nh):
        piece = jnp.concatenate([gma[i].astype(F32), gmb[i].astype(F32)], axis=1)
        lane = lanes_of(piece)
        gate = widen(jnp.where(lane < fl, piece, 0.0), tiles(2 * ff))
        up = jnp.where(jnp.logical_and(lane >= fl, lane < 2 * fl), piece, 0.0)
        up = widen(up, tiles(2 * ff))
        gate_up = gate_up + lane_roll(gate, i * fl) + lane_roll(up, ff - fl + i * fl)
        dn = jnp.where(jnp.logical_and(lane >= 2 * fl, lane < 3 * fl), piece, 0.0)
        down = down + lane_roll(widen(dn, max(total, tiles(ff))), i * fl - 2 * fl)
    gate_up = gate_up[:, : 2 * ff]
    dwd_ref[...] = down[:, :ff]
    din_ref[...] = gate_up * column(gf_ref[...].astype(F32))
    lnm_ref[...] = as_row(jnp.sum(gate_up * win_ref[...].astype(F32), axis=1, keepdims=True))


def finish(dn, x, dh, y, quarters, d_wout, gma, gmb, w_qkv, w_in, gain_attn, gain_mlp, fl):
    nh, _ = dims()
    rows, width = x.shape
    own_rows = w_qkv.shape[0]
    ff = nh * fl
    f32 = lambda *shape: jax.ShapeDtypeStruct(shape, F32)
    return pl.pallas_call(
        functools.partial(finish_body, nh, fl),
        out_shape=(
            f32(rows, width),
            f32(rows, width),
            f32(1, own_rows),
            f32(own_rows, 3 * width),
            f32(own_rows, width),
            f32(1, own_rows),
            f32(own_rows, 2 * ff),
            f32(own_rows, ff),
        ),
        in_specs=[VM] * 12,
        out_specs=[VM] * 8,
        name="finish",
        compiler_params=pltpu.CompilerParams(vmem_limit_bytes=60 << 20),
    )(dn, x, dh, y, quarters, d_wout, gma, gmb, w_qkv, w_in, gain_attn, gain_mlp)


def shards(layer_input, out_grad, lengths, ln_attn, w_qkv, w_attn_out, ln_mlp, w_in, w_mlp_out):
    nh, nb = dims()
    h, b = me()
    rows, width = layer_input.shape
    heads = width // DH
    hl = heads // nh
    group = nh * rows
    slots = nh * nb * rows
    own_rows = w_qkv.shape[0]
    ff = w_mlp_out.shape[0]
    fl = ff // nh
    nz, qs = hl, nb // hl
    lw = nh * DH

    gain_attn = ln_attn.reshape(1, own_rows)
    gain_mlp = ln_mlp.reshape(1, own_rows)
    n1, wma, wmb, wmc, wq, gg, cos, sin = first_exchange(
        lengths, layer_input, w_qkv, gain_attn, w_in, gain_mlp, w_mlp_out.T, out_grad, hl, fl
    )
    wma = lax.all_gather(wma, "blk", axis=1, tiled=True).reshape(width, -1)
    wq = wq.reshape(width, 3 * lw)
    n1 = n1.reshape(group, width)
    qin, kvin, wo, wmb = to_heads(n1, wq, cos, sin, w_attn_out[None], wmb, hl)
    wo = wo.reshape(nz * DH, width)
    kv_all = kvin.reshape(slots, 2 * DH)
    ot, of, lse = attend(lengths, qin, kv_all, 4 * rows, 1024, hl)
    og, hid, n2, wmc = mid_exchange(ot, wo, layer_input, wmc, hl)
    weights = [w.reshape(width, -1) for w in (wma, wmb, wmc)]
    ypart, dpart, gma, gmb = ffn(lengths, n2, gg, weights, fl, own_rows, GRAD_CUT)
    if gma.ndim == 4:
        gma = lax.psum_scatter(gma, "blk", scatter_dimension=0, tiled=True)
        gmb = gmb.reshape((nz, qs) + gmb.shape[1:])
    else:
        gma = gma.reshape(nh, nb * own_rows, gma.shape[1])
        gma = lax.psum_scatter(gma, "blk", scatter_dimension=1, tiled=True)
        gmb = gmb.reshape(nh, nz, qs, own_rows, gmb.shape[1]).transpose(1, 2, 0, 3, 4)
    gma = gma.reshape(nh, own_rows, gma.shape[-1])
    y_out, dh, do_in, go, gmb = back_exchange(
        lengths, dpart, ypart, hid, out_grad, wo, og, gmb
    )
    dq, dkv = attend_grad(lengths, qin, do_in, of, kv_all, lse, 2 * rows, 1024, hl)
    go = go.reshape(nz, qs, own_rows, width)
    gq, dpart1, d_wout, gmb = grads_back(
        dq, dkv.reshape(kvin.shape), cos, sin, n1, wq, go, gmb, hl
    )
    dn, quarters, gma, gmb = last_exchange(
        dpart1, gq.reshape(nh, nz, qs, own_rows, 3 * lw), gma, gmb
    )
    y_out, dx, d_ln_attn, d_wqkv, d_wout, d_ln_mlp, d_win, d_wd = finish(
        dn,
        layer_input,
        dh,
        y_out,
        quarters,
        d_wout,
        gma,
        gmb,
        w_qkv,
        w_in,
        gain_attn,
        gain_mlp,
        fl,
    )
    return (
        y_out,
        dx,
        d_ln_attn.reshape(own_rows),
        d_wqkv,
        d_wout,
        d_ln_mlp.reshape(own_rows),
        d_win,
        d_wd.T,
    )


def solution(mesh):
    both = ("head", "blk")
    row_split = P(both, None)
    return jax.shard_map(
        shards,
        mesh=mesh,
        in_specs=(
            row_split,
            row_split,
            P(),
            P(both),
            row_split,
            row_split,
            P(both),
            row_split,
            P(None, both),
        ),
        out_specs=(
            row_split,
            row_split,
            P(both),
            row_split,
            row_split,
            P(both),
            row_split,
            P(None, both),
        ),
        check_vma=False,
    )
```

```python
import functools
import math

import jax
import jax.numpy as jnp
from jax import lax
from jax.experimental import pallas as pl
from jax.experimental.pallas import tpu as pltpu
from jax.sharding import PartitionSpec as P

DH = 64
ROPE_BASE = 160000.0
NORM_EPS = 1e-05
MASK_FLOOR = -1e30
GRAD_CUT = 1280
FF_BLOCKS = 2
WEIGHT_CUTS = (1280, 1408)
EXP_SCALE = 0.125 * math.log2(math.e)
BF16 = jnp.bfloat16
F32 = jnp.float32
MESH_ID = pl.DeviceIdType.MESH
ANY = pl.BlockSpec(memory_space=pl.ANY)
VM = pl.BlockSpec(memory_space=pltpu.VMEM)
SM = pl.BlockSpec(memory_space=pltpu.SMEM)


def dims():
    nh = lax.axis_size("head")
    nb = lax.axis_size("blk")
    return nh, nb


def me():
    return lax.axis_index("head"), lax.axis_index("blk")


class Staged:
    def __init__(self, loads, drains):
        self.loads, self.drains = loads, drains

    def need(self, *which):
        for i in which:
            self.loads[i].wait()

    def put(self, *which):
        for i in which:
            self.drains[i].start()


def comm_call(body, name, cid, out_shape, in_specs, out_specs, scratch, args, vmem=None, late=(), early=()):
    n_in, n_out, n_late, n_early = len(args), len(out_shape), len(late), len(early)
    in_specs = [ANY if i in late else spec for i, spec in enumerate(in_specs)]
    out_specs = [ANY if i in early else spec for i, spec in enumerate(out_specs)]
    held = [pltpu.VMEM(args[i].shape, args[i].dtype) for i in late]
    held += [pltpu.VMEM(out_shape[i].shape, out_shape[i].dtype) for i in early]
    held.append(pltpu.SemaphoreType.DMA((max(n_late + n_early, 1),)))

    def staged_body(*refs):
        ins, outs = list(refs[:n_in]), list(refs[n_in : n_in + n_out])
        bufs = refs[n_in + n_out : n_in + n_out + n_late + n_early]
        sems = refs[n_in + n_out + n_late + n_early]
        rest = refs[n_in + n_out + n_late + n_early + 1 :]
        loads, drains = {}, {}
        for k, i in enumerate(late):
            loads[i] = pltpu.make_async_copy(ins[i], bufs[k], sems.at[k])
            loads[i].start()
            ins[i] = bufs[k]
        for k, i in enumerate(early):
            k += n_late
            drains[i] = pltpu.make_async_copy(bufs[k], outs[i], sems.at[k])
            outs[i] = bufs[k]
        body(Staged(loads, drains), *ins, *outs, *rest)
        for cp in drains.values():
            cp.wait()

    return pl.pallas_call(
        staged_body,
        out_shape=out_shape,
        in_specs=in_specs,
        out_specs=out_specs,
        scratch_shapes=held + list(scratch),
        name=name,
        compiler_params=pltpu.CompilerParams(
            collective_id=cid, has_side_effects=True, vmem_limit_bytes=vmem
        ),
    )(*args)


def remote(src, dst, send, recv, h, b):
    return pltpu.make_async_remote_copy(
        src_ref=src,
        dst_ref=dst,
        send_sem=send,
        recv_sem=recv,
        device_id=(h, b),
        device_id_type=MESH_ID,
    )


def signal(h, b):
    pl.semaphore_signal(
        pltpu.get_barrier_semaphore(), inc=1, device_id=(h, b), device_id_type=MESH_ID
    )


class HeadGather:
    def __init__(self, nh, h, b, src, dst, sems):
        self.nh, self.h, self.b, self.dst, self.sems = nh, h, b, dst, sems
        nx = nh // 2
        self.nx = nx
        x, c = h // 2, h % 2
        sib = x * 2 + 1 - c
        self.sib = sib
        self.across = []
        for k in range(1, nx):
            self.across.append(
                remote(src, dst.at[h], sems.at[0, k], sems.at[1, k], ((x + k) % nx) * 2 + c, b)
            )
        self.near = remote(src, dst.at[h], sems.at[0, 0], sems.at[1, 0], sib, b)
        self.local = pltpu.make_async_copy(src, dst.at[h], sems.at[2, 0])
        self.forward = []
        for k in range(1, nx):
            got = ((x + nx - k) % nx) * 2 + c
            self.forward.append(
                remote(dst.at[got], dst.at[got], sems.at[2, k], sems.at[3, k], sib, b)
            )

    @staticmethod
    def sem_shape(nh):
        return pltpu.SemaphoreType.DMA((4, nh // 2))

    def start(self):
        for cp in self.across:
            cp.start()
        self.near.start()
        self.local.start()

    def pass_on(self):
        for cp, fw in zip(self.across, self.forward):
            cp.wait_recv()
            fw.start()

    def finish(self):
        for cp in self.across:
            cp.wait_send()
        self.near.wait()
        self.local.wait()
        for fw in self.forward:
            fw.wait()


def lane_roll(values, shift):
    return pltpu.roll(values, shift % values.shape[1], 1)


def lanes_of(values):
    return lax.broadcasted_iota(jnp.int32, (1, values.shape[1]), 1)


def widen(values, width):
    extra = width - values.shape[1]
    if extra <= 0:
        return values[:, :width]
    return jnp.concatenate([values, jnp.zeros((values.shape[0], extra), values.dtype)], axis=1)


def weight_parts(total):
    marks = (0,) + WEIGHT_CUTS + (total,)
    return list(zip(marks[:-1], marks[1:]))


def column(row):
    n = row.shape[1]
    same = lax.broadcasted_iota(jnp.int32, (n, n), 0) == lax.broadcasted_iota(jnp.int32, (n, n), 1)
    return jnp.sum(jnp.where(same, row, 0.0), axis=1, keepdims=True)


def as_row(col):
    n = col.shape[0]
    same = lax.broadcasted_iota(jnp.int32, (n, n), 0) == lax.broadcasted_iota(jnp.int32, (n, n), 1)
    return jnp.sum(jnp.where(same, col, 0.0), axis=0, keepdims=True)


def sequence_ends(len_ref):
    ends, total = [], 0
    for i in range(len_ref.shape[0]):
        total = total + len_ref[i]
        ends.append(total)
    return ends


def segment_first(slot, ends):
    first = jnp.zeros_like(slot)
    for end in ends:
        first = jnp.where(slot >= end, end, first)
    return first


def segment_end(slot, ends, slots):
    last = jnp.zeros_like(slot) + slots
    for end in reversed(ends):
        last = jnp.where(slot < end, end, last)
    return last


def half_pick(low_src, high_src, low_at, high_at):
    low = low_src if low_at == 0 else lane_roll(low_src, DH)
    high = high_src if high_at == 1 else lane_roll(high_src, DH)
    return jnp.where(lanes_of(low) < DH, low, high)


def ff_widths(fl):
    up = lambda v: (v + 127) // 128 * 128
    return up(3 * fl), up(2 * fl), 2 * fl // 128 * 128


class LineGather:
    def __init__(self, pc, src, place, sems):
        self.pc, self.src, self.place, self.sems = pc, src, place, sems

    @staticmethod
    def sem_shape(nz):
        return pltpu.SemaphoreType.DMA((5, nz))

    def origin(self, t, up):
        return self.pc.zi - t if up else self.pc.zi + t

    def move(self, t, up):
        pc = self.pc
        at = self.place(self.origin(t, up))
        n = 0 if up else 2
        return remote(
            self.src if t == 0 else at,
            at,
            self.sems.at[n, t],
            self.sems.at[n + 1, t],
            pc.h,
            pc.b + pc.qs if up else pc.b - pc.qs,
        )

    def sends(self, t, up):
        zi, nz = self.pc.zi, self.pc.nz
        if up:
            return jnp.logical_and(zi - t >= 0, zi + 1 < nz)
        return jnp.logical_and(zi + t < nz, zi - 1 >= 0)

    def local(self):
        return pltpu.make_async_copy(self.src, self.place(self.pc.zi), self.sems.at[4, 0])

    def start(self):
        for up in (True, False):

            @pl.when(self.sends(0, up))
            def _():
                self.move(0, up).start()

        self.local().start()

    def step(self, t, arrived=None):
        low = self.pc.zi < self.pc.nz // 2
        self.take(t, False, jnp.logical_not(low), arrived)
        self.take(t, True, True, arrived)
        self.take(t, False, low, arrived)

    def take(self, t, up, now, arrived):
        zi, nz = self.pc.zi, self.pc.nz
        origin = self.origin(t, up)
        here = jnp.logical_and(now, origin >= 0 if up else origin < nz)

        @pl.when(here)
        def _():
            wait_on(self.place(origin), self.sems.at[1 if up else 3, t - 1])

        if t < nz - 1:

            @pl.when(jnp.logical_and(now, self.sends(t, up)))
            def _():
                self.move(t, up).start()

        if arrived is not None:

            @pl.when(here)
            def _():
                arrived(origin)

    def finish(self):
        self.local().wait()
        for t in range(self.pc.nz - 1):
            for up in (True, False):

                @pl.when(self.sends(t, up))
                def _():
                    self.move(t, up).wait_send()


class BlkGather:
    def __init__(self, pc, src, out, sems, ssem):
        self.pc, self.out, self.ssem, self.src = pc, out, ssem, src
        self.line = LineGather(pc, src, lambda zi: out.at[:, zi, pc.s], sems)

    @staticmethod
    def sem_shapes(nz, qs):
        return [LineGather.sem_shape(nz), pltpu.SemaphoreType.DMA((2, nz, qs))]

    def side(self, zi, ds, own=False):
        pc = self.pc
        ref = self.out.at[:, zi, pc.s]
        return remote(
            self.src if own else ref,
            ref,
            self.ssem.at[0, zi, ds],
            self.ssem.at[1, zi, ds],
            pc.h,
            pc.zi * pc.qs + (pc.s + ds) % pc.qs,
        )

    def spread(self, zi, own=False):
        for ds in range(1, self.pc.qs):
            self.side(zi, ds, own).start()

    def start(self):
        self.line.start()
        self.spread(self.pc.zi, True)

    def step(self, t):
        self.line.step(t, self.spread)

    def finish(self):
        self.line.finish()

        @pl.loop(0, self.pc.nz)
        def _(zi):
            for ds in range(1, self.pc.qs):
                self.side(zi, ds).wait()


class LineSum:
    def __init__(self, pc, term, sent, got, sems):
        self.pc, self.term, self.sent, self.got, self.sems = pc, term, sent, got, sems

    @staticmethod
    def scratch(nz, shape):
        return [
            pltpu.VMEM((2, nz) + shape, BF16),
            pltpu.VMEM((2, nz) + shape, BF16),
            pltpu.SemaphoreType.DMA((4, nz)),
        ]

    def move(self, d, up):
        pc = self.pc
        n = 0 if up else 1
        return remote(
            self.sent.at[n, d],
            self.got.at[n, d],
            self.sems.at[2 * n, d],
            self.sems.at[2 * n + 1, d],
            pc.h,
            pc.b + pc.qs if up else pc.b - pc.qs,
        )

    def takes(self, up):
        return self.pc.zi > 0 if up else self.pc.zi < self.pc.nz - 1

    def lead(self, j):
        self.step(j, False)

    def follow(self, j):
        self.step(j, True)

    def step(self, j, taking):
        low = self.pc.zi < self.pc.nz // 2
        if taking:
            self.one(j, False, jnp.logical_not(low), True)
            self.one(j, True, True, True)
            self.one(j, False, low, True)
        else:
            self.one(j, True, True, False)
            self.one(j, False, True, False)

    def one(self, j, up, now, taking):
        zi, nz = self.pc.zi, self.pc.nz
        d = nz - 1 - j if up else j
        n = 0 if up else 1
        takes = self.takes(up)
        far = jnp.logical_and(now, zi < d if up else zi > d)

        @pl.when(jnp.logical_and(far, takes if taking else jnp.logical_not(takes)))
        def _():
            if taking:
                wait_on(self.got.at[n, d], self.sems.at[2 * n + 1, d])
                self.sent[n, d] = (self.term(d) + self.got[n, d].astype(F32)).astype(BF16)
            else:
                self.sent[n, d] = self.term(d).astype(BF16)
            self.move(d, up).start()

    def total(self, total_ref):
        zi = self.pc.zi
        total_ref[...] = self.term(zi)
        for up in (True, False):
            n = 0 if up else 1

            @pl.when(self.takes(up))
            def _():
                wait_on(self.got.at[n, zi], self.sems.at[2 * n + 1, zi])
                total_ref[...] += self.got[n, zi].astype(F32)

    def finish(self):
        zi, nz = self.pc.zi, self.pc.nz
        for j in range(nz - 1):
            for up in (True, False):
                d = nz - 1 - j if up else j

                @pl.when(zi < d if up else zi > d)
                def _():
                    self.move(d, up).wait_send()


class StretchSum:
    def __init__(self, pc, part, got, sems):
        self.pc, self.part, self.got, self.sems = pc, part, got, sems

    @staticmethod
    def scratch(nz, shape):
        return [pltpu.VMEM((nz,) + shape, BF16), pltpu.SemaphoreType.DMA((2, nz))]

    def move(self, i):
        pc = self.pc
        to = (pc.zi + i) % pc.nz
        return remote(
            self.part.at[to],
            self.got.at[pc.zi],
            self.sems.at[0, i],
            self.sems.at[1, i],
            pc.h,
            to * pc.qs + pc.s,
        )

    def start(self):
        for i in range(1, self.pc.nz):
            self.move(i).start()

    def total(self):
        pc = self.pc
        total = self.part[pc.zi].astype(F32)
        for i in range(1, pc.nz):
            self.move(i).wait_recv()
            total = total + self.got[(pc.zi + pc.nz - i) % pc.nz].astype(F32)
        return total

    def finish(self):
        for i in range(1, self.pc.nz):
            self.move(i).wait_send()


class PlaneWeights:
    def __init__(self, pc, pack, out, sems, ksem):
        self.pc, self.pack, self.out, self.sems, self.ksem = pc, pack, out, sems, ksem

    @staticmethod
    def sem_shapes(nh, nz, qs):
        dma = pltpu.SemaphoreType.DMA
        return [dma((2, nz)), dma((4, nh // 2 * qs))]

    def along(self, i):
        pc = self.pc
        to = (pc.zi + i) % pc.nz
        return remote(
            self.pack.at[to],
            self.out.at[pc.h, pc.zi, pc.s],
            self.sems.at[0, i],
            self.sems.at[1, i],
            pc.h,
            to * pc.qs + pc.s,
        )

    def local(self):
        pc = self.pc
        return pltpu.make_async_copy(
            self.pack.at[pc.zi], self.out.at[pc.h, pc.zi, pc.s], self.sems.at[0, 0]
        )

    def place(self, i, sign):
        pc = self.pc
        nx = pc.nh // 2
        dx, ds = i // pc.qs, i % pc.qs
        if sign < 0:
            dx, ds = nx - dx, pc.qs - ds
        return ((pc.x + dx) % nx) * 2 + pc.c, (pc.s + ds) % pc.qs

    def across(self, i):
        pc = self.pc
        th, ts = self.place(i, 1)
        ref = self.out.at[pc.h, :, pc.s]
        return remote(
            ref, ref, self.ksem.at[0, i], self.ksem.at[1, i], th, pc.zi * pc.qs + ts
        )

    def near(self, i):
        pc = self.pc
        gh, gs = self.place(i, -1)
        ref = self.out.at[gh, :, gs]
        return remote(ref, ref, self.ksem.at[2, i], self.ksem.at[3, i], pc.sib, pc.b)

    def start(self):
        for i in range(1, self.pc.nz):
            self.along(i).start()
        self.local().start()

    def spread(self):
        pc = self.pc
        self.local().wait()
        for i in range(1, pc.nz):
            self.along(i).wait_recv()

        @pl.loop(1, pc.nh // 2 * pc.qs)
        def _(i):
            self.across(i).start()

        self.near(0).start()

    def pass_on(self):
        @pl.loop(1, self.pc.nh // 2 * self.pc.qs)
        def _(i):
            self.across(i).wait_recv()
            self.near(i).start()

    def finish(self):
        for i in range(1, self.pc.nz):
            self.along(i).wait_send()

        @pl.loop(1, self.pc.nh // 2 * self.pc.qs)
        def _(i):
            self.across(i).wait_send()

        @pl.loop(0, self.pc.nh // 2 * self.pc.qs)
        def _(i):
            self.near(i).wait()


def first_body(nh, nb, hl, fl, io, len_ref, x_ref, wq_ref, ga_ref, win_hbm, gf_ref, wd_hbm, g_ref, n1_all, wma, wmb, wmc, wq_all, gg, cos_ref, sin_ref, own_n, pack, wmp, win_ref, wd_ref, lsem, wsem, ksem, gsem, msem, stage):
    pc = Place(nh, nb, hl)
    h, b = pc.h, pc.b
    loads = [
        pltpu.make_async_copy(win_hbm, win_ref, stage.at[0]),
        pltpu.make_async_copy(wd_hbm, wd_ref, stage.at[1]),
    ]
    for cp in loads:
        cp.start()
    signal_near(pc)
    width = x_ref.shape[1]
    lw = width // pc.nz
    gain = column(ga_ref[...].astype(F32))
    io.need(2)
    for c in range(3):
        w = wq_ref[:, c * width : (c + 1) * width].astype(F32) * gain
        tile = lambda l, i: w[:, l * pc.nz * DH + i // 2 * 128 : l * pc.nz * DH + i // 2 * 128 + 128]
        for i in range(pc.nz):
            for p in range(nh // 2):
                both = half_pick(tile(2 * p, i), tile(2 * p + 1, i), i % 2, i % 2)
                at = c * lw + p * 128
                pack[i, :, at : at + 128] = both.astype(BF16)
    io.need(1)
    own_n[...] = norm_of(x_ref[...].astype(F32))[0].astype(BF16)
    wait_near(pc)
    weights = PlaneWeights(pc, pack, wq_all, wsem, ksem)
    line = LineGather(pc, own_n, lambda zi: n1_all.at[zi], lsem)
    gather = HeadGather(nh, h, b, g_ref, gg, gsem)
    weights.start()
    line.start()
    gather.start()
    for cp in loads:
        cp.wait()
    total = ff_widths(fl)[0]
    ff = nh * fl
    win = win_ref[...].astype(F32) * column(gf_ref[...].astype(F32))
    wd = widen(wd_ref[...].astype(F32), total if total > ff else (ff + 127) // 128 * 128)
    lane = lax.broadcasted_iota(jnp.int32, (1, total), 1)
    for i in range(nh):
        gate = widen(lane_roll(win, -i * fl), total)
        up = widen(lane_roll(win, fl - ff - i * fl), total)
        down = widen(lane_roll(wd, 2 * fl - i * fl), total)
        piece = jnp.where(
            lane < fl,
            gate,
            jnp.where(lane < 2 * fl, up, jnp.where(lane < 3 * fl, down, 0.0)),
        )
        wmp[i] = piece.astype(BF16)
    copies = []
    for n, (dst, (begin, end)) in enumerate(zip((wma, wmb, wmc), weight_parts(total))):
        cols = pl.ds(begin, end - begin)
        for i in range(1, nh):
            th = (h + i) % nh
            src = wmp.at[th, :, cols]
            copies.append(remote(src, dst.at[h], msem.at[0, n, i], msem.at[1, n, i], th, b))
        copies.append(pltpu.make_async_copy(wmp.at[h, :, cols], dst.at[h], msem.at[0, n, 0]))
    weights.spread()
    for cp in copies:
        cp.start()
    ends = sequence_ends(len_ref)
    rows = x_ref.shape[0]
    lane = lax.broadcasted_iota(jnp.int32, (1, 2 * DH), 1)
    power = (lane % (DH // 2)).astype(F32) * (-2.0 / DH)
    inv_freq = jnp.exp2(power * math.log2(ROPE_BASE))
    sign = jnp.where(lane % DH < DH // 2, -1.0, 1.0)
    line.step(1)
    for i in range(pc.nz):
        slot = (h * nb + i * pc.qs + pc.s) * rows + lax.broadcasted_iota(jnp.int32, (rows, 1), 0)
        angle = (slot - segment_first(slot, ends)).astype(F32) * inv_freq
        cos_ref[i * rows : (i + 1) * rows, :] = jnp.cos(angle)
        sin_ref[i * rows : (i + 1) * rows, :] = jnp.sin(angle) * sign
    io.put(6, 7)
    gather.pass_on()
    for t in range(2, pc.nz):
        line.step(t)
    weights.pass_on()
    for cp in copies:
        cp.wait()
    weights.finish()
    line.finish()
    gather.finish()


def first_exchange(lengths, x, w_qkv, gain_attn, w_in, gain_mlp, wd_t, g, hl, fl):
    nh, nb = dims()
    rows, width = x.shape
    nz, qs = hl, nb // hl
    lw = width // nz
    own_rows = w_in.shape[0]
    total = ff_widths(fl)[0]
    dma = pltpu.SemaphoreType.DMA
    return comm_call(
        functools.partial(first_body, nh, nb, hl, fl),
        "first_exchange",
        0,
        (
            jax.ShapeDtypeStruct((nz, rows, width), BF16),
            *[
                jax.ShapeDtypeStruct((nh, own_rows, end - begin), BF16)
                for begin, end in weight_parts(total)
            ],
            jax.ShapeDtypeStruct((nh, nz, qs, own_rows, 3 * lw), BF16),
            jax.ShapeDtypeStruct((nh, rows, width), BF16),
            jax.ShapeDtypeStruct((nz * rows, 2 * DH), F32),
            jax.ShapeDtypeStruct((nz * rows, 2 * DH), F32),
        ),
        [SM, VM, VM, VM, ANY, VM, ANY, ANY],
        [ANY] * 6 + [VM] * 2,
        [
            pltpu.VMEM((rows, width), BF16),
            pltpu.VMEM((nz, own_rows, 3 * lw), BF16),
            pltpu.VMEM((nh, own_rows, total), BF16),
            pltpu.VMEM(w_in.shape, BF16),
            pltpu.VMEM(wd_t.shape, BF16),
            LineGather.sem_shape(nz),
        ]
        + PlaneWeights.sem_shapes(nh, nz, qs)
        + [
            HeadGather.sem_shape(nh),
            dma((2, 3, nh)),
            dma((2,)),
        ],
        (lengths, x, w_qkv, gain_attn, w_in, gain_mlp, wd_t, g),
        vmem=60 << 20,
        late=(2, 1),
        early=(6, 7),
    )


class Place:
    def __init__(self, nh, nb, hl):
        h, b = me()
        self.nh, self.nb, self.h, self.b = nh, nb, h, b
        self.x, self.c = h // 2, h % 2
        self.nz = hl
        self.qs = nb // hl
        self.cb = self.qs // 2
        self.sib = self.x * 2 + 1 - self.c
        self.zi, self.s = b // self.qs, b % self.qs
        self.head = self.x * 2 + self.s // self.cb
        self.u = self.s % self.cb
        self.from_s = self.u * 2 + self.c

    def attends(self, zi, l, core, u):
        return (l // 2) * 2 + core, zi * self.qs + (l % 2) * self.cb + u


def signal_near(pc):
    here = pc.nh * pc.qs

    @pl.loop(1, here)
    def _(i):
        signal((pc.h + i // pc.qs) % pc.nh, pc.zi * pc.qs + (pc.s + i % pc.qs) % pc.qs)

    @pl.loop(1, pc.nz)
    def _(i):
        signal(pc.h, (pc.zi + i) % pc.nz * pc.qs + pc.s)


def wait_near(pc, more=0):
    pl.semaphore_wait(pltpu.get_barrier_semaphore(), pc.nh * pc.qs + pc.nz - 2 + more)


def enter_with(pc, source):
    signal_near(pc)
    for i in range(1, pc.nz):
        signal(*source((pc.zi + i) % pc.nz))
    wait_near(pc, pc.nz - 1)


def routed(pc, src, dst, send, recv, th, tb, act):
    mine = jnp.logical_and(th == pc.h, tb == pc.b)

    @pl.when(mine)
    def _():
        if act == "start":
            pltpu.make_async_copy(src, dst, recv).start()

    @pl.when(jnp.logical_not(mine))
    def _():
        cp = remote(src, dst, send, recv, th, tb)
        if act == "start":
            cp.start()
        else:
            cp.wait_send()


def wait_on(ref, sem):
    pltpu.make_async_copy(ref, ref, sem).wait()


def stretch_lanes(ref, zi, rows):
    return ref.at[:, :, pl.ds(pl.multiple_of(zi * rows, rows), rows)]


def outputs_back(pc, o_ref, og, osem, act):
    rows = og.shape[3]
    for zi in range(pc.nz):
        routed(
            pc,
            stretch_lanes(o_ref, zi, rows),
            og.at[pc.zi],
            osem.at[0, zi],
            osem.at[1, pc.zi],
            pc.head,
            zi * pc.qs + pc.from_s,
            act,
        )


def grads_out(pc, dots, do_in, qsem, act):
    rows = dots.shape[3]
    for zi in range(pc.nz):
        th, tb = pc.attends(zi, pc.h, pc.s % 2, pc.s // 2)
        routed(
            pc,
            dots.at[zi],
            stretch_lanes(do_in, pc.zi, rows),
            qsem.at[0, zi],
            qsem.at[1, pc.zi],
            th,
            tb,
            act,
        )


def halves_swapped(tile):
    lane = lanes_of(tile)
    return jnp.where(lane % DH < DH // 2, lane_roll(tile, -(DH // 2)), lane_roll(tile, DH // 2))


def turned(tile, cos, sin):
    return tile * cos + halves_swapped(tile) * sin


def to_heads_body(nh, nb, hl, io, n1_hbm, w_hbm, cos_ref, sin_ref, wo_ref, wmb_ref, wmc_ref, qin, kvin, wo_all, wmb_all, wmc_line, qbuf, kvbuf, n1_ref, w_ref, qsem, ksem, fsem, osem, osem2, bsem, bsem2, csem, stage):
    pc = Place(nh, nb, hl)
    loads = [
        pltpu.make_async_copy(n1_hbm, n1_ref, stage.at[0]),
        pltpu.make_async_copy(w_hbm, w_ref, stage.at[1]),
    ]
    for cp in loads:
        cp.start()
    signal_near(pc)
    rows = kvbuf.shape[2]
    lw = nh * DH
    for cp in loads:
        cp.wait()
    n1 = n1_ref[...]
    io.need(2, 3)
    cos, sin = cos_ref[...], sin_ref[...]
    kk = jnp.dot(n1, w_ref[:, lw : 2 * lw], preferred_element_type=F32)
    vv = jnp.dot(n1, w_ref[:, 2 * lw :], preferred_element_type=F32)
    for p in range(nh // 2):
        k = turned(kk[:, p * 128 : (p + 1) * 128], cos, sin)
        v = vv[:, p * 128 : (p + 1) * 128]
        low = lanes_of(k) < DH
        even = jnp.where(low, k, lane_roll(v, DH)).astype(BF16)
        odd = jnp.where(low, lane_roll(k, DH), v).astype(BF16)
        for i in range(pc.nz):
            kvbuf[2 * p, i] = even[i * rows : (i + 1) * rows]
            kvbuf[2 * p + 1, i] = odd[i * rows : (i + 1) * rows]
    wait_near(pc)

    def keys_out(act):
        for l in range(nh):
            for u in range(pc.cb):
                th, tb = pc.attends(pc.zi, l, pc.s % 2, u)
                routed(
                    pc,
                    kvbuf.at[l],
                    kvin.at[pc.h, :, pc.s],
                    ksem.at[0, l * pc.cb + u],
                    ksem.at[1, pc.h * pc.cb + pc.s // 2],
                    th,
                    tb,
                    act,
                )

    def queries_out(act):
        for l in range(nh):
            th, tb = pc.attends(pc.zi, l, pc.s % 2, pc.s // 2)
            routed(
                pc, qbuf.at[l], qin.at[pc.h], qsem.at[0, l], qsem.at[1, pc.h], th, tb, act
            )

    spread = BlkGather(pc, wo_ref, wo_all, osem, osem2)
    spread_b = BlkGather(pc, wmb_ref, wmb_all, bsem, bsem2)
    line_c = LineGather(pc, wmc_ref, lambda zi: wmc_line.at[:, zi], csem)
    keys_out("start")
    spread.start()
    spread_b.start()
    line_c.start()
    qq = jnp.dot(n1, w_ref[:, :lw], preferred_element_type=F32)
    for p in range(nh // 2):
        q = turned(qq[:, p * 128 : (p + 1) * 128], cos, sin).T.astype(BF16)
        qbuf[2 * p] = q[:DH]
        qbuf[2 * p + 1] = q[DH:]
    queries_out("start")
    count = nh * pc.cb

    def forward(i):
        at = kvin.at[i // pc.cb, :, 2 * (i % pc.cb) + pc.c]
        return remote(at, at, fsem.at[0, i], fsem.at[1, i], pc.sib, pc.b)

    @pl.loop(0, count)
    def _(i):
        wait_on(kvin.at[i // pc.cb, :, 2 * (i % pc.cb) + pc.c], ksem.at[1, i])
        forward(i).start()

    for t in range(1, pc.nz):
        spread.step(t)
        spread_b.step(t)
        line_c.step(t)
    keys_out("wait_send")
    queries_out("wait_send")
    for i in range(nh):
        wait_on(qin.at[i], qsem.at[1, i])

    @pl.loop(0, count)
    def _(i):
        forward(i).wait()

    spread.finish()
    spread_b.finish()
    line_c.finish()


def to_heads(n1, wq, cos, sin, wo, wmb, wmc, hl):
    nh, nb = dims()
    group, width = n1.shape
    nz, qs = hl, nb // hl
    cb = qs // 2
    rows = group // nz
    dma = pltpu.SemaphoreType.DMA
    return comm_call(
        functools.partial(to_heads_body, nh, nb, hl),
        "to_heads",
        1,
        (
            jax.ShapeDtypeStruct((nh, DH, group), BF16),
            jax.ShapeDtypeStruct((nh, nz, qs, rows, 2 * DH), BF16),
            jax.ShapeDtypeStruct((1, nz, qs) + wo.shape[1:], BF16),
            jax.ShapeDtypeStruct((nh, nz, qs) + wmb.shape[1:], BF16),
            jax.ShapeDtypeStruct((nh, nz) + wmc.shape[1:], BF16),
        ),
        [ANY, ANY, VM, VM, ANY, ANY, ANY],
        [ANY] * 5,
        [
            pltpu.VMEM((nh, DH, group), BF16),
            pltpu.VMEM((nh, nz, rows, 2 * DH), BF16),
            pltpu.VMEM(n1.shape, BF16),
            pltpu.VMEM(wq.shape, BF16),
            dma((2, nh)),
            dma((2, nh * cb)),
            dma((2, nh * cb)),
        ]
        + BlkGather.sem_shapes(nz, qs) * 2
        + [LineGather.sem_shape(nz), dma((2,))],
        (n1, wq, cos, sin, wo, wmb, wmc),
        vmem=60 << 20,
        late=(2, 3),
    )


class Queries:
    def __init__(self, nh, nb, hl, len_ref, lanes, slots, size):
        pc = Place(nh, nb, hl)
        tile = pl.program_id(0)
        rows = slots // (nh * nb)
        count = lanes // rows
        each = pc.nz // count
        ends = sequence_ends(len_ref)
        base = (tile // each) * nb + (tile % each) * count * pc.qs + pc.from_s
        lane = lax.broadcasted_iota(jnp.int32, (1, lanes), 1)
        slot = (base + lane // rows * pc.qs) * rows + lane % rows
        self.first = segment_first(slot, ends)
        self.last = segment_end(slot, ends, slots)
        near = base * rows
        far = (base + (count - 1) * pc.qs) * rows + rows - 1
        self.size = size
        self.lo = segment_first(near, ends) // size
        self.hi = (segment_end(far, ends, slots) + size - 1) // size
        self.open = jnp.minimum((segment_first(far, ends) + size - 1) // size, self.hi)
        self.close = jnp.maximum(segment_end(near, ends, slots) // size, self.open)
        self.lanes = lanes

    def allowed(self, block_at):
        at = block_at * self.size + lax.broadcasted_iota(jnp.int32, (self.size, self.lanes), 0)
        return jnp.logical_and(at >= self.first, at < self.last)

    def walk(self, step, carry):
        masked = lambda j, kept: step(j, kept, True)
        carry = lax.fori_loop(self.lo, self.open, masked, carry)
        carry = lax.fori_loop(self.open, self.close, lambda j, kept: step(j, kept, False), carry)
        return lax.fori_loop(self.close, self.hi, masked, carry)


def attend_body(nh, nb, hl, size, len_ref, q_ref, kv_ref, o_ref, of_ref, lse_ref):
    q = q_ref[0]
    lanes = q.shape[1]
    at = Queries(nh, nb, hl, len_ref, lanes, kv_ref.shape[0], size)
    q_pad = jnp.concatenate([q, jnp.zeros_like(q)], axis=0)
    is_key = lax.broadcasted_iota(jnp.int32, (1, 2 * DH), 1) < DH

    def step(j, carry, masked):
        top, acc = carry
        kv = kv_ref[pl.ds(pl.multiple_of(j * size, size), size), :]
        s = jnp.dot(kv, q_pad, preferred_element_type=F32)
        if masked:
            s = jnp.where(at.allowed(j), s, MASK_FLOOR)
        new_top = jnp.maximum(top, jnp.max(s, axis=0, keepdims=True))
        p = jnp.exp2((s - new_top) * EXP_SCALE).astype(BF16)
        alpha = jnp.exp2((top - new_top) * EXP_SCALE)
        ones_values = jnp.where(is_key, jnp.ones_like(kv), kv)
        acc = acc * alpha + lax.dot_general(
            ones_values, p, (((0,), (0,)), ((), ())), preferred_element_type=F32
        )
        return new_top, acc

    top, acc = at.walk(
        step, (jnp.full((1, lanes), MASK_FLOOR, F32), jnp.zeros((2 * DH, lanes), F32))
    )
    total = acc[:1]
    o = acc[DH:] / total
    of_ref[0] = o
    o_ref[0] = o.astype(BF16)
    lse_ref[0] = top * EXP_SCALE + jnp.log2(total)


def attend_specs(kv_rows, lanes, tiles_each):
    tile_spec = pl.BlockSpec((1, DH, lanes), lambda i, *_: (i // tiles_each, 0, i % tiles_each))
    row_spec = pl.BlockSpec((1, 1, lanes), lambda i, *_: (i, 0, 0))
    kv_spec = pl.BlockSpec((kv_rows, 2 * DH), lambda i, *_: (0, 0))
    return tile_spec, row_spec, kv_spec


def attend(lengths, q, kv, lanes, size, hl):
    nh, nb = dims()
    each = q.shape[2] // lanes
    tiles = q.shape[0] * each
    tile_spec, row_spec, kv_spec = attend_specs(kv.shape[0], lanes, each)
    return pl.pallas_call(
        functools.partial(attend_body, nh, nb, hl, size),
        grid_spec=pltpu.PrefetchScalarGridSpec(
            num_scalar_prefetch=1,
            grid=(tiles,),
            in_specs=[tile_spec, kv_spec],
            out_specs=[tile_spec, tile_spec, row_spec],
        ),
        out_shape=(
            jax.ShapeDtypeStruct(q.shape, BF16),
            jax.ShapeDtypeStruct(q.shape, F32),
            jax.ShapeDtypeStruct((tiles, 1, lanes), F32),
        ),
        name="attend",
        compiler_params=pltpu.CompilerParams(vmem_limit_bytes=60 << 20),
    )(lengths, q, kv)


def attend_grad_body(nh, nb, hl, size, len_ref, q_ref, do_ref, of_ref, kv_ref, lse_ref, dq_ref, dkv_ref, acc_ref):
    tile = pl.program_id(0)

    @pl.when(tile == 0)
    def _():
        acc_ref[...] = jnp.zeros_like(acc_ref)

    q = q_ref[0]
    do = do_ref[0]
    lanes = q.shape[1]
    place = Queries(nh, nb, hl, len_ref, lanes, kv_ref.shape[0], size)
    zero = jnp.zeros_like(q)
    both = jnp.concatenate(
        [jnp.concatenate([q, zero], axis=0), jnp.concatenate([zero, do], axis=0)], axis=1
    )
    delta = jnp.sum(do.astype(F32) * of_ref[0], axis=0, keepdims=True)
    lse = lse_ref[0]

    def step(j, dq, masked):
        at = pl.ds(pl.multiple_of(j * size, size), size)
        kv = kv_ref[at, :]
        sd = jnp.dot(kv, both, preferred_element_type=F32)
        s, dp = sd[:, :lanes], sd[:, lanes:]
        power = s * EXP_SCALE - lse
        if masked:
            power = jnp.where(place.allowed(j), power, MASK_FLOOR)
        p = jnp.exp2(power)
        ds = (p * (dp - delta)).astype(BF16)
        acc_ref[at, :] += lax.dot_general(
            jnp.concatenate([ds, p.astype(BF16)], axis=1),
            both,
            (((1,), (1,)), ((), ())),
            preferred_element_type=F32,
        )
        return dq + lax.dot_general(
            kv, ds, (((0,), (0,)), ((), ())), preferred_element_type=F32
        )

    dq = place.walk(step, jnp.zeros((2 * DH, lanes), F32))
    dq_ref[0] = (dq[:DH] * 0.125).astype(BF16)

    @pl.when(tile == pl.num_programs(0) - 1)
    def _():
        lane = lax.broadcasted_iota(jnp.int32, (1, 2 * DH), 1)
        dkv_ref[...] = (acc_ref[...] * jnp.where(lane < DH, 0.125, 1.0)).astype(BF16)


def attend_grad(lengths, q, do, of, kv, lse, lanes, size, hl):
    nh, nb = dims()
    tiles = lse.size // lanes
    lse = lse.reshape(tiles, 1, lanes)
    tile_spec, row_spec, kv_spec = attend_specs(kv.shape[0], lanes, tiles // q.shape[0])
    return pl.pallas_call(
        functools.partial(attend_grad_body, nh, nb, hl, size),
        grid_spec=pltpu.PrefetchScalarGridSpec(
            num_scalar_prefetch=1,
            grid=(tiles,),
            in_specs=[tile_spec, tile_spec, tile_spec, kv_spec, row_spec],
            out_specs=[tile_spec, kv_spec],
            scratch_shapes=[pltpu.VMEM(kv.shape, F32)],
        ),
        out_shape=(jax.ShapeDtypeStruct(q.shape, BF16), jax.ShapeDtypeStruct(kv.shape, BF16)),
        name="attend_grad",
        compiler_params=pltpu.CompilerParams(vmem_limit_bytes=60 << 20),
    )(lengths, q, do, of, kv, lse)


class HeadSum:
    def __init__(self, nh, h, b, part, near, far, out, sems):
        self.nx = nh // 2
        self.x, self.c = h // 2, h % 2
        self.h, self.part, self.near, self.far, self.out = h, part, near, far, out
        sib = self.x * 2 + 1 - self.c
        self.pairs = [
            remote(
                part.at[((self.x + k) % self.nx) * 2 + 1 - self.c],
                near.at[k],
                sems.at[0, k],
                sems.at[1, k],
                sib,
                b,
            )
            for k in range(self.nx)
        ]
        self.across = [
            remote(
                out.at[k],
                far.at[k],
                sems.at[2, k],
                sems.at[3, k],
                ((self.x + k) % self.nx) * 2 + self.c,
                b,
            )
            for k in range(1, self.nx)
        ]

    @staticmethod
    def sem_shape(nh):
        return pltpu.SemaphoreType.DMA((4, nh // 2))

    @staticmethod
    def buffers(nh, rows, width):
        return [pltpu.VMEM((nh // 2, rows, width), BF16)] * 3

    def start(self):
        for k in list(range(1, self.nx)) + [0]:
            self.pairs[k].start()

    def send(self):
        for k in range(1, self.nx):
            self.pairs[k].wait_recv()
            at = ((self.x + k) % self.nx) * 2 + self.c
            self.out[k] = (self.part[at].astype(F32) + self.near[k].astype(F32)).astype(BF16)
            self.across[k - 1].start()

    def total(self):
        self.pairs[0].wait_recv()
        total = self.part[self.h].astype(F32) + self.near[0].astype(F32)
        for k in range(1, self.nx):
            self.across[k - 1].wait_recv()
            total = total + self.far[k].astype(F32)
        return total

    def finish(self):
        for cp in self.pairs:
            cp.wait_send()
        for cp in self.across:
            cp.wait_send()


def norm_of(values):
    centre = values - jnp.mean(values, axis=-1, keepdims=True)
    scale = lax.rsqrt(jnp.mean(centre * centre, axis=-1, keepdims=True) + NORM_EPS)
    return centre * scale, scale


def norm_pull(grad, normed, scale):
    one = jnp.mean(grad, axis=-1, keepdims=True)
    two = jnp.mean(grad * normed, axis=-1, keepdims=True)
    return scale * (grad - one - normed * two)


CHUNKS = 2


def chunk_of(ref, j, axis):
    size = ref.shape[axis] // CHUNKS
    at = pl.ds(j * size, size)
    return ref.at[at] if axis == 0 else ref.at[:, at]


def head_sums(nh, h, b, part, bufs, sems):
    near, far, out = bufs
    return [
        HeadSum(
            nh,
            h,
            b,
            chunk_of(part, j, 1),
            chunk_of(near, j, 1),
            chunk_of(far, j, 1),
            chunk_of(out, j, 1),
            sems.at[j],
        )
        for j in range(CHUNKS)
    ]


def head_gathers(nh, h, b, src, dst, sems):
    return [
        HeadGather(nh, h, b, chunk_of(src, j, 0), chunk_of(dst, j, 1), sems.at[j])
        for j in range(CHUNKS)
    ]


def chunk_sems(nh):
    return pltpu.SemaphoreType.DMA((CHUNKS, 4, nh // 2))


def mid_body(nh, nb, hl, io, o_ref, wo_ref, x_ref, wmb_ref, og, hid_ref, ng_ref, wmb_all, part, near, far, out, nbuf, osem, ssem, gsem, wsem):
    pc = Place(nh, nb, hl)
    h, b = pc.h, pc.b
    enter_with(pc, lambda zi: pc.attends(zi, h, pc.s % 2, pc.s // 2))
    rows, width = x_ref.shape
    outputs_back(pc, o_ref, og, osem, "start")
    sides = [
        remote(
            wmb_ref,
            wmb_all.at[:, :, pc.s],
            wsem.at[0, ds],
            wsem.at[1, ds],
            h,
            pc.zi * pc.qs + (pc.s + ds) % pc.qs,
        )
        for ds in range(1, pc.qs)
    ]
    sides.append(pltpu.make_async_copy(wmb_ref, wmb_all.at[:, :, pc.s], wsem.at[0, 0]))
    for cp in sides:
        cp.start()
    outputs_back(pc, o_ref, og, osem, "wait_send")
    for zi in range(pc.nz):
        wait_on(og.at[zi], osem.at[1, zi])
    io.put(0)
    io.need(1)
    wo = wo_ref[...]
    for i in range(nh):
        part[i] = lax.dot_general(
            og[:, i].reshape(pc.nz * DH, rows),
            wo,
            (((0,), (0,)), ((), ())),
            preferred_element_type=F32,
        ).astype(BF16)
    hss = head_sums(nh, h, b, part, (near, far, out), ssem)
    hgs = head_gathers(nh, h, b, nbuf, ng_ref, gsem)
    for hs in hss:
        hs.start()
    for hs in hss:
        hs.send()
    size = rows // CHUNKS
    io.need(2)
    for j, (hs, hg) in enumerate(zip(hss, hgs)):
        at = pl.ds(j * size, size)
        hid = x_ref[at, :].astype(F32) + hs.total()
        hid_ref[at, :] = hid
        nbuf[at, :] = norm_of(hid)[0].astype(BF16)
        hg.start()
    io.put(1)
    for hg in hgs:
        hg.pass_on()
    for hs, hg in zip(hss, hgs):
        hs.finish()
        hg.finish()
    for cp in sides:
        cp.wait()


def mid_exchange(ot, wo, x, wmb, hl):
    nh, nb = dims()
    rows, width = x.shape
    nz = hl
    return comm_call(
        functools.partial(mid_body, nh, nb, hl),
        "mid_exchange",
        2,
        (
            jax.ShapeDtypeStruct((nz, nh, DH, rows), BF16),
            jax.ShapeDtypeStruct(x.shape, F32),
            jax.ShapeDtypeStruct((nh, rows, width), BF16),
            jax.ShapeDtypeStruct((nh, nz, nb // nz) + wmb.shape[2:], BF16),
        ),
        [ANY] * 4,
        [ANY] * 4,
        [pltpu.VMEM((nh, rows, width), BF16)]
        + HeadSum.buffers(nh, rows, width)
        + [
            pltpu.VMEM((rows, width), BF16),
            pltpu.SemaphoreType.DMA((2, nz)),
            chunk_sems(nh),
            chunk_sems(nh),
            pltpu.SemaphoreType.DMA((2, nb // nz)),
        ],
        (ot, wo, x, wmb),
        vmem=60 << 20,
        late=(1, 2),
        early=(0, 1),
    )


def ffn_body(nh, nb, fl, split_rows, cut, len_ref, n_hbm, g_hbm, wa_hbm, wb_hbm, wc_hbm, y_hbm, d_hbm, ga_hbm, gb_hbm, n_ref, g_ref, w_ref, y_ref, d_ref, ga_ref, gb_ref, gy, mm, dz, stage, drain):
    rows, width = n_ref.shape[1], n_ref.shape[2]
    group = nh * rows
    total, zc, off = ff_widths(fl)
    wide = total - off
    shift = 2 * fl - off
    step = FF_BLOCKS * rows
    lane = lax.broadcasted_iota(jnp.int32, (1, wide), 1)
    real = lane < fl
    valid = sequence_ends(len_ref)[-1]
    blk = lax.axis_index("blk")
    loads = [
        pltpu.make_async_copy(n_hbm, n_ref, stage.at[0]),
        pltpu.make_async_copy(g_hbm, g_ref, stage.at[1]),
    ]
    for n, (w, (begin, end)) in enumerate(zip((wa_hbm, wb_hbm, wc_hbm), weight_parts(total))):
        dst = w_ref.at[:, pl.ds(begin, end - begin)]
        loads.append(pltpu.make_async_copy(w, dst, stage.at[2 + n]))
    for cp in loads:
        cp.start()
    for cp in loads:
        cp.wait()

    def out_rows(r):
        at = pl.ds(r * FF_BLOCKS, FF_BLOCKS)
        return [
            pltpu.make_async_copy(d_ref.at[at], d_hbm.at[at], drain.at[0, r]),
            pltpu.make_async_copy(y_ref.at[at], y_hbm.at[at], drain.at[1, r]),
        ]

    @pl.loop(0, group // step)
    def _(r):
        at = pl.ds(pl.multiple_of(r * step, step), step)
        n = n_ref[pl.ds(r * FF_BLOCKS, FF_BLOCKS)].reshape(step, width)
        row = lax.broadcasted_iota(jnp.int32, (step, 1), 0)
        slot = ((r * FF_BLOCKS + row // rows) * nb + blk) * rows + row % rows
        g = g_ref[pl.ds(r * FF_BLOCKS, FF_BLOCKS)].reshape(step, width)
        g = jnp.where(slot < valid, g.astype(F32), 0.0).astype(BF16)
        gy[at, :] = g
        z = jnp.dot(n, w_ref[:, :zc], preferred_element_type=F32)
        dm = lane_roll(jnp.dot(g, w_ref[:, off:], preferred_element_type=F32), -shift)
        gate, up = z[:, :wide], lane_roll(z, -fl)[:, :wide]
        cdf = 0.5 * (1.0 + lax.erf(gate * math.sqrt(0.5)))
        act = gate * cdf
        slope = cdf + gate * jnp.exp(-0.5 * gate * gate) * (1.0 / math.sqrt(2.0 * math.pi))
        m = lane_roll(jnp.where(real, act * up, 0.0), shift).astype(BF16)
        mm[at, :] = m
        d_gate = widen(jnp.where(real, dm * up * slope, 0.0), zc)
        d_up = lane_roll(widen(jnp.where(real, dm * act, 0.0), zc), fl)
        d = (d_gate + d_up).astype(BF16)
        dz[at, :] = d
        nt = (((1,), (1,)), ((), ()))
        dpart = lax.dot_general(d, w_ref[:, :zc], nt, preferred_element_type=F32)
        d_ref[pl.ds(r * FF_BLOCKS, FF_BLOCKS)] = dpart.astype(BF16).reshape(FF_BLOCKS, rows, width)
        ypart = lax.dot_general(m, w_ref[:, off:], nt, preferred_element_type=F32)
        y_ref[pl.ds(r * FF_BLOCKS, FF_BLOCKS)] = ypart.astype(BF16).reshape(FF_BLOCKS, rows, width)
        for cp in out_rows(r):
            cp.start()

    block = width // nh

    def out_block(i):
        at = (slice(None), i) if split_rows else (pl.ds(i * block, block),)
        return [
            pltpu.make_async_copy(ga_ref.at[i], ga_hbm.at[at], drain.at[2, i]),
            pltpu.make_async_copy(gb_ref.at[i], gb_hbm.at[at], drain.at[3, i]),
        ]

    @pl.loop(0, nh)
    def _(i):
        cols = pl.ds(pl.multiple_of(i * block, block), block)
        tn = (((0,), (0,)), ((), ()))
        n = n_ref[:, :, cols].reshape(group, block)
        g_in = lax.dot_general(n, dz[...], tn, preferred_element_type=F32)
        g_down = lax.dot_general(gy[:, cols], mm[...], tn, preferred_element_type=F32)
        both = jnp.concatenate(
            [g_in[:, :off], g_in[:, off:] + g_down[:, : zc - off], g_down[:, zc - off :]], axis=1
        ).astype(BF16)
        for ref, part in ((ga_ref, both[:, :cut]), (gb_ref, both[:, cut:])):
            if split_rows:
                part = part.reshape(nb, block // nb, part.shape[1])
            ref[i] = part
        for cp in out_block(i):
            cp.start()

    @pl.loop(0, nh)
    def _(i):
        for cp in out_block(i):
            cp.wait()

    @pl.loop(0, group // step)
    def _(r):
        for cp in out_rows(r):
            cp.wait()


def ffn(lengths, n2, g, weights, fl, own_rows, cut):
    nh, nb = dims()
    _, rows, width = n2.shape
    group = nh * rows
    total, zc, off = ff_widths(fl)
    split_rows = own_rows % 16 == 0
    lead = (nb, nh, own_rows) if split_rows else (width,)
    held = (nh, nb, own_rows) if split_rows else (nh, width // nh)
    return pl.pallas_call(
        functools.partial(ffn_body, nh, nb, fl, split_rows, cut),
        out_shape=(
            jax.ShapeDtypeStruct(n2.shape, BF16),
            jax.ShapeDtypeStruct(n2.shape, BF16),
            jax.ShapeDtypeStruct(lead + (cut,), BF16),
            jax.ShapeDtypeStruct(lead + (total - cut,), BF16),
        ),
        in_specs=[SM] + [ANY] * 5,
        out_specs=[ANY] * 4,
        scratch_shapes=[
            pltpu.VMEM(n2.shape, BF16),
            pltpu.VMEM(n2.shape, BF16),
            pltpu.VMEM((width, total), BF16),
            pltpu.VMEM(n2.shape, BF16),
            pltpu.VMEM(n2.shape, BF16),
            pltpu.VMEM(held + (cut,), BF16),
            pltpu.VMEM(held + (total - cut,), BF16),
            pltpu.VMEM((group, width), BF16),
            pltpu.VMEM((group, total - off), BF16),
            pltpu.VMEM((group, zc), BF16),
            pltpu.SemaphoreType.DMA((5,)),
            pltpu.SemaphoreType.DMA((4, nh)),
        ],
        name="ffn",
        compiler_params=pltpu.CompilerParams(vmem_limit_bytes=60 << 20),
    )(lengths, n2, g, *weights)


def back_body(nh, nb, hl, io, len_ref, dpart, ypart, hid_ref, g_ref, wo_ref, og_ref, gb_hbm, y_ref, dh_ref, do_in, go_ref, gb_out, n1, f1, o1, n2, f2, o2, dbuf, dg, dots, gb_ref, nearb, s1, s2, gsem, qsem, pb, stage):
    pc = Place(nh, nb, hl)
    h, b = pc.h, pc.b
    mine = pltpu.make_async_copy(gb_hbm.at[:, pc.s], gb_ref, stage)
    mine.start()
    enter_with(pc, lambda zi: (pc.head, zi * pc.qs + pc.from_s))
    pairs = [
        remote(
            gb_hbm.at[:, (pc.s + ds) % pc.qs],
            nearb.at[ds - 1],
            pb.at[0, ds],
            pb.at[1, ds],
            h,
            pc.zi * pc.qs + (pc.s + ds) % pc.qs,
        )
        for ds in range(1, pc.qs)
    ]
    rows, width = hid_ref.shape
    slot = (h * nb + b) * rows + lax.broadcasted_iota(jnp.int32, (rows, 1), 0)
    valid = slot < sequence_ends(len_ref)[-1]
    hds = head_sums(nh, h, b, dpart, (n1, f1, o1), s1)
    hy = HeadSum(nh, h, b, ypart, n2, f2, o2, s2)
    hgs = head_gathers(nh, h, b, dbuf, dg, gsem)
    io.need(1)
    for hd in hds:
        hd.start()
    for cp in pairs:
        cp.start()
    for hd in hds:
        hd.send()
    size = rows // CHUNKS
    io.need(3, 4)
    for j, (hd, hg) in enumerate(zip(hds, hgs)):
        at = pl.ds(j * size, size)
        normed, scale = norm_of(hid_ref[at, :])
        gy = jnp.where(valid[j * size : (j + 1) * size], g_ref[at, :].astype(F32), 0.0)
        dh = gy + norm_pull(hd.total(), normed, scale)
        dh_ref[at, :] = dh
        dbuf[at, :] = dh.astype(BF16)
        hg.start()
    io.put(1)
    io.need(2)
    hy.start()
    for hg in hgs:
        hg.pass_on()
    hy.send()
    for hd, hg in zip(hds, hgs):
        hd.finish()
        hg.finish()
    io.need(5)
    wo = wo_ref[...]
    nt = (((1,), (1,)), ((), ()))
    for i in range(nh):
        part = lax.dot_general(wo, dg[i], nt, preferred_element_type=F32).astype(BF16)
        dots[:, i] = part.reshape(pc.nz, DH, rows)
    grads_out(pc, dots, do_in, qsem, "start")
    total = 0.0
    io.need(6)
    for i in range(nh):
        total = total + jnp.dot(
            og_ref[:, i].reshape(pc.nz * DH, rows), dg[i], preferred_element_type=F32
        )
    go_ref[...] = total.astype(BF16)
    io.put(3)
    y_ref[...] = jnp.where(valid, hid_ref[...] + hy.total(), 0.0)
    io.put(0)
    hy.finish()
    mine.wait()
    for cp in pairs:
        cp.wait()

    @pl.loop(0, pc.nz)
    def _(d):
        others = jnp.sum(nearb[:, d].astype(F32), axis=0)
        gb_out[d] = (gb_ref[d].astype(F32) + others).astype(BF16)

    io.put(4)
    grads_out(pc, dots, do_in, qsem, "wait_send")
    for zi in range(pc.nz):
        wait_on(stretch_lanes(do_in, zi, rows), qsem.at[1, zi])


def back_exchange(lengths, dpart, ypart, hid, g, wo, og, gb):
    nh, nb = dims()
    rows, width = hid.shape
    nz = hl = og.shape[0]
    return comm_call(
        functools.partial(back_body, nh, nb, hl),
        "back_exchange",
        3,
        (
            jax.ShapeDtypeStruct(hid.shape, F32),
            jax.ShapeDtypeStruct(hid.shape, F32),
            jax.ShapeDtypeStruct((nh, DH, nz * rows), BF16),
            jax.ShapeDtypeStruct((nz * DH, width), BF16),
            jax.ShapeDtypeStruct(gb.shape[:1] + gb.shape[2:], BF16),
        ),
        [SM] + [VM] * 6 + [ANY],
        [VM, VM, ANY, VM, VM],
        HeadSum.buffers(nh, rows, width)
        + HeadSum.buffers(nh, rows, width)
        + [
            pltpu.VMEM((rows, width), BF16),
            pltpu.VMEM((nh, rows, width), BF16),
            pltpu.VMEM(og.shape, BF16),
            pltpu.VMEM(gb.shape[:1] + gb.shape[2:], BF16),
            pltpu.VMEM((gb.shape[1] - 1, nz) + gb.shape[2:], BF16),
            chunk_sems(nh),
            HeadSum.sem_shape(nh),
            chunk_sems(nh),
            pltpu.SemaphoreType.DMA((2, nz)),
            pltpu.SemaphoreType.DMA((2, gb.shape[1])),
            pltpu.SemaphoreType.DMA,
        ],
        (lengths, dpart, ypart, hid, g, wo, og, gb),
        vmem=60 << 20,
        late=(1, 3, 4, 2, 5, 6),
        early=(0, 1, 3, 4),
    )


def grads_back_body(nh, nb, hl, io, dq_ref, dkv_ref, cos_ref, sin_ref, n1_hbm, w_hbm, go_ref, gb_ref, gq_ref, dpart, do_ref, gb_sum, got, sums, dq_out, dkv_out, dqkv, n1_ref, w_ref, nearo, sumo, goto, lsem, gotb, bsem, qsem, psem, ksem, stage, po):
    pc = Place(nh, nb, hl)
    loads = [
        pltpu.make_async_copy(n1_hbm, n1_ref, stage.at[0]),
        pltpu.make_async_copy(w_hbm, w_ref, stage.at[1]),
    ]
    for cp in loads:
        cp.start()
    signal_near(pc)
    wait_near(pc)
    rows = dkv_ref.shape[3]
    group = pc.nz * rows
    width = n1_ref.shape[1]
    lw = nh * DH
    count = nh * pc.cb

    def pair(k):
        src = dkv_ref.at[k // pc.cb, :, 2 * (k % pc.cb) + 1 - pc.c]
        return remote(src, got.at[k], psem.at[0, k], psem.at[1, k], pc.sib, pc.b)

    def back(k, act):
        routed(
            pc,
            sums.at[k],
            dkv_out.at[pc.head, pc.u],
            ksem.at[0, k],
            ksem.at[1, pc.head * pc.cb + pc.u],
            k // pc.cb,
            pc.zi * pc.qs + 2 * (k % pc.cb) + pc.c,
            act,
        )

    def queries_back(act):
        for i in range(nh):
            routed(
                pc,
                dq_ref.at[i],
                dq_out.at[pc.head],
                qsem.at[0, i],
                qsem.at[1, pc.head],
                i,
                pc.zi * pc.qs + pc.from_s,
                act,
            )

    pairs_o = [
        remote(
            go_ref.at[:, (pc.s + ds) % pc.qs],
            nearo.at[ds - 1],
            po.at[0, ds],
            po.at[1, ds],
            pc.h,
            pc.zi * pc.qs + (pc.s + ds) % pc.qs,
        )
        for ds in range(1, pc.qs)
    ]
    along_o = StretchSum(pc, sumo, goto, lsem)
    along_b = StretchSum(pc, gb_ref, gotb, bsem)

    io.need(1)

    @pl.loop(0, count)
    def _(k):
        pair(k).start()

    queries_back("start")
    io.need(6, 7)
    for cp in pairs_o:
        cp.start()
    along_b.start()

    @pl.loop(0, count)
    def _(k):
        pair(k).wait_recv()
        mine = dkv_ref[k // pc.cb, :, 2 * (k % pc.cb) + pc.c]
        sums[k] = (mine.astype(F32) + got[k].astype(F32)).astype(BF16)
        back(k, "start")

    for cp in pairs_o:
        cp.wait_recv()
    sumo[...] = (go_ref[:, pc.s].astype(F32) + jnp.sum(nearo[...].astype(F32), axis=0)).astype(BF16)
    along_o.start()
    io.need(2, 3)
    cos, sin = cos_ref[...], -sin_ref[...]
    for l in range(nh):
        wait_on(dq_out.at[l], qsem.at[1, l])
    for p in range(nh // 2):
        q = dq_out[2 * p : 2 * p + 2].reshape(2 * DH, group).astype(F32).T
        dqkv[:, p * 128 : (p + 1) * 128] = turned(q, cos, sin).astype(BF16)
    for l in range(nh):
        for u in range(pc.cb):
            wait_on(dkv_out.at[l, u], ksem.at[1, l * pc.cb + u])
    for p in range(nh // 2):
        even, odd = [
            jnp.sum(dkv_out[2 * p + i].astype(F32), axis=0).reshape(group, 2 * DH)
            for i in range(2)
        ]
        low = lanes_of(even) < DH
        k = jnp.where(low, even, lane_roll(odd, DH)).astype(BF16).astype(F32)
        v = jnp.where(low, lane_roll(even, DH), odd)
        dqkv[:, lw + p * 128 : lw + (p + 1) * 128] = turned(k, cos, sin).astype(BF16)
        dqkv[:, 2 * lw + p * 128 : 2 * lw + (p + 1) * 128] = v.astype(BF16)
    nt = (((1,), (1,)), ((), ()))
    tn = (((0,), (0,)), ((), ()))
    for cp in loads:
        cp.wait()

    @pl.loop(0, nh)
    def _(i):
        cols = pl.ds(pl.multiple_of(i * (width // nh), width // nh), width // nh)
        gq_ref[cols, :] = lax.dot_general(
            n1_ref[:, cols], dqkv[...], tn, preferred_element_type=F32
        ).astype(BF16)

    io.put(0)

    @pl.loop(0, pc.nz)
    def _(i):
        at = pl.ds(pl.multiple_of(i * rows, rows), rows)
        dpart[i] = lax.dot_general(
            dqkv[at, :], w_ref[...], nt, preferred_element_type=F32
        ).astype(BF16)

    io.put(1)

    @pl.loop(0, count)
    def _(k):
        pair(k).wait_send()
        back(k, "wait_send")

    queries_back("wait_send")
    do_ref[...] = along_o.total()
    io.put(2)
    gb_sum[...] = along_b.total().astype(BF16)
    io.put(3)
    along_o.finish()
    along_b.finish()
    for cp in pairs_o:
        cp.wait_send()


def grads_back(dq, dkv, cos, sin, n1, wq, go, gb, hl):
    nh, nb = dims()
    nz, qs = hl, nb // hl
    cb = qs // 2
    rows = dkv.shape[3]
    width = n1.shape[1]
    lw = nh * DH
    dma = pltpu.SemaphoreType.DMA
    return comm_call(
        functools.partial(grads_back_body, nh, nb, hl),
        "grads_back",
        4,
        (
            jax.ShapeDtypeStruct((width, 3 * lw), BF16),
            jax.ShapeDtypeStruct((nz, rows, width), BF16),
            jax.ShapeDtypeStruct(go.shape[2:], F32),
            jax.ShapeDtypeStruct(gb.shape[1:], BF16),
        ),
        [ANY, VM, VM, VM, ANY, ANY, VM, VM],
        [VM] * 4,
        [
            pltpu.VMEM((nh * cb, nz, rows, 2 * DH), BF16),
            pltpu.VMEM((nh * cb, nz, rows, 2 * DH), BF16),
            pltpu.VMEM(dq.shape, BF16),
            pltpu.VMEM((nh, cb, nz, rows, 2 * DH), BF16),
            pltpu.VMEM((nz * rows, 3 * lw), BF16),
            pltpu.VMEM(n1.shape, BF16),
            pltpu.VMEM(wq.shape, BF16),
            pltpu.VMEM((qs - 1, nz) + go.shape[2:], BF16),
            pltpu.VMEM((nz,) + go.shape[2:], BF16),
        ]
        + StretchSum.scratch(nz, go.shape[2:])
        + StretchSum.scratch(nz, gb.shape[1:])
        + [
            dma((2, nh)),
            dma((2, nh * cb)),
            dma((2, nh * cb)),
            dma((2,)),
            dma((2, qs)),
        ],
        (dq, dkv, cos, sin, n1, wq, go, gb),
        vmem=60 << 20,
        late=(1, 6, 7, 2, 3),
        early=(0, 1, 2, 3),
    )


def last_body(nh, nb, hl, io, dpart, gq_ref, gma_ref, gmb_ref, dn_ref, quarters, gma_all, gmb_all, nearq, sumq, farq, totq, sentz, gotz, zsem, pq, fq, cq, msem):
    pc = Place(nh, nb, hl)
    h, b = pc.h, pc.b
    signal_near(pc)
    wait_near(pc)
    nx, nz, qs = nh // 2, pc.nz, pc.qs
    def pair_q(k):
        return remote(
            gq_ref.at[2 * k + 1 - pc.c], nearq.at[k], pq.at[0, k], pq.at[1, k], pc.sib, b
        )

    line = LineSum(pc, lambda d: dpart[d].astype(F32), sentz, gotz, zsem)

    def plane_q(i):
        tx, ts = (pc.x + i // qs) % nx, (pc.s + i % qs) % qs
        return remote(
            sumq.at[tx, :, ts],
            farq.at[pc.x, pc.s],
            fq.at[0, i],
            fq.at[1, i],
            tx * 2 + pc.c,
            pc.zi * qs + ts,
        )

    def quarter(i):
        to = (pc.zi + i) % nz
        return remote(
            totq.at[to], quarters.at[pc.zi], cq.at[0, i], cq.at[1, i], h, to * qs + pc.s
        )

    io.need(1)
    for k in range(nx):
        pair_q(k).start()
    io.need(0)
    line.lead(0)
    moves = []
    for n, (ref, dst) in enumerate(((gma_ref, gma_all), (gmb_ref, gmb_all))):
        for i in range(1, nh):
            th = (h + i) % nh
            moves.append(remote(ref.at[th], dst.at[h], msem.at[0, n, i], msem.at[1, n, i], th, b))
        moves.append(pltpu.make_async_copy(ref.at[h], dst.at[h], msem.at[0, n, 0]))
    for k in range(nx):
        pair_q(k).wait_recv()
        sumq[k] = (gq_ref[2 * k + pc.c].astype(F32) + nearq[k].astype(F32)).astype(BF16)

    @pl.loop(1, nx * qs)
    def _(i):
        plane_q(i).start()

    farq[pc.x, pc.s] = sumq[pc.x, :, pc.s]
    for cp in moves:
        cp.start()
    line.follow(0)
    line.lead(1)

    @pl.loop(1, nx * qs)
    def _(i):
        plane_q(i).wait_recv()

    totq[...] = jnp.sum(
        farq[...].astype(F32).reshape((nx * qs,) + totq.shape), axis=0
    ).astype(BF16)
    for i in range(1, nz):
        quarter(i).start()
    quarters[pc.zi] = totq[pc.zi]
    for j in range(1, nz - 1):
        line.follow(j)
        if j + 1 < nz - 1:
            line.lead(j + 1)
    line.total(dn_ref)
    io.put(0)
    line.finish()
    for i in range(1, nz):
        quarter(i).wait()
    io.put(1)
    for cp in moves:
        cp.wait()
    for k in range(nx):
        pair_q(k).wait_send()

    @pl.loop(1, nx * qs)
    def _(i):
        plane_q(i).wait_send()


def last_exchange(dpart, gq, gma, gmb):
    nh, nb = dims()
    nz, rows, width = dpart.shape
    qs = nb // nz
    own_rows, cols = gq.shape[3:]
    nx = nh // 2
    dma = pltpu.SemaphoreType.DMA
    return comm_call(
        functools.partial(last_body, nh, nb, nz),
        "last_exchange",
        5,
        (
            jax.ShapeDtypeStruct((rows, width), F32),
            jax.ShapeDtypeStruct((nz, own_rows, cols), BF16),
            jax.ShapeDtypeStruct(gma.shape, BF16),
            jax.ShapeDtypeStruct(gmb.shape, BF16),
        ),
        [VM] * 2 + [ANY] * 2,
        [VM] * 2 + [ANY] * 2,
        [
            pltpu.VMEM((nx, nz, qs, own_rows, cols), BF16),
            pltpu.VMEM((nx, nz, qs, own_rows, cols), BF16),
            pltpu.VMEM((nx, qs, nz, own_rows, cols), BF16),
            pltpu.VMEM((nz, own_rows, cols), BF16),
        ]
        + LineSum.scratch(nz, (rows, width))
        + [
            dma((2, nx)),
            dma((2, nx * qs)),
            dma((2, nz)),
            dma((2, 2, nh)),
        ],
        (dpart, gq, gma, gmb),
        vmem=60 << 20,
        late=(1, 0),
        early=(0, 1),
    )


def finish_body(nh, fl, dn_ref, x_ref, dh_ref, y_in, quarters, do_in, gma, gmb, wq_ref, win_ref, ga_ref, gf_ref,
                y_ref, dx_ref, lna_ref, dq_ref, do_ref, lnm_ref, din_ref, dwd_ref):
    y_ref[...] = y_in[...]
    do_ref[...] = do_in[...]
    normed, scale = norm_of(x_ref[...].astype(F32))
    dx_ref[...] = dh_ref[...] + norm_pull(dn_ref[...], normed, scale)
    width = x_ref.shape[1]
    gain = column(ga_ref[...].astype(F32))
    nz = quarters.shape[0]
    rowsum = 0.0
    for c in range(3):
        for l in range(nh):
            src = (c * nh * DH + l // 2 * 128) // 128 * 128
            for p in range(nz // 2):
                tiles = [quarters[2 * p + i, :, src : src + 128].astype(F32) for i in range(2)]
                piece = half_pick(tiles[0], tiles[1], l % 2, l % 2)
                at = c * width + l * nz * DH + p * 128
                dq_ref[:, at : at + 128] = piece * gain
                rowsum = rowsum + jnp.sum(
                    piece * wq_ref[:, at : at + 128].astype(F32), axis=1, keepdims=True
                )
    lna_ref[...] = as_row(rowsum)
    ff = nh * fl
    total, _, _ = ff_widths(fl)
    tiles = lambda v: (v + 127) // 128 * 128
    gate_up, down = 0.0, 0.0
    for i in range(nh):
        piece = jnp.concatenate([gma[i].astype(F32), gmb[i].astype(F32)], axis=1)
        lane = lanes_of(piece)
        gate = widen(jnp.where(lane < fl, piece, 0.0), tiles(2 * ff))
        up = jnp.where(jnp.logical_and(lane >= fl, lane < 2 * fl), piece, 0.0)
        up = widen(up, tiles(2 * ff))
        gate_up = gate_up + lane_roll(gate, i * fl) + lane_roll(up, ff - fl + i * fl)
        dn = jnp.where(jnp.logical_and(lane >= 2 * fl, lane < 3 * fl), piece, 0.0)
        down = down + lane_roll(widen(dn, max(total, tiles(ff))), i * fl - 2 * fl)
    gate_up = gate_up[:, : 2 * ff]
    dwd_ref[...] = down[:, :ff]
    din_ref[...] = gate_up * column(gf_ref[...].astype(F32))
    lnm_ref[...] = as_row(jnp.sum(gate_up * win_ref[...].astype(F32), axis=1, keepdims=True))


def finish(dn, x, dh, y, quarters, d_wout, gma, gmb, w_qkv, w_in, gain_attn, gain_mlp, fl):
    nh, _ = dims()
    rows, width = x.shape
    own_rows = w_qkv.shape[0]
    ff = nh * fl
    f32 = lambda *shape: jax.ShapeDtypeStruct(shape, F32)
    return pl.pallas_call(
        functools.partial(finish_body, nh, fl),
        out_shape=(
            f32(rows, width),
            f32(rows, width),
            f32(1, own_rows),
            f32(own_rows, 3 * width),
            f32(own_rows, width),
            f32(1, own_rows),
            f32(own_rows, 2 * ff),
            f32(own_rows, ff),
        ),
        in_specs=[VM] * 12,
        out_specs=[VM] * 8,
        name="finish",
        compiler_params=pltpu.CompilerParams(vmem_limit_bytes=60 << 20),
    )(dn, x, dh, y, quarters, d_wout, gma, gmb, w_qkv, w_in, gain_attn, gain_mlp)


def shards(layer_input, out_grad, lengths, ln_attn, w_qkv, w_attn_out, ln_mlp, w_in, w_mlp_out):
    nh, nb = dims()
    h, b = me()
    rows, width = layer_input.shape
    heads = width // DH
    hl = heads // nh
    group = nh * rows
    slots = nh * nb * rows
    own_rows = w_qkv.shape[0]
    ff = w_mlp_out.shape[0]
    fl = ff // nh
    nz, qs = hl, nb // hl
    lw = nh * DH

    gain_attn = ln_attn.reshape(1, own_rows)
    gain_mlp = ln_mlp.reshape(1, own_rows)
    n1, wma, wmb, wmc, wq, gg, cos, sin = first_exchange(
        lengths, layer_input, w_qkv, gain_attn, w_in, gain_mlp, w_mlp_out.T, out_grad, hl, fl
    )
    wma = lax.all_gather(wma, "blk", axis=1, tiled=True).reshape(width, -1)
    wq = wq.reshape(width, 3 * lw)
    n1 = n1.reshape(group, width)
    qin, kvin, wo, wmb, wmc = to_heads(n1, wq, cos, sin, w_attn_out[None], wmb, wmc, hl)
    wo = wo.reshape(nz * DH, width)
    kv_all = kvin.reshape(slots, 2 * DH)
    ot, of, lse = attend(lengths, qin, kv_all, 4 * rows, 1024, hl)
    og, hid, n2, wmc = mid_exchange(ot, wo, layer_input, wmc, hl)
    weights = [w.reshape(width, -1) for w in (wma, wmb, wmc)]
    ypart, dpart, gma, gmb = ffn(lengths, n2, gg, weights, fl, own_rows, GRAD_CUT)
    if gma.ndim == 4:
        gma = lax.psum_scatter(gma, "blk", scatter_dimension=0, tiled=True)
        gmb = gmb.reshape((nz, qs) + gmb.shape[1:])
    else:
        gma = gma.reshape(nh, nb * own_rows, gma.shape[1])
        gma = lax.psum_scatter(gma, "blk", scatter_dimension=1, tiled=True)
        gmb = gmb.reshape(nh, nz, qs, own_rows, gmb.shape[1]).transpose(1, 2, 0, 3, 4)
    gma = gma.reshape(nh, own_rows, gma.shape[-1])
    y_out, dh, do_in, go, gmb = back_exchange(
        lengths, dpart, ypart, hid, out_grad, wo, og, gmb
    )
    dq, dkv = attend_grad(lengths, qin, do_in, of, kv_all, lse, 2 * rows, 1024, hl)
    go = go.reshape(nz, qs, own_rows, width)
    gq, dpart1, d_wout, gmb = grads_back(
        dq, dkv.reshape(kvin.shape), cos, sin, n1, wq, go, gmb, hl
    )
    dn, quarters, gma, gmb = last_exchange(
        dpart1, gq.reshape(nh, nz, qs, own_rows, 3 * lw), gma, gmb
    )
    y_out, dx, d_ln_attn, d_wqkv, d_wout, d_ln_mlp, d_win, d_wd = finish(
        dn,
        layer_input,
        dh,
        y_out,
        quarters,
        d_wout,
        gma,
        gmb,
        w_qkv,
        w_in,
        gain_attn,
        gain_mlp,
        fl,
    )
    return (
        y_out,
        dx,
        d_ln_attn.reshape(own_rows),
        d_wqkv,
        d_wout,
        d_ln_mlp.reshape(own_rows),
        d_win,
        d_wd.T,
    )


def solution(mesh):
    both = ("head", "blk")
    row_split = P(both, None)
    return jax.shard_map(
        shards,
        mesh=mesh,
        in_specs=(
            row_split,
            row_split,
            P(),
            P(both),
            row_split,
            row_split,
            P(both),
            row_split,
            P(None, both),
        ),
        out_specs=(
            row_split,
            row_split,
            P(both),
            row_split,
            row_split,
            P(both),
            row_split,
            P(None, both),
        ),
        check_vma=False,
    )
```

```python
import functools
import math

import jax
import jax.numpy as jnp
from jax import lax
from jax.experimental import pallas as pl
from jax.experimental.pallas import tpu as pltpu
from jax.sharding import PartitionSpec as P

DH = 64
ROPE_BASE = 160000.0
NORM_EPS = 1e-05
MASK_FLOOR = -1e30
GRAD_CUT = 1280
FF_BLOCKS = 2
WEIGHT_CUTS = (1280, 1408)
EXP_SCALE = 0.125 * math.log2(math.e)
BF16 = jnp.bfloat16
F32 = jnp.float32
MESH_ID = pl.DeviceIdType.MESH
ANY = pl.BlockSpec(memory_space=pl.ANY)
VM = pl.BlockSpec(memory_space=pltpu.VMEM)
SM = pl.BlockSpec(memory_space=pltpu.SMEM)


def dims():
    nh = lax.axis_size("head")
    nb = lax.axis_size("blk")
    return nh, nb


def me():
    return lax.axis_index("head"), lax.axis_index("blk")


class Staged:
    def __init__(self, loads, drains):
        self.loads, self.drains = loads, drains

    def need(self, *which):
        for i in which:
            self.loads[i].wait()

    def put(self, *which):
        for i in which:
            self.drains[i].start()


def comm_call(body, name, cid, out_shape, in_specs, out_specs, scratch, args, vmem=None, late=(), early=()):
    n_in, n_out, n_late, n_early = len(args), len(out_shape), len(late), len(early)
    in_specs = [ANY if i in late else spec for i, spec in enumerate(in_specs)]
    out_specs = [ANY if i in early else spec for i, spec in enumerate(out_specs)]
    held = [pltpu.VMEM(args[i].shape, args[i].dtype) for i in late]
    held += [pltpu.VMEM(out_shape[i].shape, out_shape[i].dtype) for i in early]
    held.append(pltpu.SemaphoreType.DMA((max(n_late + n_early, 1),)))

    def staged_body(*refs):
        ins, outs = list(refs[:n_in]), list(refs[n_in : n_in + n_out])
        bufs = refs[n_in + n_out : n_in + n_out + n_late + n_early]
        sems = refs[n_in + n_out + n_late + n_early]
        rest = refs[n_in + n_out + n_late + n_early + 1 :]
        loads, drains = {}, {}
        for k, i in enumerate(late):
            loads[i] = pltpu.make_async_copy(ins[i], bufs[k], sems.at[k])
            loads[i].start()
            ins[i] = bufs[k]
        for k, i in enumerate(early):
            k += n_late
            drains[i] = pltpu.make_async_copy(bufs[k], outs[i], sems.at[k])
            outs[i] = bufs[k]
        body(Staged(loads, drains), *ins, *outs, *rest)
        for cp in drains.values():
            cp.wait()

    return pl.pallas_call(
        staged_body,
        out_shape=out_shape,
        in_specs=in_specs,
        out_specs=out_specs,
        scratch_shapes=held + list(scratch),
        name=name,
        compiler_params=pltpu.CompilerParams(
            collective_id=cid, has_side_effects=True, vmem_limit_bytes=vmem
        ),
    )(*args)


def remote(src, dst, send, recv, h, b):
    return pltpu.make_async_remote_copy(
        src_ref=src,
        dst_ref=dst,
        send_sem=send,
        recv_sem=recv,
        device_id=(h, b),
        device_id_type=MESH_ID,
    )


def signal(h, b):
    pl.semaphore_signal(
        pltpu.get_barrier_semaphore(), inc=1, device_id=(h, b), device_id_type=MESH_ID
    )


class HeadGather:
    def __init__(self, nh, h, b, src, dst, sems):
        self.nh, self.h, self.b, self.dst, self.sems = nh, h, b, dst, sems
        nx = nh // 2
        self.nx = nx
        x, c = h // 2, h % 2
        sib = x * 2 + 1 - c
        self.sib = sib
        self.across = []
        for k in range(1, nx):
            self.across.append(
                remote(src, dst.at[h], sems.at[0, k], sems.at[1, k], ((x + k) % nx) * 2 + c, b)
            )
        self.near = remote(src, dst.at[h], sems.at[0, 0], sems.at[1, 0], sib, b)
        self.local = pltpu.make_async_copy(src, dst.at[h], sems.at[2, 0])
        self.forward = []
        for k in range(1, nx):
            got = ((x + nx - k) % nx) * 2 + c
            self.forward.append(
                remote(dst.at[got], dst.at[got], sems.at[2, k], sems.at[3, k], sib, b)
            )

    @staticmethod
    def sem_shape(nh):
        return pltpu.SemaphoreType.DMA((4, nh // 2))

    def start(self):
        for cp in self.across:
            cp.start()
        self.near.start()
        self.local.start()

    def pass_on(self):
        for cp, fw in zip(self.across, self.forward):
            cp.wait_recv()
            fw.start()

    def finish(self):
        for cp in self.across:
            cp.wait_send()
        self.near.wait()
        self.local.wait()
        for fw in self.forward:
            fw.wait()


def lane_roll(values, shift):
    return pltpu.roll(values, shift % values.shape[1], 1)


def lanes_of(values):
    return lax.broadcasted_iota(jnp.int32, (1, values.shape[1]), 1)


def widen(values, width):
    extra = width - values.shape[1]
    if extra <= 0:
        return values[:, :width]
    return jnp.concatenate([values, jnp.zeros((values.shape[0], extra), values.dtype)], axis=1)


def weight_parts(total):
    marks = (0,) + WEIGHT_CUTS + (total,)
    return list(zip(marks[:-1], marks[1:]))


def column(row):
    n = row.shape[1]
    same = lax.broadcasted_iota(jnp.int32, (n, n), 0) == lax.broadcasted_iota(jnp.int32, (n, n), 1)
    return jnp.sum(jnp.where(same, row, 0.0), axis=1, keepdims=True)


def as_row(col):
    n = col.shape[0]
    same = lax.broadcasted_iota(jnp.int32, (n, n), 0) == lax.broadcasted_iota(jnp.int32, (n, n), 1)
    return jnp.sum(jnp.where(same, col, 0.0), axis=0, keepdims=True)


def sequence_ends(len_ref):
    ends, total = [], 0
    for i in range(len_ref.shape[0]):
        total = total + len_ref[i]
        ends.append(total)
    return ends


def segment_first(slot, ends):
    first = jnp.zeros_like(slot)
    for end in ends:
        first = jnp.where(slot >= end, end, first)
    return first


def segment_end(slot, ends, slots):
    last = jnp.zeros_like(slot) + slots
    for end in reversed(ends):
        last = jnp.where(slot < end, end, last)
    return last


def half_pick(low_src, high_src, low_at, high_at):
    low = low_src if low_at == 0 else lane_roll(low_src, DH)
    high = high_src if high_at == 1 else lane_roll(high_src, DH)
    return jnp.where(lanes_of(low) < DH, low, high)


def ff_widths(fl):
    up = lambda v: (v + 127) // 128 * 128
    return up(3 * fl), up(2 * fl), 2 * fl // 128 * 128


class LineGather:
    def __init__(self, pc, src, place, sems):
        self.pc, self.src, self.place, self.sems = pc, src, place, sems

    @staticmethod
    def sem_shape(nz):
        return pltpu.SemaphoreType.DMA((5, nz))

    def origin(self, t, up):
        return self.pc.zi - t if up else self.pc.zi + t

    def move(self, t, up):
        pc = self.pc
        at = self.place(self.origin(t, up))
        n = 0 if up else 2
        return remote(
            self.src if t == 0 else at,
            at,
            self.sems.at[n, t],
            self.sems.at[n + 1, t],
            pc.h,
            pc.b + pc.qs if up else pc.b - pc.qs,
        )

    def sends(self, t, up):
        zi, nz = self.pc.zi, self.pc.nz
        if up:
            return jnp.logical_and(zi - t >= 0, zi + 1 < nz)
        return jnp.logical_and(zi + t < nz, zi - 1 >= 0)

    def local(self):
        return pltpu.make_async_copy(self.src, self.place(self.pc.zi), self.sems.at[4, 0])

    def start(self):
        for up in (True, False):

            @pl.when(self.sends(0, up))
            def _():
                self.move(0, up).start()

        self.local().start()

    def step(self, t, arrived=None):
        low = self.pc.zi < self.pc.nz // 2
        self.take(t, False, jnp.logical_not(low), arrived)
        self.take(t, True, True, arrived)
        self.take(t, False, low, arrived)

    def take(self, t, up, now, arrived):
        zi, nz = self.pc.zi, self.pc.nz
        origin = self.origin(t, up)
        here = jnp.logical_and(now, origin >= 0 if up else origin < nz)

        @pl.when(here)
        def _():
            wait_on(self.place(origin), self.sems.at[1 if up else 3, t - 1])

        if t < nz - 1:

            @pl.when(jnp.logical_and(now, self.sends(t, up)))
            def _():
                self.move(t, up).start()

        if arrived is not None:

            @pl.when(here)
            def _():
                arrived(origin)

    def finish(self):
        self.local().wait()
        for t in range(self.pc.nz - 1):
            for up in (True, False):

                @pl.when(self.sends(t, up))
                def _():
                    self.move(t, up).wait_send()


class BlkGather:
    def __init__(self, pc, src, out, sems, ssem):
        self.pc, self.out, self.ssem, self.src = pc, out, ssem, src
        self.line = LineGather(pc, src, lambda zi: out.at[:, zi, pc.s], sems)

    @staticmethod
    def sem_shapes(nz, qs):
        return [LineGather.sem_shape(nz), pltpu.SemaphoreType.DMA((2, nz, qs))]

    def side(self, zi, ds, own=False):
        pc = self.pc
        ref = self.out.at[:, zi, pc.s]
        return remote(
            self.src if own else ref,
            ref,
            self.ssem.at[0, zi, ds],
            self.ssem.at[1, zi, ds],
            pc.h,
            pc.zi * pc.qs + (pc.s + ds) % pc.qs,
        )

    def spread(self, zi, own=False):
        for ds in range(1, self.pc.qs):
            self.side(zi, ds, own).start()

    def start(self):
        self.line.start()
        self.spread(self.pc.zi, True)

    def step(self, t):
        self.line.step(t, self.spread)

    def finish(self):
        self.line.finish()

        @pl.loop(0, self.pc.nz)
        def _(zi):
            for ds in range(1, self.pc.qs):
                self.side(zi, ds).wait()


class LineSum:
    def __init__(self, pc, term, sent, got, sems):
        self.pc, self.term, self.sent, self.got, self.sems = pc, term, sent, got, sems

    @staticmethod
    def scratch(nz, shape):
        return [
            pltpu.VMEM((2, nz) + shape, BF16),
            pltpu.VMEM((2, nz) + shape, BF16),
            pltpu.SemaphoreType.DMA((4, nz)),
        ]

    def move(self, d, up):
        pc = self.pc
        n = 0 if up else 1
        return remote(
            self.sent.at[n, d],
            self.got.at[n, d],
            self.sems.at[2 * n, d],
            self.sems.at[2 * n + 1, d],
            pc.h,
            pc.b + pc.qs if up else pc.b - pc.qs,
        )

    def takes(self, up):
        return self.pc.zi > 0 if up else self.pc.zi < self.pc.nz - 1

    def lead(self, j):
        self.step(j, False)

    def follow(self, j):
        self.step(j, True)

    def step(self, j, taking):
        low = self.pc.zi < self.pc.nz // 2
        if taking:
            self.one(j, False, jnp.logical_not(low), True)
            self.one(j, True, True, True)
            self.one(j, False, low, True)
        else:
            self.one(j, True, True, False)
            self.one(j, False, True, False)

    def one(self, j, up, now, taking):
        zi, nz = self.pc.zi, self.pc.nz
        d = nz - 1 - j if up else j
        n = 0 if up else 1
        takes = self.takes(up)
        far = jnp.logical_and(now, zi < d if up else zi > d)

        @pl.when(jnp.logical_and(far, takes if taking else jnp.logical_not(takes)))
        def _():
            if taking:
                wait_on(self.got.at[n, d], self.sems.at[2 * n + 1, d])
                self.sent[n, d] = (self.term(d) + self.got[n, d].astype(F32)).astype(BF16)
            else:
                self.sent[n, d] = self.term(d).astype(BF16)
            self.move(d, up).start()

    def total(self, total_ref):
        zi = self.pc.zi
        total_ref[...] = self.term(zi)
        for up in (True, False):
            n = 0 if up else 1

            @pl.when(self.takes(up))
            def _():
                wait_on(self.got.at[n, zi], self.sems.at[2 * n + 1, zi])
                total_ref[...] += self.got[n, zi].astype(F32)

    def finish(self):
        zi, nz = self.pc.zi, self.pc.nz
        for j in range(nz - 1):
            for up in (True, False):
                d = nz - 1 - j if up else j

                @pl.when(zi < d if up else zi > d)
                def _():
                    self.move(d, up).wait_send()


class StretchSum:
    def __init__(self, pc, part, got, sems):
        self.pc, self.part, self.got, self.sems = pc, part, got, sems

    @staticmethod
    def scratch(nz, shape):
        return [pltpu.VMEM((nz,) + shape, BF16), pltpu.SemaphoreType.DMA((2, nz))]

    def move(self, i):
        pc = self.pc
        to = (pc.zi + i) % pc.nz
        return remote(
            self.part.at[to],
            self.got.at[pc.zi],
            self.sems.at[0, i],
            self.sems.at[1, i],
            pc.h,
            to * pc.qs + pc.s,
        )

    def start(self):
        for i in range(1, self.pc.nz):
            self.move(i).start()

    def total(self):
        pc = self.pc
        total = self.part[pc.zi].astype(F32)
        for i in range(1, pc.nz):
            self.move(i).wait_recv()
            total = total + self.got[(pc.zi + pc.nz - i) % pc.nz].astype(F32)
        return total

    def finish(self):
        for i in range(1, self.pc.nz):
            self.move(i).wait_send()


class PlaneWeights:
    def __init__(self, pc, pack, out, sems, ksem):
        self.pc, self.pack, self.out, self.sems, self.ksem = pc, pack, out, sems, ksem

    @staticmethod
    def sem_shapes(nh, nz, qs):
        dma = pltpu.SemaphoreType.DMA
        return [dma((2, nz)), dma((4, nh // 2 * qs))]

    def along(self, i):
        pc = self.pc
        to = (pc.zi + i) % pc.nz
        return remote(
            self.pack.at[to],
            self.out.at[pc.h, pc.zi, pc.s],
            self.sems.at[0, i],
            self.sems.at[1, i],
            pc.h,
            to * pc.qs + pc.s,
        )

    def local(self):
        pc = self.pc
        return pltpu.make_async_copy(
            self.pack.at[pc.zi], self.out.at[pc.h, pc.zi, pc.s], self.sems.at[0, 0]
        )

    def place(self, i, sign):
        pc = self.pc
        nx = pc.nh // 2
        dx, ds = i // pc.qs, i % pc.qs
        if sign < 0:
            dx, ds = nx - dx, pc.qs - ds
        return ((pc.x + dx) % nx) * 2 + pc.c, (pc.s + ds) % pc.qs

    def across(self, i):
        pc = self.pc
        th, ts = self.place(i, 1)
        ref = self.out.at[pc.h, :, pc.s]
        return remote(
            ref, ref, self.ksem.at[0, i], self.ksem.at[1, i], th, pc.zi * pc.qs + ts
        )

    def near(self, i):
        pc = self.pc
        gh, gs = self.place(i, -1)
        ref = self.out.at[gh, :, gs]
        return remote(ref, ref, self.ksem.at[2, i], self.ksem.at[3, i], pc.sib, pc.b)

    def start(self):
        for i in range(1, self.pc.nz):
            self.along(i).start()
        self.local().start()

    def spread(self):
        pc = self.pc
        self.local().wait()
        for i in range(1, pc.nz):
            self.along(i).wait_recv()

        @pl.loop(1, pc.nh // 2 * pc.qs)
        def _(i):
            self.across(i).start()

        self.near(0).start()

    def pass_on(self):
        @pl.loop(1, self.pc.nh // 2 * self.pc.qs)
        def _(i):
            self.across(i).wait_recv()
            self.near(i).start()

    def finish(self):
        for i in range(1, self.pc.nz):
            self.along(i).wait_send()

        @pl.loop(1, self.pc.nh // 2 * self.pc.qs)
        def _(i):
            self.across(i).wait_send()

        @pl.loop(0, self.pc.nh // 2 * self.pc.qs)
        def _(i):
            self.near(i).wait()


def first_body(nh, nb, hl, fl, io, len_ref, x_ref, wq_ref, ga_ref, win_hbm, gf_ref, wd_hbm, g_ref, n1_all, wma, wmb, wmc, wq_all, gg, cos_ref, sin_ref, own_n, pack, wmp, win_ref, wd_ref, lsem, wsem, ksem, gsem, msem, stage):
    pc = Place(nh, nb, hl)
    h, b = pc.h, pc.b
    loads = [
        pltpu.make_async_copy(win_hbm, win_ref, stage.at[0]),
        pltpu.make_async_copy(wd_hbm, wd_ref, stage.at[1]),
    ]
    for cp in loads:
        cp.start()
    signal_near(pc)
    width = x_ref.shape[1]
    lw = width // pc.nz
    gain = column(ga_ref[...].astype(F32))
    io.need(2)
    for c in range(3):
        w = wq_ref[:, c * width : (c + 1) * width].astype(F32) * gain
        tile = lambda l, i: w[:, l * pc.nz * DH + i // 2 * 128 : l * pc.nz * DH + i // 2 * 128 + 128]
        for i in range(pc.nz):
            for p in range(nh // 2):
                both = half_pick(tile(2 * p, i), tile(2 * p + 1, i), i % 2, i % 2)
                at = c * lw + p * 128
                pack[i, :, at : at + 128] = both.astype(BF16)
    io.need(1)
    own_n[...] = norm_of(x_ref[...].astype(F32))[0].astype(BF16)
    wait_near(pc)
    weights = PlaneWeights(pc, pack, wq_all, wsem, ksem)
    line = LineGather(pc, own_n, lambda zi: n1_all.at[zi], lsem)
    gather = HeadGather(nh, h, b, g_ref, gg, gsem)
    weights.start()
    line.start()
    gather.start()
    for cp in loads:
        cp.wait()
    total = ff_widths(fl)[0]
    ff = nh * fl
    win = win_ref[...].astype(F32) * column(gf_ref[...].astype(F32))
    wd = widen(wd_ref[...].astype(F32), total if total > ff else (ff + 127) // 128 * 128)
    lane = lax.broadcasted_iota(jnp.int32, (1, total), 1)
    for i in range(nh):
        gate = widen(lane_roll(win, -i * fl), total)
        up = widen(lane_roll(win, fl - ff - i * fl), total)
        down = widen(lane_roll(wd, 2 * fl - i * fl), total)
        piece = jnp.where(
            lane < fl,
            gate,
            jnp.where(lane < 2 * fl, up, jnp.where(lane < 3 * fl, down, 0.0)),
        )
        wmp[i] = piece.astype(BF16)
    copies = []
    for n, (dst, (begin, end)) in enumerate(zip((wma, wmb, wmc), weight_parts(total))):
        cols = pl.ds(begin, end - begin)
        for i in range(1, nh):
            th = (h + i) % nh
            src = wmp.at[th, :, cols]
            copies.append(remote(src, dst.at[h], msem.at[0, n, i], msem.at[1, n, i], th, b))
        copies.append(pltpu.make_async_copy(wmp.at[h, :, cols], dst.at[h], msem.at[0, n, 0]))
    weights.spread()
    for cp in copies:
        cp.start()
    ends = sequence_ends(len_ref)
    rows = x_ref.shape[0]
    lane = lax.broadcasted_iota(jnp.int32, (1, 2 * DH), 1)
    power = (lane % (DH // 2)).astype(F32) * (-2.0 / DH)
    inv_freq = jnp.exp2(power * math.log2(ROPE_BASE))
    sign = jnp.where(lane % DH < DH // 2, -1.0, 1.0)
    line.step(1)
    for i in range(pc.nz):
        slot = (h * nb + i * pc.qs + pc.s) * rows + lax.broadcasted_iota(jnp.int32, (rows, 1), 0)
        angle = (slot - segment_first(slot, ends)).astype(F32) * inv_freq
        cos_ref[i * rows : (i + 1) * rows, :] = jnp.cos(angle)
        sin_ref[i * rows : (i + 1) * rows, :] = jnp.sin(angle) * sign
    io.put(6, 7)
    gather.pass_on()
    for t in range(2, pc.nz):
        line.step(t)
    weights.pass_on()
    for cp in copies:
        cp.wait()
    weights.finish()
    line.finish()
    gather.finish()


def first_exchange(lengths, x, w_qkv, gain_attn, w_in, gain_mlp, wd_t, g, hl, fl):
    nh, nb = dims()
    rows, width = x.shape
    nz, qs = hl, nb // hl
    lw = width // nz
    own_rows = w_in.shape[0]
    total = ff_widths(fl)[0]
    dma = pltpu.SemaphoreType.DMA
    return comm_call(
        functools.partial(first_body, nh, nb, hl, fl),
        "first_exchange",
        0,
        (
            jax.ShapeDtypeStruct((nz, rows, width), BF16),
            *[
                jax.ShapeDtypeStruct((nh, own_rows, end - begin), BF16)
                for begin, end in weight_parts(total)
            ],
            jax.ShapeDtypeStruct((nh, nz, qs, own_rows, 3 * lw), BF16),
            jax.ShapeDtypeStruct((nh, rows, width), BF16),
            jax.ShapeDtypeStruct((nz * rows, 2 * DH), F32),
            jax.ShapeDtypeStruct((nz * rows, 2 * DH), F32),
        ),
        [SM, VM, VM, VM, ANY, VM, ANY, ANY],
        [ANY] * 6 + [VM] * 2,
        [
            pltpu.VMEM((rows, width), BF16),
            pltpu.VMEM((nz, own_rows, 3 * lw), BF16),
            pltpu.VMEM((nh, own_rows, total), BF16),
            pltpu.VMEM(w_in.shape, BF16),
            pltpu.VMEM(wd_t.shape, BF16),
            LineGather.sem_shape(nz),
        ]
        + PlaneWeights.sem_shapes(nh, nz, qs)
        + [
            HeadGather.sem_shape(nh),
            dma((2, 3, nh)),
            dma((2,)),
        ],
        (lengths, x, w_qkv, gain_attn, w_in, gain_mlp, wd_t, g),
        vmem=60 << 20,
        late=(2, 1),
        early=(6, 7),
    )


class Place:
    def __init__(self, nh, nb, hl):
        h, b = me()
        self.nh, self.nb, self.h, self.b = nh, nb, h, b
        self.x, self.c = h // 2, h % 2
        self.nz = hl
        self.qs = nb // hl
        self.cb = self.qs // 2
        self.sib = self.x * 2 + 1 - self.c
        self.zi, self.s = b // self.qs, b % self.qs
        self.head = self.x * 2 + self.s // self.cb
        self.u = self.s % self.cb
        self.from_s = self.u * 2 + self.c

    def attends(self, zi, l, core, u):
        return (l // 2) * 2 + core, zi * self.qs + (l % 2) * self.cb + u


def signal_near(pc):
    here = pc.nh * pc.qs

    @pl.loop(1, here)
    def _(i):
        signal((pc.h + i // pc.qs) % pc.nh, pc.zi * pc.qs + (pc.s + i % pc.qs) % pc.qs)

    @pl.loop(1, pc.nz)
    def _(i):
        signal(pc.h, (pc.zi + i) % pc.nz * pc.qs + pc.s)


def wait_near(pc, more=0):
    pl.semaphore_wait(pltpu.get_barrier_semaphore(), pc.nh * pc.qs + pc.nz - 2 + more)


def enter_with(pc, source):
    signal_near(pc)
    for i in range(1, pc.nz):
        signal(*source((pc.zi + i) % pc.nz))
    wait_near(pc, pc.nz - 1)


def routed(pc, src, dst, send, recv, th, tb, act):
    mine = jnp.logical_and(th == pc.h, tb == pc.b)

    @pl.when(mine)
    def _():
        if act == "start":
            pltpu.make_async_copy(src, dst, recv).start()

    @pl.when(jnp.logical_not(mine))
    def _():
        cp = remote(src, dst, send, recv, th, tb)
        if act == "start":
            cp.start()
        else:
            cp.wait_send()


def wait_on(ref, sem):
    pltpu.make_async_copy(ref, ref, sem).wait()


def stretch_lanes(ref, zi, rows):
    return ref.at[:, :, pl.ds(pl.multiple_of(zi * rows, rows), rows)]


def outputs_back(pc, o_ref, og, osem, act):
    rows = og.shape[3]
    for zi in range(pc.nz):
        routed(
            pc,
            stretch_lanes(o_ref, zi, rows),
            og.at[pc.zi],
            osem.at[0, zi],
            osem.at[1, pc.zi],
            pc.head,
            zi * pc.qs + pc.from_s,
            act,
        )


def grads_out(pc, dots, do_in, qsem, act):
    rows = dots.shape[3]
    for zi in range(pc.nz):
        th, tb = pc.attends(zi, pc.h, pc.s % 2, pc.s // 2)
        routed(
            pc,
            dots.at[zi],
            stretch_lanes(do_in, pc.zi, rows),
            qsem.at[0, zi],
            qsem.at[1, pc.zi],
            th,
            tb,
            act,
        )


def halves_swapped(tile):
    lane = lanes_of(tile)
    return jnp.where(lane % DH < DH // 2, lane_roll(tile, -(DH // 2)), lane_roll(tile, DH // 2))


def turned(tile, cos, sin):
    return tile * cos + halves_swapped(tile) * sin


def to_heads_body(nh, nb, hl, io, n1_hbm, w_hbm, cos_ref, sin_ref, wo_ref, wmb_ref, wmc_ref, qin, kvin, wo_all, wmb_all, wmc_line, qbuf, kvbuf, n1_ref, w_ref, qsem, ksem, fsem, osem, osem2, bsem, bsem2, csem, stage):
    pc = Place(nh, nb, hl)
    loads = [
        pltpu.make_async_copy(n1_hbm, n1_ref, stage.at[0]),
        pltpu.make_async_copy(w_hbm, w_ref, stage.at[1]),
    ]
    for cp in loads:
        cp.start()
    signal_near(pc)
    rows = kvbuf.shape[2]
    lw = nh * DH
    for cp in loads:
        cp.wait()
    n1 = n1_ref[...]
    io.need(2, 3)
    cos, sin = cos_ref[...], sin_ref[...]
    kk = jnp.dot(n1, w_ref[:, lw : 2 * lw], preferred_element_type=F32)
    vv = jnp.dot(n1, w_ref[:, 2 * lw :], preferred_element_type=F32)
    for p in range(nh // 2):
        k = turned(kk[:, p * 128 : (p + 1) * 128], cos, sin)
        v = vv[:, p * 128 : (p + 1) * 128]
        low = lanes_of(k) < DH
        even = jnp.where(low, k, lane_roll(v, DH)).astype(BF16)
        odd = jnp.where(low, lane_roll(k, DH), v).astype(BF16)
        for i in range(pc.nz):
            kvbuf[2 * p, i] = even[i * rows : (i + 1) * rows]
            kvbuf[2 * p + 1, i] = odd[i * rows : (i + 1) * rows]
    wait_near(pc)

    def keys_out(act):
        for l in range(nh):
            for u in range(pc.cb):
                th, tb = pc.attends(pc.zi, l, pc.s % 2, u)
                routed(
                    pc,
                    kvbuf.at[l],
                    kvin.at[pc.h, :, pc.s],
                    ksem.at[0, l * pc.cb + u],
                    ksem.at[1, pc.h * pc.cb + pc.s // 2],
                    th,
                    tb,
                    act,
                )

    def queries_out(act):
        for l in range(nh):
            th, tb = pc.attends(pc.zi, l, pc.s % 2, pc.s // 2)
            routed(
                pc, qbuf.at[l], qin.at[pc.h], qsem.at[0, l], qsem.at[1, pc.h], th, tb, act
            )

    spread = BlkGather(pc, wo_ref, wo_all, osem, osem2)
    spread_b = BlkGather(pc, wmb_ref, wmb_all, bsem, bsem2)
    line_c = LineGather(pc, wmc_ref, lambda zi: wmc_line.at[:, zi], csem)
    keys_out("start")
    spread.start()
    spread_b.start()
    line_c.start()
    qq = jnp.dot(n1, w_ref[:, :lw], preferred_element_type=F32)
    for p in range(nh // 2):
        q = turned(qq[:, p * 128 : (p + 1) * 128], cos, sin).T.astype(BF16)
        qbuf[2 * p] = q[:DH]
        qbuf[2 * p + 1] = q[DH:]
    queries_out("start")
    count = nh * pc.cb

    def forward(i):
        at = kvin.at[i // pc.cb, :, 2 * (i % pc.cb) + pc.c]
        return remote(at, at, fsem.at[0, i], fsem.at[1, i], pc.sib, pc.b)

    @pl.loop(0, count)
    def _(i):
        wait_on(kvin.at[i // pc.cb, :, 2 * (i % pc.cb) + pc.c], ksem.at[1, i])
        forward(i).start()

    for t in range(1, pc.nz):
        spread.step(t)
        spread_b.step(t)
        line_c.step(t)
    keys_out("wait_send")
    queries_out("wait_send")
    for i in range(nh):
        wait_on(qin.at[i], qsem.at[1, i])

    @pl.loop(0, count)
    def _(i):
        forward(i).wait()

    spread.finish()
    spread_b.finish()
    line_c.finish()


def to_heads(n1, wq, cos, sin, wo, wmb, wmc, hl):
    nh, nb = dims()
    group, width = n1.shape
    nz, qs = hl, nb // hl
    cb = qs // 2
    rows = group // nz
    dma = pltpu.SemaphoreType.DMA
    return comm_call(
        functools.partial(to_heads_body, nh, nb, hl),
        "to_heads",
        1,
        (
            jax.ShapeDtypeStruct((nh, DH, group), BF16),
            jax.ShapeDtypeStruct((nh, nz, qs, rows, 2 * DH), BF16),
            jax.ShapeDtypeStruct((1, nz, qs) + wo.shape[1:], BF16),
            jax.ShapeDtypeStruct((nh, nz, qs) + wmb.shape[1:], BF16),
            jax.ShapeDtypeStruct((nh, nz) + wmc.shape[1:], BF16),
        ),
        [ANY, ANY, VM, VM, ANY, ANY, ANY],
        [ANY] * 5,
        [
            pltpu.VMEM((nh, DH, group), BF16),
            pltpu.VMEM((nh, nz, rows, 2 * DH), BF16),
            pltpu.VMEM(n1.shape, BF16),
            pltpu.VMEM(wq.shape, BF16),
            dma((2, nh)),
            dma((2, nh * cb)),
            dma((2, nh * cb)),
        ]
        + BlkGather.sem_shapes(nz, qs) * 2
        + [LineGather.sem_shape(nz), dma((2,))],
        (n1, wq, cos, sin, wo, wmb, wmc),
        vmem=60 << 20,
        late=(2, 3),
    )


class Queries:
    def __init__(self, nh, nb, hl, len_ref, lanes, slots, size):
        pc = Place(nh, nb, hl)
        tile = pl.program_id(0)
        rows = slots // (nh * nb)
        count = lanes // rows
        each = pc.nz // count
        ends = sequence_ends(len_ref)
        base = (tile // each) * nb + (tile % each) * count * pc.qs + pc.from_s
        lane = lax.broadcasted_iota(jnp.int32, (1, lanes), 1)
        slot = (base + lane // rows * pc.qs) * rows + lane % rows
        self.first = segment_first(slot, ends)
        self.last = segment_end(slot, ends, slots)
        near = base * rows
        far = (base + (count - 1) * pc.qs) * rows + rows - 1
        self.size = size
        self.lo = segment_first(near, ends) // size
        self.hi = (segment_end(far, ends, slots) + size - 1) // size
        self.open = jnp.minimum((segment_first(far, ends) + size - 1) // size, self.hi)
        self.close = jnp.maximum(segment_end(near, ends, slots) // size, self.open)
        self.lanes = lanes

    def allowed(self, block_at):
        at = block_at * self.size + lax.broadcasted_iota(jnp.int32, (self.size, self.lanes), 0)
        return jnp.logical_and(at >= self.first, at < self.last)

    def walk(self, step, carry):
        masked = lambda j, kept: step(j, kept, True)
        carry = lax.fori_loop(self.lo, self.open, masked, carry)
        carry = lax.fori_loop(self.open, self.close, lambda j, kept: step(j, kept, False), carry)
        return lax.fori_loop(self.close, self.hi, masked, carry)


def attend_body(nh, nb, hl, size, len_ref, q_ref, kv_ref, o_ref, of_ref, lse_ref):
    q = q_ref[0]
    lanes = q.shape[1]
    at = Queries(nh, nb, hl, len_ref, lanes, kv_ref.shape[0], size)
    q_pad = jnp.concatenate([q, jnp.zeros_like(q)], axis=0)
    is_key = lax.broadcasted_iota(jnp.int32, (1, 2 * DH), 1) < DH

    def step(j, carry, masked):
        top, acc = carry
        kv = kv_ref[pl.ds(pl.multiple_of(j * size, size), size), :]
        s = jnp.dot(kv, q_pad, preferred_element_type=F32)
        if masked:
            s = jnp.where(at.allowed(j), s, MASK_FLOOR)
        new_top = jnp.maximum(top, jnp.max(s, axis=0, keepdims=True))
        p = jnp.exp2((s - new_top) * EXP_SCALE).astype(BF16)
        alpha = jnp.exp2((top - new_top) * EXP_SCALE)
        ones_values = jnp.where(is_key, jnp.ones_like(kv), kv)
        acc = acc * alpha + lax.dot_general(
            ones_values, p, (((0,), (0,)), ((), ())), preferred_element_type=F32
        )
        return new_top, acc

    top, acc = at.walk(
        step, (jnp.full((1, lanes), MASK_FLOOR, F32), jnp.zeros((2 * DH, lanes), F32))
    )
    total = acc[:1]
    o = acc[DH:] / total
    of_ref[0] = o
    o_ref[0] = o.astype(BF16)
    lse_ref[0] = top * EXP_SCALE + jnp.log2(total)


def attend_specs(kv_rows, lanes, tiles_each):
    tile_spec = pl.BlockSpec((1, DH, lanes), lambda i, *_: (i // tiles_each, 0, i % tiles_each))
    row_spec = pl.BlockSpec((1, 1, lanes), lambda i, *_: (i, 0, 0))
    kv_spec = pl.BlockSpec((kv_rows, 2 * DH), lambda i, *_: (0, 0))
    return tile_spec, row_spec, kv_spec


def attend(lengths, q, kv, lanes, size, hl):
    nh, nb = dims()
    each = q.shape[2] // lanes
    tiles = q.shape[0] * each
    tile_spec, row_spec, kv_spec = attend_specs(kv.shape[0], lanes, each)
    return pl.pallas_call(
        functools.partial(attend_body, nh, nb, hl, size),
        grid_spec=pltpu.PrefetchScalarGridSpec(
            num_scalar_prefetch=1,
            grid=(tiles,),
            in_specs=[tile_spec, kv_spec],
            out_specs=[tile_spec, tile_spec, row_spec],
        ),
        out_shape=(
            jax.ShapeDtypeStruct(q.shape, BF16),
            jax.ShapeDtypeStruct(q.shape, F32),
            jax.ShapeDtypeStruct((tiles, 1, lanes), F32),
        ),
        name="attend",
        compiler_params=pltpu.CompilerParams(vmem_limit_bytes=60 << 20),
    )(lengths, q, kv)


def attend_grad_body(nh, nb, hl, size, len_ref, q_ref, do_ref, of_ref, kv_ref, lse_ref, dq_ref, dkv_ref, acc_ref):
    tile = pl.program_id(0)

    @pl.when(tile == 0)
    def _():
        acc_ref[...] = jnp.zeros_like(acc_ref)

    q = q_ref[0]
    do = do_ref[0]
    lanes = q.shape[1]
    place = Queries(nh, nb, hl, len_ref, lanes, kv_ref.shape[0], size)
    zero = jnp.zeros_like(q)
    both = jnp.concatenate(
        [jnp.concatenate([q, zero], axis=0), jnp.concatenate([zero, do], axis=0)], axis=1
    )
    delta = jnp.sum(do.astype(F32) * of_ref[0], axis=0, keepdims=True)
    lse = lse_ref[0]

    def step(j, dq, masked):
        at = pl.ds(pl.multiple_of(j * size, size), size)
        kv = kv_ref[at, :]
        sd = jnp.dot(kv, both, preferred_element_type=F32)
        s, dp = sd[:, :lanes], sd[:, lanes:]
        power = s * EXP_SCALE - lse
        if masked:
            power = jnp.where(place.allowed(j), power, MASK_FLOOR)
        p = jnp.exp2(power)
        ds = (p * (dp - delta)).astype(BF16)
        acc_ref[at, :] += lax.dot_general(
            jnp.concatenate([ds, p.astype(BF16)], axis=1),
            both,
            (((1,), (1,)), ((), ())),
            preferred_element_type=F32,
        )
        return dq + lax.dot_general(
            kv, ds, (((0,), (0,)), ((), ())), preferred_element_type=F32
        )

    dq = place.walk(step, jnp.zeros((2 * DH, lanes), F32))
    dq_ref[0] = (dq[:DH] * 0.125).astype(BF16)

    @pl.when(tile == pl.num_programs(0) - 1)
    def _():
        lane = lax.broadcasted_iota(jnp.int32, (1, 2 * DH), 1)
        dkv_ref[...] = (acc_ref[...] * jnp.where(lane < DH, 0.125, 1.0)).astype(BF16)


def attend_grad(lengths, q, do, of, kv, lse, lanes, size, hl):
    nh, nb = dims()
    tiles = lse.size // lanes
    lse = lse.reshape(tiles, 1, lanes)
    tile_spec, row_spec, kv_spec = attend_specs(kv.shape[0], lanes, tiles // q.shape[0])
    return pl.pallas_call(
        functools.partial(attend_grad_body, nh, nb, hl, size),
        grid_spec=pltpu.PrefetchScalarGridSpec(
            num_scalar_prefetch=1,
            grid=(tiles,),
            in_specs=[tile_spec, tile_spec, tile_spec, kv_spec, row_spec],
            out_specs=[tile_spec, kv_spec],
            scratch_shapes=[pltpu.VMEM(kv.shape, F32)],
        ),
        out_shape=(jax.ShapeDtypeStruct(q.shape, BF16), jax.ShapeDtypeStruct(kv.shape, BF16)),
        name="attend_grad",
        compiler_params=pltpu.CompilerParams(vmem_limit_bytes=60 << 20),
    )(lengths, q, do, of, kv, lse)


class HeadSum:
    def __init__(self, nh, h, b, part, near, far, out, sems):
        self.nx = nh // 2
        self.x, self.c = h // 2, h % 2
        self.h, self.part, self.near, self.far, self.out = h, part, near, far, out
        sib = self.x * 2 + 1 - self.c
        self.pairs = [
            remote(
                part.at[((self.x + k) % self.nx) * 2 + 1 - self.c],
                near.at[k],
                sems.at[0, k],
                sems.at[1, k],
                sib,
                b,
            )
            for k in range(self.nx)
        ]
        self.across = [
            remote(
                out.at[k],
                far.at[k],
                sems.at[2, k],
                sems.at[3, k],
                ((self.x + k) % self.nx) * 2 + self.c,
                b,
            )
            for k in range(1, self.nx)
        ]

    @staticmethod
    def sem_shape(nh):
        return pltpu.SemaphoreType.DMA((4, nh // 2))

    @staticmethod
    def buffers(nh, rows, width):
        return [pltpu.VMEM((nh // 2, rows, width), BF16)] * 3

    def start(self):
        for k in list(range(1, self.nx)) + [0]:
            self.pairs[k].start()

    def send(self):
        for k in range(1, self.nx):
            self.pairs[k].wait_recv()
            at = ((self.x + k) % self.nx) * 2 + self.c
            self.out[k] = (self.part[at].astype(F32) + self.near[k].astype(F32)).astype(BF16)
            self.across[k - 1].start()

    def total(self):
        self.pairs[0].wait_recv()
        total = self.part[self.h].astype(F32) + self.near[0].astype(F32)
        for k in range(1, self.nx):
            self.across[k - 1].wait_recv()
            total = total + self.far[k].astype(F32)
        return total

    def finish(self):
        for cp in self.pairs:
            cp.wait_send()
        for cp in self.across:
            cp.wait_send()


def norm_of(values):
    centre = values - jnp.mean(values, axis=-1, keepdims=True)
    scale = lax.rsqrt(jnp.mean(centre * centre, axis=-1, keepdims=True) + NORM_EPS)
    return centre * scale, scale


def norm_pull(grad, normed, scale):
    one = jnp.mean(grad, axis=-1, keepdims=True)
    two = jnp.mean(grad * normed, axis=-1, keepdims=True)
    return scale * (grad - one - normed * two)


CHUNKS = 2


def chunk_of(ref, j, axis):
    size = ref.shape[axis] // CHUNKS
    at = pl.ds(j * size, size)
    return ref.at[at] if axis == 0 else ref.at[:, at]


def head_sums(nh, h, b, part, bufs, sems):
    near, far, out = bufs
    return [
        HeadSum(
            nh,
            h,
            b,
            chunk_of(part, j, 1),
            chunk_of(near, j, 1),
            chunk_of(far, j, 1),
            chunk_of(out, j, 1),
            sems.at[j],
        )
        for j in range(CHUNKS)
    ]


def head_gathers(nh, h, b, src, dst, sems):
    return [
        HeadGather(nh, h, b, chunk_of(src, j, 0), chunk_of(dst, j, 1), sems.at[j])
        for j in range(CHUNKS)
    ]


def chunk_sems(nh):
    return pltpu.SemaphoreType.DMA((CHUNKS, 4, nh // 2))


def mid_body(nh, nb, hl, io, o_ref, wo_ref, x_ref, wmb_ref, og, hid_ref, ng_ref, wmb_all, part, near, far, out, nbuf, osem, ssem, gsem, wsem):
    pc = Place(nh, nb, hl)
    h, b = pc.h, pc.b
    enter_with(pc, lambda zi: pc.attends(zi, h, pc.s % 2, pc.s // 2))
    rows, width = x_ref.shape
    outputs_back(pc, o_ref, og, osem, "start")
    sides = [
        remote(
            wmb_ref,
            wmb_all.at[:, :, pc.s],
            wsem.at[0, ds],
            wsem.at[1, ds],
            h,
            pc.zi * pc.qs + (pc.s + ds) % pc.qs,
        )
        for ds in range(1, pc.qs)
    ]
    sides.append(pltpu.make_async_copy(wmb_ref, wmb_all.at[:, :, pc.s], wsem.at[0, 0]))
    for cp in sides:
        cp.start()
    outputs_back(pc, o_ref, og, osem, "wait_send")
    for zi in range(pc.nz):
        wait_on(og.at[zi], osem.at[1, zi])
    io.put(0)
    io.need(1)
    wo = wo_ref[...]
    for i in range(nh):
        part[i] = lax.dot_general(
            og[:, i].reshape(pc.nz * DH, rows),
            wo,
            (((0,), (0,)), ((), ())),
            preferred_element_type=F32,
        ).astype(BF16)
    hss = head_sums(nh, h, b, part, (near, far, out), ssem)
    hgs = head_gathers(nh, h, b, nbuf, ng_ref, gsem)
    for hs in hss:
        hs.start()
    for hs in hss:
        hs.send()
    size = rows // CHUNKS
    io.need(2)
    for j, (hs, hg) in enumerate(zip(hss, hgs)):
        at = pl.ds(j * size, size)
        hid = x_ref[at, :].astype(F32) + hs.total()
        hid_ref[at, :] = hid
        nbuf[at, :] = norm_of(hid)[0].astype(BF16)
        hg.start()
    io.put(1)
    for hg in hgs:
        hg.pass_on()
    for hs, hg in zip(hss, hgs):
        hs.finish()
        hg.finish()
    for cp in sides:
        cp.wait()


def mid_exchange(ot, wo, x, wmb, hl):
    nh, nb = dims()
    rows, width = x.shape
    nz = hl
    return comm_call(
        functools.partial(mid_body, nh, nb, hl),
        "mid_exchange",
        2,
        (
            jax.ShapeDtypeStruct((nz, nh, DH, rows), BF16),
            jax.ShapeDtypeStruct(x.shape, F32),
            jax.ShapeDtypeStruct((nh, rows, width), BF16),
            jax.ShapeDtypeStruct((nh, nz, nb // nz) + wmb.shape[2:], BF16),
        ),
        [ANY] * 4,
        [ANY] * 4,
        [pltpu.VMEM((nh, rows, width), BF16)]
        + HeadSum.buffers(nh, rows, width)
        + [
            pltpu.VMEM((rows, width), BF16),
            pltpu.SemaphoreType.DMA((2, nz)),
            chunk_sems(nh),
            chunk_sems(nh),
            pltpu.SemaphoreType.DMA((2, nb // nz)),
        ],
        (ot, wo, x, wmb),
        vmem=60 << 20,
        late=(1, 2),
        early=(0, 1),
    )


def ffn_body(nh, nb, fl, split_rows, cut, len_ref, n_hbm, g_hbm, wa_hbm, wb_hbm, wc_hbm, y_hbm, d_hbm, ga_hbm, gb_hbm, n_ref, g_ref, w_ref, y_ref, d_ref, ga_ref, gb_ref, gy, mm, dz, stage, drain):
    rows, width = n_ref.shape[1], n_ref.shape[2]
    group = nh * rows
    total, zc, off = ff_widths(fl)
    wide = total - off
    shift = 2 * fl - off
    step = FF_BLOCKS * rows
    lane = lax.broadcasted_iota(jnp.int32, (1, wide), 1)
    real = lane < fl
    valid = sequence_ends(len_ref)[-1]
    blk = lax.axis_index("blk")
    loads = [
        pltpu.make_async_copy(n_hbm, n_ref, stage.at[0]),
        pltpu.make_async_copy(g_hbm, g_ref, stage.at[1]),
    ]
    for n, (w, (begin, end)) in enumerate(zip((wa_hbm, wb_hbm, wc_hbm), weight_parts(total))):
        dst = w_ref.at[:, pl.ds(begin, end - begin)]
        loads.append(pltpu.make_async_copy(w, dst, stage.at[2 + n]))
    for cp in loads:
        cp.start()
    for cp in loads:
        cp.wait()

    def out_rows(r):
        at = pl.ds(r * FF_BLOCKS, FF_BLOCKS)
        return [
            pltpu.make_async_copy(d_ref.at[at], d_hbm.at[at], drain.at[0, r]),
            pltpu.make_async_copy(y_ref.at[at], y_hbm.at[at], drain.at[1, r]),
        ]

    @pl.loop(0, group // step)
    def _(r):
        at = pl.ds(pl.multiple_of(r * step, step), step)
        n = n_ref[pl.ds(r * FF_BLOCKS, FF_BLOCKS)].reshape(step, width)
        row = lax.broadcasted_iota(jnp.int32, (step, 1), 0)
        slot = ((r * FF_BLOCKS + row // rows) * nb + blk) * rows + row % rows
        g = g_ref[pl.ds(r * FF_BLOCKS, FF_BLOCKS)].reshape(step, width)
        g = jnp.where(slot < valid, g.astype(F32), 0.0).astype(BF16)
        gy[at, :] = g
        z = jnp.dot(n, w_ref[:, :zc], preferred_element_type=F32)
        dm = lane_roll(jnp.dot(g, w_ref[:, off:], preferred_element_type=F32), -shift)
        gate, up = z[:, :wide], lane_roll(z, -fl)[:, :wide]
        cdf = 0.5 * (1.0 + lax.erf(gate * math.sqrt(0.5)))
        act = gate * cdf
        slope = cdf + gate * jnp.exp(-0.5 * gate * gate) * (1.0 / math.sqrt(2.0 * math.pi))
        m = lane_roll(jnp.where(real, act * up, 0.0), shift).astype(BF16)
        mm[at, :] = m
        d_gate = widen(jnp.where(real, dm * up * slope, 0.0), zc)
        d_up = lane_roll(widen(jnp.where(real, dm * act, 0.0), zc), fl)
        d = (d_gate + d_up).astype(BF16)
        dz[at, :] = d
        nt = (((1,), (1,)), ((), ()))
        dpart = lax.dot_general(d, w_ref[:, :zc], nt, preferred_element_type=F32)
        d_ref[pl.ds(r * FF_BLOCKS, FF_BLOCKS)] = dpart.astype(BF16).reshape(FF_BLOCKS, rows, width)
        ypart = lax.dot_general(m, w_ref[:, off:], nt, preferred_element_type=F32)
        y_ref[pl.ds(r * FF_BLOCKS, FF_BLOCKS)] = ypart.astype(BF16).reshape(FF_BLOCKS, rows, width)
        for cp in out_rows(r):
            cp.start()

    block = width // nh

    def out_block(i):
        at = (slice(None), i) if split_rows else (pl.ds(i * block, block),)
        return [
            pltpu.make_async_copy(ga_ref.at[i], ga_hbm.at[at], drain.at[2, i]),
            pltpu.make_async_copy(gb_ref.at[i], gb_hbm.at[at], drain.at[3, i]),
        ]

    @pl.loop(0, nh)
    def _(i):
        cols = pl.ds(pl.multiple_of(i * block, block), block)
        tn = (((0,), (0,)), ((), ()))
        n = n_ref[:, :, cols].reshape(group, block)
        g_in = lax.dot_general(n, dz[...], tn, preferred_element_type=F32)
        g_down = lax.dot_general(gy[:, cols], mm[...], tn, preferred_element_type=F32)
        both = jnp.concatenate(
            [g_in[:, :off], g_in[:, off:] + g_down[:, : zc - off], g_down[:, zc - off :]], axis=1
        ).astype(BF16)
        for ref, part in ((ga_ref, both[:, :cut]), (gb_ref, both[:, cut:])):
            if split_rows:
                part = part.reshape(nb, block // nb, part.shape[1])
            ref[i] = part
        for cp in out_block(i):
            cp.start()

    @pl.loop(0, nh)
    def _(i):
        for cp in out_block(i):
            cp.wait()

    @pl.loop(0, group // step)
    def _(r):
        for cp in out_rows(r):
            cp.wait()


def ffn(lengths, n2, g, weights, fl, own_rows, cut):
    nh, nb = dims()
    _, rows, width = n2.shape
    group = nh * rows
    total, zc, off = ff_widths(fl)
    split_rows = own_rows % 16 == 0
    lead = (nb, nh, own_rows) if split_rows else (width,)
    held = (nh, nb, own_rows) if split_rows else (nh, width // nh)
    return pl.pallas_call(
        functools.partial(ffn_body, nh, nb, fl, split_rows, cut),
        out_shape=(
            jax.ShapeDtypeStruct(n2.shape, BF16),
            jax.ShapeDtypeStruct(n2.shape, BF16),
            jax.ShapeDtypeStruct(lead + (cut,), BF16),
            jax.ShapeDtypeStruct(lead + (total - cut,), BF16),
        ),
        in_specs=[SM] + [ANY] * 5,
        out_specs=[ANY] * 4,
        scratch_shapes=[
            pltpu.VMEM(n2.shape, BF16),
            pltpu.VMEM(n2.shape, BF16),
            pltpu.VMEM((width, total), BF16),
            pltpu.VMEM(n2.shape, BF16),
            pltpu.VMEM(n2.shape, BF16),
            pltpu.VMEM(held + (cut,), BF16),
            pltpu.VMEM(held + (total - cut,), BF16),
            pltpu.VMEM((group, width), BF16),
            pltpu.VMEM((group, total - off), BF16),
            pltpu.VMEM((group, zc), BF16),
            pltpu.SemaphoreType.DMA((5,)),
            pltpu.SemaphoreType.DMA((4, nh)),
        ],
        name="ffn",
        compiler_params=pltpu.CompilerParams(vmem_limit_bytes=60 << 20),
    )(lengths, n2, g, *weights)


def back_body(nh, nb, hl, io, len_ref, dpart, ypart, hid_ref, g_ref, wo_ref, og_ref, gb_hbm, y_ref, dh_ref, do_in, go_ref, gb_out, n1, f1, o1, n2, f2, o2, dbuf, dg, dots, gb_ref, nearb, s1, s2, gsem, qsem, pb, stage):
    pc = Place(nh, nb, hl)
    h, b = pc.h, pc.b
    mine = pltpu.make_async_copy(gb_hbm.at[:, pc.s], gb_ref, stage)
    mine.start()
    enter_with(pc, lambda zi: (pc.head, zi * pc.qs + pc.from_s))
    pairs = [
        remote(
            gb_hbm.at[:, (pc.s + ds) % pc.qs],
            nearb.at[ds - 1],
            pb.at[0, ds],
            pb.at[1, ds],
            h,
            pc.zi * pc.qs + (pc.s + ds) % pc.qs,
        )
        for ds in range(1, pc.qs)
    ]
    rows, width = hid_ref.shape
    slot = (h * nb + b) * rows + lax.broadcasted_iota(jnp.int32, (rows, 1), 0)
    valid = slot < sequence_ends(len_ref)[-1]
    hds = head_sums(nh, h, b, dpart, (n1, f1, o1), s1)
    hy = HeadSum(nh, h, b, ypart, n2, f2, o2, s2)
    hgs = head_gathers(nh, h, b, dbuf, dg, gsem)
    io.need(1)
    for hd in hds:
        hd.start()
    for cp in pairs:
        cp.start()
    for hd in hds:
        hd.send()
    size = rows // CHUNKS
    io.need(3, 4)
    for j, (hd, hg) in enumerate(zip(hds, hgs)):
        at = pl.ds(j * size, size)
        normed, scale = norm_of(hid_ref[at, :])
        gy = jnp.where(valid[j * size : (j + 1) * size], g_ref[at, :].astype(F32), 0.0)
        dh = gy + norm_pull(hd.total(), normed, scale)
        dh_ref[at, :] = dh
        dbuf[at, :] = dh.astype(BF16)
        hg.start()
    io.put(1)
    io.need(2)
    hy.start()
    for hg in hgs:
        hg.pass_on()
    hy.send()
    for hd, hg in zip(hds, hgs):
        hd.finish()
        hg.finish()
    io.need(5)
    wo = wo_ref[...]
    nt = (((1,), (1,)), ((), ()))
    for i in range(nh):
        part = lax.dot_general(wo, dg[i], nt, preferred_element_type=F32).astype(BF16)
        dots[:, i] = part.reshape(pc.nz, DH, rows)
    grads_out(pc, dots, do_in, qsem, "start")
    total = 0.0
    io.need(6)
    for i in range(nh):
        total = total + jnp.dot(
            og_ref[:, i].reshape(pc.nz * DH, rows), dg[i], preferred_element_type=F32
        )
    go_ref[...] = total.astype(BF16)
    io.put(3)
    y_ref[...] = jnp.where(valid, hid_ref[...] + hy.total(), 0.0)
    io.put(0)
    hy.finish()
    mine.wait()
    for cp in pairs:
        cp.wait()

    @pl.loop(0, pc.nz)
    def _(d):
        others = jnp.sum(nearb[:, d].astype(F32), axis=0)
        gb_out[d] = (gb_ref[d].astype(F32) + others).astype(BF16)

    io.put(4)
    grads_out(pc, dots, do_in, qsem, "wait_send")
    for zi in range(pc.nz):
        wait_on(stretch_lanes(do_in, zi, rows), qsem.at[1, zi])


def back_exchange(lengths, dpart, ypart, hid, g, wo, og, gb):
    nh, nb = dims()
    rows, width = hid.shape
    nz = hl = og.shape[0]
    return comm_call(
        functools.partial(back_body, nh, nb, hl),
        "back_exchange",
        3,
        (
            jax.ShapeDtypeStruct(hid.shape, F32),
            jax.ShapeDtypeStruct(hid.shape, F32),
            jax.ShapeDtypeStruct((nh, DH, nz * rows), BF16),
            jax.ShapeDtypeStruct((nz * DH, width), BF16),
            jax.ShapeDtypeStruct(gb.shape[:1] + gb.shape[2:], BF16),
        ),
        [SM] + [VM] * 6 + [ANY],
        [VM, VM, ANY, VM, VM],
        HeadSum.buffers(nh, rows, width)
        + HeadSum.buffers(nh, rows, width)
        + [
            pltpu.VMEM((rows, width), BF16),
            pltpu.VMEM((nh, rows, width), BF16),
            pltpu.VMEM(og.shape, BF16),
            pltpu.VMEM(gb.shape[:1] + gb.shape[2:], BF16),
            pltpu.VMEM((gb.shape[1] - 1, nz) + gb.shape[2:], BF16),
            chunk_sems(nh),
            HeadSum.sem_shape(nh),
            chunk_sems(nh),
            pltpu.SemaphoreType.DMA((2, nz)),
            pltpu.SemaphoreType.DMA((2, gb.shape[1])),
            pltpu.SemaphoreType.DMA,
        ],
        (lengths, dpart, ypart, hid, g, wo, og, gb),
        vmem=60 << 20,
        late=(1, 3, 4, 2, 5, 6),
        early=(0, 1, 3, 4),
    )


def grads_back_body(nh, nb, hl, io, dq_ref, dkv_ref, cos_ref, sin_ref, n1_hbm, w_hbm, go_ref, gb_ref, gq_ref, dpart, do_ref, gb_sum, got, sums, dq_out, dkv_out, dqkv, n1_ref, w_ref, nearo, sumo, goto, lsem, gotb, bsem, qsem, psem, ksem, stage, po):
    pc = Place(nh, nb, hl)
    loads = [
        pltpu.make_async_copy(n1_hbm, n1_ref, stage.at[0]),
        pltpu.make_async_copy(w_hbm, w_ref, stage.at[1]),
    ]
    for cp in loads:
        cp.start()
    signal_near(pc)
    wait_near(pc)
    rows = dkv_ref.shape[3]
    group = pc.nz * rows
    width = n1_ref.shape[1]
    lw = nh * DH
    count = nh * pc.cb

    def pair(k):
        src = dkv_ref.at[k // pc.cb, :, 2 * (k % pc.cb) + 1 - pc.c]
        return remote(src, got.at[k], psem.at[0, k], psem.at[1, k], pc.sib, pc.b)

    def back(k, act):
        routed(
            pc,
            sums.at[k],
            dkv_out.at[pc.head, pc.u],
            ksem.at[0, k],
            ksem.at[1, pc.head * pc.cb + pc.u],
            k // pc.cb,
            pc.zi * pc.qs + 2 * (k % pc.cb) + pc.c,
            act,
        )

    def queries_back(act):
        for i in range(nh):
            routed(
                pc,
                dq_ref.at[i],
                dq_out.at[pc.head],
                qsem.at[0, i],
                qsem.at[1, pc.head],
                i,
                pc.zi * pc.qs + pc.from_s,
                act,
            )

    pairs_o = [
        remote(
            go_ref.at[:, (pc.s + ds) % pc.qs],
            nearo.at[ds - 1],
            po.at[0, ds],
            po.at[1, ds],
            pc.h,
            pc.zi * pc.qs + (pc.s + ds) % pc.qs,
        )
        for ds in range(1, pc.qs)
    ]
    along_o = StretchSum(pc, sumo, goto, lsem)
    along_b = StretchSum(pc, gb_ref, gotb, bsem)

    io.need(1)

    @pl.loop(0, count)
    def _(k):
        pair(k).start()

    queries_back("start")
    io.need(6, 7)
    for cp in pairs_o:
        cp.start()
    along_b.start()

    @pl.loop(0, count)
    def _(k):
        pair(k).wait_recv()
        mine = dkv_ref[k // pc.cb, :, 2 * (k % pc.cb) + pc.c]
        sums[k] = (mine.astype(F32) + got[k].astype(F32)).astype(BF16)
        back(k, "start")

    for cp in pairs_o:
        cp.wait_recv()
    sumo[...] = (go_ref[:, pc.s].astype(F32) + jnp.sum(nearo[...].astype(F32), axis=0)).astype(BF16)
    along_o.start()
    io.need(2, 3)
    cos, sin = cos_ref[...], -sin_ref[...]
    for l in range(nh):
        wait_on(dq_out.at[l], qsem.at[1, l])
    for p in range(nh // 2):
        q = dq_out[2 * p : 2 * p + 2].reshape(2 * DH, group).astype(F32).T
        dqkv[:, p * 128 : (p + 1) * 128] = turned(q, cos, sin).astype(BF16)
    for l in range(nh):
        for u in range(pc.cb):
            wait_on(dkv_out.at[l, u], ksem.at[1, l * pc.cb + u])
    for p in range(nh // 2):
        even, odd = [
            jnp.sum(dkv_out[2 * p + i].astype(F32), axis=0).reshape(group, 2 * DH)
            for i in range(2)
        ]
        low = lanes_of(even) < DH
        k = jnp.where(low, even, lane_roll(odd, DH)).astype(BF16).astype(F32)
        v = jnp.where(low, lane_roll(even, DH), odd)
        dqkv[:, lw + p * 128 : lw + (p + 1) * 128] = turned(k, cos, sin).astype(BF16)
        dqkv[:, 2 * lw + p * 128 : 2 * lw + (p + 1) * 128] = v.astype(BF16)
    nt = (((1,), (1,)), ((), ()))
    tn = (((0,), (0,)), ((), ()))
    for cp in loads:
        cp.wait()

    @pl.loop(0, nh)
    def _(i):
        cols = pl.ds(pl.multiple_of(i * (width // nh), width // nh), width // nh)
        gq_ref[cols, :] = lax.dot_general(
            n1_ref[:, cols], dqkv[...], tn, preferred_element_type=F32
        ).astype(BF16)

    io.put(0)

    @pl.loop(0, pc.nz)
    def _(i):
        at = pl.ds(pl.multiple_of(i * rows, rows), rows)
        dpart[i] = lax.dot_general(
            dqkv[at, :], w_ref[...], nt, preferred_element_type=F32
        ).astype(BF16)

    io.put(1)

    @pl.loop(0, count)
    def _(k):
        pair(k).wait_send()
        back(k, "wait_send")

    queries_back("wait_send")
    do_ref[...] = along_o.total()
    io.put(2)
    gb_sum[...] = along_b.total().astype(BF16)
    io.put(3)
    along_o.finish()
    along_b.finish()
    for cp in pairs_o:
        cp.wait_send()


def grads_back(dq, dkv, cos, sin, n1, wq, go, gb, hl):
    nh, nb = dims()
    nz, qs = hl, nb // hl
    cb = qs // 2
    rows = dkv.shape[3]
    width = n1.shape[1]
    lw = nh * DH
    dma = pltpu.SemaphoreType.DMA
    return comm_call(
        functools.partial(grads_back_body, nh, nb, hl),
        "grads_back",
        4,
        (
            jax.ShapeDtypeStruct((width, 3 * lw), BF16),
            jax.ShapeDtypeStruct((nz, rows, width), BF16),
            jax.ShapeDtypeStruct(go.shape[2:], F32),
            jax.ShapeDtypeStruct(gb.shape[1:], BF16),
        ),
        [ANY, VM, VM, VM, ANY, ANY, VM, VM],
        [VM] * 4,
        [
            pltpu.VMEM((nh * cb, nz, rows, 2 * DH), BF16),
            pltpu.VMEM((nh * cb, nz, rows, 2 * DH), BF16),
            pltpu.VMEM(dq.shape, BF16),
            pltpu.VMEM((nh, cb, nz, rows, 2 * DH), BF16),
            pltpu.VMEM((nz * rows, 3 * lw), BF16),
            pltpu.VMEM(n1.shape, BF16),
            pltpu.VMEM(wq.shape, BF16),
            pltpu.VMEM((qs - 1, nz) + go.shape[2:], BF16),
            pltpu.VMEM((nz,) + go.shape[2:], BF16),
        ]
        + StretchSum.scratch(nz, go.shape[2:])
        + StretchSum.scratch(nz, gb.shape[1:])
        + [
            dma((2, nh)),
            dma((2, nh * cb)),
            dma((2, nh * cb)),
            dma((2,)),
            dma((2, qs)),
        ],
        (dq, dkv, cos, sin, n1, wq, go, gb),
        vmem=60 << 20,
        late=(1, 6, 7, 2, 3),
        early=(0, 1, 2, 3),
    )


def last_body(nh, nb, hl, io, dpart, gq_ref, gma_ref, gmb_ref, dn_ref, quarters, gma_all, gmb_all, nearq, sumq, farq, totq, sentz, gotz, zsem, pq, fq, cq, msem, asem):
    pc = Place(nh, nb, hl)
    h, b = pc.h, pc.b
    signal_near(pc)
    wait_near(pc)
    nx, nz, qs = nh // 2, pc.nz, pc.qs
    def pair_q(k):
        return remote(
            gq_ref.at[2 * k + 1 - pc.c], nearq.at[k], pq.at[0, k], pq.at[1, k], pc.sib, b
        )

    line = LineSum(pc, lambda d: dpart[d].astype(F32), sentz, gotz, zsem)

    def plane_q(i):
        tx, ts = (pc.x + i // qs) % nx, (pc.s + i % qs) % qs
        return remote(
            sumq.at[tx, :, ts],
            farq.at[pc.x, pc.s],
            fq.at[0, i],
            fq.at[1, i],
            tx * 2 + pc.c,
            pc.zi * qs + ts,
        )

    def quarter(i):
        to = (pc.zi + i) % nz
        return remote(
            totq.at[to], quarters.at[pc.zi], cq.at[0, i], cq.at[1, i], h, to * qs + pc.s
        )

    io.need(1)
    for k in range(nx):
        pair_q(k).start()
    io.need(0)
    line.lead(0)
    moves = [
        remote(
            gmb_ref.at[(h + i) % nh],
            gmb_all.at[h],
            msem.at[0, i],
            msem.at[1, i],
            (h + i) % nh,
            b,
        )
        for i in range(1, nh)
    ]
    moves.append(pltpu.make_async_copy(gmb_ref.at[h], gmb_all.at[h], msem.at[0, 0]))
    moves.append(
        pltpu.make_async_copy(gma_ref.at[pc.s, h], gma_all.at[pc.s, h], asem.at[0, 0])
    )

    def plane_move(i):
        th, ts = (h + i // qs) % nh, (pc.s + i % qs) % qs
        return remote(
            gma_ref.at[ts, th],
            gma_all.at[pc.s, h],
            asem.at[0, i],
            asem.at[1, i],
            th,
            pc.zi * qs + ts,
        )

    for k in range(nx):
        pair_q(k).wait_recv()
        sumq[k] = (gq_ref[2 * k + pc.c].astype(F32) + nearq[k].astype(F32)).astype(BF16)

    @pl.loop(1, nx * qs)
    def _(i):
        plane_q(i).start()

    farq[pc.x, pc.s] = sumq[pc.x, :, pc.s]
    for cp in moves:
        cp.start()

    @pl.loop(1, nh * qs)
    def _(i):
        plane_move(i).start()

    line.follow(0)
    line.lead(1)

    @pl.loop(1, nx * qs)
    def _(i):
        plane_q(i).wait_recv()

    totq[...] = jnp.sum(
        farq[...].astype(F32).reshape((nx * qs,) + totq.shape), axis=0
    ).astype(BF16)
    for i in range(1, nz):
        quarter(i).start()
    quarters[pc.zi] = totq[pc.zi]
    for j in range(1, nz - 1):
        line.follow(j)
        if j + 1 < nz - 1:
            line.lead(j + 1)
    line.total(dn_ref)
    io.put(0)
    line.finish()
    for i in range(1, nz):
        quarter(i).wait()
    io.put(1)
    for cp in moves:
        cp.wait()

    @pl.loop(1, nh * qs)
    def _(i):
        plane_move(i).wait()

    for k in range(nx):
        pair_q(k).wait_send()

    @pl.loop(1, nx * qs)
    def _(i):
        plane_q(i).wait_send()


def last_exchange(dpart, gq, gma, gmb):
    nh, nb = dims()
    nz, rows, width = dpart.shape
    qs = nb // nz
    own_rows, cols = gq.shape[3:]
    nx = nh // 2
    dma = pltpu.SemaphoreType.DMA
    return comm_call(
        functools.partial(last_body, nh, nb, nz),
        "last_exchange",
        5,
        (
            jax.ShapeDtypeStruct((rows, width), F32),
            jax.ShapeDtypeStruct((nz, own_rows, cols), BF16),
            jax.ShapeDtypeStruct(gma.shape, BF16),
            jax.ShapeDtypeStruct(gmb.shape, BF16),
        ),
        [VM] * 2 + [ANY] * 2,
        [VM] * 2 + [ANY] * 2,
        [
            pltpu.VMEM((nx, nz, qs, own_rows, cols), BF16),
            pltpu.VMEM((nx, nz, qs, own_rows, cols), BF16),
            pltpu.VMEM((nx, qs, nz, own_rows, cols), BF16),
            pltpu.VMEM((nz, own_rows, cols), BF16),
        ]
        + LineSum.scratch(nz, (rows, width))
        + [
            dma((2, nx)),
            dma((2, nx * qs)),
            dma((2, nz)),
            dma((2, nh)),
            dma((2, nh * qs)),
        ],
        (dpart, gq, gma, gmb),
        vmem=60 << 20,
        late=(1, 0),
        early=(0, 1),
    )


def finish_body(nh, fl, dn_ref, x_ref, dh_ref, y_in, quarters, do_in, gma, gmb, wq_ref, win_ref, ga_ref, gf_ref,
                y_ref, dx_ref, lna_ref, dq_ref, do_ref, lnm_ref, din_ref, dwd_ref):
    y_ref[...] = y_in[...]
    do_ref[...] = do_in[...]
    normed, scale = norm_of(x_ref[...].astype(F32))
    dx_ref[...] = dh_ref[...] + norm_pull(dn_ref[...], normed, scale)
    width = x_ref.shape[1]
    gain = column(ga_ref[...].astype(F32))
    nz = quarters.shape[0]
    rowsum = 0.0
    for c in range(3):
        for l in range(nh):
            src = (c * nh * DH + l // 2 * 128) // 128 * 128
            for p in range(nz // 2):
                tiles = [quarters[2 * p + i, :, src : src + 128].astype(F32) for i in range(2)]
                piece = half_pick(tiles[0], tiles[1], l % 2, l % 2)
                at = c * width + l * nz * DH + p * 128
                dq_ref[:, at : at + 128] = piece * gain
                rowsum = rowsum + jnp.sum(
                    piece * wq_ref[:, at : at + 128].astype(F32), axis=1, keepdims=True
                )
    lna_ref[...] = as_row(rowsum)
    ff = nh * fl
    total, _, _ = ff_widths(fl)
    tiles = lambda v: (v + 127) // 128 * 128
    gate_up, down = 0.0, 0.0
    for i in range(nh):
        first = jnp.sum(gma[:, i].astype(F32), axis=0)
        piece = jnp.concatenate([first, gmb[i].astype(F32)], axis=1)
        lane = lanes_of(piece)
        gate = widen(jnp.where(lane < fl, piece, 0.0), tiles(2 * ff))
        up = jnp.where(jnp.logical_and(lane >= fl, lane < 2 * fl), piece, 0.0)
        up = widen(up, tiles(2 * ff))
        gate_up = gate_up + lane_roll(gate, i * fl) + lane_roll(up, ff - fl + i * fl)
        dn = jnp.where(jnp.logical_and(lane >= 2 * fl, lane < 3 * fl), piece, 0.0)
        down = down + lane_roll(widen(dn, max(total, tiles(ff))), i * fl - 2 * fl)
    gate_up = gate_up[:, : 2 * ff]
    dwd_ref[...] = down[:, :ff]
    din_ref[...] = gate_up * column(gf_ref[...].astype(F32))
    lnm_ref[...] = as_row(jnp.sum(gate_up * win_ref[...].astype(F32), axis=1, keepdims=True))


def finish(dn, x, dh, y, quarters, d_wout, gma, gmb, w_qkv, w_in, gain_attn, gain_mlp, fl):
    nh, _ = dims()
    rows, width = x.shape
    own_rows = w_qkv.shape[0]
    ff = nh * fl
    f32 = lambda *shape: jax.ShapeDtypeStruct(shape, F32)
    return pl.pallas_call(
        functools.partial(finish_body, nh, fl),
        out_shape=(
            f32(rows, width),
            f32(rows, width),
            f32(1, own_rows),
            f32(own_rows, 3 * width),
            f32(own_rows, width),
            f32(1, own_rows),
            f32(own_rows, 2 * ff),
            f32(own_rows, ff),
        ),
        in_specs=[VM] * 12,
        out_specs=[VM] * 8,
        name="finish",
        compiler_params=pltpu.CompilerParams(vmem_limit_bytes=60 << 20),
    )(dn, x, dh, y, quarters, d_wout, gma, gmb, w_qkv, w_in, gain_attn, gain_mlp)


def shards(layer_input, out_grad, lengths, ln_attn, w_qkv, w_attn_out, ln_mlp, w_in, w_mlp_out):
    nh, nb = dims()
    h, b = me()
    rows, width = layer_input.shape
    heads = width // DH
    hl = heads // nh
    group = nh * rows
    slots = nh * nb * rows
    own_rows = w_qkv.shape[0]
    ff = w_mlp_out.shape[0]
    fl = ff // nh
    nz, qs = hl, nb // hl
    lw = nh * DH

    gain_attn = ln_attn.reshape(1, own_rows)
    gain_mlp = ln_mlp.reshape(1, own_rows)
    n1, wma, wmb, wmc, wq, gg, cos, sin = first_exchange(
        lengths, layer_input, w_qkv, gain_attn, w_in, gain_mlp, w_mlp_out.T, out_grad, hl, fl
    )
    wma = lax.all_gather(wma, "blk", axis=1, tiled=True).reshape(width, -1)
    wq = wq.reshape(width, 3 * lw)
    n1 = n1.reshape(group, width)
    qin, kvin, wo, wmb, wmc = to_heads(n1, wq, cos, sin, w_attn_out[None], wmb, wmc, hl)
    wo = wo.reshape(nz * DH, width)
    kv_all = kvin.reshape(slots, 2 * DH)
    ot, of, lse = attend(lengths, qin, kv_all, 4 * rows, 1024, hl)
    og, hid, n2, wmc = mid_exchange(ot, wo, layer_input, wmc, hl)
    weights = [w.reshape(width, -1) for w in (wma, wmb, wmc)]
    ypart, dpart, gma, gmb = ffn(lengths, n2, gg, weights, fl, own_rows, GRAD_CUT)
    by_owner = []
    for gm in (gma, gmb):
        if gm.ndim == 4:
            gm = gm.reshape((nz, qs) + gm.shape[1:])
        else:
            gm = gm.reshape(nh, nz, qs, own_rows, gm.shape[1]).transpose(1, 2, 0, 3, 4)
        by_owner.append(gm)
    gma, gmb = by_owner
    lines = [[zi * qs + s for zi in range(nz)] for s in range(qs)]
    gma = lax.psum_scatter(
        gma, "blk", scatter_dimension=0, tiled=True, axis_index_groups=lines
    ).reshape(gma.shape[1:])
    y_out, dh, do_in, go, gmb = back_exchange(
        lengths, dpart, ypart, hid, out_grad, wo, og, gmb
    )
    dq, dkv = attend_grad(lengths, qin, do_in, of, kv_all, lse, 2 * rows, 1024, hl)
    go = go.reshape(nz, qs, own_rows, width)
    gq, dpart1, d_wout, gmb = grads_back(
        dq, dkv.reshape(kvin.shape), cos, sin, n1, wq, go, gmb, hl
    )
    dn, quarters, gma, gmb = last_exchange(
        dpart1, gq.reshape(nh, nz, qs, own_rows, 3 * lw), gma, gmb
    )
    y_out, dx, d_ln_attn, d_wqkv, d_wout, d_ln_mlp, d_win, d_wd = finish(
        dn,
        layer_input,
        dh,
        y_out,
        quarters,
        d_wout,
        gma,
        gmb,
        w_qkv,
        w_in,
        gain_attn,
        gain_mlp,
        fl,
    )
    return (
        y_out,
        dx,
        d_ln_attn.reshape(own_rows),
        d_wqkv,
        d_wout,
        d_ln_mlp.reshape(own_rows),
        d_win,
        d_wd.T,
    )


def solution(mesh):
    both = ("head", "blk")
    row_split = P(both, None)
    return jax.shard_map(
        shards,
        mesh=mesh,
        in_specs=(
            row_split,
            row_split,
            P(),
            P(both),
            row_split,
            row_split,
            P(both),
            row_split,
            P(None, both),
        ),
        out_specs=(
            row_split,
            row_split,
            P(both),
            row_split,
            row_split,
            P(both),
            row_split,
            P(None, both),
        ),
        check_vma=False,
    )
```

```python
import functools
import math

import jax
import jax.numpy as jnp
from jax import lax
from jax.experimental import pallas as pl
from jax.experimental.pallas import tpu as pltpu
from jax.sharding import PartitionSpec as P

DH = 64
ROPE_BASE = 160000.0
NORM_EPS = 1e-05
MASK_FLOOR = -1e30
GRAD_CUT = 1280
FF_BLOCKS = 2
WEIGHT_CUTS = (1280, 1408)
EXP_SCALE = 0.125 * math.log2(math.e)
BF16 = jnp.bfloat16
F32 = jnp.float32
MESH_ID = pl.DeviceIdType.MESH
ANY = pl.BlockSpec(memory_space=pl.ANY)
VM = pl.BlockSpec(memory_space=pltpu.VMEM)
SM = pl.BlockSpec(memory_space=pltpu.SMEM)


def dims():
    nh = lax.axis_size("head")
    nb = lax.axis_size("blk")
    return nh, nb


def me():
    return lax.axis_index("head"), lax.axis_index("blk")


class Staged:
    def __init__(self, loads, drains):
        self.loads, self.drains = loads, drains

    def need(self, *which):
        for i in which:
            self.loads[i].wait()

    def put(self, *which):
        for i in which:
            self.drains[i].start()


def comm_call(body, name, cid, out_shape, in_specs, out_specs, scratch, args, vmem=None, late=(), early=()):
    n_in, n_out, n_late, n_early = len(args), len(out_shape), len(late), len(early)
    in_specs = [ANY if i in late else spec for i, spec in enumerate(in_specs)]
    out_specs = [ANY if i in early else spec for i, spec in enumerate(out_specs)]
    held = [pltpu.VMEM(args[i].shape, args[i].dtype) for i in late]
    held += [pltpu.VMEM(out_shape[i].shape, out_shape[i].dtype) for i in early]
    held.append(pltpu.SemaphoreType.DMA((max(n_late + n_early, 1),)))

    def staged_body(*refs):
        ins, outs = list(refs[:n_in]), list(refs[n_in : n_in + n_out])
        bufs = refs[n_in + n_out : n_in + n_out + n_late + n_early]
        sems = refs[n_in + n_out + n_late + n_early]
        rest = refs[n_in + n_out + n_late + n_early + 1 :]
        loads, drains = {}, {}
        for k, i in enumerate(late):
            loads[i] = pltpu.make_async_copy(ins[i], bufs[k], sems.at[k])
            loads[i].start()
            ins[i] = bufs[k]
        for k, i in enumerate(early):
            k += n_late
            drains[i] = pltpu.make_async_copy(bufs[k], outs[i], sems.at[k])
            outs[i] = bufs[k]
        body(Staged(loads, drains), *ins, *outs, *rest)
        for cp in drains.values():
            cp.wait()

    return pl.pallas_call(
        staged_body,
        out_shape=out_shape,
        in_specs=in_specs,
        out_specs=out_specs,
        scratch_shapes=held + list(scratch),
        name=name,
        compiler_params=pltpu.CompilerParams(
            collective_id=cid, has_side_effects=True, vmem_limit_bytes=vmem
        ),
    )(*args)


def remote(src, dst, send, recv, h, b):
    return pltpu.make_async_remote_copy(
        src_ref=src,
        dst_ref=dst,
        send_sem=send,
        recv_sem=recv,
        device_id=(h, b),
        device_id_type=MESH_ID,
    )


def signal(h, b):
    pl.semaphore_signal(
        pltpu.get_barrier_semaphore(), inc=1, device_id=(h, b), device_id_type=MESH_ID
    )


class HeadGather:
    def __init__(self, nh, h, b, src, dst, sems):
        self.nh, self.h, self.b, self.dst, self.sems = nh, h, b, dst, sems
        nx = nh // 2
        self.nx = nx
        x, c = h // 2, h % 2
        sib = x * 2 + 1 - c
        self.sib = sib
        self.across = []
        for k in range(1, nx):
            self.across.append(
                remote(src, dst.at[h], sems.at[0, k], sems.at[1, k], ((x + k) % nx) * 2 + c, b)
            )
        self.near = remote(src, dst.at[h], sems.at[0, 0], sems.at[1, 0], sib, b)
        self.local = pltpu.make_async_copy(src, dst.at[h], sems.at[2, 0])
        self.forward = []
        for k in range(1, nx):
            got = ((x + nx - k) % nx) * 2 + c
            self.forward.append(
                remote(dst.at[got], dst.at[got], sems.at[2, k], sems.at[3, k], sib, b)
            )

    @staticmethod
    def sem_shape(nh):
        return pltpu.SemaphoreType.DMA((4, nh // 2))

    def start(self):
        for cp in self.across:
            cp.start()
        self.near.start()
        self.local.start()

    def pass_on(self):
        for cp, fw in zip(self.across, self.forward):
            cp.wait_recv()
            fw.start()

    def finish(self):
        for cp in self.across:
            cp.wait_send()
        self.near.wait()
        self.local.wait()
        for fw in self.forward:
            fw.wait()


def lane_roll(values, shift):
    return pltpu.roll(values, shift % values.shape[1], 1)


def lanes_of(values):
    return lax.broadcasted_iota(jnp.int32, (1, values.shape[1]), 1)


def widen(values, width):
    extra = width - values.shape[1]
    if extra <= 0:
        return values[:, :width]
    return jnp.concatenate([values, jnp.zeros((values.shape[0], extra), values.dtype)], axis=1)


def weight_parts(total):
    marks = (0,) + WEIGHT_CUTS + (total,)
    return list(zip(marks[:-1], marks[1:]))


def column(row):
    n = row.shape[1]
    same = lax.broadcasted_iota(jnp.int32, (n, n), 0) == lax.broadcasted_iota(jnp.int32, (n, n), 1)
    return jnp.sum(jnp.where(same, row, 0.0), axis=1, keepdims=True)


def as_row(col):
    n = col.shape[0]
    same = lax.broadcasted_iota(jnp.int32, (n, n), 0) == lax.broadcasted_iota(jnp.int32, (n, n), 1)
    return jnp.sum(jnp.where(same, col, 0.0), axis=0, keepdims=True)


def sequence_ends(len_ref):
    ends, total = [], 0
    for i in range(len_ref.shape[0]):
        total = total + len_ref[i]
        ends.append(total)
    return ends


def segment_first(slot, ends):
    first = jnp.zeros_like(slot)
    for end in ends:
        first = jnp.where(slot >= end, end, first)
    return first


def segment_end(slot, ends, slots):
    last = jnp.zeros_like(slot) + slots
    for end in reversed(ends):
        last = jnp.where(slot < end, end, last)
    return last


def half_pick(low_src, high_src, low_at, high_at):
    low = low_src if low_at == 0 else lane_roll(low_src, DH)
    high = high_src if high_at == 1 else lane_roll(high_src, DH)
    return jnp.where(lanes_of(low) < DH, low, high)


def ff_widths(fl):
    up = lambda v: (v + 127) // 128 * 128
    return up(3 * fl), up(2 * fl), 2 * fl // 128 * 128


class LineGather:
    def __init__(self, pc, src, place, sems):
        self.pc, self.src, self.place, self.sems = pc, src, place, sems

    @staticmethod
    def sem_shape(nz):
        return pltpu.SemaphoreType.DMA((5, nz))

    def origin(self, t, up):
        return self.pc.zi - t if up else self.pc.zi + t

    def move(self, t, up):
        pc = self.pc
        at = self.place(self.origin(t, up))
        n = 0 if up else 2
        return remote(
            self.src if t == 0 else at,
            at,
            self.sems.at[n, t],
            self.sems.at[n + 1, t],
            pc.h,
            pc.b + pc.qs if up else pc.b - pc.qs,
        )

    def sends(self, t, up):
        zi, nz = self.pc.zi, self.pc.nz
        if up:
            return jnp.logical_and(zi - t >= 0, zi + 1 < nz)
        return jnp.logical_and(zi + t < nz, zi - 1 >= 0)

    def local(self):
        return pltpu.make_async_copy(self.src, self.place(self.pc.zi), self.sems.at[4, 0])

    def start(self):
        for up in (True, False):

            @pl.when(self.sends(0, up))
            def _():
                self.move(0, up).start()

        self.local().start()

    def step(self, t, arrived=None):
        low = self.pc.zi < self.pc.nz // 2
        self.take(t, False, jnp.logical_not(low), arrived)
        self.take(t, True, True, arrived)
        self.take(t, False, low, arrived)

    def take(self, t, up, now, arrived):
        zi, nz = self.pc.zi, self.pc.nz
        origin = self.origin(t, up)
        here = jnp.logical_and(now, origin >= 0 if up else origin < nz)

        @pl.when(here)
        def _():
            wait_on(self.place(origin), self.sems.at[1 if up else 3, t - 1])

        if t < nz - 1:

            @pl.when(jnp.logical_and(now, self.sends(t, up)))
            def _():
                self.move(t, up).start()

        if arrived is not None:

            @pl.when(here)
            def _():
                arrived(origin)

    def finish(self):
        self.local().wait()
        for t in range(self.pc.nz - 1):
            for up in (True, False):

                @pl.when(self.sends(t, up))
                def _():
                    self.move(t, up).wait_send()


class BlkGather:
    def __init__(self, pc, src, out, sems, ssem):
        self.pc, self.out, self.ssem, self.src = pc, out, ssem, src
        self.line = LineGather(pc, src, lambda zi: out.at[:, zi, pc.s], sems)

    @staticmethod
    def sem_shapes(nz, qs):
        return [LineGather.sem_shape(nz), pltpu.SemaphoreType.DMA((2, nz, qs))]

    def side(self, zi, ds, own=False):
        pc = self.pc
        ref = self.out.at[:, zi, pc.s]
        return remote(
            self.src if own else ref,
            ref,
            self.ssem.at[0, zi, ds],
            self.ssem.at[1, zi, ds],
            pc.h,
            pc.zi * pc.qs + (pc.s + ds) % pc.qs,
        )

    def spread(self, zi, own=False):
        for ds in range(1, self.pc.qs):
            self.side(zi, ds, own).start()

    def start(self):
        self.line.start()
        self.spread(self.pc.zi, True)

    def step(self, t):
        self.line.step(t, self.spread)

    def finish(self):
        self.line.finish()

        @pl.loop(0, self.pc.nz)
        def _(zi):
            for ds in range(1, self.pc.qs):
                self.side(zi, ds).wait()


class LineSum:
    def __init__(self, pc, term, sent, got, sems):
        self.pc, self.term, self.sent, self.got, self.sems = pc, term, sent, got, sems

    @staticmethod
    def scratch(nz, shape):
        return [
            pltpu.VMEM((2, nz) + shape, BF16),
            pltpu.VMEM((2, nz) + shape, BF16),
            pltpu.SemaphoreType.DMA((4, nz)),
        ]

    def move(self, d, up):
        pc = self.pc
        n = 0 if up else 1
        return remote(
            self.sent.at[n, d],
            self.got.at[n, d],
            self.sems.at[2 * n, d],
            self.sems.at[2 * n + 1, d],
            pc.h,
            pc.b + pc.qs if up else pc.b - pc.qs,
        )

    def takes(self, up):
        return self.pc.zi > 0 if up else self.pc.zi < self.pc.nz - 1

    def lead(self, j):
        self.step(j, False)

    def follow(self, j):
        self.step(j, True)

    def step(self, j, taking):
        low = self.pc.zi < self.pc.nz // 2
        if taking:
            self.one(j, False, jnp.logical_not(low), True)
            self.one(j, True, True, True)
            self.one(j, False, low, True)
        else:
            self.one(j, True, True, False)
            self.one(j, False, True, False)

    def one(self, j, up, now, taking):
        zi, nz = self.pc.zi, self.pc.nz
        d = nz - 1 - j if up else j
        n = 0 if up else 1
        takes = self.takes(up)
        far = jnp.logical_and(now, zi < d if up else zi > d)

        @pl.when(jnp.logical_and(far, takes if taking else jnp.logical_not(takes)))
        def _():
            if taking:
                wait_on(self.got.at[n, d], self.sems.at[2 * n + 1, d])
                self.sent[n, d] = (self.term(d) + self.got[n, d].astype(F32)).astype(BF16)
            else:
                self.sent[n, d] = self.term(d).astype(BF16)
            self.move(d, up).start()

    def total(self, total_ref):
        zi = self.pc.zi
        total_ref[...] = self.term(zi)
        for up in (True, False):
            n = 0 if up else 1

            @pl.when(self.takes(up))
            def _():
                wait_on(self.got.at[n, zi], self.sems.at[2 * n + 1, zi])
                total_ref[...] += self.got[n, zi].astype(F32)

    def finish(self):
        zi, nz = self.pc.zi, self.pc.nz
        for j in range(nz - 1):
            for up in (True, False):
                d = nz - 1 - j if up else j

                @pl.when(zi < d if up else zi > d)
                def _():
                    self.move(d, up).wait_send()


class StretchSum:
    def __init__(self, pc, part, got, sems):
        self.pc, self.part, self.got, self.sems = pc, part, got, sems

    @staticmethod
    def scratch(nz, shape):
        return [pltpu.VMEM((nz,) + shape, BF16), pltpu.SemaphoreType.DMA((2, nz))]

    def move(self, i):
        pc = self.pc
        to = (pc.zi + i) % pc.nz
        return remote(
            self.part.at[to],
            self.got.at[pc.zi],
            self.sems.at[0, i],
            self.sems.at[1, i],
            pc.h,
            to * pc.qs + pc.s,
        )

    def start(self):
        for i in range(1, self.pc.nz):
            self.move(i).start()

    def total(self):
        pc = self.pc
        total = self.part[pc.zi].astype(F32)
        for i in range(1, pc.nz):
            self.move(i).wait_recv()
            total = total + self.got[(pc.zi + pc.nz - i) % pc.nz].astype(F32)
        return total

    def finish(self):
        for i in range(1, self.pc.nz):
            self.move(i).wait_send()


class PlaneWeights:
    def __init__(self, pc, pack, out, sems, ksem):
        self.pc, self.pack, self.out, self.sems, self.ksem = pc, pack, out, sems, ksem

    @staticmethod
    def sem_shapes(nh, nz, qs):
        dma = pltpu.SemaphoreType.DMA
        return [dma((2, nz)), dma((4, nh // 2 * qs))]

    def along(self, i):
        pc = self.pc
        to = (pc.zi + i) % pc.nz
        return remote(
            self.pack.at[to],
            self.out.at[pc.h, pc.zi, pc.s],
            self.sems.at[0, i],
            self.sems.at[1, i],
            pc.h,
            to * pc.qs + pc.s,
        )

    def local(self):
        pc = self.pc
        return pltpu.make_async_copy(
            self.pack.at[pc.zi], self.out.at[pc.h, pc.zi, pc.s], self.sems.at[0, 0]
        )

    def place(self, i, sign):
        pc = self.pc
        nx = pc.nh // 2
        dx, ds = i // pc.qs, i % pc.qs
        if sign < 0:
            dx, ds = nx - dx, pc.qs - ds
        return ((pc.x + dx) % nx) * 2 + pc.c, (pc.s + ds) % pc.qs

    def across(self, i):
        pc = self.pc
        th, ts = self.place(i, 1)
        ref = self.out.at[pc.h, :, pc.s]
        return remote(
            ref, ref, self.ksem.at[0, i], self.ksem.at[1, i], th, pc.zi * pc.qs + ts
        )

    def near(self, i):
        pc = self.pc
        gh, gs = self.place(i, -1)
        ref = self.out.at[gh, :, gs]
        return remote(ref, ref, self.ksem.at[2, i], self.ksem.at[3, i], pc.sib, pc.b)

    def start(self):
        for i in range(1, self.pc.nz):
            self.along(i).start()
        self.local().start()

    def spread(self):
        pc = self.pc
        self.local().wait()
        for i in range(1, pc.nz):
            self.along(i).wait_recv()

        @pl.loop(1, pc.nh // 2 * pc.qs)
        def _(i):
            self.across(i).start()

        self.near(0).start()

    def pass_on(self):
        @pl.loop(1, self.pc.nh // 2 * self.pc.qs)
        def _(i):
            self.across(i).wait_recv()
            self.near(i).start()

    def finish(self):
        for i in range(1, self.pc.nz):
            self.along(i).wait_send()

        @pl.loop(1, self.pc.nh // 2 * self.pc.qs)
        def _(i):
            self.across(i).wait_send()

        @pl.loop(0, self.pc.nh // 2 * self.pc.qs)
        def _(i):
            self.near(i).wait()


def first_body(nh, nb, hl, fl, io, len_ref, x_ref, wq_ref, ga_ref, win_hbm, gf_ref, wd_hbm, g_ref, n1_all, wma, wmb, wmc, wq_all, gg, cos_ref, sin_ref, own_n, pack, wmp, win_ref, wd_ref, lsem, wsem, ksem, gsem, msem, stage):
    pc = Place(nh, nb, hl)
    h, b = pc.h, pc.b
    loads = [
        pltpu.make_async_copy(win_hbm, win_ref, stage.at[0]),
        pltpu.make_async_copy(wd_hbm, wd_ref, stage.at[1]),
    ]
    for cp in loads:
        cp.start()
    signal_near(pc)
    width = x_ref.shape[1]
    lw = width // pc.nz
    gain = column(ga_ref[...].astype(F32))
    io.need(2)
    for c in range(3):
        w = wq_ref[:, c * width : (c + 1) * width].astype(F32) * gain
        tile = lambda l, i: w[:, l * pc.nz * DH + i // 2 * 128 : l * pc.nz * DH + i // 2 * 128 + 128]
        for i in range(pc.nz):
            for p in range(nh // 2):
                both = half_pick(tile(2 * p, i), tile(2 * p + 1, i), i % 2, i % 2)
                at = c * lw + p * 128
                pack[i, :, at : at + 128] = both.astype(BF16)
    io.need(1)
    own_n[...] = norm_of(x_ref[...].astype(F32))[0].astype(BF16)
    wait_near(pc)
    weights = PlaneWeights(pc, pack, wq_all, wsem, ksem)
    line = LineGather(pc, own_n, lambda zi: n1_all.at[zi], lsem)
    gather = HeadGather(nh, h, b, g_ref, gg, gsem)
    weights.start()
    line.start()
    gather.start()
    for cp in loads:
        cp.wait()
    total = ff_widths(fl)[0]
    ff = nh * fl
    win = win_ref[...].astype(F32) * column(gf_ref[...].astype(F32))
    wd = widen(wd_ref[...].astype(F32), total if total > ff else (ff + 127) // 128 * 128)
    lane = lax.broadcasted_iota(jnp.int32, (1, total), 1)
    for i in range(nh):
        gate = widen(lane_roll(win, -i * fl), total)
        up = widen(lane_roll(win, fl - ff - i * fl), total)
        down = widen(lane_roll(wd, 2 * fl - i * fl), total)
        piece = jnp.where(
            lane < fl,
            gate,
            jnp.where(lane < 2 * fl, up, jnp.where(lane < 3 * fl, down, 0.0)),
        )
        wmp[i] = piece.astype(BF16)
    copies = []
    for n, (dst, (begin, end)) in enumerate(zip((wma, wmb, wmc), weight_parts(total))):
        cols = pl.ds(begin, end - begin)
        for i in range(1, nh):
            th = (h + i) % nh
            src = wmp.at[th, :, cols]
            copies.append(remote(src, dst.at[h], msem.at[0, n, i], msem.at[1, n, i], th, b))
        copies.append(pltpu.make_async_copy(wmp.at[h, :, cols], dst.at[h], msem.at[0, n, 0]))
    weights.spread()
    for cp in copies:
        cp.start()
    ends = sequence_ends(len_ref)
    rows = x_ref.shape[0]
    lane = lax.broadcasted_iota(jnp.int32, (1, 2 * DH), 1)
    power = (lane % (DH // 2)).astype(F32) * (-2.0 / DH)
    inv_freq = jnp.exp2(power * math.log2(ROPE_BASE))
    sign = jnp.where(lane % DH < DH // 2, -1.0, 1.0)
    line.step(1)
    for i in range(pc.nz):
        slot = (h * nb + i * pc.qs + pc.s) * rows + lax.broadcasted_iota(jnp.int32, (rows, 1), 0)
        angle = (slot - segment_first(slot, ends)).astype(F32) * inv_freq
        cos_ref[i * rows : (i + 1) * rows, :] = jnp.cos(angle)
        sin_ref[i * rows : (i + 1) * rows, :] = jnp.sin(angle) * sign
    io.put(6, 7)
    gather.pass_on()
    for t in range(2, pc.nz):
        line.step(t)
    weights.pass_on()
    for cp in copies:
        cp.wait()
    weights.finish()
    line.finish()
    gather.finish()


def first_exchange(lengths, x, w_qkv, gain_attn, w_in, gain_mlp, wd_t, g, hl, fl):
    nh, nb = dims()
    rows, width = x.shape
    nz, qs = hl, nb // hl
    lw = width // nz
    own_rows = w_in.shape[0]
    total = ff_widths(fl)[0]
    dma = pltpu.SemaphoreType.DMA
    return comm_call(
        functools.partial(first_body, nh, nb, hl, fl),
        "first_exchange",
        0,
        (
            jax.ShapeDtypeStruct((nz, rows, width), BF16),
            *[
                jax.ShapeDtypeStruct((nh, own_rows, end - begin), BF16)
                for begin, end in weight_parts(total)
            ],
            jax.ShapeDtypeStruct((nh, nz, qs, own_rows, 3 * lw), BF16),
            jax.ShapeDtypeStruct((nh, rows, width), BF16),
            jax.ShapeDtypeStruct((nz * rows, 2 * DH), F32),
            jax.ShapeDtypeStruct((nz * rows, 2 * DH), F32),
        ),
        [SM, VM, VM, VM, ANY, VM, ANY, ANY],
        [ANY] * 6 + [VM] * 2,
        [
            pltpu.VMEM((rows, width), BF16),
            pltpu.VMEM((nz, own_rows, 3 * lw), BF16),
            pltpu.VMEM((nh, own_rows, total), BF16),
            pltpu.VMEM(w_in.shape, BF16),
            pltpu.VMEM(wd_t.shape, BF16),
            LineGather.sem_shape(nz),
        ]
        + PlaneWeights.sem_shapes(nh, nz, qs)
        + [
            HeadGather.sem_shape(nh),
            dma((2, 3, nh)),
            dma((2,)),
        ],
        (lengths, x, w_qkv, gain_attn, w_in, gain_mlp, wd_t, g),
        vmem=60 << 20,
        late=(2, 1),
        early=(6, 7),
    )


class Place:
    def __init__(self, nh, nb, hl):
        h, b = me()
        self.nh, self.nb, self.h, self.b = nh, nb, h, b
        self.x, self.c = h // 2, h % 2
        self.nz = hl
        self.qs = nb // hl
        self.cb = self.qs // 2
        self.sib = self.x * 2 + 1 - self.c
        self.zi, self.s = b // self.qs, b % self.qs
        self.head = self.x * 2 + self.s // self.cb
        self.u = self.s % self.cb
        self.from_s = self.u * 2 + self.c

    def attends(self, zi, l, core, u):
        return (l // 2) * 2 + core, zi * self.qs + (l % 2) * self.cb + u


def signal_near(pc):
    here = pc.nh * pc.qs

    @pl.loop(1, here)
    def _(i):
        signal((pc.h + i // pc.qs) % pc.nh, pc.zi * pc.qs + (pc.s + i % pc.qs) % pc.qs)

    @pl.loop(1, pc.nz)
    def _(i):
        signal(pc.h, (pc.zi + i) % pc.nz * pc.qs + pc.s)


def wait_near(pc, more=0):
    pl.semaphore_wait(pltpu.get_barrier_semaphore(), pc.nh * pc.qs + pc.nz - 2 + more)


def enter_with(pc, source):
    signal_near(pc)
    for i in range(1, pc.nz):
        signal(*source((pc.zi + i) % pc.nz))
    wait_near(pc, pc.nz - 1)


def routed(pc, src, dst, send, recv, th, tb, act):
    mine = jnp.logical_and(th == pc.h, tb == pc.b)

    @pl.when(mine)
    def _():
        if act == "start":
            pltpu.make_async_copy(src, dst, recv).start()

    @pl.when(jnp.logical_not(mine))
    def _():
        cp = remote(src, dst, send, recv, th, tb)
        if act == "start":
            cp.start()
        else:
            cp.wait_send()


def wait_on(ref, sem):
    pltpu.make_async_copy(ref, ref, sem).wait()


def stretch_lanes(ref, zi, rows):
    return ref.at[:, :, pl.ds(pl.multiple_of(zi * rows, rows), rows)]


def outputs_back(pc, o_ref, og, osem, act):
    rows = og.shape[3]
    for zi in range(pc.nz):
        routed(
            pc,
            stretch_lanes(o_ref, zi, rows),
            og.at[pc.zi],
            osem.at[0, zi],
            osem.at[1, pc.zi],
            pc.head,
            zi * pc.qs + pc.from_s,
            act,
        )


def grads_out(pc, dots, do_in, qsem, i, act):
    rows = dots.shape[3]
    for zi in range(pc.nz):
        th, tb = pc.attends(zi, pc.h, pc.s % 2, pc.s // 2)
        routed(
            pc,
            dots.at[zi, i],
            stretch_of(do_in, i, pc.zi, rows),
            qsem.at[0, zi, i],
            qsem.at[1, pc.zi, i],
            th,
            tb,
            act,
        )


def stretch_of(ref, i, zi, rows):
    return ref.at[i, :, pl.ds(pl.multiple_of(zi * rows, rows), rows)]


def halves_swapped(tile):
    lane = lanes_of(tile)
    return jnp.where(lane % DH < DH // 2, lane_roll(tile, -(DH // 2)), lane_roll(tile, DH // 2))


def turned(tile, cos, sin):
    return tile * cos + halves_swapped(tile) * sin


def to_heads_body(nh, nb, hl, io, n1_hbm, w_hbm, cos_ref, sin_ref, wo_ref, wmb_ref, wmc_ref, qin, kvin, wo_all, wmb_all, wmc_line, qbuf, kvbuf, n1_ref, w_ref, qsem, ksem, fsem, osem, osem2, bsem, bsem2, csem, stage):
    pc = Place(nh, nb, hl)
    loads = [
        pltpu.make_async_copy(n1_hbm, n1_ref, stage.at[0]),
        pltpu.make_async_copy(w_hbm, w_ref, stage.at[1]),
    ]
    for cp in loads:
        cp.start()
    signal_near(pc)
    rows = kvbuf.shape[2]
    lw = nh * DH
    for cp in loads:
        cp.wait()
    n1 = n1_ref[...]
    io.need(2, 3)
    cos, sin = cos_ref[...], sin_ref[...]
    kk = jnp.dot(n1, w_ref[:, lw : 2 * lw], preferred_element_type=F32)
    vv = jnp.dot(n1, w_ref[:, 2 * lw :], preferred_element_type=F32)
    for p in range(nh // 2):
        k = turned(kk[:, p * 128 : (p + 1) * 128], cos, sin)
        v = vv[:, p * 128 : (p + 1) * 128]
        low = lanes_of(k) < DH
        even = jnp.where(low, k, lane_roll(v, DH)).astype(BF16)
        odd = jnp.where(low, lane_roll(k, DH), v).astype(BF16)
        for i in range(pc.nz):
            kvbuf[2 * p, i] = even[i * rows : (i + 1) * rows]
            kvbuf[2 * p + 1, i] = odd[i * rows : (i + 1) * rows]
    wait_near(pc)

    def keys_out(act):
        for l in range(nh):
            for u in range(pc.cb):
                th, tb = pc.attends(pc.zi, l, pc.s % 2, u)
                routed(
                    pc,
                    kvbuf.at[l],
                    kvin.at[pc.h, :, pc.s],
                    ksem.at[0, l * pc.cb + u],
                    ksem.at[1, pc.h * pc.cb + pc.s // 2],
                    th,
                    tb,
                    act,
                )

    def queries_out(act):
        for l in range(nh):
            th, tb = pc.attends(pc.zi, l, pc.s % 2, pc.s // 2)
            routed(
                pc, qbuf.at[l], qin.at[pc.h], qsem.at[0, l], qsem.at[1, pc.h], th, tb, act
            )

    spread = BlkGather(pc, wo_ref, wo_all, osem, osem2)
    spread_b = BlkGather(pc, wmb_ref, wmb_all, bsem, bsem2)
    line_c = LineGather(pc, wmc_ref, lambda zi: wmc_line.at[:, zi], csem)
    keys_out("start")
    spread.start()
    spread_b.start()
    line_c.start()
    qq = jnp.dot(n1, w_ref[:, :lw], preferred_element_type=F32)
    for p in range(nh // 2):
        q = turned(qq[:, p * 128 : (p + 1) * 128], cos, sin).T.astype(BF16)
        qbuf[2 * p] = q[:DH]
        qbuf[2 * p + 1] = q[DH:]
    queries_out("start")
    count = nh * pc.cb

    def forward(i):
        at = kvin.at[i // pc.cb, :, 2 * (i % pc.cb) + pc.c]
        return remote(at, at, fsem.at[0, i], fsem.at[1, i], pc.sib, pc.b)

    @pl.loop(0, count)
    def _(i):
        wait_on(kvin.at[i // pc.cb, :, 2 * (i % pc.cb) + pc.c], ksem.at[1, i])
        forward(i).start()

    for t in range(1, pc.nz):
        spread.step(t)
        spread_b.step(t)
        line_c.step(t)
    keys_out("wait_send")
    queries_out("wait_send")
    for i in range(nh):
        wait_on(qin.at[i], qsem.at[1, i])

    @pl.loop(0, count)
    def _(i):
        forward(i).wait()

    spread.finish()
    spread_b.finish()
    line_c.finish()


def to_heads(n1, wq, cos, sin, wo, wmb, wmc, hl):
    nh, nb = dims()
    group, width = n1.shape
    nz, qs = hl, nb // hl
    cb = qs // 2
    rows = group // nz
    dma = pltpu.SemaphoreType.DMA
    return comm_call(
        functools.partial(to_heads_body, nh, nb, hl),
        "to_heads",
        1,
        (
            jax.ShapeDtypeStruct((nh, DH, group), BF16),
            jax.ShapeDtypeStruct((nh, nz, qs, rows, 2 * DH), BF16),
            jax.ShapeDtypeStruct((1, nz, qs) + wo.shape[1:], BF16),
            jax.ShapeDtypeStruct((nh, nz, qs) + wmb.shape[1:], BF16),
            jax.ShapeDtypeStruct((nh, nz) + wmc.shape[1:], BF16),
        ),
        [ANY, ANY, VM, VM, ANY, ANY, ANY],
        [ANY] * 5,
        [
            pltpu.VMEM((nh, DH, group), BF16),
            pltpu.VMEM((nh, nz, rows, 2 * DH), BF16),
            pltpu.VMEM(n1.shape, BF16),
            pltpu.VMEM(wq.shape, BF16),
            dma((2, nh)),
            dma((2, nh * cb)),
            dma((2, nh * cb)),
        ]
        + BlkGather.sem_shapes(nz, qs) * 2
        + [LineGather.sem_shape(nz), dma((2,))],
        (n1, wq, cos, sin, wo, wmb, wmc),
        vmem=60 << 20,
        late=(2, 3),
    )


class Queries:
    def __init__(self, nh, nb, hl, len_ref, lanes, slots, size):
        pc = Place(nh, nb, hl)
        tile = pl.program_id(0)
        rows = slots // (nh * nb)
        count = lanes // rows
        each = pc.nz // count
        ends = sequence_ends(len_ref)
        base = (tile // each) * nb + (tile % each) * count * pc.qs + pc.from_s
        lane = lax.broadcasted_iota(jnp.int32, (1, lanes), 1)
        slot = (base + lane // rows * pc.qs) * rows + lane % rows
        self.first = segment_first(slot, ends)
        self.last = segment_end(slot, ends, slots)
        near = base * rows
        far = (base + (count - 1) * pc.qs) * rows + rows - 1
        self.size = size
        self.lo = segment_first(near, ends) // size
        self.hi = (segment_end(far, ends, slots) + size - 1) // size
        self.open = jnp.minimum((segment_first(far, ends) + size - 1) // size, self.hi)
        self.close = jnp.maximum(segment_end(near, ends, slots) // size, self.open)
        self.lanes = lanes

    def allowed(self, block_at):
        at = block_at * self.size + lax.broadcasted_iota(jnp.int32, (self.size, self.lanes), 0)
        return jnp.logical_and(at >= self.first, at < self.last)

    def walk(self, step, carry):
        masked = lambda j, kept: step(j, kept, True)
        carry = lax.fori_loop(self.lo, self.open, masked, carry)
        carry = lax.fori_loop(self.open, self.close, lambda j, kept: step(j, kept, False), carry)
        return lax.fori_loop(self.close, self.hi, masked, carry)


def attend_body(nh, nb, hl, size, len_ref, q_ref, kv_ref, o_ref, of_ref, lse_ref):
    q = q_ref[0]
    lanes = q.shape[1]
    at = Queries(nh, nb, hl, len_ref, lanes, kv_ref.shape[0], size)
    q_pad = jnp.concatenate([q, jnp.zeros_like(q)], axis=0)
    is_key = lax.broadcasted_iota(jnp.int32, (1, 2 * DH), 1) < DH

    def step(j, carry, masked):
        top, acc = carry
        kv = kv_ref[pl.ds(pl.multiple_of(j * size, size), size), :]
        s = jnp.dot(kv, q_pad, preferred_element_type=F32)
        if masked:
            s = jnp.where(at.allowed(j), s, MASK_FLOOR)
        new_top = jnp.maximum(top, jnp.max(s, axis=0, keepdims=True))
        p = jnp.exp2((s - new_top) * EXP_SCALE).astype(BF16)
        alpha = jnp.exp2((top - new_top) * EXP_SCALE)
        ones_values = jnp.where(is_key, jnp.ones_like(kv), kv)
        acc = acc * alpha + lax.dot_general(
            ones_values, p, (((0,), (0,)), ((), ())), preferred_element_type=F32
        )
        return new_top, acc

    top, acc = at.walk(
        step, (jnp.full((1, lanes), MASK_FLOOR, F32), jnp.zeros((2 * DH, lanes), F32))
    )
    total = acc[:1]
    o = acc[DH:] / total
    of_ref[0] = o
    o_ref[0] = o.astype(BF16)
    lse_ref[0] = top * EXP_SCALE + jnp.log2(total)


def attend_specs(kv_rows, lanes, tiles_each):
    tile_spec = pl.BlockSpec((1, DH, lanes), lambda i, *_: (i // tiles_each, 0, i % tiles_each))
    row_spec = pl.BlockSpec((1, 1, lanes), lambda i, *_: (i, 0, 0))
    kv_spec = pl.BlockSpec((kv_rows, 2 * DH), lambda i, *_: (0, 0))
    return tile_spec, row_spec, kv_spec


def attend(lengths, q, kv, lanes, size, hl):
    nh, nb = dims()
    each = q.shape[2] // lanes
    tiles = q.shape[0] * each
    tile_spec, row_spec, kv_spec = attend_specs(kv.shape[0], lanes, each)
    return pl.pallas_call(
        functools.partial(attend_body, nh, nb, hl, size),
        grid_spec=pltpu.PrefetchScalarGridSpec(
            num_scalar_prefetch=1,
            grid=(tiles,),
            in_specs=[tile_spec, kv_spec],
            out_specs=[tile_spec, tile_spec, row_spec],
        ),
        out_shape=(
            jax.ShapeDtypeStruct(q.shape, BF16),
            jax.ShapeDtypeStruct(q.shape, F32),
            jax.ShapeDtypeStruct((tiles, 1, lanes), F32),
        ),
        name="attend",
        compiler_params=pltpu.CompilerParams(vmem_limit_bytes=60 << 20),
    )(lengths, q, kv)


def attend_grad_body(nh, nb, hl, size, len_ref, q_ref, do_ref, of_ref, kv_ref, lse_ref, dq_ref, dkv_ref, acc_ref):
    tile = pl.program_id(0)

    @pl.when(tile == 0)
    def _():
        acc_ref[...] = jnp.zeros_like(acc_ref)

    q = q_ref[0]
    do = do_ref[0]
    lanes = q.shape[1]
    place = Queries(nh, nb, hl, len_ref, lanes, kv_ref.shape[0], size)
    zero = jnp.zeros_like(q)
    both = jnp.concatenate(
        [jnp.concatenate([q, zero], axis=0), jnp.concatenate([zero, do], axis=0)], axis=1
    )
    delta = jnp.sum(do.astype(F32) * of_ref[0], axis=0, keepdims=True)
    lse = lse_ref[0]

    def step(j, dq, masked):
        at = pl.ds(pl.multiple_of(j * size, size), size)
        kv = kv_ref[at, :]
        sd = jnp.dot(kv, both, preferred_element_type=F32)
        s, dp = sd[:, :lanes], sd[:, lanes:]
        power = s * EXP_SCALE - lse
        if masked:
            power = jnp.where(place.allowed(j), power, MASK_FLOOR)
        p = jnp.exp2(power)
        ds = (p * (dp - delta)).astype(BF16)
        acc_ref[at, :] += lax.dot_general(
            jnp.concatenate([ds, p.astype(BF16)], axis=1),
            both,
            (((1,), (1,)), ((), ())),
            preferred_element_type=F32,
        )
        return dq + lax.dot_general(
            kv, ds, (((0,), (0,)), ((), ())), preferred_element_type=F32
        )

    dq = place.walk(step, jnp.zeros((2 * DH, lanes), F32))
    dq_ref[0] = (dq[:DH] * 0.125).astype(BF16)

    @pl.when(tile == pl.num_programs(0) - 1)
    def _():
        lane = lax.broadcasted_iota(jnp.int32, (1, 2 * DH), 1)
        dkv_ref[...] = (acc_ref[...] * jnp.where(lane < DH, 0.125, 1.0)).astype(BF16)


def attend_grad(lengths, q, do, of, kv, lse, lanes, size, hl):
    nh, nb = dims()
    tiles = lse.size // lanes
    lse = lse.reshape(tiles, 1, lanes)
    tile_spec, row_spec, kv_spec = attend_specs(kv.shape[0], lanes, tiles // q.shape[0])
    return pl.pallas_call(
        functools.partial(attend_grad_body, nh, nb, hl, size),
        grid_spec=pltpu.PrefetchScalarGridSpec(
            num_scalar_prefetch=1,
            grid=(tiles,),
            in_specs=[tile_spec, tile_spec, tile_spec, kv_spec, row_spec],
            out_specs=[tile_spec, kv_spec],
            scratch_shapes=[pltpu.VMEM(kv.shape, F32)],
        ),
        out_shape=(jax.ShapeDtypeStruct(q.shape, BF16), jax.ShapeDtypeStruct(kv.shape, BF16)),
        name="attend_grad",
        compiler_params=pltpu.CompilerParams(vmem_limit_bytes=60 << 20),
    )(lengths, q, do, of, kv, lse)


class HeadSum:
    def __init__(self, nh, h, b, part, near, far, out, sems):
        self.nx = nh // 2
        self.x, self.c = h // 2, h % 2
        self.h, self.part, self.near, self.far, self.out = h, part, near, far, out
        sib = self.x * 2 + 1 - self.c
        self.pairs = [
            remote(
                part.at[((self.x + k) % self.nx) * 2 + 1 - self.c],
                near.at[k],
                sems.at[0, k],
                sems.at[1, k],
                sib,
                b,
            )
            for k in range(self.nx)
        ]
        self.across = [
            remote(
                out.at[k],
                far.at[k],
                sems.at[2, k],
                sems.at[3, k],
                ((self.x + k) % self.nx) * 2 + self.c,
                b,
            )
            for k in range(1, self.nx)
        ]

    @staticmethod
    def sem_shape(nh):
        return pltpu.SemaphoreType.DMA((4, nh // 2))

    @staticmethod
    def buffers(nh, rows, width):
        return [pltpu.VMEM((nh // 2, rows, width), BF16)] * 3

    def start(self):
        for k in list(range(1, self.nx)) + [0]:
            self.pairs[k].start()

    def send(self):
        for k in range(1, self.nx):
            self.pairs[k].wait_recv()
            at = ((self.x + k) % self.nx) * 2 + self.c
            self.out[k] = (self.part[at].astype(F32) + self.near[k].astype(F32)).astype(BF16)
            self.across[k - 1].start()

    def total(self):
        self.pairs[0].wait_recv()
        total = self.part[self.h].astype(F32) + self.near[0].astype(F32)
        for k in range(1, self.nx):
            self.across[k - 1].wait_recv()
            total = total + self.far[k].astype(F32)
        return total

    def finish(self):
        for cp in self.pairs:
            cp.wait_send()
        for cp in self.across:
            cp.wait_send()


def norm_of(values):
    centre = values - jnp.mean(values, axis=-1, keepdims=True)
    scale = lax.rsqrt(jnp.mean(centre * centre, axis=-1, keepdims=True) + NORM_EPS)
    return centre * scale, scale


def norm_pull(grad, normed, scale):
    one = jnp.mean(grad, axis=-1, keepdims=True)
    two = jnp.mean(grad * normed, axis=-1, keepdims=True)
    return scale * (grad - one - normed * two)


CHUNKS = 2


def chunk_of(ref, j, axis):
    size = ref.shape[axis] // CHUNKS
    at = pl.ds(j * size, size)
    return ref.at[at] if axis == 0 else ref.at[:, at]


def head_sums(nh, h, b, part, bufs, sems):
    near, far, out = bufs
    return [
        HeadSum(
            nh,
            h,
            b,
            chunk_of(part, j, 1),
            chunk_of(near, j, 1),
            chunk_of(far, j, 1),
            chunk_of(out, j, 1),
            sems.at[j],
        )
        for j in range(CHUNKS)
    ]


def head_gathers(nh, h, b, src, dst, sems):
    return [
        HeadGather(nh, h, b, chunk_of(src, j, 0), chunk_of(dst, j, 1), sems.at[j])
        for j in range(CHUNKS)
    ]


def chunk_sems(nh):
    return pltpu.SemaphoreType.DMA((CHUNKS, 4, nh // 2))


def mid_body(nh, nb, hl, io, o_ref, wo_ref, x_ref, wmb_ref, og, hid_ref, ng_ref, wmb_all, part, near, far, out, nbuf, osem, ssem, gsem, wsem):
    pc = Place(nh, nb, hl)
    h, b = pc.h, pc.b
    enter_with(pc, lambda zi: pc.attends(zi, h, pc.s % 2, pc.s // 2))
    rows, width = x_ref.shape
    outputs_back(pc, o_ref, og, osem, "start")
    sides = [
        remote(
            wmb_ref,
            wmb_all.at[:, :, pc.s],
            wsem.at[0, ds],
            wsem.at[1, ds],
            h,
            pc.zi * pc.qs + (pc.s + ds) % pc.qs,
        )
        for ds in range(1, pc.qs)
    ]
    sides.append(pltpu.make_async_copy(wmb_ref, wmb_all.at[:, :, pc.s], wsem.at[0, 0]))
    for cp in sides:
        cp.start()
    outputs_back(pc, o_ref, og, osem, "wait_send")
    for zi in range(pc.nz):
        wait_on(og.at[zi], osem.at[1, zi])
    io.put(0)
    io.need(1)
    wo = wo_ref[...]
    for i in range(nh):
        part[i] = lax.dot_general(
            og[:, i].reshape(pc.nz * DH, rows),
            wo,
            (((0,), (0,)), ((), ())),
            preferred_element_type=F32,
        ).astype(BF16)
    hss = head_sums(nh, h, b, part, (near, far, out), ssem)
    hgs = head_gathers(nh, h, b, nbuf, ng_ref, gsem)
    for hs in hss:
        hs.start()
    for hs in hss:
        hs.send()
    size = rows // CHUNKS
    io.need(2)
    for j, (hs, hg) in enumerate(zip(hss, hgs)):
        at = pl.ds(j * size, size)
        hid = x_ref[at, :].astype(F32) + hs.total()
        hid_ref[at, :] = hid
        nbuf[at, :] = norm_of(hid)[0].astype(BF16)
        hg.start()
    io.put(1)
    for hg in hgs:
        hg.pass_on()
    for hs, hg in zip(hss, hgs):
        hs.finish()
        hg.finish()
    for cp in sides:
        cp.wait()


def mid_exchange(ot, wo, x, wmb, hl):
    nh, nb = dims()
    rows, width = x.shape
    nz = hl
    return comm_call(
        functools.partial(mid_body, nh, nb, hl),
        "mid_exchange",
        2,
        (
            jax.ShapeDtypeStruct((nz, nh, DH, rows), BF16),
            jax.ShapeDtypeStruct(x.shape, F32),
            jax.ShapeDtypeStruct((nh, rows, width), BF16),
            jax.ShapeDtypeStruct((nh, nz, nb // nz) + wmb.shape[2:], BF16),
        ),
        [ANY] * 4,
        [ANY] * 4,
        [pltpu.VMEM((nh, rows, width), BF16)]
        + HeadSum.buffers(nh, rows, width)
        + [
            pltpu.VMEM((rows, width), BF16),
            pltpu.SemaphoreType.DMA((2, nz)),
            chunk_sems(nh),
            chunk_sems(nh),
            pltpu.SemaphoreType.DMA((2, nb // nz)),
        ],
        (ot, wo, x, wmb),
        vmem=60 << 20,
        late=(1, 2),
        early=(0, 1),
    )


def ffn_body(nh, nb, fl, split_rows, cut, len_ref, n_hbm, g_hbm, wa_hbm, wb_hbm, wc_hbm, y_hbm, d_hbm, ga_hbm, gb_hbm, n_ref, g_ref, w_ref, y_ref, d_ref, ga_ref, gb_ref, gy, mm, dz, stage, drain):
    rows, width = n_ref.shape[1], n_ref.shape[2]
    group = nh * rows
    total, zc, off = ff_widths(fl)
    wide = total - off
    shift = 2 * fl - off
    step = FF_BLOCKS * rows
    lane = lax.broadcasted_iota(jnp.int32, (1, wide), 1)
    real = lane < fl
    valid = sequence_ends(len_ref)[-1]
    blk = lax.axis_index("blk")
    loads = [
        pltpu.make_async_copy(n_hbm, n_ref, stage.at[0]),
        pltpu.make_async_copy(g_hbm, g_ref, stage.at[1]),
    ]
    for n, (w, (begin, end)) in enumerate(zip((wa_hbm, wb_hbm, wc_hbm), weight_parts(total))):
        dst = w_ref.at[:, pl.ds(begin, end - begin)]
        loads.append(pltpu.make_async_copy(w, dst, stage.at[2 + n]))
    for cp in loads:
        cp.start()
    for cp in loads:
        cp.wait()

    def out_rows(r):
        at = pl.ds(r * FF_BLOCKS, FF_BLOCKS)
        return [
            pltpu.make_async_copy(d_ref.at[at], d_hbm.at[at], drain.at[0, r]),
            pltpu.make_async_copy(y_ref.at[at], y_hbm.at[at], drain.at[1, r]),
        ]

    @pl.loop(0, group // step)
    def _(r):
        at = pl.ds(pl.multiple_of(r * step, step), step)
        n = n_ref[pl.ds(r * FF_BLOCKS, FF_BLOCKS)].reshape(step, width)
        row = lax.broadcasted_iota(jnp.int32, (step, 1), 0)
        slot = ((r * FF_BLOCKS + row // rows) * nb + blk) * rows + row % rows
        g = g_ref[pl.ds(r * FF_BLOCKS, FF_BLOCKS)].reshape(step, width)
        g = jnp.where(slot < valid, g.astype(F32), 0.0).astype(BF16)
        gy[at, :] = g
        z = jnp.dot(n, w_ref[:, :zc], preferred_element_type=F32)
        dm = lane_roll(jnp.dot(g, w_ref[:, off:], preferred_element_type=F32), -shift)
        gate, up = z[:, :wide], lane_roll(z, -fl)[:, :wide]
        cdf = 0.5 * (1.0 + lax.erf(gate * math.sqrt(0.5)))
        act = gate * cdf
        slope = cdf + gate * jnp.exp(-0.5 * gate * gate) * (1.0 / math.sqrt(2.0 * math.pi))
        m = lane_roll(jnp.where(real, act * up, 0.0), shift).astype(BF16)
        mm[at, :] = m
        d_gate = widen(jnp.where(real, dm * up * slope, 0.0), zc)
        d_up = lane_roll(widen(jnp.where(real, dm * act, 0.0), zc), fl)
        d = (d_gate + d_up).astype(BF16)
        dz[at, :] = d
        nt = (((1,), (1,)), ((), ()))
        dpart = lax.dot_general(d, w_ref[:, :zc], nt, preferred_element_type=F32)
        d_ref[pl.ds(r * FF_BLOCKS, FF_BLOCKS)] = dpart.astype(BF16).reshape(FF_BLOCKS, rows, width)
        ypart = lax.dot_general(m, w_ref[:, off:], nt, preferred_element_type=F32)
        y_ref[pl.ds(r * FF_BLOCKS, FF_BLOCKS)] = ypart.astype(BF16).reshape(FF_BLOCKS, rows, width)
        for cp in out_rows(r):
            cp.start()

    block = width // nh

    def out_block(i):
        at = (slice(None), i) if split_rows else (pl.ds(i * block, block),)
        return [
            pltpu.make_async_copy(ga_ref.at[i], ga_hbm.at[at], drain.at[2, i]),
            pltpu.make_async_copy(gb_ref.at[i], gb_hbm.at[at], drain.at[3, i]),
        ]

    @pl.loop(0, nh)
    def _(i):
        cols = pl.ds(pl.multiple_of(i * block, block), block)
        tn = (((0,), (0,)), ((), ()))
        n = n_ref[:, :, cols].reshape(group, block)
        g_in = lax.dot_general(n, dz[...], tn, preferred_element_type=F32)
        g_down = lax.dot_general(gy[:, cols], mm[...], tn, preferred_element_type=F32)
        both = jnp.concatenate(
            [g_in[:, :off], g_in[:, off:] + g_down[:, : zc - off], g_down[:, zc - off :]], axis=1
        ).astype(BF16)
        for ref, part in ((ga_ref, both[:, :cut]), (gb_ref, both[:, cut:])):
            if split_rows:
                part = part.reshape(nb, block // nb, part.shape[1])
            ref[i] = part
        for cp in out_block(i):
            cp.start()

    @pl.loop(0, nh)
    def _(i):
        for cp in out_block(i):
            cp.wait()

    @pl.loop(0, group // step)
    def _(r):
        for cp in out_rows(r):
            cp.wait()


def ffn(lengths, n2, g, weights, fl, own_rows, cut):
    nh, nb = dims()
    _, rows, width = n2.shape
    group = nh * rows
    total, zc, off = ff_widths(fl)
    split_rows = own_rows % 16 == 0
    lead = (nb, nh, own_rows) if split_rows else (width,)
    held = (nh, nb, own_rows) if split_rows else (nh, width // nh)
    return pl.pallas_call(
        functools.partial(ffn_body, nh, nb, fl, split_rows, cut),
        out_shape=(
            jax.ShapeDtypeStruct(n2.shape, BF16),
            jax.ShapeDtypeStruct(n2.shape, BF16),
            jax.ShapeDtypeStruct(lead + (cut,), BF16),
            jax.ShapeDtypeStruct(lead + (total - cut,), BF16),
        ),
        in_specs=[SM] + [ANY] * 5,
        out_specs=[ANY] * 4,
        scratch_shapes=[
            pltpu.VMEM(n2.shape, BF16),
            pltpu.VMEM(n2.shape, BF16),
            pltpu.VMEM((width, total), BF16),
            pltpu.VMEM(n2.shape, BF16),
            pltpu.VMEM(n2.shape, BF16),
            pltpu.VMEM(held + (cut,), BF16),
            pltpu.VMEM(held + (total - cut,), BF16),
            pltpu.VMEM((group, width), BF16),
            pltpu.VMEM((group, total - off), BF16),
            pltpu.VMEM((group, zc), BF16),
            pltpu.SemaphoreType.DMA((5,)),
            pltpu.SemaphoreType.DMA((4, nh)),
        ],
        name="ffn",
        compiler_params=pltpu.CompilerParams(vmem_limit_bytes=60 << 20),
    )(lengths, n2, g, *weights)


def back_body(nh, nb, hl, io, len_ref, dpart, ypart, hid_ref, g_ref, wo_ref, og_ref, gb_hbm, y_ref, dh_ref, do_in, go_ref, gb_out, n1, f1, o1, n2, f2, o2, dbuf, dg, dots, gb_ref, nearb, s1, s2, gsem, qsem, pb, stage):
    pc = Place(nh, nb, hl)
    h, b = pc.h, pc.b
    mine = pltpu.make_async_copy(gb_hbm.at[:, pc.s], gb_ref, stage)
    mine.start()
    enter_with(pc, lambda zi: (pc.head, zi * pc.qs + pc.from_s))
    pairs = [
        remote(
            gb_hbm.at[:, (pc.s + ds) % pc.qs],
            nearb.at[ds - 1],
            pb.at[0, ds],
            pb.at[1, ds],
            h,
            pc.zi * pc.qs + (pc.s + ds) % pc.qs,
        )
        for ds in range(1, pc.qs)
    ]
    rows, width = hid_ref.shape
    slot = (h * nb + b) * rows + lax.broadcasted_iota(jnp.int32, (rows, 1), 0)
    valid = slot < sequence_ends(len_ref)[-1]
    hds = head_sums(nh, h, b, dpart, (n1, f1, o1), s1)
    hy = HeadSum(nh, h, b, ypart, n2, f2, o2, s2)
    hgs = head_gathers(nh, h, b, dbuf, dg, gsem)
    io.need(1)
    for hd in hds:
        hd.start()
    for cp in pairs:
        cp.start()
    for hd in hds:
        hd.send()
    size = rows // CHUNKS
    io.need(3, 4)
    for j, (hd, hg) in enumerate(zip(hds, hgs)):
        at = pl.ds(j * size, size)
        normed, scale = norm_of(hid_ref[at, :])
        gy = jnp.where(valid[j * size : (j + 1) * size], g_ref[at, :].astype(F32), 0.0)
        dh = gy + norm_pull(hd.total(), normed, scale)
        dh_ref[at, :] = dh
        dbuf[at, :] = dh.astype(BF16)
        hg.start()
    io.put(1)
    io.need(2)
    hy.start()
    io.need(5)
    wo = wo_ref[...]
    nt = (((1,), (1,)), ((), ()))

    def emit(i):
        part = lax.dot_general(wo, dg[i], nt, preferred_element_type=F32).astype(BF16)
        dots[:, i] = part.reshape(pc.nz, DH, rows)
        grads_out(pc, dots, do_in, qsem, i, "start")

    nx = nh // 2
    for hg in hgs:
        hg.local.wait()
        hg.near.wait_recv()
    emit(h)
    emit(pc.sib)
    for hg in hgs:
        hg.pass_on()
    for k in range(1, nx):
        emit(((pc.x + nx - k) % nx) * 2 + pc.c)
    hy.send()
    for hg in hgs:
        for cp in hg.forward:
            cp.wait_recv()
    for k in range(1, nx):
        emit(((pc.x + nx - k) % nx) * 2 + 1 - pc.c)
    for hd, hg in zip(hds, hgs):
        hd.finish()
        hg.near.wait_send()
        for cp in hg.across + hg.forward:
            cp.wait_send()
    total = 0.0
    io.need(6)
    for i in range(nh):
        total = total + jnp.dot(
            og_ref[:, i].reshape(pc.nz * DH, rows), dg[i], preferred_element_type=F32
        )
    go_ref[...] = total.astype(BF16)
    io.put(3)
    y_ref[...] = jnp.where(valid, hid_ref[...] + hy.total(), 0.0)
    io.put(0)
    hy.finish()
    mine.wait()
    for cp in pairs:
        cp.wait()

    @pl.loop(0, pc.nz)
    def _(d):
        others = jnp.sum(nearb[:, d].astype(F32), axis=0)
        gb_out[d] = (gb_ref[d].astype(F32) + others).astype(BF16)

    io.put(4)

    @pl.loop(0, nh)
    def _(i):
        grads_out(pc, dots, do_in, qsem, i, "wait_send")
        for zi in range(pc.nz):
            wait_on(stretch_of(do_in, i, zi, rows), qsem.at[1, zi, i])


def back_exchange(lengths, dpart, ypart, hid, g, wo, og, gb):
    nh, nb = dims()
    rows, width = hid.shape
    nz = hl = og.shape[0]
    return comm_call(
        functools.partial(back_body, nh, nb, hl),
        "back_exchange",
        3,
        (
            jax.ShapeDtypeStruct(hid.shape, F32),
            jax.ShapeDtypeStruct(hid.shape, F32),
            jax.ShapeDtypeStruct((nh, DH, nz * rows), BF16),
            jax.ShapeDtypeStruct((nz * DH, width), BF16),
            jax.ShapeDtypeStruct(gb.shape[:1] + gb.shape[2:], BF16),
        ),
        [SM] + [VM] * 6 + [ANY],
        [VM, VM, ANY, VM, VM],
        HeadSum.buffers(nh, rows, width)
        + HeadSum.buffers(nh, rows, width)
        + [
            pltpu.VMEM((rows, width), BF16),
            pltpu.VMEM((nh, rows, width), BF16),
            pltpu.VMEM(og.shape, BF16),
            pltpu.VMEM(gb.shape[:1] + gb.shape[2:], BF16),
            pltpu.VMEM((gb.shape[1] - 1, nz) + gb.shape[2:], BF16),
            chunk_sems(nh),
            HeadSum.sem_shape(nh),
            chunk_sems(nh),
            pltpu.SemaphoreType.DMA((2, nz, nh)),
            pltpu.SemaphoreType.DMA((2, gb.shape[1])),
            pltpu.SemaphoreType.DMA,
        ],
        (lengths, dpart, ypart, hid, g, wo, og, gb),
        vmem=60 << 20,
        late=(1, 3, 4, 2, 5, 6),
        early=(0, 1, 3, 4),
    )


def grads_back_body(nh, nb, hl, io, dq_ref, dkv_ref, cos_ref, sin_ref, n1_hbm, w_hbm, go_ref, gb_ref, gq_ref, dpart, do_ref, gb_sum, got, sums, dq_out, dkv_out, dqkv, n1_ref, w_ref, nearo, sumo, goto, lsem, gotb, bsem, qsem, psem, ksem, stage, po):
    pc = Place(nh, nb, hl)
    loads = [
        pltpu.make_async_copy(n1_hbm, n1_ref, stage.at[0]),
        pltpu.make_async_copy(w_hbm, w_ref, stage.at[1]),
    ]
    for cp in loads:
        cp.start()
    signal_near(pc)
    wait_near(pc)
    rows = dkv_ref.shape[3]
    group = pc.nz * rows
    width = n1_ref.shape[1]
    lw = nh * DH
    count = nh * pc.cb

    def pair(k):
        src = dkv_ref.at[k // pc.cb, :, 2 * (k % pc.cb) + 1 - pc.c]
        return remote(src, got.at[k], psem.at[0, k], psem.at[1, k], pc.sib, pc.b)

    def back(k, act):
        routed(
            pc,
            sums.at[k],
            dkv_out.at[pc.head, pc.u],
            ksem.at[0, k],
            ksem.at[1, pc.head * pc.cb + pc.u],
            k // pc.cb,
            pc.zi * pc.qs + 2 * (k % pc.cb) + pc.c,
            act,
        )

    def queries_back(act):
        for i in range(nh):
            routed(
                pc,
                dq_ref.at[i],
                dq_out.at[pc.head],
                qsem.at[0, i],
                qsem.at[1, pc.head],
                i,
                pc.zi * pc.qs + pc.from_s,
                act,
            )

    pairs_o = [
        remote(
            go_ref.at[:, (pc.s + ds) % pc.qs],
            nearo.at[ds - 1],
            po.at[0, ds],
            po.at[1, ds],
            pc.h,
            pc.zi * pc.qs + (pc.s + ds) % pc.qs,
        )
        for ds in range(1, pc.qs)
    ]
    along_o = StretchSum(pc, sumo, goto, lsem)
    along_b = StretchSum(pc, gb_ref, gotb, bsem)

    io.need(1)

    @pl.loop(0, count)
    def _(k):
        pair(k).start()

    queries_back("start")
    io.need(6, 7)
    for cp in pairs_o:
        cp.start()
    along_b.start()

    @pl.loop(0, count)
    def _(k):
        pair(k).wait_recv()
        mine = dkv_ref[k // pc.cb, :, 2 * (k % pc.cb) + pc.c]
        sums[k] = (mine.astype(F32) + got[k].astype(F32)).astype(BF16)
        back(k, "start")

    for cp in pairs_o:
        cp.wait_recv()
    sumo[...] = (go_ref[:, pc.s].astype(F32) + jnp.sum(nearo[...].astype(F32), axis=0)).astype(BF16)
    along_o.start()
    io.need(2, 3)
    cos, sin = cos_ref[...], -sin_ref[...]
    for l in range(nh):
        wait_on(dq_out.at[l], qsem.at[1, l])
    for p in range(nh // 2):
        q = dq_out[2 * p : 2 * p + 2].reshape(2 * DH, group).astype(F32).T
        dqkv[:, p * 128 : (p + 1) * 128] = turned(q, cos, sin).astype(BF16)
    for l in range(nh):
        for u in range(pc.cb):
            wait_on(dkv_out.at[l, u], ksem.at[1, l * pc.cb + u])
    for p in range(nh // 2):
        even, odd = [
            jnp.sum(dkv_out[2 * p + i].astype(F32), axis=0).reshape(group, 2 * DH)
            for i in range(2)
        ]
        low = lanes_of(even) < DH
        k = jnp.where(low, even, lane_roll(odd, DH)).astype(BF16).astype(F32)
        v = jnp.where(low, lane_roll(even, DH), odd)
        dqkv[:, lw + p * 128 : lw + (p + 1) * 128] = turned(k, cos, sin).astype(BF16)
        dqkv[:, 2 * lw + p * 128 : 2 * lw + (p + 1) * 128] = v.astype(BF16)
    nt = (((1,), (1,)), ((), ()))
    tn = (((0,), (0,)), ((), ()))
    for cp in loads:
        cp.wait()

    @pl.loop(0, nh)
    def _(i):
        cols = pl.ds(pl.multiple_of(i * (width // nh), width // nh), width // nh)
        gq_ref[cols, :] = lax.dot_general(
            n1_ref[:, cols], dqkv[...], tn, preferred_element_type=F32
        ).astype(BF16)

    io.put(0)

    @pl.loop(0, pc.nz)
    def _(i):
        at = pl.ds(pl.multiple_of(i * rows, rows), rows)
        dpart[i] = lax.dot_general(
            dqkv[at, :], w_ref[...], nt, preferred_element_type=F32
        ).astype(BF16)

    io.put(1)

    @pl.loop(0, count)
    def _(k):
        pair(k).wait_send()
        back(k, "wait_send")

    queries_back("wait_send")
    do_ref[...] = along_o.total()
    io.put(2)
    gb_sum[...] = along_b.total().astype(BF16)
    io.put(3)
    along_o.finish()
    along_b.finish()
    for cp in pairs_o:
        cp.wait_send()


def grads_back(dq, dkv, cos, sin, n1, wq, go, gb, hl):
    nh, nb = dims()
    nz, qs = hl, nb // hl
    cb = qs // 2
    rows = dkv.shape[3]
    width = n1.shape[1]
    lw = nh * DH
    dma = pltpu.SemaphoreType.DMA
    return comm_call(
        functools.partial(grads_back_body, nh, nb, hl),
        "grads_back",
        4,
        (
            jax.ShapeDtypeStruct((width, 3 * lw), BF16),
            jax.ShapeDtypeStruct((nz, rows, width), BF16),
            jax.ShapeDtypeStruct(go.shape[2:], F32),
            jax.ShapeDtypeStruct(gb.shape[1:], BF16),
        ),
        [ANY, VM, VM, VM, ANY, ANY, VM, VM],
        [VM] * 4,
        [
            pltpu.VMEM((nh * cb, nz, rows, 2 * DH), BF16),
            pltpu.VMEM((nh * cb, nz, rows, 2 * DH), BF16),
            pltpu.VMEM(dq.shape, BF16),
            pltpu.VMEM((nh, cb, nz, rows, 2 * DH), BF16),
            pltpu.VMEM((nz * rows, 3 * lw), BF16),
            pltpu.VMEM(n1.shape, BF16),
            pltpu.VMEM(wq.shape, BF16),
            pltpu.VMEM((qs - 1, nz) + go.shape[2:], BF16),
            pltpu.VMEM((nz,) + go.shape[2:], BF16),
        ]
        + StretchSum.scratch(nz, go.shape[2:])
        + StretchSum.scratch(nz, gb.shape[1:])
        + [
            dma((2, nh)),
            dma((2, nh * cb)),
            dma((2, nh * cb)),
            dma((2,)),
            dma((2, qs)),
        ],
        (dq, dkv, cos, sin, n1, wq, go, gb),
        vmem=60 << 20,
        late=(1, 6, 7, 2, 3),
        early=(0, 1, 2, 3),
    )


def last_body(nh, nb, hl, io, dpart, gq_ref, gma_ref, gmb_ref, dn_ref, quarters, gma_all, gmb_all, nearq, sumq, farq, totq, sentz, gotz, zsem, pq, fq, cq, msem, asem):
    pc = Place(nh, nb, hl)
    h, b = pc.h, pc.b
    signal_near(pc)
    wait_near(pc)
    nx, nz, qs = nh // 2, pc.nz, pc.qs
    def pair_q(k):
        return remote(
            gq_ref.at[2 * k + 1 - pc.c], nearq.at[k], pq.at[0, k], pq.at[1, k], pc.sib, b
        )

    line = LineSum(pc, lambda d: dpart[d].astype(F32), sentz, gotz, zsem)

    def plane_q(i):
        tx, ts = (pc.x + i // qs) % nx, (pc.s + i % qs) % qs
        return remote(
            sumq.at[tx, :, ts],
            farq.at[pc.x, pc.s],
            fq.at[0, i],
            fq.at[1, i],
            tx * 2 + pc.c,
            pc.zi * qs + ts,
        )

    def quarter(i):
        to = (pc.zi + i) % nz
        return remote(
            totq.at[to], quarters.at[pc.zi], cq.at[0, i], cq.at[1, i], h, to * qs + pc.s
        )

    io.need(1)
    for k in range(nx):
        pair_q(k).start()
    io.need(0)
    line.lead(0)
    moves = [
        remote(
            gmb_ref.at[(h + i) % nh],
            gmb_all.at[h],
            msem.at[0, i],
            msem.at[1, i],
            (h + i) % nh,
            b,
        )
        for i in range(1, nh)
    ]
    moves.append(pltpu.make_async_copy(gmb_ref.at[h], gmb_all.at[h], msem.at[0, 0]))
    moves.append(
        pltpu.make_async_copy(gma_ref.at[pc.s, h], gma_all.at[pc.s, h], asem.at[0, 0])
    )

    def plane_move(i):
        th, ts = (h + i // qs) % nh, (pc.s + i % qs) % qs
        return remote(
            gma_ref.at[ts, th],
            gma_all.at[pc.s, h],
            asem.at[0, i],
            asem.at[1, i],
            th,
            pc.zi * qs + ts,
        )

    for k in range(nx):
        pair_q(k).wait_recv()
        sumq[k] = (gq_ref[2 * k + pc.c].astype(F32) + nearq[k].astype(F32)).astype(BF16)

    @pl.loop(1, nx * qs)
    def _(i):
        plane_q(i).start()

    farq[pc.x, pc.s] = sumq[pc.x, :, pc.s]
    for cp in moves:
        cp.start()

    @pl.loop(1, nh * qs)
    def _(i):
        plane_move(i).start()

    line.follow(0)
    line.lead(1)

    @pl.loop(1, nx * qs)
    def _(i):
        plane_q(i).wait_recv()

    totq[...] = jnp.sum(
        farq[...].astype(F32).reshape((nx * qs,) + totq.shape), axis=0
    ).astype(BF16)
    for i in range(1, nz):
        quarter(i).start()
    quarters[pc.zi] = totq[pc.zi]
    for j in range(1, nz - 1):
        line.follow(j)
        if j + 1 < nz - 1:
            line.lead(j + 1)
    line.total(dn_ref)
    io.put(0)
    line.finish()
    for i in range(1, nz):
        quarter(i).wait()
    io.put(1)
    for cp in moves:
        cp.wait()

    @pl.loop(1, nh * qs)
    def _(i):
        plane_move(i).wait()

    for k in range(nx):
        pair_q(k).wait_send()

    @pl.loop(1, nx * qs)
    def _(i):
        plane_q(i).wait_send()


def last_exchange(dpart, gq, gma, gmb):
    nh, nb = dims()
    nz, rows, width = dpart.shape
    qs = nb // nz
    own_rows, cols = gq.shape[3:]
    nx = nh // 2
    dma = pltpu.SemaphoreType.DMA
    return comm_call(
        functools.partial(last_body, nh, nb, nz),
        "last_exchange",
        5,
        (
            jax.ShapeDtypeStruct((rows, width), F32),
            jax.ShapeDtypeStruct((nz, own_rows, cols), BF16),
            jax.ShapeDtypeStruct(gma.shape, BF16),
            jax.ShapeDtypeStruct(gmb.shape, BF16),
        ),
        [VM] * 2 + [ANY] * 2,
        [VM] * 2 + [ANY] * 2,
        [
            pltpu.VMEM((nx, nz, qs, own_rows, cols), BF16),
            pltpu.VMEM((nx, nz, qs, own_rows, cols), BF16),
            pltpu.VMEM((nx, qs, nz, own_rows, cols), BF16),
            pltpu.VMEM((nz, own_rows, cols), BF16),
        ]
        + LineSum.scratch(nz, (rows, width))
        + [
            dma((2, nx)),
            dma((2, nx * qs)),
            dma((2, nz)),
            dma((2, nh)),
            dma((2, nh * qs)),
        ],
        (dpart, gq, gma, gmb),
        vmem=60 << 20,
        late=(1, 0),
        early=(0, 1),
    )


def finish_body(nh, fl, dn_ref, x_ref, dh_ref, y_in, quarters, do_in, gma, gmb, wq_ref, win_ref, ga_ref, gf_ref,
                y_ref, dx_ref, lna_ref, dq_ref, do_ref, lnm_ref, din_ref, dwd_ref):
    y_ref[...] = y_in[...]
    do_ref[...] = do_in[...]
    normed, scale = norm_of(x_ref[...].astype(F32))
    dx_ref[...] = dh_ref[...] + norm_pull(dn_ref[...], normed, scale)
    width = x_ref.shape[1]
    gain = column(ga_ref[...].astype(F32))
    nz = quarters.shape[0]
    rowsum = 0.0
    for c in range(3):
        for l in range(nh):
            src = (c * nh * DH + l // 2 * 128) // 128 * 128
            for p in range(nz // 2):
                tiles = [quarters[2 * p + i, :, src : src + 128].astype(F32) for i in range(2)]
                piece = half_pick(tiles[0], tiles[1], l % 2, l % 2)
                at = c * width + l * nz * DH + p * 128
                dq_ref[:, at : at + 128] = piece * gain
                rowsum = rowsum + jnp.sum(
                    piece * wq_ref[:, at : at + 128].astype(F32), axis=1, keepdims=True
                )
    lna_ref[...] = as_row(rowsum)
    ff = nh * fl
    total, _, _ = ff_widths(fl)
    tiles = lambda v: (v + 127) // 128 * 128
    gate_up, down = 0.0, 0.0
    for i in range(nh):
        first = jnp.sum(gma[:, i].astype(F32), axis=0)
        piece = jnp.concatenate([first, gmb[i].astype(F32)], axis=1)
        lane = lanes_of(piece)
        gate = widen(jnp.where(lane < fl, piece, 0.0), tiles(2 * ff))
        up = jnp.where(jnp.logical_and(lane >= fl, lane < 2 * fl), piece, 0.0)
        up = widen(up, tiles(2 * ff))
        gate_up = gate_up + lane_roll(gate, i * fl) + lane_roll(up, ff - fl + i * fl)
        dn = jnp.where(jnp.logical_and(lane >= 2 * fl, lane < 3 * fl), piece, 0.0)
        down = down + lane_roll(widen(dn, max(total, tiles(ff))), i * fl - 2 * fl)
    gate_up = gate_up[:, : 2 * ff]
    dwd_ref[...] = down[:, :ff]
    din_ref[...] = gate_up * column(gf_ref[...].astype(F32))
    lnm_ref[...] = as_row(jnp.sum(gate_up * win_ref[...].astype(F32), axis=1, keepdims=True))


def finish(dn, x, dh, y, quarters, d_wout, gma, gmb, w_qkv, w_in, gain_attn, gain_mlp, fl):
    nh, _ = dims()
    rows, width = x.shape
    own_rows = w_qkv.shape[0]
    ff = nh * fl
    f32 = lambda *shape: jax.ShapeDtypeStruct(shape, F32)
    return pl.pallas_call(
        functools.partial(finish_body, nh, fl),
        out_shape=(
            f32(rows, width),
            f32(rows, width),
            f32(1, own_rows),
            f32(own_rows, 3 * width),
            f32(own_rows, width),
            f32(1, own_rows),
            f32(own_rows, 2 * ff),
            f32(own_rows, ff),
        ),
        in_specs=[VM] * 12,
        out_specs=[VM] * 8,
        name="finish",
        compiler_params=pltpu.CompilerParams(vmem_limit_bytes=60 << 20),
    )(dn, x, dh, y, quarters, d_wout, gma, gmb, w_qkv, w_in, gain_attn, gain_mlp)


def shards(layer_input, out_grad, lengths, ln_attn, w_qkv, w_attn_out, ln_mlp, w_in, w_mlp_out):
    nh, nb = dims()
    h, b = me()
    rows, width = layer_input.shape
    heads = width // DH
    hl = heads // nh
    group = nh * rows
    slots = nh * nb * rows
    own_rows = w_qkv.shape[0]
    ff = w_mlp_out.shape[0]
    fl = ff // nh
    nz, qs = hl, nb // hl
    lw = nh * DH

    gain_attn = ln_attn.reshape(1, own_rows)
    gain_mlp = ln_mlp.reshape(1, own_rows)
    n1, wma, wmb, wmc, wq, gg, cos, sin = first_exchange(
        lengths, layer_input, w_qkv, gain_attn, w_in, gain_mlp, w_mlp_out.T, out_grad, hl, fl
    )
    wma = lax.all_gather(wma, "blk", axis=1, tiled=True).reshape(width, -1)
    wq = wq.reshape(width, 3 * lw)
    n1 = n1.reshape(group, width)
    qin, kvin, wo, wmb, wmc = to_heads(n1, wq, cos, sin, w_attn_out[None], wmb, wmc, hl)
    wo = wo.reshape(nz * DH, width)
    kv_all = kvin.reshape(slots, 2 * DH)
    ot, of, lse = attend(lengths, qin, kv_all, 4 * rows, 1024, hl)
    og, hid, n2, wmc = mid_exchange(ot, wo, layer_input, wmc, hl)
    weights = [w.reshape(width, -1) for w in (wma, wmb, wmc)]
    ypart, dpart, gma, gmb = ffn(lengths, n2, gg, weights, fl, own_rows, GRAD_CUT)
    by_owner = []
    for gm in (gma, gmb):
        if gm.ndim == 4:
            gm = gm.reshape((nz, qs) + gm.shape[1:])
        else:
            gm = gm.reshape(nh, nz, qs, own_rows, gm.shape[1]).transpose(1, 2, 0, 3, 4)
        by_owner.append(gm)
    gma, gmb = by_owner
    lines = [[zi * qs + s for zi in range(nz)] for s in range(qs)]
    gma = lax.psum_scatter(
        gma, "blk", scatter_dimension=0, tiled=True, axis_index_groups=lines
    ).reshape(gma.shape[1:])
    y_out, dh, do_in, go, gmb = back_exchange(
        lengths, dpart, ypart, hid, out_grad, wo, og, gmb
    )
    dq, dkv = attend_grad(lengths, qin, do_in, of, kv_all, lse, 2 * rows, 1024, hl)
    go = go.reshape(nz, qs, own_rows, width)
    gq, dpart1, d_wout, gmb = grads_back(
        dq, dkv.reshape(kvin.shape), cos, sin, n1, wq, go, gmb, hl
    )
    dn, quarters, gma, gmb = last_exchange(
        dpart1, gq.reshape(nh, nz, qs, own_rows, 3 * lw), gma, gmb
    )
    y_out, dx, d_ln_attn, d_wqkv, d_wout, d_ln_mlp, d_win, d_wd = finish(
        dn,
        layer_input,
        dh,
        y_out,
        quarters,
        d_wout,
        gma,
        gmb,
        w_qkv,
        w_in,
        gain_attn,
        gain_mlp,
        fl,
    )
    return (
        y_out,
        dx,
        d_ln_attn.reshape(own_rows),
        d_wqkv,
        d_wout,
        d_ln_mlp.reshape(own_rows),
        d_win,
        d_wd.T,
    )


def solution(mesh):
    both = ("head", "blk")
    row_split = P(both, None)
    return jax.shard_map(
        shards,
        mesh=mesh,
        in_specs=(
            row_split,
            row_split,
            P(),
            P(both),
            row_split,
            row_split,
            P(both),
            row_split,
            P(None, both),
        ),
        out_specs=(
            row_split,
            row_split,
            P(both),
            row_split,
            row_split,
            P(both),
            row_split,
            P(None, both),
        ),
        check_vma=False,
    )
```

```python
import functools
import math

import jax
import jax.numpy as jnp
from jax import lax
from jax.experimental import pallas as pl
from jax.experimental.pallas import tpu as pltpu
from jax.sharding import PartitionSpec as P

DH = 64
ROPE_BASE = 160000.0
NORM_EPS = 1e-05
MASK_FLOOR = -1e30
GRAD_CUT = 1152
FF_BLOCKS = 2
WEIGHT_CUTS = (1280, 1408)
EXP_SCALE = 0.125 * math.log2(math.e)
BF16 = jnp.bfloat16
F32 = jnp.float32
MESH_ID = pl.DeviceIdType.MESH
ANY = pl.BlockSpec(memory_space=pl.ANY)
VM = pl.BlockSpec(memory_space=pltpu.VMEM)
SM = pl.BlockSpec(memory_space=pltpu.SMEM)


def dims():
    nh = lax.axis_size("head")
    nb = lax.axis_size("blk")
    return nh, nb


def me():
    return lax.axis_index("head"), lax.axis_index("blk")


class Staged:
    def __init__(self, loads, drains):
        self.loads, self.drains = loads, drains

    def need(self, *which):
        for i in which:
            self.loads[i].wait()

    def put(self, *which):
        for i in which:
            self.drains[i].start()


def comm_call(body, name, cid, out_shape, in_specs, out_specs, scratch, args, vmem=None, late=(), early=()):
    n_in, n_out, n_late, n_early = len(args), len(out_shape), len(late), len(early)
    in_specs = [ANY if i in late else spec for i, spec in enumerate(in_specs)]
    out_specs = [ANY if i in early else spec for i, spec in enumerate(out_specs)]
    held = [pltpu.VMEM(args[i].shape, args[i].dtype) for i in late]
    held += [pltpu.VMEM(out_shape[i].shape, out_shape[i].dtype) for i in early]
    held.append(pltpu.SemaphoreType.DMA((max(n_late + n_early, 1),)))

    def staged_body(*refs):
        ins, outs = list(refs[:n_in]), list(refs[n_in : n_in + n_out])
        bufs = refs[n_in + n_out : n_in + n_out + n_late + n_early]
        sems = refs[n_in + n_out + n_late + n_early]
        rest = refs[n_in + n_out + n_late + n_early + 1 :]
        loads, drains = {}, {}
        for k, i in enumerate(late):
            loads[i] = pltpu.make_async_copy(ins[i], bufs[k], sems.at[k])
            loads[i].start()
            ins[i] = bufs[k]
        for k, i in enumerate(early):
            k += n_late
            drains[i] = pltpu.make_async_copy(bufs[k], outs[i], sems.at[k])
            outs[i] = bufs[k]
        body(Staged(loads, drains), *ins, *outs, *rest)
        for cp in drains.values():
            cp.wait()

    return pl.pallas_call(
        staged_body,
        out_shape=out_shape,
        in_specs=in_specs,
        out_specs=out_specs,
        scratch_shapes=held + list(scratch),
        name=name,
        compiler_params=pltpu.CompilerParams(
            collective_id=cid, has_side_effects=True, vmem_limit_bytes=vmem
        ),
    )(*args)


def remote(src, dst, send, recv, h, b):
    return pltpu.make_async_remote_copy(
        src_ref=src,
        dst_ref=dst,
        send_sem=send,
        recv_sem=recv,
        device_id=(h, b),
        device_id_type=MESH_ID,
    )


def signal(h, b):
    pl.semaphore_signal(
        pltpu.get_barrier_semaphore(), inc=1, device_id=(h, b), device_id_type=MESH_ID
    )


class HeadGather:
    def __init__(self, nh, h, b, src, dst, sems):
        self.nh, self.h, self.b, self.dst, self.sems = nh, h, b, dst, sems
        nx = nh // 2
        self.nx = nx
        x, c = h // 2, h % 2
        sib = x * 2 + 1 - c
        self.sib = sib
        self.across = []
        for k in range(1, nx):
            self.across.append(
                remote(src, dst.at[h], sems.at[0, k], sems.at[1, k], ((x + k) % nx) * 2 + c, b)
            )
        self.near = remote(src, dst.at[h], sems.at[0, 0], sems.at[1, 0], sib, b)
        self.local = pltpu.make_async_copy(src, dst.at[h], sems.at[2, 0])
        self.forward = []
        for k in range(1, nx):
            got = ((x + nx - k) % nx) * 2 + c
            self.forward.append(
                remote(dst.at[got], dst.at[got], sems.at[2, k], sems.at[3, k], sib, b)
            )

    @staticmethod
    def sem_shape(nh):
        return pltpu.SemaphoreType.DMA((4, nh // 2))

    def start(self):
        for cp in self.across:
            cp.start()
        self.near.start()
        self.local.start()

    def pass_on(self):
        for cp, fw in zip(self.across, self.forward):
            cp.wait_recv()
            fw.start()

    def finish(self):
        for cp in self.across:
            cp.wait_send()
        self.near.wait()
        self.local.wait()
        for fw in self.forward:
            fw.wait()


def lane_roll(values, shift):
    return pltpu.roll(values, shift % values.shape[1], 1)


def lanes_of(values):
    return lax.broadcasted_iota(jnp.int32, (1, values.shape[1]), 1)


def widen(values, width):
    extra = width - values.shape[1]
    if extra <= 0:
        return values[:, :width]
    return jnp.concatenate([values, jnp.zeros((values.shape[0], extra), values.dtype)], axis=1)


def weight_parts(total):
    marks = (0,) + WEIGHT_CUTS + (total,)
    return list(zip(marks[:-1], marks[1:]))


def column(row):
    n = row.shape[1]
    same = lax.broadcasted_iota(jnp.int32, (n, n), 0) == lax.broadcasted_iota(jnp.int32, (n, n), 1)
    return jnp.sum(jnp.where(same, row, 0.0), axis=1, keepdims=True)


def as_row(col):
    n = col.shape[0]
    same = lax.broadcasted_iota(jnp.int32, (n, n), 0) == lax.broadcasted_iota(jnp.int32, (n, n), 1)
    return jnp.sum(jnp.where(same, col, 0.0), axis=0, keepdims=True)


def sequence_ends(len_ref):
    ends, total = [], 0
    for i in range(len_ref.shape[0]):
        total = total + len_ref[i]
        ends.append(total)
    return ends


def segment_first(slot, ends):
    first = jnp.zeros_like(slot)
    for end in ends:
        first = jnp.where(slot >= end, end, first)
    return first


def segment_end(slot, ends, slots):
    last = jnp.zeros_like(slot) + slots
    for end in reversed(ends):
        last = jnp.where(slot < end, end, last)
    return last


def half_pick(low_src, high_src, low_at, high_at):
    low = low_src if low_at == 0 else lane_roll(low_src, DH)
    high = high_src if high_at == 1 else lane_roll(high_src, DH)
    return jnp.where(lanes_of(low) < DH, low, high)


def ff_widths(fl):
    up = lambda v: (v + 127) // 128 * 128
    return up(3 * fl), up(2 * fl), 2 * fl // 128 * 128


class LineGather:
    def __init__(self, pc, src, place, sems):
        self.pc, self.src, self.place, self.sems = pc, src, place, sems

    @staticmethod
    def sem_shape(nz):
        return pltpu.SemaphoreType.DMA((5, nz))

    def origin(self, t, up):
        return self.pc.zi - t if up else self.pc.zi + t

    def move(self, t, up):
        pc = self.pc
        at = self.place(self.origin(t, up))
        n = 0 if up else 2
        return remote(
            self.src if t == 0 else at,
            at,
            self.sems.at[n, t],
            self.sems.at[n + 1, t],
            pc.h,
            pc.b + pc.qs if up else pc.b - pc.qs,
        )

    def sends(self, t, up):
        zi, nz = self.pc.zi, self.pc.nz
        if up:
            return jnp.logical_and(zi - t >= 0, zi + 1 < nz)
        return jnp.logical_and(zi + t < nz, zi - 1 >= 0)

    def local(self):
        return pltpu.make_async_copy(self.src, self.place(self.pc.zi), self.sems.at[4, 0])

    def start(self):
        for up in (True, False):

            @pl.when(self.sends(0, up))
            def _():
                self.move(0, up).start()

        self.local().start()

    def step(self, t, arrived=None):
        low = self.pc.zi < self.pc.nz // 2
        self.take(t, False, jnp.logical_not(low), arrived)
        self.take(t, True, True, arrived)
        self.take(t, False, low, arrived)

    def take(self, t, up, now, arrived):
        zi, nz = self.pc.zi, self.pc.nz
        origin = self.origin(t, up)
        here = jnp.logical_and(now, origin >= 0 if up else origin < nz)

        @pl.when(here)
        def _():
            wait_on(self.place(origin), self.sems.at[1 if up else 3, t - 1])

        if t < nz - 1:

            @pl.when(jnp.logical_and(now, self.sends(t, up)))
            def _():
                self.move(t, up).start()

        if arrived is not None:

            @pl.when(here)
            def _():
                arrived(origin)

    def finish(self):
        self.local().wait()
        for t in range(self.pc.nz - 1):
            for up in (True, False):

                @pl.when(self.sends(t, up))
                def _():
                    self.move(t, up).wait_send()


class BlkGather:
    def __init__(self, pc, src, out, sems, ssem):
        self.pc, self.out, self.ssem, self.src = pc, out, ssem, src
        self.line = LineGather(pc, src, lambda zi: out.at[:, zi, pc.s], sems)

    @staticmethod
    def sem_shapes(nz, qs):
        return [LineGather.sem_shape(nz), pltpu.SemaphoreType.DMA((2, nz, qs))]

    def side(self, zi, ds, own=False):
        pc = self.pc
        ref = self.out.at[:, zi, pc.s]
        return remote(
            self.src if own else ref,
            ref,
            self.ssem.at[0, zi, ds],
            self.ssem.at[1, zi, ds],
            pc.h,
            pc.zi * pc.qs + (pc.s + ds) % pc.qs,
        )

    def spread(self, zi, own=False):
        for ds in range(1, self.pc.qs):
            self.side(zi, ds, own).start()

    def start(self):
        self.line.start()
        self.spread(self.pc.zi, True)

    def step(self, t):
        self.line.step(t, self.spread)

    def finish(self):
        self.line.finish()

        @pl.loop(0, self.pc.nz)
        def _(zi):
            for ds in range(1, self.pc.qs):
                self.side(zi, ds).wait()


class LineSum:
    def __init__(self, pc, term, sent, got, sems):
        self.pc, self.term, self.sent, self.got, self.sems = pc, term, sent, got, sems

    @staticmethod
    def scratch(nz, shape):
        return [
            pltpu.VMEM((2, nz) + shape, BF16),
            pltpu.VMEM((2, nz) + shape, BF16),
            pltpu.SemaphoreType.DMA((4, nz)),
        ]

    def move(self, d, up):
        pc = self.pc
        n = 0 if up else 1
        return remote(
            self.sent.at[n, d],
            self.got.at[n, d],
            self.sems.at[2 * n, d],
            self.sems.at[2 * n + 1, d],
            pc.h,
            pc.b + pc.qs if up else pc.b - pc.qs,
        )

    def takes(self, up):
        return self.pc.zi > 0 if up else self.pc.zi < self.pc.nz - 1

    def lead(self, j):
        self.step(j, False)

    def follow(self, j):
        self.step(j, True)

    def step(self, j, taking):
        low = self.pc.zi < self.pc.nz // 2
        if taking:
            self.one(j, False, jnp.logical_not(low), True)
            self.one(j, True, True, True)
            self.one(j, False, low, True)
        else:
            self.one(j, True, True, False)
            self.one(j, False, True, False)

    def one(self, j, up, now, taking):
        zi, nz = self.pc.zi, self.pc.nz
        d = nz - 1 - j if up else j
        n = 0 if up else 1
        takes = self.takes(up)
        far = jnp.logical_and(now, zi < d if up else zi > d)

        @pl.when(jnp.logical_and(far, takes if taking else jnp.logical_not(takes)))
        def _():
            if taking:
                wait_on(self.got.at[n, d], self.sems.at[2 * n + 1, d])
                self.sent[n, d] = (self.term(d) + self.got[n, d].astype(F32)).astype(BF16)
            else:
                self.sent[n, d] = self.term(d).astype(BF16)
            self.move(d, up).start()

    def total(self, total_ref):
        zi = self.pc.zi
        total_ref[...] = self.term(zi)
        for up in (True, False):
            n = 0 if up else 1

            @pl.when(self.takes(up))
            def _():
                wait_on(self.got.at[n, zi], self.sems.at[2 * n + 1, zi])
                total_ref[...] += self.got[n, zi].astype(F32)

    def finish(self):
        zi, nz = self.pc.zi, self.pc.nz
        for j in range(nz - 1):
            for up in (True, False):
                d = nz - 1 - j if up else j

                @pl.when(zi < d if up else zi > d)
                def _():
                    self.move(d, up).wait_send()


class StretchSum:
    def __init__(self, pc, part, got, sems):
        self.pc, self.part, self.got, self.sems = pc, part, got, sems

    @staticmethod
    def scratch(nz, shape):
        return [pltpu.VMEM((nz,) + shape, BF16), pltpu.SemaphoreType.DMA((2, nz))]

    def move(self, i):
        pc = self.pc
        to = (pc.zi + i) % pc.nz
        return remote(
            self.part.at[to],
            self.got.at[pc.zi],
            self.sems.at[0, i],
            self.sems.at[1, i],
            pc.h,
            to * pc.qs + pc.s,
        )

    def start(self):
        for i in range(1, self.pc.nz):
            self.move(i).start()

    def total(self):
        pc = self.pc
        total = self.part[pc.zi].astype(F32)
        for i in range(1, pc.nz):
            self.move(i).wait_recv()
            total = total + self.got[(pc.zi + pc.nz - i) % pc.nz].astype(F32)
        return total

    def finish(self):
        for i in range(1, self.pc.nz):
            self.move(i).wait_send()


class PlaneWeights:
    def __init__(self, pc, pack, out, sems, ksem):
        self.pc, self.pack, self.out, self.sems, self.ksem = pc, pack, out, sems, ksem

    @staticmethod
    def sem_shapes(nh, nz, qs):
        dma = pltpu.SemaphoreType.DMA
        return [dma((2, nz)), dma((4, nh // 2 * qs))]

    def along(self, i):
        pc = self.pc
        to = (pc.zi + i) % pc.nz
        return remote(
            self.pack.at[to],
            self.out.at[pc.h, pc.zi, pc.s],
            self.sems.at[0, i],
            self.sems.at[1, i],
            pc.h,
            to * pc.qs + pc.s,
        )

    def local(self):
        pc = self.pc
        return pltpu.make_async_copy(
            self.pack.at[pc.zi], self.out.at[pc.h, pc.zi, pc.s], self.sems.at[0, 0]
        )

    def place(self, i, sign):
        pc = self.pc
        nx = pc.nh // 2
        dx, ds = i // pc.qs, i % pc.qs
        if sign < 0:
            dx, ds = nx - dx, pc.qs - ds
        return ((pc.x + dx) % nx) * 2 + pc.c, (pc.s + ds) % pc.qs

    def across(self, i):
        pc = self.pc
        th, ts = self.place(i, 1)
        ref = self.out.at[pc.h, :, pc.s]
        return remote(
            ref, ref, self.ksem.at[0, i], self.ksem.at[1, i], th, pc.zi * pc.qs + ts
        )

    def near(self, i):
        pc = self.pc
        gh, gs = self.place(i, -1)
        ref = self.out.at[gh, :, gs]
        return remote(ref, ref, self.ksem.at[2, i], self.ksem.at[3, i], pc.sib, pc.b)

    def start(self):
        for i in range(1, self.pc.nz):
            self.along(i).start()
        self.local().start()

    def spread(self):
        pc = self.pc
        self.local().wait()
        for i in range(1, pc.nz):
            self.along(i).wait_recv()

        @pl.loop(1, pc.nh // 2 * pc.qs)
        def _(i):
            self.across(i).start()

        self.near(0).start()

    def pass_on(self):
        @pl.loop(1, self.pc.nh // 2 * self.pc.qs)
        def _(i):
            self.across(i).wait_recv()
            self.near(i).start()

    def finish(self):
        for i in range(1, self.pc.nz):
            self.along(i).wait_send()

        @pl.loop(1, self.pc.nh // 2 * self.pc.qs)
        def _(i):
            self.across(i).wait_send()

        @pl.loop(0, self.pc.nh // 2 * self.pc.qs)
        def _(i):
            self.near(i).wait()


def first_body(nh, nb, hl, fl, io, len_ref, x_ref, wq_ref, ga_ref, win_hbm, gf_ref, wd_hbm, g_ref, n1_all, wma, wmb, wmc, wq_all, gg, cos_ref, sin_ref, own_n, pack, wmp, win_ref, wd_ref, lsem, wsem, ksem, gsem, msem, stage):
    pc = Place(nh, nb, hl)
    h, b = pc.h, pc.b
    loads = [
        pltpu.make_async_copy(win_hbm, win_ref, stage.at[0]),
        pltpu.make_async_copy(wd_hbm, wd_ref, stage.at[1]),
    ]
    for cp in loads:
        cp.start()
    signal_near(pc)
    width = x_ref.shape[1]
    lw = width // pc.nz
    gain = column(ga_ref[...].astype(F32))
    io.need(2)
    for c in range(3):
        w = wq_ref[:, c * width : (c + 1) * width].astype(F32) * gain
        tile = lambda l, i: w[:, l * pc.nz * DH + i // 2 * 128 : l * pc.nz * DH + i // 2 * 128 + 128]
        for i in range(pc.nz):
            for p in range(nh // 2):
                both = half_pick(tile(2 * p, i), tile(2 * p + 1, i), i % 2, i % 2)
                at = c * lw + p * 128
                pack[i, :, at : at + 128] = both.astype(BF16)
    io.need(1)
    own_n[...] = norm_of(x_ref[...].astype(F32))[0].astype(BF16)
    wait_near(pc)
    weights = PlaneWeights(pc, pack, wq_all, wsem, ksem)
    line = LineGather(pc, own_n, lambda zi: n1_all.at[zi], lsem)
    gather = HeadGather(nh, h, b, g_ref, gg, gsem)
    weights.start()
    line.start()
    gather.start()
    for cp in loads:
        cp.wait()
    total = ff_widths(fl)[0]
    ff = nh * fl
    win = win_ref[...].astype(F32) * column(gf_ref[...].astype(F32))
    wd = widen(wd_ref[...].astype(F32), total if total > ff else (ff + 127) // 128 * 128)
    lane = lax.broadcasted_iota(jnp.int32, (1, total), 1)
    for i in range(nh):
        gate = widen(lane_roll(win, -i * fl), total)
        up = widen(lane_roll(win, fl - ff - i * fl), total)
        down = widen(lane_roll(wd, 2 * fl - i * fl), total)
        piece = jnp.where(
            lane < fl,
            gate,
            jnp.where(lane < 2 * fl, up, jnp.where(lane < 3 * fl, down, 0.0)),
        )
        wmp[i] = piece.astype(BF16)
    copies = []
    for n, (dst, (begin, end)) in enumerate(zip((wma, wmb, wmc), weight_parts(total))):
        cols = pl.ds(begin, end - begin)
        for i in range(1, nh):
            th = (h + i) % nh
            src = wmp.at[th, :, cols]
            copies.append(remote(src, dst.at[h], msem.at[0, n, i], msem.at[1, n, i], th, b))
        copies.append(pltpu.make_async_copy(wmp.at[h, :, cols], dst.at[h], msem.at[0, n, 0]))
    weights.spread()
    for cp in copies:
        cp.start()
    ends = sequence_ends(len_ref)
    rows = x_ref.shape[0]
    lane = lax.broadcasted_iota(jnp.int32, (1, 2 * DH), 1)
    power = (lane % (DH // 2)).astype(F32) * (-2.0 / DH)
    inv_freq = jnp.exp2(power * math.log2(ROPE_BASE))
    sign = jnp.where(lane % DH < DH // 2, -1.0, 1.0)
    line.step(1)
    for i in range(pc.nz):
        slot = (h * nb + i * pc.qs + pc.s) * rows + lax.broadcasted_iota(jnp.int32, (rows, 1), 0)
        angle = (slot - segment_first(slot, ends)).astype(F32) * inv_freq
        cos_ref[i * rows : (i + 1) * rows, :] = jnp.cos(angle)
        sin_ref[i * rows : (i + 1) * rows, :] = jnp.sin(angle) * sign
    io.put(6, 7)
    gather.pass_on()
    for t in range(2, pc.nz):
        line.step(t)
    weights.pass_on()
    for cp in copies:
        cp.wait()
    weights.finish()
    line.finish()
    gather.finish()


def first_exchange(lengths, x, w_qkv, gain_attn, w_in, gain_mlp, wd_t, g, hl, fl):
    nh, nb = dims()
    rows, width = x.shape
    nz, qs = hl, nb // hl
    lw = width // nz
    own_rows = w_in.shape[0]
    total = ff_widths(fl)[0]
    dma = pltpu.SemaphoreType.DMA
    return comm_call(
        functools.partial(first_body, nh, nb, hl, fl),
        "first_exchange",
        0,
        (
            jax.ShapeDtypeStruct((nz, rows, width), BF16),
            *[
                jax.ShapeDtypeStruct((nh, own_rows, end - begin), BF16)
                for begin, end in weight_parts(total)
            ],
            jax.ShapeDtypeStruct((nh, nz, qs, own_rows, 3 * lw), BF16),
            jax.ShapeDtypeStruct((nh, rows, width), BF16),
            jax.ShapeDtypeStruct((nz * rows, 2 * DH), F32),
            jax.ShapeDtypeStruct((nz * rows, 2 * DH), F32),
        ),
        [SM, VM, VM, VM, ANY, VM, ANY, ANY],
        [ANY] * 6 + [VM] * 2,
        [
            pltpu.VMEM((rows, width), BF16),
            pltpu.VMEM((nz, own_rows, 3 * lw), BF16),
            pltpu.VMEM((nh, own_rows, total), BF16),
            pltpu.VMEM(w_in.shape, BF16),
            pltpu.VMEM(wd_t.shape, BF16),
            LineGather.sem_shape(nz),
        ]
        + PlaneWeights.sem_shapes(nh, nz, qs)
        + [
            HeadGather.sem_shape(nh),
            dma((2, 3, nh)),
            dma((2,)),
        ],
        (lengths, x, w_qkv, gain_attn, w_in, gain_mlp, wd_t, g),
        vmem=60 << 20,
        late=(2, 1),
        early=(6, 7),
    )


class Place:
    def __init__(self, nh, nb, hl):
        h, b = me()
        self.nh, self.nb, self.h, self.b = nh, nb, h, b
        self.x, self.c = h // 2, h % 2
        self.nz = hl
        self.qs = nb // hl
        self.cb = self.qs // 2
        self.sib = self.x * 2 + 1 - self.c
        self.zi, self.s = b // self.qs, b % self.qs
        self.head = self.x * 2 + self.s // self.cb
        self.u = self.s % self.cb
        self.from_s = self.u * 2 + self.c

    def attends(self, zi, l, core, u):
        return (l // 2) * 2 + core, zi * self.qs + (l % 2) * self.cb + u


def signal_near(pc):
    here = pc.nh * pc.qs

    @pl.loop(1, here)
    def _(i):
        signal((pc.h + i // pc.qs) % pc.nh, pc.zi * pc.qs + (pc.s + i % pc.qs) % pc.qs)

    @pl.loop(1, pc.nz)
    def _(i):
        signal(pc.h, (pc.zi + i) % pc.nz * pc.qs + pc.s)


def wait_near(pc, more=0):
    pl.semaphore_wait(pltpu.get_barrier_semaphore(), pc.nh * pc.qs + pc.nz - 2 + more)


def enter_with(pc, source):
    signal_near(pc)
    for i in range(1, pc.nz):
        signal(*source((pc.zi + i) % pc.nz))
    wait_near(pc, pc.nz - 1)


def routed(pc, src, dst, send, recv, th, tb, act):
    mine = jnp.logical_and(th == pc.h, tb == pc.b)

    @pl.when(mine)
    def _():
        if act == "start":
            pltpu.make_async_copy(src, dst, recv).start()

    @pl.when(jnp.logical_not(mine))
    def _():
        cp = remote(src, dst, send, recv, th, tb)
        if act == "start":
            cp.start()
        else:
            cp.wait_send()


def wait_on(ref, sem):
    pltpu.make_async_copy(ref, ref, sem).wait()


def stretch_lanes(ref, zi, rows):
    return ref.at[:, :, pl.ds(pl.multiple_of(zi * rows, rows), rows)]


def outputs_back(pc, o_ref, og, osem, act):
    rows = og.shape[3]
    for zi in range(pc.nz):
        routed(
            pc,
            stretch_lanes(o_ref, zi, rows),
            og.at[pc.zi],
            osem.at[0, zi],
            osem.at[1, pc.zi],
            pc.head,
            zi * pc.qs + pc.from_s,
            act,
        )


def grads_out(pc, dots, do_in, qsem, i, act):
    rows = dots.shape[3]
    for zi in range(pc.nz):
        th, tb = pc.attends(zi, pc.h, pc.s % 2, pc.s // 2)
        routed(
            pc,
            dots.at[zi, i],
            stretch_of(do_in, i, pc.zi, rows),
            qsem.at[0, zi, i],
            qsem.at[1, pc.zi, i],
            th,
            tb,
            act,
        )


def stretch_of(ref, i, zi, rows):
    return ref.at[i, :, pl.ds(pl.multiple_of(zi * rows, rows), rows)]


def halves_swapped(tile):
    lane = lanes_of(tile)
    return jnp.where(lane % DH < DH // 2, lane_roll(tile, -(DH // 2)), lane_roll(tile, DH // 2))


def turned(tile, cos, sin):
    return tile * cos + halves_swapped(tile) * sin


def to_heads_body(nh, nb, hl, io, n1_hbm, w_hbm, cos_ref, sin_ref, wo_ref, wmb_ref, wmc_ref, qin, kvin, wo_all, wmb_all, wmc_line, qbuf, kvbuf, n1_ref, w_ref, qsem, ksem, fsem, osem, osem2, bsem, bsem2, csem, stage):
    pc = Place(nh, nb, hl)
    loads = [
        pltpu.make_async_copy(n1_hbm, n1_ref, stage.at[0]),
        pltpu.make_async_copy(w_hbm, w_ref, stage.at[1]),
    ]
    for cp in loads:
        cp.start()
    signal_near(pc)
    rows = kvbuf.shape[2]
    lw = nh * DH
    for cp in loads:
        cp.wait()
    n1 = n1_ref[...]
    io.need(2, 3)
    cos, sin = cos_ref[...], sin_ref[...]
    kk = jnp.dot(n1, w_ref[:, lw : 2 * lw], preferred_element_type=F32)
    vv = jnp.dot(n1, w_ref[:, 2 * lw :], preferred_element_type=F32)
    for p in range(nh // 2):
        k = turned(kk[:, p * 128 : (p + 1) * 128], cos, sin)
        v = vv[:, p * 128 : (p + 1) * 128]
        low = lanes_of(k) < DH
        even = jnp.where(low, k, lane_roll(v, DH)).astype(BF16)
        odd = jnp.where(low, lane_roll(k, DH), v).astype(BF16)
        for i in range(pc.nz):
            kvbuf[2 * p, i] = even[i * rows : (i + 1) * rows]
            kvbuf[2 * p + 1, i] = odd[i * rows : (i + 1) * rows]
    wait_near(pc)

    def keys_out(act):
        for l in range(nh):
            for u in range(pc.cb):
                th, tb = pc.attends(pc.zi, l, pc.s % 2, u)
                routed(
                    pc,
                    kvbuf.at[l],
                    kvin.at[pc.h, :, pc.s],
                    ksem.at[0, l * pc.cb + u],
                    ksem.at[1, pc.h * pc.cb + pc.s // 2],
                    th,
                    tb,
                    act,
                )

    def queries_out(act):
        for l in range(nh):
            th, tb = pc.attends(pc.zi, l, pc.s % 2, pc.s // 2)
            routed(
                pc, qbuf.at[l], qin.at[pc.h], qsem.at[0, l], qsem.at[1, pc.h], th, tb, act
            )

    spread = BlkGather(pc, wo_ref, wo_all, osem, osem2)
    spread_b = BlkGather(pc, wmb_ref, wmb_all, bsem, bsem2)
    line_c = LineGather(pc, wmc_ref, lambda zi: wmc_line.at[:, zi], csem)
    keys_out("start")
    spread.start()
    spread_b.start()
    line_c.start()
    qq = jnp.dot(n1, w_ref[:, :lw], preferred_element_type=F32)
    for p in range(nh // 2):
        q = turned(qq[:, p * 128 : (p + 1) * 128], cos, sin).T.astype(BF16)
        qbuf[2 * p] = q[:DH]
        qbuf[2 * p + 1] = q[DH:]
    queries_out("start")
    count = nh * pc.cb

    def forward(i):
        at = kvin.at[i // pc.cb, :, 2 * (i % pc.cb) + pc.c]
        return remote(at, at, fsem.at[0, i], fsem.at[1, i], pc.sib, pc.b)

    @pl.loop(0, count)
    def _(i):
        wait_on(kvin.at[i // pc.cb, :, 2 * (i % pc.cb) + pc.c], ksem.at[1, i])
        forward(i).start()

    for t in range(1, pc.nz):
        spread.step(t)
        spread_b.step(t)
        line_c.step(t)
    keys_out("wait_send")
    queries_out("wait_send")
    for i in range(nh):
        wait_on(qin.at[i], qsem.at[1, i])

    @pl.loop(0, count)
    def _(i):
        forward(i).wait()

    spread.finish()
    spread_b.finish()
    line_c.finish()


def to_heads(n1, wq, cos, sin, wo, wmb, wmc, hl):
    nh, nb = dims()
    group, width = n1.shape
    nz, qs = hl, nb // hl
    cb = qs // 2
    rows = group // nz
    dma = pltpu.SemaphoreType.DMA
    return comm_call(
        functools.partial(to_heads_body, nh, nb, hl),
        "to_heads",
        1,
        (
            jax.ShapeDtypeStruct((nh, DH, group), BF16),
            jax.ShapeDtypeStruct((nh, nz, qs, rows, 2 * DH), BF16),
            jax.ShapeDtypeStruct((1, nz, qs) + wo.shape[1:], BF16),
            jax.ShapeDtypeStruct((nh, nz, qs) + wmb.shape[1:], BF16),
            jax.ShapeDtypeStruct((nh, nz) + wmc.shape[1:], BF16),
        ),
        [ANY, ANY, VM, VM, ANY, ANY, ANY],
        [ANY] * 5,
        [
            pltpu.VMEM((nh, DH, group), BF16),
            pltpu.VMEM((nh, nz, rows, 2 * DH), BF16),
            pltpu.VMEM(n1.shape, BF16),
            pltpu.VMEM(wq.shape, BF16),
            dma((2, nh)),
            dma((2, nh * cb)),
            dma((2, nh * cb)),
        ]
        + BlkGather.sem_shapes(nz, qs) * 2
        + [LineGather.sem_shape(nz), dma((2,))],
        (n1, wq, cos, sin, wo, wmb, wmc),
        vmem=60 << 20,
        late=(2, 3),
    )


class Queries:
    def __init__(self, nh, nb, hl, len_ref, lanes, slots, size):
        pc = Place(nh, nb, hl)
        tile = pl.program_id(0)
        rows = slots // (nh * nb)
        count = lanes // rows
        each = pc.nz // count
        ends = sequence_ends(len_ref)
        base = (tile // each) * nb + (tile % each) * count * pc.qs + pc.from_s
        lane = lax.broadcasted_iota(jnp.int32, (1, lanes), 1)
        slot = (base + lane // rows * pc.qs) * rows + lane % rows
        self.first = segment_first(slot, ends)
        self.last = segment_end(slot, ends, slots)
        near = base * rows
        far = (base + (count - 1) * pc.qs) * rows + rows - 1
        self.size = size
        self.lo = segment_first(near, ends) // size
        self.hi = (segment_end(far, ends, slots) + size - 1) // size
        self.open = jnp.minimum((segment_first(far, ends) + size - 1) // size, self.hi)
        self.close = jnp.maximum(segment_end(near, ends, slots) // size, self.open)
        self.lanes = lanes

    def allowed(self, block_at):
        at = block_at * self.size + lax.broadcasted_iota(jnp.int32, (self.size, self.lanes), 0)
        return jnp.logical_and(at >= self.first, at < self.last)

    def walk(self, step, carry):
        masked = lambda j, kept: step(j, kept, True)
        carry = lax.fori_loop(self.lo, self.open, masked, carry)
        carry = lax.fori_loop(self.open, self.close, lambda j, kept: step(j, kept, False), carry)
        return lax.fori_loop(self.close, self.hi, masked, carry)


def attend_body(nh, nb, hl, size, len_ref, q_ref, kv_ref, o_ref, of_ref, lse_ref):
    q = q_ref[0]
    lanes = q.shape[1]
    at = Queries(nh, nb, hl, len_ref, lanes, kv_ref.shape[0], size)
    q_pad = jnp.concatenate([q, jnp.zeros_like(q)], axis=0)
    is_key = lax.broadcasted_iota(jnp.int32, (1, 2 * DH), 1) < DH

    def step(j, carry, masked):
        top, acc = carry
        kv = kv_ref[pl.ds(pl.multiple_of(j * size, size), size), :]
        s = jnp.dot(kv, q_pad, preferred_element_type=F32)
        if masked:
            s = jnp.where(at.allowed(j), s, MASK_FLOOR)
        new_top = jnp.maximum(top, jnp.max(s, axis=0, keepdims=True))
        p = jnp.exp2((s - new_top) * EXP_SCALE).astype(BF16)
        alpha = jnp.exp2((top - new_top) * EXP_SCALE)
        ones_values = jnp.where(is_key, jnp.ones_like(kv), kv)
        acc = acc * alpha + lax.dot_general(
            ones_values, p, (((0,), (0,)), ((), ())), preferred_element_type=F32
        )
        return new_top, acc

    top, acc = at.walk(
        step, (jnp.full((1, lanes), MASK_FLOOR, F32), jnp.zeros((2 * DH, lanes), F32))
    )
    total = acc[:1]
    o = acc[DH:] / total
    of_ref[0] = o
    o_ref[0] = o.astype(BF16)
    lse_ref[0] = top * EXP_SCALE + jnp.log2(total)


def attend_specs(kv_rows, lanes, tiles_each):
    tile_spec = pl.BlockSpec((1, DH, lanes), lambda i, *_: (i // tiles_each, 0, i % tiles_each))
    row_spec = pl.BlockSpec((1, 1, lanes), lambda i, *_: (i, 0, 0))
    kv_spec = pl.BlockSpec((kv_rows, 2 * DH), lambda i, *_: (0, 0))
    return tile_spec, row_spec, kv_spec


def attend(lengths, q, kv, lanes, size, hl):
    nh, nb = dims()
    each = q.shape[2] // lanes
    tiles = q.shape[0] * each
    tile_spec, row_spec, kv_spec = attend_specs(kv.shape[0], lanes, each)
    return pl.pallas_call(
        functools.partial(attend_body, nh, nb, hl, size),
        grid_spec=pltpu.PrefetchScalarGridSpec(
            num_scalar_prefetch=1,
            grid=(tiles,),
            in_specs=[tile_spec, kv_spec],
            out_specs=[tile_spec, tile_spec, row_spec],
        ),
        out_shape=(
            jax.ShapeDtypeStruct(q.shape, BF16),
            jax.ShapeDtypeStruct(q.shape, F32),
            jax.ShapeDtypeStruct((tiles, 1, lanes), F32),
        ),
        name="attend",
        compiler_params=pltpu.CompilerParams(vmem_limit_bytes=60 << 20),
    )(lengths, q, kv)


def attend_grad_body(nh, nb, hl, size, len_ref, q_ref, do_ref, of_ref, kv_ref, lse_ref, dq_ref, dkv_ref, acc_ref):
    tile = pl.program_id(0)

    @pl.when(tile == 0)
    def _():
        acc_ref[...] = jnp.zeros_like(acc_ref)

    q = q_ref[0]
    do = do_ref[0]
    lanes = q.shape[1]
    place = Queries(nh, nb, hl, len_ref, lanes, kv_ref.shape[0], size)
    zero = jnp.zeros_like(q)
    both = jnp.concatenate(
        [jnp.concatenate([q, zero], axis=0), jnp.concatenate([zero, do], axis=0)], axis=1
    )
    delta = jnp.sum(do.astype(F32) * of_ref[0], axis=0, keepdims=True)
    lse = lse_ref[0]

    def step(j, dq, masked):
        at = pl.ds(pl.multiple_of(j * size, size), size)
        kv = kv_ref[at, :]
        sd = jnp.dot(kv, both, preferred_element_type=F32)
        s, dp = sd[:, :lanes], sd[:, lanes:]
        power = s * EXP_SCALE - lse
        if masked:
            power = jnp.where(place.allowed(j), power, MASK_FLOOR)
        p = jnp.exp2(power)
        ds = (p * (dp - delta)).astype(BF16)
        acc_ref[at, :] += lax.dot_general(
            jnp.concatenate([ds, p.astype(BF16)], axis=1),
            both,
            (((1,), (1,)), ((), ())),
            preferred_element_type=F32,
        )
        return dq + lax.dot_general(
            kv, ds, (((0,), (0,)), ((), ())), preferred_element_type=F32
        )

    dq = place.walk(step, jnp.zeros((2 * DH, lanes), F32))
    dq_ref[0] = (dq[:DH] * 0.125).astype(BF16)

    @pl.when(tile == pl.num_programs(0) - 1)
    def _():
        lane = lax.broadcasted_iota(jnp.int32, (1, 2 * DH), 1)
        dkv_ref[...] = (acc_ref[...] * jnp.where(lane < DH, 0.125, 1.0)).astype(BF16)


def attend_grad(lengths, q, do, of, kv, lse, lanes, size, hl):
    nh, nb = dims()
    tiles = lse.size // lanes
    lse = lse.reshape(tiles, 1, lanes)
    tile_spec, row_spec, kv_spec = attend_specs(kv.shape[0], lanes, tiles // q.shape[0])
    return pl.pallas_call(
        functools.partial(attend_grad_body, nh, nb, hl, size),
        grid_spec=pltpu.PrefetchScalarGridSpec(
            num_scalar_prefetch=1,
            grid=(tiles,),
            in_specs=[tile_spec, tile_spec, tile_spec, kv_spec, row_spec],
            out_specs=[tile_spec, kv_spec],
            scratch_shapes=[pltpu.VMEM(kv.shape, F32)],
        ),
        out_shape=(jax.ShapeDtypeStruct(q.shape, BF16), jax.ShapeDtypeStruct(kv.shape, BF16)),
        name="attend_grad",
        compiler_params=pltpu.CompilerParams(vmem_limit_bytes=60 << 20),
    )(lengths, q, do, of, kv, lse)


class HeadSum:
    def __init__(self, nh, h, b, part, near, far, out, sems):
        self.nx = nh // 2
        self.x, self.c = h // 2, h % 2
        self.h, self.part, self.near, self.far, self.out = h, part, near, far, out
        sib = self.x * 2 + 1 - self.c
        self.pairs = [
            remote(
                part.at[((self.x + k) % self.nx) * 2 + 1 - self.c],
                near.at[k],
                sems.at[0, k],
                sems.at[1, k],
                sib,
                b,
            )
            for k in range(self.nx)
        ]
        self.across = [
            remote(
                out.at[k],
                far.at[k],
                sems.at[2, k],
                sems.at[3, k],
                ((self.x + k) % self.nx) * 2 + self.c,
                b,
            )
            for k in range(1, self.nx)
        ]

    @staticmethod
    def sem_shape(nh):
        return pltpu.SemaphoreType.DMA((4, nh // 2))

    @staticmethod
    def buffers(nh, rows, width):
        return [pltpu.VMEM((nh // 2, rows, width), BF16)] * 3

    def start(self):
        for k in list(range(1, self.nx)) + [0]:
            self.pairs[k].start()

    def send(self):
        for k in range(1, self.nx):
            self.pairs[k].wait_recv()
            at = ((self.x + k) % self.nx) * 2 + self.c
            self.out[k] = (self.part[at].astype(F32) + self.near[k].astype(F32)).astype(BF16)
            self.across[k - 1].start()

    def total(self):
        self.pairs[0].wait_recv()
        total = self.part[self.h].astype(F32) + self.near[0].astype(F32)
        for k in range(1, self.nx):
            self.across[k - 1].wait_recv()
            total = total + self.far[k].astype(F32)
        return total

    def finish(self):
        for cp in self.pairs:
            cp.wait_send()
        for cp in self.across:
            cp.wait_send()


def norm_of(values):
    centre = values - jnp.mean(values, axis=-1, keepdims=True)
    scale = lax.rsqrt(jnp.mean(centre * centre, axis=-1, keepdims=True) + NORM_EPS)
    return centre * scale, scale


def norm_pull(grad, normed, scale):
    one = jnp.mean(grad, axis=-1, keepdims=True)
    two = jnp.mean(grad * normed, axis=-1, keepdims=True)
    return scale * (grad - one - normed * two)


CHUNKS = 2


def chunk_of(ref, j, axis):
    size = ref.shape[axis] // CHUNKS
    at = pl.ds(j * size, size)
    return ref.at[at] if axis == 0 else ref.at[:, at]


def head_sums(nh, h, b, part, bufs, sems):
    near, far, out = bufs
    return [
        HeadSum(
            nh,
            h,
            b,
            chunk_of(part, j, 1),
            chunk_of(near, j, 1),
            chunk_of(far, j, 1),
            chunk_of(out, j, 1),
            sems.at[j],
        )
        for j in range(CHUNKS)
    ]


def head_gathers(nh, h, b, src, dst, sems):
    return [
        HeadGather(nh, h, b, chunk_of(src, j, 0), chunk_of(dst, j, 1), sems.at[j])
        for j in range(CHUNKS)
    ]


def chunk_sems(nh):
    return pltpu.SemaphoreType.DMA((CHUNKS, 4, nh // 2))


def mid_body(nh, nb, hl, io, o_ref, wo_ref, x_ref, wmb_ref, og, hid_ref, ng_ref, wmb_all, part, near, far, out, nbuf, osem, ssem, gsem, wsem):
    pc = Place(nh, nb, hl)
    h, b = pc.h, pc.b
    enter_with(pc, lambda zi: pc.attends(zi, h, pc.s % 2, pc.s // 2))
    rows, width = x_ref.shape
    outputs_back(pc, o_ref, og, osem, "start")
    sides = [
        remote(
            wmb_ref,
            wmb_all.at[:, :, pc.s],
            wsem.at[0, ds],
            wsem.at[1, ds],
            h,
            pc.zi * pc.qs + (pc.s + ds) % pc.qs,
        )
        for ds in range(1, pc.qs)
    ]
    sides.append(pltpu.make_async_copy(wmb_ref, wmb_all.at[:, :, pc.s], wsem.at[0, 0]))
    for cp in sides:
        cp.start()
    outputs_back(pc, o_ref, og, osem, "wait_send")
    for zi in range(pc.nz):
        wait_on(og.at[zi], osem.at[1, zi])
    io.put(0)
    io.need(1)
    wo = wo_ref[...]
    for i in range(nh):
        part[i] = lax.dot_general(
            og[:, i].reshape(pc.nz * DH, rows),
            wo,
            (((0,), (0,)), ((), ())),
            preferred_element_type=F32,
        ).astype(BF16)
    hss = head_sums(nh, h, b, part, (near, far, out), ssem)
    hgs = head_gathers(nh, h, b, nbuf, ng_ref, gsem)
    for hs in hss:
        hs.start()
    for hs in hss:
        hs.send()
    size = rows // CHUNKS
    io.need(2)
    for j, (hs, hg) in enumerate(zip(hss, hgs)):
        at = pl.ds(j * size, size)
        hid = x_ref[at, :].astype(F32) + hs.total()
        hid_ref[at, :] = hid
        nbuf[at, :] = norm_of(hid)[0].astype(BF16)
        hg.start()
    io.put(1)
    for hg in hgs:
        hg.pass_on()
    for hs, hg in zip(hss, hgs):
        hs.finish()
        hg.finish()
    for cp in sides:
        cp.wait()


def mid_exchange(ot, wo, x, wmb, hl):
    nh, nb = dims()
    rows, width = x.shape
    nz = hl
    return comm_call(
        functools.partial(mid_body, nh, nb, hl),
        "mid_exchange",
        2,
        (
            jax.ShapeDtypeStruct((nz, nh, DH, rows), BF16),
            jax.ShapeDtypeStruct(x.shape, F32),
            jax.ShapeDtypeStruct((nh, rows, width), BF16),
            jax.ShapeDtypeStruct((nh, nz, nb // nz) + wmb.shape[2:], BF16),
        ),
        [ANY] * 4,
        [ANY] * 4,
        [pltpu.VMEM((nh, rows, width), BF16)]
        + HeadSum.buffers(nh, rows, width)
        + [
            pltpu.VMEM((rows, width), BF16),
            pltpu.SemaphoreType.DMA((2, nz)),
            chunk_sems(nh),
            chunk_sems(nh),
            pltpu.SemaphoreType.DMA((2, nb // nz)),
        ],
        (ot, wo, x, wmb),
        vmem=60 << 20,
        late=(1, 2),
        early=(0, 1),
    )


def ffn_body(nh, nb, fl, split_rows, cut, len_ref, n_hbm, g_hbm, wa_hbm, wb_hbm, wc_hbm, y_hbm, d_hbm, ga_hbm, gb_hbm, n_ref, g_ref, w_ref, y_ref, d_ref, ga_ref, gb_ref, gy, mm, dz, stage, drain):
    rows, width = n_ref.shape[1], n_ref.shape[2]
    group = nh * rows
    total, zc, off = ff_widths(fl)
    wide = total - off
    shift = 2 * fl - off
    step = FF_BLOCKS * rows
    lane = lax.broadcasted_iota(jnp.int32, (1, wide), 1)
    real = lane < fl
    valid = sequence_ends(len_ref)[-1]
    blk = lax.axis_index("blk")
    loads = [
        pltpu.make_async_copy(n_hbm, n_ref, stage.at[0]),
        pltpu.make_async_copy(g_hbm, g_ref, stage.at[1]),
    ]
    for n, (w, (begin, end)) in enumerate(zip((wa_hbm, wb_hbm, wc_hbm), weight_parts(total))):
        dst = w_ref.at[:, pl.ds(begin, end - begin)]
        loads.append(pltpu.make_async_copy(w, dst, stage.at[2 + n]))
    for cp in loads:
        cp.start()
    for cp in loads:
        cp.wait()

    def out_rows(r):
        at = pl.ds(r * FF_BLOCKS, FF_BLOCKS)
        return [
            pltpu.make_async_copy(d_ref.at[at], d_hbm.at[at], drain.at[0, r]),
            pltpu.make_async_copy(y_ref.at[at], y_hbm.at[at], drain.at[1, r]),
        ]

    @pl.loop(0, group // step)
    def _(r):
        at = pl.ds(pl.multiple_of(r * step, step), step)
        n = n_ref[pl.ds(r * FF_BLOCKS, FF_BLOCKS)].reshape(step, width)
        row = lax.broadcasted_iota(jnp.int32, (step, 1), 0)
        slot = ((r * FF_BLOCKS + row // rows) * nb + blk) * rows + row % rows
        g = g_ref[pl.ds(r * FF_BLOCKS, FF_BLOCKS)].reshape(step, width)
        g = jnp.where(slot < valid, g.astype(F32), 0.0).astype(BF16)
        gy[at, :] = g
        z = jnp.dot(n, w_ref[:, :zc], preferred_element_type=F32)
        dm = lane_roll(jnp.dot(g, w_ref[:, off:], preferred_element_type=F32), -shift)
        gate, up = z[:, :wide], lane_roll(z, -fl)[:, :wide]
        cdf = 0.5 * (1.0 + lax.erf(gate * math.sqrt(0.5)))
        act = gate * cdf
        slope = cdf + gate * jnp.exp(-0.5 * gate * gate) * (1.0 / math.sqrt(2.0 * math.pi))
        m = lane_roll(jnp.where(real, act * up, 0.0), shift).astype(BF16)
        mm[at, :] = m
        d_gate = widen(jnp.where(real, dm * up * slope, 0.0), zc)
        d_up = lane_roll(widen(jnp.where(real, dm * act, 0.0), zc), fl)
        d = (d_gate + d_up).astype(BF16)
        dz[at, :] = d
        nt = (((1,), (1,)), ((), ()))
        dpart = lax.dot_general(d, w_ref[:, :zc], nt, preferred_element_type=F32)
        d_ref[pl.ds(r * FF_BLOCKS, FF_BLOCKS)] = dpart.astype(BF16).reshape(FF_BLOCKS, rows, width)
        ypart = lax.dot_general(m, w_ref[:, off:], nt, preferred_element_type=F32)
        y_ref[pl.ds(r * FF_BLOCKS, FF_BLOCKS)] = ypart.astype(BF16).reshape(FF_BLOCKS, rows, width)
        for cp in out_rows(r):
            cp.start()

    block = width // nh

    def out_block(i):
        at = (slice(None), i) if split_rows else (pl.ds(i * block, block),)
        return [
            pltpu.make_async_copy(ga_ref.at[i], ga_hbm.at[at], drain.at[2, i]),
            pltpu.make_async_copy(gb_ref.at[i], gb_hbm.at[at], drain.at[3, i]),
        ]

    @pl.loop(0, nh)
    def _(i):
        cols = pl.ds(pl.multiple_of(i * block, block), block)
        tn = (((0,), (0,)), ((), ()))
        n = n_ref[:, :, cols].reshape(group, block)
        g_in = lax.dot_general(n, dz[...], tn, preferred_element_type=F32)
        g_down = lax.dot_general(gy[:, cols], mm[...], tn, preferred_element_type=F32)
        both = jnp.concatenate(
            [g_in[:, :off], g_in[:, off:] + g_down[:, : zc - off], g_down[:, zc - off :]], axis=1
        ).astype(BF16)
        for ref, part in ((ga_ref, both[:, :cut]), (gb_ref, both[:, cut:])):
            if split_rows:
                part = part.reshape(nb, block // nb, part.shape[1])
            ref[i] = part
        for cp in out_block(i):
            cp.start()

    @pl.loop(0, nh)
    def _(i):
        for cp in out_block(i):
            cp.wait()

    @pl.loop(0, group // step)
    def _(r):
        for cp in out_rows(r):
            cp.wait()


def ffn(lengths, n2, g, weights, fl, own_rows, cut):
    nh, nb = dims()
    _, rows, width = n2.shape
    group = nh * rows
    total, zc, off = ff_widths(fl)
    split_rows = own_rows % 16 == 0
    lead = (nb, nh, own_rows) if split_rows else (width,)
    held = (nh, nb, own_rows) if split_rows else (nh, width // nh)
    return pl.pallas_call(
        functools.partial(ffn_body, nh, nb, fl, split_rows, cut),
        out_shape=(
            jax.ShapeDtypeStruct(n2.shape, BF16),
            jax.ShapeDtypeStruct(n2.shape, BF16),
            jax.ShapeDtypeStruct(lead + (cut,), BF16),
            jax.ShapeDtypeStruct(lead + (total - cut,), BF16),
        ),
        in_specs=[SM] + [ANY] * 5,
        out_specs=[ANY] * 4,
        scratch_shapes=[
            pltpu.VMEM(n2.shape, BF16),
            pltpu.VMEM(n2.shape, BF16),
            pltpu.VMEM((width, total), BF16),
            pltpu.VMEM(n2.shape, BF16),
            pltpu.VMEM(n2.shape, BF16),
            pltpu.VMEM(held + (cut,), BF16),
            pltpu.VMEM(held + (total - cut,), BF16),
            pltpu.VMEM((group, width), BF16),
            pltpu.VMEM((group, total - off), BF16),
            pltpu.VMEM((group, zc), BF16),
            pltpu.SemaphoreType.DMA((5,)),
            pltpu.SemaphoreType.DMA((4, nh)),
        ],
        name="ffn",
        compiler_params=pltpu.CompilerParams(vmem_limit_bytes=60 << 20),
    )(lengths, n2, g, *weights)


def back_body(nh, nb, hl, io, len_ref, dpart, ypart, hid_ref, g_ref, wo_ref, og_ref, gb_hbm, y_ref, dh_ref, do_in, go_ref, gb_out, n1, f1, o1, n2, f2, o2, dbuf, dg, dots, gb_ref, nearb, s1, s2, gsem, qsem, pb, stage):
    pc = Place(nh, nb, hl)
    h, b = pc.h, pc.b
    mine = pltpu.make_async_copy(gb_hbm.at[:, pc.s], gb_ref, stage)
    mine.start()
    enter_with(pc, lambda zi: (pc.head, zi * pc.qs + pc.from_s))
    pairs = [
        remote(
            gb_hbm.at[:, (pc.s + ds) % pc.qs],
            nearb.at[ds - 1],
            pb.at[0, ds],
            pb.at[1, ds],
            h,
            pc.zi * pc.qs + (pc.s + ds) % pc.qs,
        )
        for ds in range(1, pc.qs)
    ]
    rows, width = hid_ref.shape
    slot = (h * nb + b) * rows + lax.broadcasted_iota(jnp.int32, (rows, 1), 0)
    valid = slot < sequence_ends(len_ref)[-1]
    hds = head_sums(nh, h, b, dpart, (n1, f1, o1), s1)
    hy = HeadSum(nh, h, b, ypart, n2, f2, o2, s2)
    hgs = head_gathers(nh, h, b, dbuf, dg, gsem)
    io.need(1)
    for hd in hds:
        hd.start()
    for cp in pairs:
        cp.start()
    for hd in hds:
        hd.send()
    size = rows // CHUNKS
    io.need(3, 4)
    for j, (hd, hg) in enumerate(zip(hds, hgs)):
        at = pl.ds(j * size, size)
        normed, scale = norm_of(hid_ref[at, :])
        gy = jnp.where(valid[j * size : (j + 1) * size], g_ref[at, :].astype(F32), 0.0)
        dh = gy + norm_pull(hd.total(), normed, scale)
        dh_ref[at, :] = dh
        dbuf[at, :] = dh.astype(BF16)
        hg.start()
    io.put(1)
    io.need(2)
    hy.start()
    io.need(5)
    wo = wo_ref[...]
    nt = (((1,), (1,)), ((), ()))

    def emit(i):
        part = lax.dot_general(wo, dg[i], nt, preferred_element_type=F32).astype(BF16)
        dots[:, i] = part.reshape(pc.nz, DH, rows)
        grads_out(pc, dots, do_in, qsem, i, "start")

    nx = nh // 2
    for hg in hgs:
        hg.local.wait()
        hg.near.wait_recv()
    emit(h)
    emit(pc.sib)
    for hg in hgs:
        hg.pass_on()
    for k in range(1, nx):
        emit(((pc.x + nx - k) % nx) * 2 + pc.c)
    hy.send()
    for hg in hgs:
        for cp in hg.forward:
            cp.wait_recv()
    for k in range(1, nx):
        emit(((pc.x + nx - k) % nx) * 2 + 1 - pc.c)
    for hd, hg in zip(hds, hgs):
        hd.finish()
        hg.near.wait_send()
        for cp in hg.across + hg.forward:
            cp.wait_send()
    total = 0.0
    io.need(6)
    for i in range(nh):
        total = total + jnp.dot(
            og_ref[:, i].reshape(pc.nz * DH, rows), dg[i], preferred_element_type=F32
        )
    go_ref[...] = total.astype(BF16)
    io.put(3)
    y_ref[...] = jnp.where(valid, hid_ref[...] + hy.total(), 0.0)
    io.put(0)
    hy.finish()
    mine.wait()
    for cp in pairs:
        cp.wait()

    @pl.loop(0, pc.nz)
    def _(d):
        others = jnp.sum(nearb[:, d].astype(F32), axis=0)
        gb_out[d] = (gb_ref[d].astype(F32) + others).astype(BF16)

    io.put(4)

    @pl.loop(0, nh)
    def _(i):
        grads_out(pc, dots, do_in, qsem, i, "wait_send")
        for zi in range(pc.nz):
            wait_on(stretch_of(do_in, i, zi, rows), qsem.at[1, zi, i])


def back_exchange(lengths, dpart, ypart, hid, g, wo, og, gb):
    nh, nb = dims()
    rows, width = hid.shape
    nz = hl = og.shape[0]
    return comm_call(
        functools.partial(back_body, nh, nb, hl),
        "back_exchange",
        3,
        (
            jax.ShapeDtypeStruct(hid.shape, F32),
            jax.ShapeDtypeStruct(hid.shape, F32),
            jax.ShapeDtypeStruct((nh, DH, nz * rows), BF16),
            jax.ShapeDtypeStruct((nz * DH, width), BF16),
            jax.ShapeDtypeStruct(gb.shape[:1] + gb.shape[2:], BF16),
        ),
        [SM] + [VM] * 6 + [ANY],
        [VM, VM, ANY, VM, VM],
        HeadSum.buffers(nh, rows, width)
        + HeadSum.buffers(nh, rows, width)
        + [
            pltpu.VMEM((rows, width), BF16),
            pltpu.VMEM((nh, rows, width), BF16),
            pltpu.VMEM(og.shape, BF16),
            pltpu.VMEM(gb.shape[:1] + gb.shape[2:], BF16),
            pltpu.VMEM((gb.shape[1] - 1, nz) + gb.shape[2:], BF16),
            chunk_sems(nh),
            HeadSum.sem_shape(nh),
            chunk_sems(nh),
            pltpu.SemaphoreType.DMA((2, nz, nh)),
            pltpu.SemaphoreType.DMA((2, gb.shape[1])),
            pltpu.SemaphoreType.DMA,
        ],
        (lengths, dpart, ypart, hid, g, wo, og, gb),
        vmem=60 << 20,
        late=(1, 3, 4, 2, 5, 6),
        early=(0, 1, 3, 4),
    )


def grads_back_body(nh, nb, hl, io, dq_ref, dkv_ref, cos_ref, sin_ref, n1_hbm, w_hbm, go_ref, gb_ref, gq_ref, dpart, do_ref, gb_sum, got, sums, dq_out, dkv_out, dqkv, n1_ref, w_ref, nearo, sumo, goto, lsem, gotb, bsem, qsem, psem, ksem, stage, po):
    pc = Place(nh, nb, hl)
    loads = [
        pltpu.make_async_copy(n1_hbm, n1_ref, stage.at[0]),
        pltpu.make_async_copy(w_hbm, w_ref, stage.at[1]),
    ]
    for cp in loads:
        cp.start()
    signal_near(pc)
    wait_near(pc)
    rows = dkv_ref.shape[3]
    group = pc.nz * rows
    width = n1_ref.shape[1]
    lw = nh * DH
    count = nh * pc.cb

    def pair(k):
        src = dkv_ref.at[k // pc.cb, :, 2 * (k % pc.cb) + 1 - pc.c]
        return remote(src, got.at[k], psem.at[0, k], psem.at[1, k], pc.sib, pc.b)

    def back(k, act):
        routed(
            pc,
            sums.at[k],
            dkv_out.at[pc.head, pc.u],
            ksem.at[0, k],
            ksem.at[1, pc.head * pc.cb + pc.u],
            k // pc.cb,
            pc.zi * pc.qs + 2 * (k % pc.cb) + pc.c,
            act,
        )

    def queries_back(act):
        for i in range(nh):
            routed(
                pc,
                dq_ref.at[i],
                dq_out.at[pc.head],
                qsem.at[0, i],
                qsem.at[1, pc.head],
                i,
                pc.zi * pc.qs + pc.from_s,
                act,
            )

    pairs_o = [
        remote(
            go_ref.at[:, (pc.s + ds) % pc.qs],
            nearo.at[ds - 1],
            po.at[0, ds],
            po.at[1, ds],
            pc.h,
            pc.zi * pc.qs + (pc.s + ds) % pc.qs,
        )
        for ds in range(1, pc.qs)
    ]
    along_o = StretchSum(pc, sumo, goto, lsem)
    along_b = StretchSum(pc, gb_ref, gotb, bsem)

    io.need(1)

    @pl.loop(0, count)
    def _(k):
        pair(k).start()

    queries_back("start")
    io.need(6, 7)
    for cp in pairs_o:
        cp.start()
    along_b.start()

    @pl.loop(0, count)
    def _(k):
        pair(k).wait_recv()
        mine = dkv_ref[k // pc.cb, :, 2 * (k % pc.cb) + pc.c]
        sums[k] = (mine.astype(F32) + got[k].astype(F32)).astype(BF16)
        back(k, "start")

    for cp in pairs_o:
        cp.wait_recv()
    sumo[...] = (go_ref[:, pc.s].astype(F32) + jnp.sum(nearo[...].astype(F32), axis=0)).astype(BF16)
    along_o.start()
    io.need(2, 3)
    cos, sin = cos_ref[...], -sin_ref[...]
    for l in range(nh):
        wait_on(dq_out.at[l], qsem.at[1, l])
    for p in range(nh // 2):
        q = dq_out[2 * p : 2 * p + 2].reshape(2 * DH, group).astype(F32).T
        dqkv[:, p * 128 : (p + 1) * 128] = turned(q, cos, sin).astype(BF16)
    for l in range(nh):
        for u in range(pc.cb):
            wait_on(dkv_out.at[l, u], ksem.at[1, l * pc.cb + u])
    for p in range(nh // 2):
        even, odd = [
            jnp.sum(dkv_out[2 * p + i].astype(F32), axis=0).reshape(group, 2 * DH)
            for i in range(2)
        ]
        low = lanes_of(even) < DH
        k = jnp.where(low, even, lane_roll(odd, DH)).astype(BF16).astype(F32)
        v = jnp.where(low, lane_roll(even, DH), odd)
        dqkv[:, lw + p * 128 : lw + (p + 1) * 128] = turned(k, cos, sin).astype(BF16)
        dqkv[:, 2 * lw + p * 128 : 2 * lw + (p + 1) * 128] = v.astype(BF16)
    nt = (((1,), (1,)), ((), ()))
    tn = (((0,), (0,)), ((), ()))
    for cp in loads:
        cp.wait()

    @pl.loop(0, nh)
    def _(i):
        cols = pl.ds(pl.multiple_of(i * (width // nh), width // nh), width // nh)
        gq_ref[cols, :] = lax.dot_general(
            n1_ref[:, cols], dqkv[...], tn, preferred_element_type=F32
        ).astype(BF16)

    io.put(0)

    @pl.loop(0, pc.nz)
    def _(i):
        at = pl.ds(pl.multiple_of(i * rows, rows), rows)
        dpart[i] = lax.dot_general(
            dqkv[at, :], w_ref[...], nt, preferred_element_type=F32
        ).astype(BF16)

    io.put(1)

    @pl.loop(0, count)
    def _(k):
        pair(k).wait_send()
        back(k, "wait_send")

    queries_back("wait_send")
    do_ref[...] = along_o.total()
    io.put(2)
    gb_sum[...] = along_b.total().astype(BF16)
    io.put(3)
    along_o.finish()
    along_b.finish()
    for cp in pairs_o:
        cp.wait_send()


def grads_back(dq, dkv, cos, sin, n1, wq, go, gb, hl):
    nh, nb = dims()
    nz, qs = hl, nb // hl
    cb = qs // 2
    rows = dkv.shape[3]
    width = n1.shape[1]
    lw = nh * DH
    dma = pltpu.SemaphoreType.DMA
    return comm_call(
        functools.partial(grads_back_body, nh, nb, hl),
        "grads_back",
        4,
        (
            jax.ShapeDtypeStruct((width, 3 * lw), BF16),
            jax.ShapeDtypeStruct((nz, rows, width), BF16),
            jax.ShapeDtypeStruct(go.shape[2:], F32),
            jax.ShapeDtypeStruct(gb.shape[1:], BF16),
        ),
        [ANY, VM, VM, VM, ANY, ANY, VM, VM],
        [VM] * 4,
        [
            pltpu.VMEM((nh * cb, nz, rows, 2 * DH), BF16),
            pltpu.VMEM((nh * cb, nz, rows, 2 * DH), BF16),
            pltpu.VMEM(dq.shape, BF16),
            pltpu.VMEM((nh, cb, nz, rows, 2 * DH), BF16),
            pltpu.VMEM((nz * rows, 3 * lw), BF16),
            pltpu.VMEM(n1.shape, BF16),
            pltpu.VMEM(wq.shape, BF16),
            pltpu.VMEM((qs - 1, nz) + go.shape[2:], BF16),
            pltpu.VMEM((nz,) + go.shape[2:], BF16),
        ]
        + StretchSum.scratch(nz, go.shape[2:])
        + StretchSum.scratch(nz, gb.shape[1:])
        + [
            dma((2, nh)),
            dma((2, nh * cb)),
            dma((2, nh * cb)),
            dma((2,)),
            dma((2, qs)),
        ],
        (dq, dkv, cos, sin, n1, wq, go, gb),
        vmem=60 << 20,
        late=(1, 6, 7, 2, 3),
        early=(0, 1, 2, 3),
    )


def last_body(nh, nb, hl, io, dpart, gq_ref, gma_ref, gmb_ref, dn_ref, quarters, gma_all, gmb_all, nearq, sumq, farq, totq, sentz, gotz, zsem, pq, fq, cq, msem, asem):
    pc = Place(nh, nb, hl)
    h, b = pc.h, pc.b
    signal_near(pc)
    wait_near(pc)
    nx, nz, qs = nh // 2, pc.nz, pc.qs
    def pair_q(k):
        return remote(
            gq_ref.at[2 * k + 1 - pc.c], nearq.at[k], pq.at[0, k], pq.at[1, k], pc.sib, b
        )

    line = LineSum(pc, lambda d: dpart[d].astype(F32), sentz, gotz, zsem)

    def plane_q(i):
        tx, ts = (pc.x + i // qs) % nx, (pc.s + i % qs) % qs
        return remote(
            sumq.at[tx, :, ts],
            farq.at[pc.x, pc.s],
            fq.at[0, i],
            fq.at[1, i],
            tx * 2 + pc.c,
            pc.zi * qs + ts,
        )

    def quarter(i):
        to = (pc.zi + i) % nz
        return remote(
            totq.at[to], quarters.at[pc.zi], cq.at[0, i], cq.at[1, i], h, to * qs + pc.s
        )

    io.need(1)
    for k in range(nx):
        pair_q(k).start()
    io.need(0)
    line.lead(0)
    moves = [
        remote(
            gmb_ref.at[(h + i) % nh],
            gmb_all.at[h],
            msem.at[0, i],
            msem.at[1, i],
            (h + i) % nh,
            b,
        )
        for i in range(1, nh)
    ]
    moves.append(pltpu.make_async_copy(gmb_ref.at[h], gmb_all.at[h], msem.at[0, 0]))
    moves.append(
        pltpu.make_async_copy(gma_ref.at[pc.s, h], gma_all.at[pc.s, h], asem.at[0, 0])
    )

    def plane_move(i):
        th, ts = (h + i // qs) % nh, (pc.s + i % qs) % qs
        return remote(
            gma_ref.at[ts, th],
            gma_all.at[pc.s, h],
            asem.at[0, i],
            asem.at[1, i],
            th,
            pc.zi * qs + ts,
        )

    for k in range(nx):
        pair_q(k).wait_recv()
        sumq[k] = (gq_ref[2 * k + pc.c].astype(F32) + nearq[k].astype(F32)).astype(BF16)

    @pl.loop(1, nx * qs)
    def _(i):
        plane_q(i).start()

    farq[pc.x, pc.s] = sumq[pc.x, :, pc.s]
    for cp in moves:
        cp.start()

    @pl.loop(1, nh * qs)
    def _(i):
        plane_move(i).start()

    line.follow(0)
    line.lead(1)

    @pl.loop(1, nx * qs)
    def _(i):
        plane_q(i).wait_recv()

    totq[...] = jnp.sum(
        farq[...].astype(F32).reshape((nx * qs,) + totq.shape), axis=0
    ).astype(BF16)
    for i in range(1, nz):
        quarter(i).start()
    quarters[pc.zi] = totq[pc.zi]
    for j in range(1, nz - 1):
        line.follow(j)
        if j + 1 < nz - 1:
            line.lead(j + 1)
    line.total(dn_ref)
    io.put(0)
    line.finish()
    for i in range(1, nz):
        quarter(i).wait()
    io.put(1)
    for cp in moves:
        cp.wait()

    @pl.loop(1, nh * qs)
    def _(i):
        plane_move(i).wait()

    for k in range(nx):
        pair_q(k).wait_send()

    @pl.loop(1, nx * qs)
    def _(i):
        plane_q(i).wait_send()


def last_exchange(dpart, gq, gma, gmb):
    nh, nb = dims()
    nz, rows, width = dpart.shape
    qs = nb // nz
    own_rows, cols = gq.shape[3:]
    nx = nh // 2
    dma = pltpu.SemaphoreType.DMA
    return comm_call(
        functools.partial(last_body, nh, nb, nz),
        "last_exchange",
        5,
        (
            jax.ShapeDtypeStruct((rows, width), F32),
            jax.ShapeDtypeStruct((nz, own_rows, cols), BF16),
            jax.ShapeDtypeStruct(gma.shape, BF16),
            jax.ShapeDtypeStruct(gmb.shape, BF16),
        ),
        [VM] * 2 + [ANY] * 2,
        [VM] * 2 + [ANY] * 2,
        [
            pltpu.VMEM((nx, nz, qs, own_rows, cols), BF16),
            pltpu.VMEM((nx, nz, qs, own_rows, cols), BF16),
            pltpu.VMEM((nx, qs, nz, own_rows, cols), BF16),
            pltpu.VMEM((nz, own_rows, cols), BF16),
        ]
        + LineSum.scratch(nz, (rows, width))
        + [
            dma((2, nx)),
            dma((2, nx * qs)),
            dma((2, nz)),
            dma((2, nh)),
            dma((2, nh * qs)),
        ],
        (dpart, gq, gma, gmb),
        vmem=60 << 20,
        late=(1, 0),
        early=(0, 1),
    )


def finish_body(nh, fl, dn_ref, x_ref, dh_ref, y_in, quarters, do_in, gma, gmb, wq_ref, win_ref, ga_ref, gf_ref,
                y_ref, dx_ref, lna_ref, dq_ref, do_ref, lnm_ref, din_ref, dwd_ref):
    y_ref[...] = y_in[...]
    do_ref[...] = do_in[...]
    normed, scale = norm_of(x_ref[...].astype(F32))
    dx_ref[...] = dh_ref[...] + norm_pull(dn_ref[...], normed, scale)
    width = x_ref.shape[1]
    gain = column(ga_ref[...].astype(F32))
    nz = quarters.shape[0]
    rowsum = 0.0
    for c in range(3):
        for l in range(nh):
            src = (c * nh * DH + l // 2 * 128) // 128 * 128
            for p in range(nz // 2):
                tiles = [quarters[2 * p + i, :, src : src + 128].astype(F32) for i in range(2)]
                piece = half_pick(tiles[0], tiles[1], l % 2, l % 2)
                at = c * width + l * nz * DH + p * 128
                dq_ref[:, at : at + 128] = piece * gain
                rowsum = rowsum + jnp.sum(
                    piece * wq_ref[:, at : at + 128].astype(F32), axis=1, keepdims=True
                )
    lna_ref[...] = as_row(rowsum)
    ff = nh * fl
    total, _, _ = ff_widths(fl)
    tiles = lambda v: (v + 127) // 128 * 128
    gate_up, down = 0.0, 0.0
    for i in range(nh):
        first = jnp.sum(gma[:, i].astype(F32), axis=0)
        piece = jnp.concatenate([first, gmb[i].astype(F32)], axis=1)
        lane = lanes_of(piece)
        gate = widen(jnp.where(lane < fl, piece, 0.0), tiles(2 * ff))
        up = jnp.where(jnp.logical_and(lane >= fl, lane < 2 * fl), piece, 0.0)
        up = widen(up, tiles(2 * ff))
        gate_up = gate_up + lane_roll(gate, i * fl) + lane_roll(up, ff - fl + i * fl)
        dn = jnp.where(jnp.logical_and(lane >= 2 * fl, lane < 3 * fl), piece, 0.0)
        down = down + lane_roll(widen(dn, max(total, tiles(ff))), i * fl - 2 * fl)
    gate_up = gate_up[:, : 2 * ff]
    dwd_ref[...] = down[:, :ff]
    din_ref[...] = gate_up * column(gf_ref[...].astype(F32))
    lnm_ref[...] = as_row(jnp.sum(gate_up * win_ref[...].astype(F32), axis=1, keepdims=True))


def finish(dn, x, dh, y, quarters, d_wout, gma, gmb, w_qkv, w_in, gain_attn, gain_mlp, fl):
    nh, _ = dims()
    rows, width = x.shape
    own_rows = w_qkv.shape[0]
    ff = nh * fl
    f32 = lambda *shape: jax.ShapeDtypeStruct(shape, F32)
    return pl.pallas_call(
        functools.partial(finish_body, nh, fl),
        out_shape=(
            f32(rows, width),
            f32(rows, width),
            f32(1, own_rows),
            f32(own_rows, 3 * width),
            f32(own_rows, width),
            f32(1, own_rows),
            f32(own_rows, 2 * ff),
            f32(own_rows, ff),
        ),
        in_specs=[VM] * 12,
        out_specs=[VM] * 8,
        name="finish",
        compiler_params=pltpu.CompilerParams(vmem_limit_bytes=60 << 20),
    )(dn, x, dh, y, quarters, d_wout, gma, gmb, w_qkv, w_in, gain_attn, gain_mlp)


def shards(layer_input, out_grad, lengths, ln_attn, w_qkv, w_attn_out, ln_mlp, w_in, w_mlp_out):
    nh, nb = dims()
    h, b = me()
    rows, width = layer_input.shape
    heads = width // DH
    hl = heads // nh
    group = nh * rows
    slots = nh * nb * rows
    own_rows = w_qkv.shape[0]
    ff = w_mlp_out.shape[0]
    fl = ff // nh
    nz, qs = hl, nb // hl
    lw = nh * DH

    gain_attn = ln_attn.reshape(1, own_rows)
    gain_mlp = ln_mlp.reshape(1, own_rows)
    n1, wma, wmb, wmc, wq, gg, cos, sin = first_exchange(
        lengths, layer_input, w_qkv, gain_attn, w_in, gain_mlp, w_mlp_out.T, out_grad, hl, fl
    )
    wma = lax.all_gather(wma, "blk", axis=1, tiled=True).reshape(width, -1)
    wq = wq.reshape(width, 3 * lw)
    n1 = n1.reshape(group, width)
    qin, kvin, wo, wmb, wmc = to_heads(n1, wq, cos, sin, w_attn_out[None], wmb, wmc, hl)
    wo = wo.reshape(nz * DH, width)
    kv_all = kvin.reshape(slots, 2 * DH)
    ot, of, lse = attend(lengths, qin, kv_all, 4 * rows, 1024, hl)
    og, hid, n2, wmc = mid_exchange(ot, wo, layer_input, wmc, hl)
    weights = [w.reshape(width, -1) for w in (wma, wmb, wmc)]
    ypart, dpart, gma, gmb = ffn(lengths, n2, gg, weights, fl, own_rows, GRAD_CUT)
    by_owner = []
    for gm in (gma, gmb):
        if gm.ndim == 4:
            gm = gm.reshape((nz, qs) + gm.shape[1:])
        else:
            gm = gm.reshape(nh, nz, qs, own_rows, gm.shape[1]).transpose(1, 2, 0, 3, 4)
        by_owner.append(gm)
    gma, gmb = by_owner
    lines = [[zi * qs + s for zi in range(nz)] for s in range(qs)]
    gma = lax.psum_scatter(
        gma, "blk", scatter_dimension=0, tiled=True, axis_index_groups=lines
    ).reshape(gma.shape[1:])
    y_out, dh, do_in, go, gmb = back_exchange(
        lengths, dpart, ypart, hid, out_grad, wo, og, gmb
    )
    dq, dkv = attend_grad(lengths, qin, do_in, of, kv_all, lse, 2 * rows, 1024, hl)
    go = go.reshape(nz, qs, own_rows, width)
    gq, dpart1, d_wout, gmb = grads_back(
        dq, dkv.reshape(kvin.shape), cos, sin, n1, wq, go, gmb, hl
    )
    dn, quarters, gma, gmb = last_exchange(
        dpart1, gq.reshape(nh, nz, qs, own_rows, 3 * lw), gma, gmb
    )
    y_out, dx, d_ln_attn, d_wqkv, d_wout, d_ln_mlp, d_win, d_wd = finish(
        dn,
        layer_input,
        dh,
        y_out,
        quarters,
        d_wout,
        gma,
        gmb,
        w_qkv,
        w_in,
        gain_attn,
        gain_mlp,
        fl,
    )
    return (
        y_out,
        dx,
        d_ln_attn.reshape(own_rows),
        d_wqkv,
        d_wout,
        d_ln_mlp.reshape(own_rows),
        d_win,
        d_wd.T,
    )


def solution(mesh):
    both = ("head", "blk")
    row_split = P(both, None)
    return jax.shard_map(
        shards,
        mesh=mesh,
        in_specs=(
            row_split,
            row_split,
            P(),
            P(both),
            row_split,
            row_split,
            P(both),
            row_split,
            P(None, both),
        ),
        out_specs=(
            row_split,
            row_split,
            P(both),
            row_split,
            row_split,
            P(both),
            row_split,
            P(None, both),
        ),
        check_vma=False,
    )
```

```python
import functools
import math

import jax
import jax.numpy as jnp
from jax import lax
from jax.experimental import pallas as pl
from jax.experimental.pallas import tpu as pltpu
from jax.sharding import PartitionSpec as P

DH = 64
ROPE_BASE = 160000.0
NORM_EPS = 1e-05
MASK_FLOOR = -1e30
GRAD_CUT = 1152
FF_BLOCKS = 2
WEIGHT_CUTS = (1408, 1536)
EXP_SCALE = 0.125 * math.log2(math.e)
BF16 = jnp.bfloat16
F32 = jnp.float32
MESH_ID = pl.DeviceIdType.MESH
ANY = pl.BlockSpec(memory_space=pl.ANY)
VM = pl.BlockSpec(memory_space=pltpu.VMEM)
SM = pl.BlockSpec(memory_space=pltpu.SMEM)


def dims():
    nh = lax.axis_size("head")
    nb = lax.axis_size("blk")
    return nh, nb


def me():
    return lax.axis_index("head"), lax.axis_index("blk")


class Staged:
    def __init__(self, loads, drains):
        self.loads, self.drains = loads, drains

    def need(self, *which):
        for i in which:
            self.loads[i].wait()

    def put(self, *which):
        for i in which:
            self.drains[i].start()


def comm_call(body, name, cid, out_shape, in_specs, out_specs, scratch, args, vmem=None, late=(), early=()):
    n_in, n_out, n_late, n_early = len(args), len(out_shape), len(late), len(early)
    in_specs = [ANY if i in late else spec for i, spec in enumerate(in_specs)]
    out_specs = [ANY if i in early else spec for i, spec in enumerate(out_specs)]
    held = [pltpu.VMEM(args[i].shape, args[i].dtype) for i in late]
    held += [pltpu.VMEM(out_shape[i].shape, out_shape[i].dtype) for i in early]
    held.append(pltpu.SemaphoreType.DMA((max(n_late + n_early, 1),)))

    def staged_body(*refs):
        ins, outs = list(refs[:n_in]), list(refs[n_in : n_in + n_out])
        bufs = refs[n_in + n_out : n_in + n_out + n_late + n_early]
        sems = refs[n_in + n_out + n_late + n_early]
        rest = refs[n_in + n_out + n_late + n_early + 1 :]
        loads, drains = {}, {}
        for k, i in enumerate(late):
            loads[i] = pltpu.make_async_copy(ins[i], bufs[k], sems.at[k])
            loads[i].start()
            ins[i] = bufs[k]
        for k, i in enumerate(early):
            k += n_late
            drains[i] = pltpu.make_async_copy(bufs[k], outs[i], sems.at[k])
            outs[i] = bufs[k]
        body(Staged(loads, drains), *ins, *outs, *rest)
        for cp in drains.values():
            cp.wait()

    return pl.pallas_call(
        staged_body,
        out_shape=out_shape,
        in_specs=in_specs,
        out_specs=out_specs,
        scratch_shapes=held + list(scratch),
        name=name,
        compiler_params=pltpu.CompilerParams(
            collective_id=cid, has_side_effects=True, vmem_limit_bytes=vmem
        ),
    )(*args)


def remote(src, dst, send, recv, h, b):
    return pltpu.make_async_remote_copy(
        src_ref=src,
        dst_ref=dst,
        send_sem=send,
        recv_sem=recv,
        device_id=(h, b),
        device_id_type=MESH_ID,
    )


def signal(h, b):
    pl.semaphore_signal(
        pltpu.get_barrier_semaphore(), inc=1, device_id=(h, b), device_id_type=MESH_ID
    )


class HeadGather:
    def __init__(self, nh, h, b, src, dst, sems):
        self.nh, self.h, self.b, self.dst, self.sems = nh, h, b, dst, sems
        nx = nh // 2
        self.nx = nx
        x, c = h // 2, h % 2
        sib = x * 2 + 1 - c
        self.sib = sib
        self.across = []
        for k in range(1, nx):
            self.across.append(
                remote(src, dst.at[h], sems.at[0, k], sems.at[1, k], ((x + k) % nx) * 2 + c, b)
            )
        self.near = remote(src, dst.at[h], sems.at[0, 0], sems.at[1, 0], sib, b)
        self.local = pltpu.make_async_copy(src, dst.at[h], sems.at[2, 0])
        self.forward = []
        for k in range(1, nx):
            got = ((x + nx - k) % nx) * 2 + c
            self.forward.append(
                remote(dst.at[got], dst.at[got], sems.at[2, k], sems.at[3, k], sib, b)
            )

    @staticmethod
    def sem_shape(nh):
        return pltpu.SemaphoreType.DMA((4, nh // 2))

    def start(self):
        for cp in self.across:
            cp.start()
        self.near.start()
        self.local.start()

    def pass_on(self):
        for cp, fw in zip(self.across, self.forward):
            cp.wait_recv()
            fw.start()

    def finish(self):
        for cp in self.across:
            cp.wait_send()
        self.near.wait()
        self.local.wait()
        for fw in self.forward:
            fw.wait()


def lane_roll(values, shift):
    return pltpu.roll(values, shift % values.shape[1], 1)


def lanes_of(values):
    return lax.broadcasted_iota(jnp.int32, (1, values.shape[1]), 1)


def widen(values, width):
    extra = width - values.shape[1]
    if extra <= 0:
        return values[:, :width]
    return jnp.concatenate([values, jnp.zeros((values.shape[0], extra), values.dtype)], axis=1)


def weight_parts(total):
    marks = (0,) + WEIGHT_CUTS + (total,)
    return list(zip(marks[:-1], marks[1:]))


def column(row):
    n = row.shape[1]
    same = lax.broadcasted_iota(jnp.int32, (n, n), 0) == lax.broadcasted_iota(jnp.int32, (n, n), 1)
    return jnp.sum(jnp.where(same, row, 0.0), axis=1, keepdims=True)


def as_row(col):
    n = col.shape[0]
    same = lax.broadcasted_iota(jnp.int32, (n, n), 0) == lax.broadcasted_iota(jnp.int32, (n, n), 1)
    return jnp.sum(jnp.where(same, col, 0.0), axis=0, keepdims=True)


def sequence_ends(len_ref):
    ends, total = [], 0
    for i in range(len_ref.shape[0]):
        total = total + len_ref[i]
        ends.append(total)
    return ends


def segment_first(slot, ends):
    first = jnp.zeros_like(slot)
    for end in ends:
        first = jnp.where(slot >= end, end, first)
    return first


def segment_end(slot, ends, slots):
    last = jnp.zeros_like(slot) + slots
    for end in reversed(ends):
        last = jnp.where(slot < end, end, last)
    return last


def half_pick(low_src, high_src, low_at, high_at):
    low = low_src if low_at == 0 else lane_roll(low_src, DH)
    high = high_src if high_at == 1 else lane_roll(high_src, DH)
    return jnp.where(lanes_of(low) < DH, low, high)


def ff_widths(fl):
    up = lambda v: (v + 127) // 128 * 128
    return up(3 * fl), up(2 * fl), 2 * fl // 128 * 128


class LineGather:
    def __init__(self, pc, src, place, sems):
        self.pc, self.src, self.place, self.sems = pc, src, place, sems

    @staticmethod
    def sem_shape(nz):
        return pltpu.SemaphoreType.DMA((5, nz))

    def origin(self, t, up):
        return self.pc.zi - t if up else self.pc.zi + t

    def move(self, t, up):
        pc = self.pc
        at = self.place(self.origin(t, up))
        n = 0 if up else 2
        return remote(
            self.src if t == 0 else at,
            at,
            self.sems.at[n, t],
            self.sems.at[n + 1, t],
            pc.h,
            pc.b + pc.qs if up else pc.b - pc.qs,
        )

    def sends(self, t, up):
        zi, nz = self.pc.zi, self.pc.nz
        if up:
            return jnp.logical_and(zi - t >= 0, zi + 1 < nz)
        return jnp.logical_and(zi + t < nz, zi - 1 >= 0)

    def local(self):
        return pltpu.make_async_copy(self.src, self.place(self.pc.zi), self.sems.at[4, 0])

    def start(self):
        for up in (True, False):

            @pl.when(self.sends(0, up))
            def _():
                self.move(0, up).start()

        self.local().start()

    def step(self, t, arrived=None):
        low = self.pc.zi < self.pc.nz // 2
        self.take(t, False, jnp.logical_not(low), arrived)
        self.take(t, True, True, arrived)
        self.take(t, False, low, arrived)

    def take(self, t, up, now, arrived):
        zi, nz = self.pc.zi, self.pc.nz
        origin = self.origin(t, up)
        here = jnp.logical_and(now, origin >= 0 if up else origin < nz)

        @pl.when(here)
        def _():
            wait_on(self.place(origin), self.sems.at[1 if up else 3, t - 1])

        if t < nz - 1:

            @pl.when(jnp.logical_and(now, self.sends(t, up)))
            def _():
                self.move(t, up).start()

        if arrived is not None:

            @pl.when(here)
            def _():
                arrived(origin)

    def finish(self):
        self.local().wait()
        for t in range(self.pc.nz - 1):
            for up in (True, False):

                @pl.when(self.sends(t, up))
                def _():
                    self.move(t, up).wait_send()


class BlkGather:
    def __init__(self, pc, src, out, sems, ssem):
        self.pc, self.out, self.ssem, self.src = pc, out, ssem, src
        self.line = LineGather(pc, src, lambda zi: out.at[:, zi, pc.s], sems)

    @staticmethod
    def sem_shapes(nz, qs):
        return [LineGather.sem_shape(nz), pltpu.SemaphoreType.DMA((2, nz, qs))]

    def side(self, zi, ds, own=False):
        pc = self.pc
        ref = self.out.at[:, zi, pc.s]
        return remote(
            self.src if own else ref,
            ref,
            self.ssem.at[0, zi, ds],
            self.ssem.at[1, zi, ds],
            pc.h,
            pc.zi * pc.qs + (pc.s + ds) % pc.qs,
        )

    def spread(self, zi, own=False):
        for ds in range(1, self.pc.qs):
            self.side(zi, ds, own).start()

    def start(self):
        self.line.start()
        self.spread(self.pc.zi, True)

    def step(self, t):
        self.line.step(t, self.spread)

    def finish(self):
        self.line.finish()

        @pl.loop(0, self.pc.nz)
        def _(zi):
            for ds in range(1, self.pc.qs):
                self.side(zi, ds).wait()


class LineSum:
    def __init__(self, pc, term, sent, got, sems):
        self.pc, self.term, self.sent, self.got, self.sems = pc, term, sent, got, sems

    @staticmethod
    def scratch(nz, shape):
        return [
            pltpu.VMEM((2, nz) + shape, BF16),
            pltpu.VMEM((2, nz) + shape, BF16),
            pltpu.SemaphoreType.DMA((4, nz)),
        ]

    def move(self, d, up):
        pc = self.pc
        n = 0 if up else 1
        return remote(
            self.sent.at[n, d],
            self.got.at[n, d],
            self.sems.at[2 * n, d],
            self.sems.at[2 * n + 1, d],
            pc.h,
            pc.b + pc.qs if up else pc.b - pc.qs,
        )

    def takes(self, up):
        return self.pc.zi > 0 if up else self.pc.zi < self.pc.nz - 1

    def lead(self, j):
        self.step(j, False)

    def follow(self, j):
        self.step(j, True)

    def step(self, j, taking):
        low = self.pc.zi < self.pc.nz // 2
        if taking:
            self.one(j, False, jnp.logical_not(low), True)
            self.one(j, True, True, True)
            self.one(j, False, low, True)
        else:
            self.one(j, True, True, False)
            self.one(j, False, True, False)

    def one(self, j, up, now, taking):
        zi, nz = self.pc.zi, self.pc.nz
        d = nz - 1 - j if up else j
        n = 0 if up else 1
        takes = self.takes(up)
        far = jnp.logical_and(now, zi < d if up else zi > d)

        @pl.when(jnp.logical_and(far, takes if taking else jnp.logical_not(takes)))
        def _():
            if taking:
                wait_on(self.got.at[n, d], self.sems.at[2 * n + 1, d])
                self.sent[n, d] = (self.term(d) + self.got[n, d].astype(F32)).astype(BF16)
            else:
                self.sent[n, d] = self.term(d).astype(BF16)
            self.move(d, up).start()

    def total(self, total_ref):
        zi = self.pc.zi
        total_ref[...] = self.term(zi)
        for up in (True, False):
            n = 0 if up else 1

            @pl.when(self.takes(up))
            def _():
                wait_on(self.got.at[n, zi], self.sems.at[2 * n + 1, zi])
                total_ref[...] += self.got[n, zi].astype(F32)

    def finish(self):
        zi, nz = self.pc.zi, self.pc.nz
        for j in range(nz - 1):
            for up in (True, False):
                d = nz - 1 - j if up else j

                @pl.when(zi < d if up else zi > d)
                def _():
                    self.move(d, up).wait_send()


class StretchSum:
    def __init__(self, pc, part, got, sems):
        self.pc, self.part, self.got, self.sems = pc, part, got, sems

    @staticmethod
    def scratch(nz, shape):
        return [pltpu.VMEM((nz,) + shape, BF16), pltpu.SemaphoreType.DMA((2, nz))]

    def move(self, i):
        pc = self.pc
        to = (pc.zi + i) % pc.nz
        return remote(
            self.part.at[to],
            self.got.at[pc.zi],
            self.sems.at[0, i],
            self.sems.at[1, i],
            pc.h,
            to * pc.qs + pc.s,
        )

    def start(self):
        for i in range(1, self.pc.nz):
            self.move(i).start()

    def total(self):
        pc = self.pc
        total = self.part[pc.zi].astype(F32)
        for i in range(1, pc.nz):
            self.move(i).wait_recv()
            total = total + self.got[(pc.zi + pc.nz - i) % pc.nz].astype(F32)
        return total

    def finish(self):
        for i in range(1, self.pc.nz):
            self.move(i).wait_send()


class PlaneWeights:
    def __init__(self, pc, pack, out, sems, ksem):
        self.pc, self.pack, self.out, self.sems, self.ksem = pc, pack, out, sems, ksem

    @staticmethod
    def sem_shapes(nh, nz, qs):
        dma = pltpu.SemaphoreType.DMA
        return [dma((2, nz)), dma((4, nh // 2 * qs))]

    def along(self, i):
        pc = self.pc
        to = (pc.zi + i) % pc.nz
        return remote(
            self.pack.at[to],
            self.out.at[pc.h, pc.zi, pc.s],
            self.sems.at[0, i],
            self.sems.at[1, i],
            pc.h,
            to * pc.qs + pc.s,
        )

    def local(self):
        pc = self.pc
        return pltpu.make_async_copy(
            self.pack.at[pc.zi], self.out.at[pc.h, pc.zi, pc.s], self.sems.at[0, 0]
        )

    def place(self, i, sign):
        pc = self.pc
        nx = pc.nh // 2
        dx, ds = i // pc.qs, i % pc.qs
        if sign < 0:
            dx, ds = nx - dx, pc.qs - ds
        return ((pc.x + dx) % nx) * 2 + pc.c, (pc.s + ds) % pc.qs

    def across(self, i):
        pc = self.pc
        th, ts = self.place(i, 1)
        ref = self.out.at[pc.h, :, pc.s]
        return remote(
            ref, ref, self.ksem.at[0, i], self.ksem.at[1, i], th, pc.zi * pc.qs + ts
        )

    def near(self, i):
        pc = self.pc
        gh, gs = self.place(i, -1)
        ref = self.out.at[gh, :, gs]
        return remote(ref, ref, self.ksem.at[2, i], self.ksem.at[3, i], pc.sib, pc.b)

    def start(self):
        for i in range(1, self.pc.nz):
            self.along(i).start()
        self.local().start()

    def spread(self):
        pc = self.pc
        self.local().wait()
        for i in range(1, pc.nz):
            self.along(i).wait_recv()

        @pl.loop(1, pc.nh // 2 * pc.qs)
        def _(i):
            self.across(i).start()

        self.near(0).start()

    def pass_on(self):
        @pl.loop(1, self.pc.nh // 2 * self.pc.qs)
        def _(i):
            self.across(i).wait_recv()
            self.near(i).start()

    def finish(self):
        for i in range(1, self.pc.nz):
            self.along(i).wait_send()

        @pl.loop(1, self.pc.nh // 2 * self.pc.qs)
        def _(i):
            self.across(i).wait_send()

        @pl.loop(0, self.pc.nh // 2 * self.pc.qs)
        def _(i):
            self.near(i).wait()


def first_body(nh, nb, hl, fl, io, len_ref, x_ref, wq_ref, ga_ref, win_hbm, gf_ref, wd_hbm, g_ref, n1_all, wma, wmb, wmc, wq_all, gg, cos_ref, sin_ref, own_n, pack, wmp, win_ref, wd_ref, lsem, wsem, ksem, gsem, msem, stage):
    pc = Place(nh, nb, hl)
    h, b = pc.h, pc.b
    loads = [
        pltpu.make_async_copy(win_hbm, win_ref, stage.at[0]),
        pltpu.make_async_copy(wd_hbm, wd_ref, stage.at[1]),
    ]
    for cp in loads:
        cp.start()
    signal_near(pc)
    width = x_ref.shape[1]
    lw = width // pc.nz
    gain = column(ga_ref[...].astype(F32))
    io.need(2)
    for c in range(3):
        w = wq_ref[:, c * width : (c + 1) * width].astype(F32) * gain
        tile = lambda l, i: w[:, l * pc.nz * DH + i // 2 * 128 : l * pc.nz * DH + i // 2 * 128 + 128]
        for i in range(pc.nz):
            for p in range(nh // 2):
                both = half_pick(tile(2 * p, i), tile(2 * p + 1, i), i % 2, i % 2)
                at = c * lw + p * 128
                pack[i, :, at : at + 128] = both.astype(BF16)
    io.need(1)
    own_n[...] = norm_of(x_ref[...].astype(F32))[0].astype(BF16)
    wait_near(pc)
    weights = PlaneWeights(pc, pack, wq_all, wsem, ksem)
    line = LineGather(pc, own_n, lambda zi: n1_all.at[zi], lsem)
    gather = HeadGather(nh, h, b, g_ref, gg, gsem)
    weights.start()
    line.start()
    gather.start()
    for cp in loads:
        cp.wait()
    total = ff_widths(fl)[0]
    ff = nh * fl
    win = win_ref[...].astype(F32) * column(gf_ref[...].astype(F32))
    wd = widen(wd_ref[...].astype(F32), total if total > ff else (ff + 127) // 128 * 128)
    lane = lax.broadcasted_iota(jnp.int32, (1, total), 1)
    for i in range(nh):
        gate = widen(lane_roll(win, -i * fl), total)
        up = widen(lane_roll(win, fl - ff - i * fl), total)
        down = widen(lane_roll(wd, 2 * fl - i * fl), total)
        piece = jnp.where(
            lane < fl,
            gate,
            jnp.where(lane < 2 * fl, up, jnp.where(lane < 3 * fl, down, 0.0)),
        )
        wmp[i] = piece.astype(BF16)
    copies = []
    for n, (dst, (begin, end)) in enumerate(zip((wma, wmb, wmc), weight_parts(total))):
        cols = pl.ds(begin, end - begin)
        for i in range(1, nh):
            th = (h + i) % nh
            src = wmp.at[th, :, cols]
            copies.append(remote(src, dst.at[h], msem.at[0, n, i], msem.at[1, n, i], th, b))
        copies.append(pltpu.make_async_copy(wmp.at[h, :, cols], dst.at[h], msem.at[0, n, 0]))
    weights.spread()
    for cp in copies:
        cp.start()
    ends = sequence_ends(len_ref)
    rows = x_ref.shape[0]
    lane = lax.broadcasted_iota(jnp.int32, (1, 2 * DH), 1)
    power = (lane % (DH // 2)).astype(F32) * (-2.0 / DH)
    inv_freq = jnp.exp2(power * math.log2(ROPE_BASE))
    sign = jnp.where(lane % DH < DH // 2, -1.0, 1.0)
    line.step(1)
    for i in range(pc.nz):
        slot = (h * nb + i * pc.qs + pc.s) * rows + lax.broadcasted_iota(jnp.int32, (rows, 1), 0)
        angle = (slot - segment_first(slot, ends)).astype(F32) * inv_freq
        cos_ref[i * rows : (i + 1) * rows, :] = jnp.cos(angle)
        sin_ref[i * rows : (i + 1) * rows, :] = jnp.sin(angle) * sign
    io.put(6, 7)
    gather.pass_on()
    for t in range(2, pc.nz):
        line.step(t)
    weights.pass_on()
    for cp in copies:
        cp.wait()
    weights.finish()
    line.finish()
    gather.finish()


def first_exchange(lengths, x, w_qkv, gain_attn, w_in, gain_mlp, wd_t, g, hl, fl):
    nh, nb = dims()
    rows, width = x.shape
    nz, qs = hl, nb // hl
    lw = width // nz
    own_rows = w_in.shape[0]
    total = ff_widths(fl)[0]
    dma = pltpu.SemaphoreType.DMA
    return comm_call(
        functools.partial(first_body, nh, nb, hl, fl),
        "first_exchange",
        0,
        (
            jax.ShapeDtypeStruct((nz, rows, width), BF16),
            *[
                jax.ShapeDtypeStruct((nh, own_rows, end - begin), BF16)
                for begin, end in weight_parts(total)
            ],
            jax.ShapeDtypeStruct((nh, nz, qs, own_rows, 3 * lw), BF16),
            jax.ShapeDtypeStruct((nh, rows, width), BF16),
            jax.ShapeDtypeStruct((nz * rows, 2 * DH), F32),
            jax.ShapeDtypeStruct((nz * rows, 2 * DH), F32),
        ),
        [SM, VM, VM, VM, ANY, VM, ANY, ANY],
        [ANY] * 6 + [VM] * 2,
        [
            pltpu.VMEM((rows, width), BF16),
            pltpu.VMEM((nz, own_rows, 3 * lw), BF16),
            pltpu.VMEM((nh, own_rows, total), BF16),
            pltpu.VMEM(w_in.shape, BF16),
            pltpu.VMEM(wd_t.shape, BF16),
            LineGather.sem_shape(nz),
        ]
        + PlaneWeights.sem_shapes(nh, nz, qs)
        + [
            HeadGather.sem_shape(nh),
            dma((2, 3, nh)),
            dma((2,)),
        ],
        (lengths, x, w_qkv, gain_attn, w_in, gain_mlp, wd_t, g),
        vmem=60 << 20,
        late=(2, 1),
        early=(6, 7),
    )


class Place:
    def __init__(self, nh, nb, hl):
        h, b = me()
        self.nh, self.nb, self.h, self.b = nh, nb, h, b
        self.x, self.c = h // 2, h % 2
        self.nz = hl
        self.qs = nb // hl
        self.cb = self.qs // 2
        self.sib = self.x * 2 + 1 - self.c
        self.zi, self.s = b // self.qs, b % self.qs
        self.head = self.x * 2 + self.s // self.cb
        self.u = self.s % self.cb
        self.from_s = self.u * 2 + self.c

    def attends(self, zi, l, core, u):
        return (l // 2) * 2 + core, zi * self.qs + (l % 2) * self.cb + u


def signal_near(pc):
    here = pc.nh * pc.qs

    @pl.loop(1, here)
    def _(i):
        signal((pc.h + i // pc.qs) % pc.nh, pc.zi * pc.qs + (pc.s + i % pc.qs) % pc.qs)

    @pl.loop(1, pc.nz)
    def _(i):
        signal(pc.h, (pc.zi + i) % pc.nz * pc.qs + pc.s)


def wait_near(pc, more=0):
    pl.semaphore_wait(pltpu.get_barrier_semaphore(), pc.nh * pc.qs + pc.nz - 2 + more)


def enter_with(pc, source):
    signal_near(pc)
    for i in range(1, pc.nz):
        signal(*source((pc.zi + i) % pc.nz))
    wait_near(pc, pc.nz - 1)


def routed(pc, src, dst, send, recv, th, tb, act):
    mine = jnp.logical_and(th == pc.h, tb == pc.b)

    @pl.when(mine)
    def _():
        if act == "start":
            pltpu.make_async_copy(src, dst, recv).start()

    @pl.when(jnp.logical_not(mine))
    def _():
        cp = remote(src, dst, send, recv, th, tb)
        if act == "start":
            cp.start()
        else:
            cp.wait_send()


def wait_on(ref, sem):
    pltpu.make_async_copy(ref, ref, sem).wait()


def stretch_lanes(ref, zi, rows):
    return ref.at[:, :, pl.ds(pl.multiple_of(zi * rows, rows), rows)]


def outputs_back(pc, o_ref, og, osem, act):
    rows = og.shape[3]
    for zi in range(pc.nz):
        routed(
            pc,
            stretch_lanes(o_ref, zi, rows),
            og.at[pc.zi],
            osem.at[0, zi],
            osem.at[1, pc.zi],
            pc.head,
            zi * pc.qs + pc.from_s,
            act,
        )


def grads_out(pc, dots, do_in, qsem, i, act):
    rows = dots.shape[3]
    for zi in range(pc.nz):
        th, tb = pc.attends(zi, pc.h, pc.s % 2, pc.s // 2)
        routed(
            pc,
            dots.at[zi, i],
            stretch_of(do_in, i, pc.zi, rows),
            qsem.at[0, zi, i],
            qsem.at[1, pc.zi, i],
            th,
            tb,
            act,
        )


def stretch_of(ref, i, zi, rows):
    return ref.at[i, :, pl.ds(pl.multiple_of(zi * rows, rows), rows)]


def halves_swapped(tile):
    lane = lanes_of(tile)
    return jnp.where(lane % DH < DH // 2, lane_roll(tile, -(DH // 2)), lane_roll(tile, DH // 2))


def turned(tile, cos, sin):
    return tile * cos + halves_swapped(tile) * sin


def to_heads_body(nh, nb, hl, io, n1_hbm, w_hbm, cos_ref, sin_ref, wo_ref, wmb_ref, wmc_ref, qin, kvin, wo_all, wmb_all, wmc_line, qbuf, kvbuf, n1_ref, w_ref, qsem, ksem, fsem, osem, osem2, bsem, bsem2, csem, stage):
    pc = Place(nh, nb, hl)
    loads = [
        pltpu.make_async_copy(n1_hbm, n1_ref, stage.at[0]),
        pltpu.make_async_copy(w_hbm, w_ref, stage.at[1]),
    ]
    for cp in loads:
        cp.start()
    signal_near(pc)
    rows = kvbuf.shape[2]
    lw = nh * DH
    for cp in loads:
        cp.wait()
    n1 = n1_ref[...]
    io.need(2, 3)
    cos, sin = cos_ref[...], sin_ref[...]
    kk = jnp.dot(n1, w_ref[:, lw : 2 * lw], preferred_element_type=F32)
    vv = jnp.dot(n1, w_ref[:, 2 * lw :], preferred_element_type=F32)
    for p in range(nh // 2):
        k = turned(kk[:, p * 128 : (p + 1) * 128], cos, sin)
        v = vv[:, p * 128 : (p + 1) * 128]
        low = lanes_of(k) < DH
        even = jnp.where(low, k, lane_roll(v, DH)).astype(BF16)
        odd = jnp.where(low, lane_roll(k, DH), v).astype(BF16)
        for i in range(pc.nz):
            kvbuf[2 * p, i] = even[i * rows : (i + 1) * rows]
            kvbuf[2 * p + 1, i] = odd[i * rows : (i + 1) * rows]
    wait_near(pc)

    def keys_out(act):
        for l in range(nh):
            for u in range(pc.cb):
                th, tb = pc.attends(pc.zi, l, pc.s % 2, u)
                routed(
                    pc,
                    kvbuf.at[l],
                    kvin.at[pc.h, :, pc.s],
                    ksem.at[0, l * pc.cb + u],
                    ksem.at[1, pc.h * pc.cb + pc.s // 2],
                    th,
                    tb,
                    act,
                )

    def queries_out(act):
        for l in range(nh):
            th, tb = pc.attends(pc.zi, l, pc.s % 2, pc.s // 2)
            routed(
                pc, qbuf.at[l], qin.at[pc.h], qsem.at[0, l], qsem.at[1, pc.h], th, tb, act
            )

    spread = BlkGather(pc, wo_ref, wo_all, osem, osem2)
    spread_b = BlkGather(pc, wmb_ref, wmb_all, bsem, bsem2)
    line_c = LineGather(pc, wmc_ref, lambda zi: wmc_line.at[:, zi], csem)
    keys_out("start")
    spread.start()
    spread_b.start()
    line_c.start()
    qq = jnp.dot(n1, w_ref[:, :lw], preferred_element_type=F32)
    for p in range(nh // 2):
        q = turned(qq[:, p * 128 : (p + 1) * 128], cos, sin).T.astype(BF16)
        qbuf[2 * p] = q[:DH]
        qbuf[2 * p + 1] = q[DH:]
    queries_out("start")
    count = nh * pc.cb

    def forward(i):
        at = kvin.at[i // pc.cb, :, 2 * (i % pc.cb) + pc.c]
        return remote(at, at, fsem.at[0, i], fsem.at[1, i], pc.sib, pc.b)

    @pl.loop(0, count)
    def _(i):
        wait_on(kvin.at[i // pc.cb, :, 2 * (i % pc.cb) + pc.c], ksem.at[1, i])
        forward(i).start()

    for t in range(1, pc.nz):
        spread.step(t)
        spread_b.step(t)
        line_c.step(t)
    keys_out("wait_send")
    queries_out("wait_send")
    for i in range(nh):
        wait_on(qin.at[i], qsem.at[1, i])

    @pl.loop(0, count)
    def _(i):
        forward(i).wait()

    spread.finish()
    spread_b.finish()
    line_c.finish()


def to_heads(n1, wq, cos, sin, wo, wmb, wmc, hl):
    nh, nb = dims()
    group, width = n1.shape
    nz, qs = hl, nb // hl
    cb = qs // 2
    rows = group // nz
    dma = pltpu.SemaphoreType.DMA
    return comm_call(
        functools.partial(to_heads_body, nh, nb, hl),
        "to_heads",
        1,
        (
            jax.ShapeDtypeStruct((nh, DH, group), BF16),
            jax.ShapeDtypeStruct((nh, nz, qs, rows, 2 * DH), BF16),
            jax.ShapeDtypeStruct((1, nz, qs) + wo.shape[1:], BF16),
            jax.ShapeDtypeStruct((nh, nz, qs) + wmb.shape[1:], BF16),
            jax.ShapeDtypeStruct((nh, nz) + wmc.shape[1:], BF16),
        ),
        [ANY, ANY, VM, VM, ANY, ANY, ANY],
        [ANY] * 5,
        [
            pltpu.VMEM((nh, DH, group), BF16),
            pltpu.VMEM((nh, nz, rows, 2 * DH), BF16),
            pltpu.VMEM(n1.shape, BF16),
            pltpu.VMEM(wq.shape, BF16),
            dma((2, nh)),
            dma((2, nh * cb)),
            dma((2, nh * cb)),
        ]
        + BlkGather.sem_shapes(nz, qs) * 2
        + [LineGather.sem_shape(nz), dma((2,))],
        (n1, wq, cos, sin, wo, wmb, wmc),
        vmem=60 << 20,
        late=(2, 3),
    )


class Queries:
    def __init__(self, nh, nb, hl, len_ref, lanes, slots, size):
        pc = Place(nh, nb, hl)
        tile = pl.program_id(0)
        rows = slots // (nh * nb)
        count = lanes // rows
        each = pc.nz // count
        ends = sequence_ends(len_ref)
        base = (tile // each) * nb + (tile % each) * count * pc.qs + pc.from_s
        lane = lax.broadcasted_iota(jnp.int32, (1, lanes), 1)
        slot = (base + lane // rows * pc.qs) * rows + lane % rows
        self.first = segment_first(slot, ends)
        self.last = segment_end(slot, ends, slots)
        near = base * rows
        far = (base + (count - 1) * pc.qs) * rows + rows - 1
        self.size = size
        self.lo = segment_first(near, ends) // size
        self.hi = (segment_end(far, ends, slots) + size - 1) // size
        self.open = jnp.minimum((segment_first(far, ends) + size - 1) // size, self.hi)
        self.close = jnp.maximum(segment_end(near, ends, slots) // size, self.open)
        self.lanes = lanes

    def allowed(self, block_at):
        at = block_at * self.size + lax.broadcasted_iota(jnp.int32, (self.size, self.lanes), 0)
        return jnp.logical_and(at >= self.first, at < self.last)

    def walk(self, step, carry):
        masked = lambda j, kept: step(j, kept, True)
        carry = lax.fori_loop(self.lo, self.open, masked, carry)
        carry = lax.fori_loop(self.open, self.close, lambda j, kept: step(j, kept, False), carry)
        return lax.fori_loop(self.close, self.hi, masked, carry)


def attend_body(nh, nb, hl, size, len_ref, q_ref, kv_ref, o_ref, of_ref, lse_ref):
    q = q_ref[0]
    lanes = q.shape[1]
    at = Queries(nh, nb, hl, len_ref, lanes, kv_ref.shape[0], size)
    q_pad = jnp.concatenate([q, jnp.zeros_like(q)], axis=0)
    is_key = lax.broadcasted_iota(jnp.int32, (1, 2 * DH), 1) < DH

    def step(j, carry, masked):
        top, acc = carry
        kv = kv_ref[pl.ds(pl.multiple_of(j * size, size), size), :]
        s = jnp.dot(kv, q_pad, preferred_element_type=F32)
        if masked:
            s = jnp.where(at.allowed(j), s, MASK_FLOOR)
        new_top = jnp.maximum(top, jnp.max(s, axis=0, keepdims=True))
        p = jnp.exp2((s - new_top) * EXP_SCALE).astype(BF16)
        alpha = jnp.exp2((top - new_top) * EXP_SCALE)
        ones_values = jnp.where(is_key, jnp.ones_like(kv), kv)
        acc = acc * alpha + lax.dot_general(
            ones_values, p, (((0,), (0,)), ((), ())), preferred_element_type=F32
        )
        return new_top, acc

    top, acc = at.walk(
        step, (jnp.full((1, lanes), MASK_FLOOR, F32), jnp.zeros((2 * DH, lanes), F32))
    )
    total = acc[:1]
    o = acc[DH:] / total
    of_ref[0] = o
    o_ref[0] = o.astype(BF16)
    lse_ref[0] = top * EXP_SCALE + jnp.log2(total)


def attend_specs(kv_rows, lanes, tiles_each):
    tile_spec = pl.BlockSpec((1, DH, lanes), lambda i, *_: (i // tiles_each, 0, i % tiles_each))
    row_spec = pl.BlockSpec((1, 1, lanes), lambda i, *_: (i, 0, 0))
    kv_spec = pl.BlockSpec((kv_rows, 2 * DH), lambda i, *_: (0, 0))
    return tile_spec, row_spec, kv_spec


def attend(lengths, q, kv, lanes, size, hl):
    nh, nb = dims()
    each = q.shape[2] // lanes
    tiles = q.shape[0] * each
    tile_spec, row_spec, kv_spec = attend_specs(kv.shape[0], lanes, each)
    return pl.pallas_call(
        functools.partial(attend_body, nh, nb, hl, size),
        grid_spec=pltpu.PrefetchScalarGridSpec(
            num_scalar_prefetch=1,
            grid=(tiles,),
            in_specs=[tile_spec, kv_spec],
            out_specs=[tile_spec, tile_spec, row_spec],
        ),
        out_shape=(
            jax.ShapeDtypeStruct(q.shape, BF16),
            jax.ShapeDtypeStruct(q.shape, F32),
            jax.ShapeDtypeStruct((tiles, 1, lanes), F32),
        ),
        name="attend",
        compiler_params=pltpu.CompilerParams(vmem_limit_bytes=60 << 20),
    )(lengths, q, kv)


def attend_grad_body(nh, nb, hl, size, len_ref, q_ref, do_ref, of_ref, kv_ref, lse_ref, dq_ref, dkv_ref, acc_ref):
    tile = pl.program_id(0)

    @pl.when(tile == 0)
    def _():
        acc_ref[...] = jnp.zeros_like(acc_ref)

    q = q_ref[0]
    do = do_ref[0]
    lanes = q.shape[1]
    place = Queries(nh, nb, hl, len_ref, lanes, kv_ref.shape[0], size)
    zero = jnp.zeros_like(q)
    both = jnp.concatenate(
        [jnp.concatenate([q, zero], axis=0), jnp.concatenate([zero, do], axis=0)], axis=1
    )
    delta = jnp.sum(do.astype(F32) * of_ref[0], axis=0, keepdims=True)
    lse = lse_ref[0]

    def step(j, dq, masked):
        at = pl.ds(pl.multiple_of(j * size, size), size)
        kv = kv_ref[at, :]
        sd = jnp.dot(kv, both, preferred_element_type=F32)
        s, dp = sd[:, :lanes], sd[:, lanes:]
        power = s * EXP_SCALE - lse
        if masked:
            power = jnp.where(place.allowed(j), power, MASK_FLOOR)
        p = jnp.exp2(power)
        ds = (p * (dp - delta)).astype(BF16)
        acc_ref[at, :] += lax.dot_general(
            jnp.concatenate([ds, p.astype(BF16)], axis=1),
            both,
            (((1,), (1,)), ((), ())),
            preferred_element_type=F32,
        )
        return dq + lax.dot_general(
            kv, ds, (((0,), (0,)), ((), ())), preferred_element_type=F32
        )

    dq = place.walk(step, jnp.zeros((2 * DH, lanes), F32))
    dq_ref[0] = (dq[:DH] * 0.125).astype(BF16)

    @pl.when(tile == pl.num_programs(0) - 1)
    def _():
        lane = lax.broadcasted_iota(jnp.int32, (1, 2 * DH), 1)
        dkv_ref[...] = (acc_ref[...] * jnp.where(lane < DH, 0.125, 1.0)).astype(BF16)


def attend_grad(lengths, q, do, of, kv, lse, lanes, size, hl):
    nh, nb = dims()
    tiles = lse.size // lanes
    lse = lse.reshape(tiles, 1, lanes)
    tile_spec, row_spec, kv_spec = attend_specs(kv.shape[0], lanes, tiles // q.shape[0])
    return pl.pallas_call(
        functools.partial(attend_grad_body, nh, nb, hl, size),
        grid_spec=pltpu.PrefetchScalarGridSpec(
            num_scalar_prefetch=1,
            grid=(tiles,),
            in_specs=[tile_spec, tile_spec, tile_spec, kv_spec, row_spec],
            out_specs=[tile_spec, kv_spec],
            scratch_shapes=[pltpu.VMEM(kv.shape, F32)],
        ),
        out_shape=(jax.ShapeDtypeStruct(q.shape, BF16), jax.ShapeDtypeStruct(kv.shape, BF16)),
        name="attend_grad",
        compiler_params=pltpu.CompilerParams(vmem_limit_bytes=60 << 20),
    )(lengths, q, do, of, kv, lse)


class HeadSum:
    def __init__(self, nh, h, b, part, near, far, out, sems):
        self.nx = nh // 2
        self.x, self.c = h // 2, h % 2
        self.h, self.part, self.near, self.far, self.out = h, part, near, far, out
        sib = self.x * 2 + 1 - self.c
        self.pairs = [
            remote(
                part.at[((self.x + k) % self.nx) * 2 + 1 - self.c],
                near.at[k],
                sems.at[0, k],
                sems.at[1, k],
                sib,
                b,
            )
            for k in range(self.nx)
        ]
        self.across = [
            remote(
                out.at[k],
                far.at[k],
                sems.at[2, k],
                sems.at[3, k],
                ((self.x + k) % self.nx) * 2 + self.c,
                b,
            )
            for k in range(1, self.nx)
        ]

    @staticmethod
    def sem_shape(nh):
        return pltpu.SemaphoreType.DMA((4, nh // 2))

    @staticmethod
    def buffers(nh, rows, width):
        return [pltpu.VMEM((nh // 2, rows, width), BF16)] * 3

    def start(self):
        for k in list(range(1, self.nx)) + [0]:
            self.pairs[k].start()

    def send(self):
        for k in range(1, self.nx):
            self.pairs[k].wait_recv()
            at = ((self.x + k) % self.nx) * 2 + self.c
            self.out[k] = (self.part[at].astype(F32) + self.near[k].astype(F32)).astype(BF16)
            self.across[k - 1].start()

    def total(self):
        self.pairs[0].wait_recv()
        total = self.part[self.h].astype(F32) + self.near[0].astype(F32)
        for k in range(1, self.nx):
            self.across[k - 1].wait_recv()
            total = total + self.far[k].astype(F32)
        return total

    def finish(self):
        for cp in self.pairs:
            cp.wait_send()
        for cp in self.across:
            cp.wait_send()


def norm_of(values):
    centre = values - jnp.mean(values, axis=-1, keepdims=True)
    scale = lax.rsqrt(jnp.mean(centre * centre, axis=-1, keepdims=True) + NORM_EPS)
    return centre * scale, scale


def norm_pull(grad, normed, scale):
    one = jnp.mean(grad, axis=-1, keepdims=True)
    two = jnp.mean(grad * normed, axis=-1, keepdims=True)
    return scale * (grad - one - normed * two)


CHUNKS = 2


def chunk_of(ref, j, axis):
    size = ref.shape[axis] // CHUNKS
    at = pl.ds(j * size, size)
    return ref.at[at] if axis == 0 else ref.at[:, at]


def head_sums(nh, h, b, part, bufs, sems):
    near, far, out = bufs
    return [
        HeadSum(
            nh,
            h,
            b,
            chunk_of(part, j, 1),
            chunk_of(near, j, 1),
            chunk_of(far, j, 1),
            chunk_of(out, j, 1),
            sems.at[j],
        )
        for j in range(CHUNKS)
    ]


def head_gathers(nh, h, b, src, dst, sems):
    return [
        HeadGather(nh, h, b, chunk_of(src, j, 0), chunk_of(dst, j, 1), sems.at[j])
        for j in range(CHUNKS)
    ]


def chunk_sems(nh):
    return pltpu.SemaphoreType.DMA((CHUNKS, 4, nh // 2))


def mid_body(nh, nb, hl, io, o_ref, wo_ref, x_ref, wmb_ref, og, hid_ref, ng_ref, wmb_all, part, near, far, out, nbuf, osem, ssem, gsem, wsem):
    pc = Place(nh, nb, hl)
    h, b = pc.h, pc.b
    enter_with(pc, lambda zi: pc.attends(zi, h, pc.s % 2, pc.s // 2))
    rows, width = x_ref.shape
    outputs_back(pc, o_ref, og, osem, "start")
    sides = [
        remote(
            wmb_ref,
            wmb_all.at[:, :, pc.s],
            wsem.at[0, ds],
            wsem.at[1, ds],
            h,
            pc.zi * pc.qs + (pc.s + ds) % pc.qs,
        )
        for ds in range(1, pc.qs)
    ]
    sides.append(pltpu.make_async_copy(wmb_ref, wmb_all.at[:, :, pc.s], wsem.at[0, 0]))
    for cp in sides:
        cp.start()
    outputs_back(pc, o_ref, og, osem, "wait_send")
    for zi in range(pc.nz):
        wait_on(og.at[zi], osem.at[1, zi])
    io.put(0)
    io.need(1)
    wo = wo_ref[...]
    for i in range(nh):
        part[i] = lax.dot_general(
            og[:, i].reshape(pc.nz * DH, rows),
            wo,
            (((0,), (0,)), ((), ())),
            preferred_element_type=F32,
        ).astype(BF16)
    hss = head_sums(nh, h, b, part, (near, far, out), ssem)
    hgs = head_gathers(nh, h, b, nbuf, ng_ref, gsem)
    for hs in hss:
        hs.start()
    for hs in hss:
        hs.send()
    size = rows // CHUNKS
    io.need(2)
    for j, (hs, hg) in enumerate(zip(hss, hgs)):
        at = pl.ds(j * size, size)
        hid = x_ref[at, :].astype(F32) + hs.total()
        hid_ref[at, :] = hid
        nbuf[at, :] = norm_of(hid)[0].astype(BF16)
        hg.start()
    io.put(1)
    for hg in hgs:
        hg.pass_on()
    for hs, hg in zip(hss, hgs):
        hs.finish()
        hg.finish()
    for cp in sides:
        cp.wait()


def mid_exchange(ot, wo, x, wmb, hl):
    nh, nb = dims()
    rows, width = x.shape
    nz = hl
    return comm_call(
        functools.partial(mid_body, nh, nb, hl),
        "mid_exchange",
        2,
        (
            jax.ShapeDtypeStruct((nz, nh, DH, rows), BF16),
            jax.ShapeDtypeStruct(x.shape, F32),
            jax.ShapeDtypeStruct((nh, rows, width), BF16),
            jax.ShapeDtypeStruct((nh, nz, nb // nz) + wmb.shape[2:], BF16),
        ),
        [ANY] * 4,
        [ANY] * 4,
        [pltpu.VMEM((nh, rows, width), BF16)]
        + HeadSum.buffers(nh, rows, width)
        + [
            pltpu.VMEM((rows, width), BF16),
            pltpu.SemaphoreType.DMA((2, nz)),
            chunk_sems(nh),
            chunk_sems(nh),
            pltpu.SemaphoreType.DMA((2, nb // nz)),
        ],
        (ot, wo, x, wmb),
        vmem=60 << 20,
        late=(1, 2),
        early=(0, 1),
    )


def ffn_body(nh, nb, fl, split_rows, cut, len_ref, n_hbm, g_hbm, wa_hbm, wb_hbm, wc_hbm, y_hbm, d_hbm, ga_hbm, gb_hbm, n_ref, g_ref, w_ref, y_ref, d_ref, ga_ref, gb_ref, gy, mm, dz, stage, drain):
    rows, width = n_ref.shape[1], n_ref.shape[2]
    group = nh * rows
    total, zc, off = ff_widths(fl)
    wide = total - off
    shift = 2 * fl - off
    step = FF_BLOCKS * rows
    lane = lax.broadcasted_iota(jnp.int32, (1, wide), 1)
    real = lane < fl
    valid = sequence_ends(len_ref)[-1]
    blk = lax.axis_index("blk")
    loads = [
        pltpu.make_async_copy(n_hbm, n_ref, stage.at[0]),
        pltpu.make_async_copy(g_hbm, g_ref, stage.at[1]),
    ]
    for n, (w, (begin, end)) in enumerate(zip((wa_hbm, wb_hbm, wc_hbm), weight_parts(total))):
        dst = w_ref.at[:, pl.ds(begin, end - begin)]
        loads.append(pltpu.make_async_copy(w, dst, stage.at[2 + n]))
    for cp in loads:
        cp.start()
    for cp in loads:
        cp.wait()

    def out_rows(r):
        at = pl.ds(r * FF_BLOCKS, FF_BLOCKS)
        return [
            pltpu.make_async_copy(d_ref.at[at], d_hbm.at[at], drain.at[0, r]),
            pltpu.make_async_copy(y_ref.at[at], y_hbm.at[at], drain.at[1, r]),
        ]

    @pl.loop(0, group // step)
    def _(r):
        at = pl.ds(pl.multiple_of(r * step, step), step)
        n = n_ref[pl.ds(r * FF_BLOCKS, FF_BLOCKS)].reshape(step, width)
        row = lax.broadcasted_iota(jnp.int32, (step, 1), 0)
        slot = ((r * FF_BLOCKS + row // rows) * nb + blk) * rows + row % rows
        g = g_ref[pl.ds(r * FF_BLOCKS, FF_BLOCKS)].reshape(step, width)
        g = jnp.where(slot < valid, g.astype(F32), 0.0).astype(BF16)
        gy[at, :] = g
        z = jnp.dot(n, w_ref[:, :zc], preferred_element_type=F32)
        dm = lane_roll(jnp.dot(g, w_ref[:, off:], preferred_element_type=F32), -shift)
        gate, up = z[:, :wide], lane_roll(z, -fl)[:, :wide]
        cdf = 0.5 * (1.0 + lax.erf(gate * math.sqrt(0.5)))
        act = gate * cdf
        slope = cdf + gate * jnp.exp(-0.5 * gate * gate) * (1.0 / math.sqrt(2.0 * math.pi))
        m = lane_roll(jnp.where(real, act * up, 0.0), shift).astype(BF16)
        mm[at, :] = m
        d_gate = widen(jnp.where(real, dm * up * slope, 0.0), zc)
        d_up = lane_roll(widen(jnp.where(real, dm * act, 0.0), zc), fl)
        d = (d_gate + d_up).astype(BF16)
        dz[at, :] = d
        nt = (((1,), (1,)), ((), ()))
        dpart = lax.dot_general(d, w_ref[:, :zc], nt, preferred_element_type=F32)
        d_ref[pl.ds(r * FF_BLOCKS, FF_BLOCKS)] = dpart.astype(BF16).reshape(FF_BLOCKS, rows, width)
        ypart = lax.dot_general(m, w_ref[:, off:], nt, preferred_element_type=F32)
        y_ref[pl.ds(r * FF_BLOCKS, FF_BLOCKS)] = ypart.astype(BF16).reshape(FF_BLOCKS, rows, width)
        for cp in out_rows(r):
            cp.start()

    block = width // nh

    def out_block(i):
        at = (slice(None), i) if split_rows else (pl.ds(i * block, block),)
        return [
            pltpu.make_async_copy(ga_ref.at[i], ga_hbm.at[at], drain.at[2, i]),
            pltpu.make_async_copy(gb_ref.at[i], gb_hbm.at[at], drain.at[3, i]),
        ]

    @pl.loop(0, nh)
    def _(i):
        cols = pl.ds(pl.multiple_of(i * block, block), block)
        tn = (((0,), (0,)), ((), ()))
        n = n_ref[:, :, cols].reshape(group, block)
        g_in = lax.dot_general(n, dz[...], tn, preferred_element_type=F32)
        g_down = lax.dot_general(gy[:, cols], mm[...], tn, preferred_element_type=F32)
        both = jnp.concatenate(
            [g_in[:, :off], g_in[:, off:] + g_down[:, : zc - off], g_down[:, zc - off :]], axis=1
        ).astype(BF16)
        for ref, part in ((ga_ref, both[:, :cut]), (gb_ref, both[:, cut:])):
            if split_rows:
                part = part.reshape(nb, block // nb, part.shape[1])
            ref[i] = part
        for cp in out_block(i):
            cp.start()

    @pl.loop(0, nh)
    def _(i):
        for cp in out_block(i):
            cp.wait()

    @pl.loop(0, group // step)
    def _(r):
        for cp in out_rows(r):
            cp.wait()


def ffn(lengths, n2, g, weights, fl, own_rows, cut):
    nh, nb = dims()
    _, rows, width = n2.shape
    group = nh * rows
    total, zc, off = ff_widths(fl)
    split_rows = own_rows % 16 == 0
    lead = (nb, nh, own_rows) if split_rows else (width,)
    held = (nh, nb, own_rows) if split_rows else (nh, width // nh)
    return pl.pallas_call(
        functools.partial(ffn_body, nh, nb, fl, split_rows, cut),
        out_shape=(
            jax.ShapeDtypeStruct(n2.shape, BF16),
            jax.ShapeDtypeStruct(n2.shape, BF16),
            jax.ShapeDtypeStruct(lead + (cut,), BF16),
            jax.ShapeDtypeStruct(lead + (total - cut,), BF16),
        ),
        in_specs=[SM] + [ANY] * 5,
        out_specs=[ANY] * 4,
        scratch_shapes=[
            pltpu.VMEM(n2.shape, BF16),
            pltpu.VMEM(n2.shape, BF16),
            pltpu.VMEM((width, total), BF16),
            pltpu.VMEM(n2.shape, BF16),
            pltpu.VMEM(n2.shape, BF16),
            pltpu.VMEM(held + (cut,), BF16),
            pltpu.VMEM(held + (total - cut,), BF16),
            pltpu.VMEM((group, width), BF16),
            pltpu.VMEM((group, total - off), BF16),
            pltpu.VMEM((group, zc), BF16),
            pltpu.SemaphoreType.DMA((5,)),
            pltpu.SemaphoreType.DMA((4, nh)),
        ],
        name="ffn",
        compiler_params=pltpu.CompilerParams(vmem_limit_bytes=60 << 20),
    )(lengths, n2, g, *weights)


def back_body(nh, nb, hl, io, len_ref, dpart, ypart, hid_ref, g_ref, wo_ref, og_ref, gb_hbm, y_ref, dh_ref, do_in, go_ref, gb_out, n1, f1, o1, n2, f2, o2, dbuf, dg, dots, gb_ref, nearb, s1, s2, gsem, qsem, pb, stage):
    pc = Place(nh, nb, hl)
    h, b = pc.h, pc.b
    mine = pltpu.make_async_copy(gb_hbm.at[:, pc.s], gb_ref, stage)
    mine.start()
    enter_with(pc, lambda zi: (pc.head, zi * pc.qs + pc.from_s))
    pairs = [
        remote(
            gb_hbm.at[:, (pc.s + ds) % pc.qs],
            nearb.at[ds - 1],
            pb.at[0, ds],
            pb.at[1, ds],
            h,
            pc.zi * pc.qs + (pc.s + ds) % pc.qs,
        )
        for ds in range(1, pc.qs)
    ]
    rows, width = hid_ref.shape
    slot = (h * nb + b) * rows + lax.broadcasted_iota(jnp.int32, (rows, 1), 0)
    valid = slot < sequence_ends(len_ref)[-1]
    hds = head_sums(nh, h, b, dpart, (n1, f1, o1), s1)
    hy = HeadSum(nh, h, b, ypart, n2, f2, o2, s2)
    hgs = head_gathers(nh, h, b, dbuf, dg, gsem)
    io.need(1)
    for hd in hds:
        hd.start()
    for cp in pairs:
        cp.start()
    for hd in hds:
        hd.send()
    size = rows // CHUNKS
    io.need(3, 4)
    for j, (hd, hg) in enumerate(zip(hds, hgs)):
        at = pl.ds(j * size, size)
        normed, scale = norm_of(hid_ref[at, :])
        gy = jnp.where(valid[j * size : (j + 1) * size], g_ref[at, :].astype(F32), 0.0)
        dh = gy + norm_pull(hd.total(), normed, scale)
        dh_ref[at, :] = dh
        dbuf[at, :] = dh.astype(BF16)
        hg.start()
    io.put(1)
    io.need(2)
    hy.start()
    io.need(5)
    wo = wo_ref[...]
    nt = (((1,), (1,)), ((), ()))

    def emit(i):
        part = lax.dot_general(wo, dg[i], nt, preferred_element_type=F32).astype(BF16)
        dots[:, i] = part.reshape(pc.nz, DH, rows)
        grads_out(pc, dots, do_in, qsem, i, "start")

    nx = nh // 2
    for hg in hgs:
        hg.local.wait()
        hg.near.wait_recv()
    emit(h)
    emit(pc.sib)
    for hg in hgs:
        hg.pass_on()
    for k in range(1, nx):
        emit(((pc.x + nx - k) % nx) * 2 + pc.c)
    hy.send()
    for hg in hgs:
        for cp in hg.forward:
            cp.wait_recv()
    for k in range(1, nx):
        emit(((pc.x + nx - k) % nx) * 2 + 1 - pc.c)
    for hd, hg in zip(hds, hgs):
        hd.finish()
        hg.near.wait_send()
        for cp in hg.across + hg.forward:
            cp.wait_send()
    total = 0.0
    io.need(6)
    for i in range(nh):
        total = total + jnp.dot(
            og_ref[:, i].reshape(pc.nz * DH, rows), dg[i], preferred_element_type=F32
        )
    go_ref[...] = total.astype(BF16)
    io.put(3)
    y_ref[...] = jnp.where(valid, hid_ref[...] + hy.total(), 0.0)
    io.put(0)
    hy.finish()
    mine.wait()
    for cp in pairs:
        cp.wait()

    @pl.loop(0, pc.nz)
    def _(d):
        others = jnp.sum(nearb[:, d].astype(F32), axis=0)
        gb_out[d] = (gb_ref[d].astype(F32) + others).astype(BF16)

    io.put(4)

    @pl.loop(0, nh)
    def _(i):
        grads_out(pc, dots, do_in, qsem, i, "wait_send")
        for zi in range(pc.nz):
            wait_on(stretch_of(do_in, i, zi, rows), qsem.at[1, zi, i])


def back_exchange(lengths, dpart, ypart, hid, g, wo, og, gb):
    nh, nb = dims()
    rows, width = hid.shape
    nz = hl = og.shape[0]
    return comm_call(
        functools.partial(back_body, nh, nb, hl),
        "back_exchange",
        3,
        (
            jax.ShapeDtypeStruct(hid.shape, F32),
            jax.ShapeDtypeStruct(hid.shape, F32),
            jax.ShapeDtypeStruct((nh, DH, nz * rows), BF16),
            jax.ShapeDtypeStruct((nz * DH, width), BF16),
            jax.ShapeDtypeStruct(gb.shape[:1] + gb.shape[2:], BF16),
        ),
        [SM] + [VM] * 6 + [ANY],
        [VM, VM, ANY, VM, VM],
        HeadSum.buffers(nh, rows, width)
        + HeadSum.buffers(nh, rows, width)
        + [
            pltpu.VMEM((rows, width), BF16),
            pltpu.VMEM((nh, rows, width), BF16),
            pltpu.VMEM(og.shape, BF16),
            pltpu.VMEM(gb.shape[:1] + gb.shape[2:], BF16),
            pltpu.VMEM((gb.shape[1] - 1, nz) + gb.shape[2:], BF16),
            chunk_sems(nh),
            HeadSum.sem_shape(nh),
            chunk_sems(nh),
            pltpu.SemaphoreType.DMA((2, nz, nh)),
            pltpu.SemaphoreType.DMA((2, gb.shape[1])),
            pltpu.SemaphoreType.DMA,
        ],
        (lengths, dpart, ypart, hid, g, wo, og, gb),
        vmem=60 << 20,
        late=(1, 3, 4, 2, 5, 6),
        early=(0, 1, 3, 4),
    )


def grads_back_body(nh, nb, hl, io, dq_ref, dkv_ref, cos_ref, sin_ref, n1_hbm, w_hbm, go_ref, gb_ref, gq_ref, dpart, do_ref, gb_sum, got, sums, dq_out, dkv_out, dqkv, n1_ref, w_ref, nearo, sumo, goto, lsem, gotb, bsem, qsem, psem, ksem, stage, po):
    pc = Place(nh, nb, hl)
    loads = [
        pltpu.make_async_copy(n1_hbm, n1_ref, stage.at[0]),
        pltpu.make_async_copy(w_hbm, w_ref, stage.at[1]),
    ]
    for cp in loads:
        cp.start()
    signal_near(pc)
    wait_near(pc)
    rows = dkv_ref.shape[3]
    group = pc.nz * rows
    width = n1_ref.shape[1]
    lw = nh * DH
    count = nh * pc.cb

    def pair(k):
        src = dkv_ref.at[k // pc.cb, :, 2 * (k % pc.cb) + 1 - pc.c]
        return remote(src, got.at[k], psem.at[0, k], psem.at[1, k], pc.sib, pc.b)

    def back(k, act):
        routed(
            pc,
            sums.at[k],
            dkv_out.at[pc.head, pc.u],
            ksem.at[0, k],
            ksem.at[1, pc.head * pc.cb + pc.u],
            k // pc.cb,
            pc.zi * pc.qs + 2 * (k % pc.cb) + pc.c,
            act,
        )

    def queries_back(act):
        for i in range(nh):
            routed(
                pc,
                dq_ref.at[i],
                dq_out.at[pc.head],
                qsem.at[0, i],
                qsem.at[1, pc.head],
                i,
                pc.zi * pc.qs + pc.from_s,
                act,
            )

    pairs_o = [
        remote(
            go_ref.at[:, (pc.s + ds) % pc.qs],
            nearo.at[ds - 1],
            po.at[0, ds],
            po.at[1, ds],
            pc.h,
            pc.zi * pc.qs + (pc.s + ds) % pc.qs,
        )
        for ds in range(1, pc.qs)
    ]
    along_o = StretchSum(pc, sumo, goto, lsem)
    along_b = StretchSum(pc, gb_ref, gotb, bsem)

    io.need(1)

    @pl.loop(0, count)
    def _(k):
        pair(k).start()

    queries_back("start")
    io.need(6, 7)
    for cp in pairs_o:
        cp.start()
    along_b.start()

    @pl.loop(0, count)
    def _(k):
        pair(k).wait_recv()
        mine = dkv_ref[k // pc.cb, :, 2 * (k % pc.cb) + pc.c]
        sums[k] = (mine.astype(F32) + got[k].astype(F32)).astype(BF16)
        back(k, "start")

    for cp in pairs_o:
        cp.wait_recv()
    sumo[...] = (go_ref[:, pc.s].astype(F32) + jnp.sum(nearo[...].astype(F32), axis=0)).astype(BF16)
    along_o.start()
    io.need(2, 3)
    cos, sin = cos_ref[...], -sin_ref[...]
    for l in range(nh):
        wait_on(dq_out.at[l], qsem.at[1, l])
    for p in range(nh // 2):
        q = dq_out[2 * p : 2 * p + 2].reshape(2 * DH, group).astype(F32).T
        dqkv[:, p * 128 : (p + 1) * 128] = turned(q, cos, sin).astype(BF16)
    for l in range(nh):
        for u in range(pc.cb):
            wait_on(dkv_out.at[l, u], ksem.at[1, l * pc.cb + u])
    for p in range(nh // 2):
        even, odd = [
            jnp.sum(dkv_out[2 * p + i].astype(F32), axis=0).reshape(group, 2 * DH)
            for i in range(2)
        ]
        low = lanes_of(even) < DH
        k = jnp.where(low, even, lane_roll(odd, DH)).astype(BF16).astype(F32)
        v = jnp.where(low, lane_roll(even, DH), odd)
        dqkv[:, lw + p * 128 : lw + (p + 1) * 128] = turned(k, cos, sin).astype(BF16)
        dqkv[:, 2 * lw + p * 128 : 2 * lw + (p + 1) * 128] = v.astype(BF16)
    nt = (((1,), (1,)), ((), ()))
    tn = (((0,), (0,)), ((), ()))
    for cp in loads:
        cp.wait()

    @pl.loop(0, nh)
    def _(i):
        cols = pl.ds(pl.multiple_of(i * (width // nh), width // nh), width // nh)
        gq_ref[cols, :] = lax.dot_general(
            n1_ref[:, cols], dqkv[...], tn, preferred_element_type=F32
        ).astype(BF16)

    io.put(0)

    @pl.loop(0, pc.nz)
    def _(i):
        at = pl.ds(pl.multiple_of(i * rows, rows), rows)
        dpart[i] = lax.dot_general(
            dqkv[at, :], w_ref[...], nt, preferred_element_type=F32
        ).astype(BF16)

    io.put(1)

    @pl.loop(0, count)
    def _(k):
        pair(k).wait_send()
        back(k, "wait_send")

    queries_back("wait_send")
    do_ref[...] = along_o.total()
    io.put(2)
    gb_sum[...] = along_b.total().astype(BF16)
    io.put(3)
    along_o.finish()
    along_b.finish()
    for cp in pairs_o:
        cp.wait_send()


def grads_back(dq, dkv, cos, sin, n1, wq, go, gb, hl):
    nh, nb = dims()
    nz, qs = hl, nb // hl
    cb = qs // 2
    rows = dkv.shape[3]
    width = n1.shape[1]
    lw = nh * DH
    dma = pltpu.SemaphoreType.DMA
    return comm_call(
        functools.partial(grads_back_body, nh, nb, hl),
        "grads_back",
        4,
        (
            jax.ShapeDtypeStruct((width, 3 * lw), BF16),
            jax.ShapeDtypeStruct((nz, rows, width), BF16),
            jax.ShapeDtypeStruct(go.shape[2:], F32),
            jax.ShapeDtypeStruct(gb.shape[1:], BF16),
        ),
        [ANY, VM, VM, VM, ANY, ANY, VM, VM],
        [VM] * 4,
        [
            pltpu.VMEM((nh * cb, nz, rows, 2 * DH), BF16),
            pltpu.VMEM((nh * cb, nz, rows, 2 * DH), BF16),
            pltpu.VMEM(dq.shape, BF16),
            pltpu.VMEM((nh, cb, nz, rows, 2 * DH), BF16),
            pltpu.VMEM((nz * rows, 3 * lw), BF16),
            pltpu.VMEM(n1.shape, BF16),
            pltpu.VMEM(wq.shape, BF16),
            pltpu.VMEM((qs - 1, nz) + go.shape[2:], BF16),
            pltpu.VMEM((nz,) + go.shape[2:], BF16),
        ]
        + StretchSum.scratch(nz, go.shape[2:])
        + StretchSum.scratch(nz, gb.shape[1:])
        + [
            dma((2, nh)),
            dma((2, nh * cb)),
            dma((2, nh * cb)),
            dma((2,)),
            dma((2, qs)),
        ],
        (dq, dkv, cos, sin, n1, wq, go, gb),
        vmem=60 << 20,
        late=(1, 6, 7, 2, 3),
        early=(0, 1, 2, 3),
    )


def last_body(nh, nb, hl, io, dpart, gq_ref, gma_ref, gmb_ref, dn_ref, quarters, gma_all, gmb_all, nearq, sumq, farq, totq, sentz, gotz, zsem, pq, fq, cq, msem, asem):
    pc = Place(nh, nb, hl)
    h, b = pc.h, pc.b
    signal_near(pc)
    wait_near(pc)
    nx, nz, qs = nh // 2, pc.nz, pc.qs
    def pair_q(k):
        return remote(
            gq_ref.at[2 * k + 1 - pc.c], nearq.at[k], pq.at[0, k], pq.at[1, k], pc.sib, b
        )

    line = LineSum(pc, lambda d: dpart[d].astype(F32), sentz, gotz, zsem)

    def plane_q(i):
        tx, ts = (pc.x + i // qs) % nx, (pc.s + i % qs) % qs
        return remote(
            sumq.at[tx, :, ts],
            farq.at[pc.x, pc.s],
            fq.at[0, i],
            fq.at[1, i],
            tx * 2 + pc.c,
            pc.zi * qs + ts,
        )

    def quarter(i):
        to = (pc.zi + i) % nz
        return remote(
            totq.at[to], quarters.at[pc.zi], cq.at[0, i], cq.at[1, i], h, to * qs + pc.s
        )

    io.need(1)
    for k in range(nx):
        pair_q(k).start()
    io.need(0)
    line.lead(0)
    moves = [
        remote(
            gmb_ref.at[(h + i) % nh],
            gmb_all.at[h],
            msem.at[0, i],
            msem.at[1, i],
            (h + i) % nh,
            b,
        )
        for i in range(1, nh)
    ]
    moves.append(pltpu.make_async_copy(gmb_ref.at[h], gmb_all.at[h], msem.at[0, 0]))
    moves.append(
        pltpu.make_async_copy(gma_ref.at[pc.s, h], gma_all.at[pc.s, h], asem.at[0, 0])
    )

    def plane_move(i):
        th, ts = (h + i // qs) % nh, (pc.s + i % qs) % qs
        return remote(
            gma_ref.at[ts, th],
            gma_all.at[pc.s, h],
            asem.at[0, i],
            asem.at[1, i],
            th,
            pc.zi * qs + ts,
        )

    for k in range(nx):
        pair_q(k).wait_recv()
        sumq[k] = (gq_ref[2 * k + pc.c].astype(F32) + nearq[k].astype(F32)).astype(BF16)

    @pl.loop(1, nx * qs)
    def _(i):
        plane_q(i).start()

    farq[pc.x, pc.s] = sumq[pc.x, :, pc.s]
    for cp in moves:
        cp.start()

    @pl.loop(1, nh * qs)
    def _(i):
        plane_move(i).start()

    line.follow(0)
    line.lead(1)

    @pl.loop(1, nx * qs)
    def _(i):
        plane_q(i).wait_recv()

    totq[...] = jnp.sum(
        farq[...].astype(F32).reshape((nx * qs,) + totq.shape), axis=0
    ).astype(BF16)
    for i in range(1, nz):
        quarter(i).start()
    quarters[pc.zi] = totq[pc.zi]
    for j in range(1, nz - 1):
        line.follow(j)
        if j + 1 < nz - 1:
            line.lead(j + 1)
    line.total(dn_ref)
    io.put(0)
    line.finish()
    for i in range(1, nz):
        quarter(i).wait()
    io.put(1)
    for cp in moves:
        cp.wait()

    @pl.loop(1, nh * qs)
    def _(i):
        plane_move(i).wait()

    for k in range(nx):
        pair_q(k).wait_send()

    @pl.loop(1, nx * qs)
    def _(i):
        plane_q(i).wait_send()


def last_exchange(dpart, gq, gma, gmb):
    nh, nb = dims()
    nz, rows, width = dpart.shape
    qs = nb // nz
    own_rows, cols = gq.shape[3:]
    nx = nh // 2
    dma = pltpu.SemaphoreType.DMA
    return comm_call(
        functools.partial(last_body, nh, nb, nz),
        "last_exchange",
        5,
        (
            jax.ShapeDtypeStruct((rows, width), F32),
            jax.ShapeDtypeStruct((nz, own_rows, cols), BF16),
            jax.ShapeDtypeStruct(gma.shape, BF16),
            jax.ShapeDtypeStruct(gmb.shape, BF16),
        ),
        [VM] * 2 + [ANY] * 2,
        [VM] * 2 + [ANY] * 2,
        [
            pltpu.VMEM((nx, nz, qs, own_rows, cols), BF16),
            pltpu.VMEM((nx, nz, qs, own_rows, cols), BF16),
            pltpu.VMEM((nx, qs, nz, own_rows, cols), BF16),
            pltpu.VMEM((nz, own_rows, cols), BF16),
        ]
        + LineSum.scratch(nz, (rows, width))
        + [
            dma((2, nx)),
            dma((2, nx * qs)),
            dma((2, nz)),
            dma((2, nh)),
            dma((2, nh * qs)),
        ],
        (dpart, gq, gma, gmb),
        vmem=60 << 20,
        late=(1, 0),
        early=(0, 1),
    )


def finish_body(nh, fl, dn_ref, x_ref, dh_ref, y_in, quarters, do_in, gma, gmb, wq_ref, win_ref, ga_ref, gf_ref,
                y_ref, dx_ref, lna_ref, dq_ref, do_ref, lnm_ref, din_ref, dwd_ref):
    y_ref[...] = y_in[...]
    do_ref[...] = do_in[...]
    normed, scale = norm_of(x_ref[...].astype(F32))
    dx_ref[...] = dh_ref[...] + norm_pull(dn_ref[...], normed, scale)
    width = x_ref.shape[1]
    gain = column(ga_ref[...].astype(F32))
    nz = quarters.shape[0]
    rowsum = 0.0
    for c in range(3):
        for l in range(nh):
            src = (c * nh * DH + l // 2 * 128) // 128 * 128
            for p in range(nz // 2):
                tiles = [quarters[2 * p + i, :, src : src + 128].astype(F32) for i in range(2)]
                piece = half_pick(tiles[0], tiles[1], l % 2, l % 2)
                at = c * width + l * nz * DH + p * 128
                dq_ref[:, at : at + 128] = piece * gain
                rowsum = rowsum + jnp.sum(
                    piece * wq_ref[:, at : at + 128].astype(F32), axis=1, keepdims=True
                )
    lna_ref[...] = as_row(rowsum)
    ff = nh * fl
    total, _, _ = ff_widths(fl)
    tiles = lambda v: (v + 127) // 128 * 128
    gate_up, down = 0.0, 0.0
    for i in range(nh):
        first = jnp.sum(gma[:, i].astype(F32), axis=0)
        piece = jnp.concatenate([first, gmb[i].astype(F32)], axis=1)
        lane = lanes_of(piece)
        gate = widen(jnp.where(lane < fl, piece, 0.0), tiles(2 * ff))
        up = jnp.where(jnp.logical_and(lane >= fl, lane < 2 * fl), piece, 0.0)
        up = widen(up, tiles(2 * ff))
        gate_up = gate_up + lane_roll(gate, i * fl) + lane_roll(up, ff - fl + i * fl)
        dn = jnp.where(jnp.logical_and(lane >= 2 * fl, lane < 3 * fl), piece, 0.0)
        down = down + lane_roll(widen(dn, max(total, tiles(ff))), i * fl - 2 * fl)
    gate_up = gate_up[:, : 2 * ff]
    dwd_ref[...] = down[:, :ff]
    din_ref[...] = gate_up * column(gf_ref[...].astype(F32))
    lnm_ref[...] = as_row(jnp.sum(gate_up * win_ref[...].astype(F32), axis=1, keepdims=True))


def finish(dn, x, dh, y, quarters, d_wout, gma, gmb, w_qkv, w_in, gain_attn, gain_mlp, fl):
    nh, _ = dims()
    rows, width = x.shape
    own_rows = w_qkv.shape[0]
    ff = nh * fl
    f32 = lambda *shape: jax.ShapeDtypeStruct(shape, F32)
    return pl.pallas_call(
        functools.partial(finish_body, nh, fl),
        out_shape=(
            f32(rows, width),
            f32(rows, width),
            f32(1, own_rows),
            f32(own_rows, 3 * width),
            f32(own_rows, width),
            f32(1, own_rows),
            f32(own_rows, 2 * ff),
            f32(own_rows, ff),
        ),
        in_specs=[VM] * 12,
        out_specs=[VM] * 8,
        name="finish",
        compiler_params=pltpu.CompilerParams(vmem_limit_bytes=60 << 20),
    )(dn, x, dh, y, quarters, d_wout, gma, gmb, w_qkv, w_in, gain_attn, gain_mlp)


def shards(layer_input, out_grad, lengths, ln_attn, w_qkv, w_attn_out, ln_mlp, w_in, w_mlp_out):
    nh, nb = dims()
    h, b = me()
    rows, width = layer_input.shape
    heads = width // DH
    hl = heads // nh
    group = nh * rows
    slots = nh * nb * rows
    own_rows = w_qkv.shape[0]
    ff = w_mlp_out.shape[0]
    fl = ff // nh
    nz, qs = hl, nb // hl
    lw = nh * DH

    gain_attn = ln_attn.reshape(1, own_rows)
    gain_mlp = ln_mlp.reshape(1, own_rows)
    n1, wma, wmb, wmc, wq, gg, cos, sin = first_exchange(
        lengths, layer_input, w_qkv, gain_attn, w_in, gain_mlp, w_mlp_out.T, out_grad, hl, fl
    )
    wma = lax.all_gather(wma, "blk", axis=1, tiled=True).reshape(width, -1)
    wq = wq.reshape(width, 3 * lw)
    n1 = n1.reshape(group, width)
    qin, kvin, wo, wmb, wmc = to_heads(n1, wq, cos, sin, w_attn_out[None], wmb, wmc, hl)
    wo = wo.reshape(nz * DH, width)
    kv_all = kvin.reshape(slots, 2 * DH)
    ot, of, lse = attend(lengths, qin, kv_all, 4 * rows, 1024, hl)
    og, hid, n2, wmc = mid_exchange(ot, wo, layer_input, wmc, hl)
    weights = [w.reshape(width, -1) for w in (wma, wmb, wmc)]
    ypart, dpart, gma, gmb = ffn(lengths, n2, gg, weights, fl, own_rows, GRAD_CUT)
    by_owner = []
    for gm in (gma, gmb):
        if gm.ndim == 4:
            gm = gm.reshape((nz, qs) + gm.shape[1:])
        else:
            gm = gm.reshape(nh, nz, qs, own_rows, gm.shape[1]).transpose(1, 2, 0, 3, 4)
        by_owner.append(gm)
    gma, gmb = by_owner
    lines = [[zi * qs + s for zi in range(nz)] for s in range(qs)]
    gma = lax.psum_scatter(
        gma, "blk", scatter_dimension=0, tiled=True, axis_index_groups=lines
    ).reshape(gma.shape[1:])
    y_out, dh, do_in, go, gmb = back_exchange(
        lengths, dpart, ypart, hid, out_grad, wo, og, gmb
    )
    dq, dkv = attend_grad(lengths, qin, do_in, of, kv_all, lse, 2 * rows, 1024, hl)
    go = go.reshape(nz, qs, own_rows, width)
    gq, dpart1, d_wout, gmb = grads_back(
        dq, dkv.reshape(kvin.shape), cos, sin, n1, wq, go, gmb, hl
    )
    dn, quarters, gma, gmb = last_exchange(
        dpart1, gq.reshape(nh, nz, qs, own_rows, 3 * lw), gma, gmb
    )
    y_out, dx, d_ln_attn, d_wqkv, d_wout, d_ln_mlp, d_win, d_wd = finish(
        dn,
        layer_input,
        dh,
        y_out,
        quarters,
        d_wout,
        gma,
        gmb,
        w_qkv,
        w_in,
        gain_attn,
        gain_mlp,
        fl,
    )
    return (
        y_out,
        dx,
        d_ln_attn.reshape(own_rows),
        d_wqkv,
        d_wout,
        d_ln_mlp.reshape(own_rows),
        d_win,
        d_wd.T,
    )


def solution(mesh):
    both = ("head", "blk")
    row_split = P(both, None)
    return jax.shard_map(
        shards,
        mesh=mesh,
        in_specs=(
            row_split,
            row_split,
            P(),
            P(both),
            row_split,
            row_split,
            P(both),
            row_split,
            P(None, both),
        ),
        out_specs=(
            row_split,
            row_split,
            P(both),
            row_split,
            row_split,
            P(both),
            row_split,
            P(None, both),
        ),
        check_vma=False,
    )
```
